32 devices in a mesh: batch: 4 (over x, core), seq: 8 (over z, y).
Axes of the slice: x: 2, y: 2, z: 4, core: 2. Of those that a mesh axis runs over, the one named last changes fastest.
Arguments:
- inputs: bfloat16 [4, 1024, 768], P('batch', 'seq'), may hold values from -6 to 6
- pre_gain: bfloat16 [768], replicated, may hold values from 0.5 to 1.5
- pre_bias: bfloat16 [768], replicated, may hold values from -1.75 to 1.75
- in_weight: bfloat16 [768, 2304], replicated, may hold values from -0.21875 to 0.21875
- input_projection_bias: bfloat16 [2304], replicated, may hold values from -1.75 to 1.75
- short_weight: bfloat16 [3, 2304], replicated, may hold values from -3.5 to 3.5
- short_bias: bfloat16 [2304], replicated, may hold values from -1.75 to 1.75
- pos_weight: bfloat16 [33, 64], replicated, may hold values from -1 to 1
- pos_bias: bfloat16 [64], replicated, may hold values from -3 to 3
- inner_weight: bfloat16 [64, 64], replicated, may hold values from -0.75 to 0.75
- inner_bias: bfloat16 [64], replicated, may hold values from -3 to 3
- filter_third_weight: bfloat16 [64, 64], replicated, may hold values from -0.75 to 0.75
- third_bias: bfloat16 [64], replicated, may hold values from -3 to 3
- sine_freq: bfloat16 [64], replicated, may hold values from 0.5 to 1.5
- filter_weight: bfloat16 [2, 64, 768], replicated, may hold values from -0.09375 to 0.09375
- decay_rates: float32 [2, 768], replicated, may hold values from 0.5 to 32
- skip_gains: bfloat16 [2, 768], replicated, may hold values from -6 to 6
- out_weight: bfloat16 [768, 768], replicated, may hold values from -0.21875 to 0.21875
- out_bias: bfloat16 [768], replicated, may hold values from -1.75 to 1.75
- post_gain: bfloat16 [768], replicated, may hold values from 0.5 to 1.5
- post_bias: bfloat16 [768], replicated, may hold values from -1.75 to 1.75
- up_weight: bfloat16 [768, 3072], replicated, may hold values from -0.21875 to 0.21875
- up_bias: bfloat16 [3072], replicated, may hold values from -1.75 to 1.75
- down_weight: bfloat16 [3072, 768], replicated, may hold values from -0.109375 to 0.109375
- down_bias: bfloat16 [768], replicated, may hold values from -1.75 to 1.75
- cotangent: bfloat16 [4, 1024, 768], P('batch', 'seq'), may hold values from -6 to 6
Outputs:
- outputs: float32 [4, 1024, 768], P('batch', 'seq')
- grad_inputs: float32 [4, 1024, 768], P('batch', 'seq')
- grad_pre_gain: float32 [768], replicated
- grad_pre_bias: float32 [768], replicated
- grad_in_weight: float32 [768, 2304], P('seq')
- grad_in_bias: float32 [2304], replicated
- grad_short_weight: float32 [3, 2304], replicated
- grad_short_bias: float32 [2304], replicated
- grad_pos_weight: float32 [33, 64], replicated
- grad_pos_bias: float32 [64], replicated
- grad_inner_weight: float32 [64, 64], replicated
- grad_inner_bias: float32 [64], replicated
- grad_third_weight: float32 [64, 64], replicated
- grad_third_bias: float32 [64], replicated
- grad_sine_freq: float32 [64], replicated
- grad_filter_weight: float32 [2, 64, 768], P(None, None, 'seq')
- grad_decay_rates: float32 [2, 768], P(None, 'seq')
- grad_skip_gains: float32 [2, 768], P(None, 'seq')
- grad_out_weight: float32 [768, 768], P('seq')
- grad_out_bias: float32 [768], replicated
- grad_post_gain: float32 [768], replicated
- grad_post_bias: float32 [768], replicated
- up_weight_gradient: float32 [768, 3072], P('seq')
- grad_up_bias: float32 [3072], replicated
- grad_down_weight: float32 [3072, 768], P('seq')
- grad_down_bias: float32 [768], replicated
The draws below stay inside these ranges and needn't reach their ends.
All inputs are finite; a program needn't handle non-finite values.
Results may differ from the reference program's by a relative error of at most 0.013.
Values may be sent and summed in bfloat16 or wider, within the bound.
No kernel may reach another device: no remote copies, remote signals or barrier semaphores. Data moves between devices by JAX's collectives and lax.ppermute only.
A program may use at most 192 MiB of HBM per device.

```python
import math
import jax
import jax.numpy as jnp
from jax import lax

D = 768
FF = 3072
EMB = 33
FHID = 64
SEQS = 4
LENGTH = 1024


def spiked(entries, rng, source, target, shards_of, factor):
    owner, partner = [(jnp.arange(entries.shape[position]) // (entries.shape[position] // shards_of)).reshape([-1 if axis == position else 1 for axis in range(entries.ndim)]) for position in (source, target)]
    chosen = jax.random.permutation(rng, shards_of)[partner]
    strong = (owner == chosen) | (owner == (partner + shards_of // 2) % shards_of)
    return jnp.where(strong, factor * entries, entries)


def block_scale(rng, dims, pieces, least, largest):
    gain, own = 1.0, jax.random.fold_in(rng, 6)
    for position, parts in pieces:
        draws = jnp.exp(jax.random.uniform(jax.random.fold_in(own, position), (parts,), jnp.float32, least / len(pieces), largest / len(pieces)))
        gain = gain * jnp.repeat(draws, dims[position] // parts).reshape([-1 if axis == position else 1 for axis in range(len(dims))])
    return gain


def normal_values(key, shape, width, reach, pieces=(), held_as=jnp.bfloat16):
    values = width * jax.random.normal(key, shape, jnp.float32)
    if pieces:
        values = values * block_scale(key, shape, pieces, -0.22, 0.18)
    return jnp.clip(values, -reach, reach).astype(held_as)


def gaussian_with(stream_key, shape, width, limit, cuts, heavy, held_as=jnp.bfloat16):
    drawn = width * jax.random.normal(stream_key, shape, jnp.float32)
    if cuts:
        drawn = drawn * block_scale(stream_key, shape, cuts, -0.22, 0.18)
    return jnp.clip(spiked(drawn, jax.random.fold_in(stream_key, 3), *heavy), -limit, limit).astype(held_as)


def setup_inputs(seed: int = 0) -> dict:
    arg_keys = jax.random.split(jax.random.key(seed), 27)
    inputs = gaussian_with(arg_keys[0], (SEQS, LENGTH, D), 1.0, 6.0, ((0, 4), (1, 8)), (1, 2, 8, 2.0))
    pre_gain = jnp.clip(1.0 + 0.1 * jax.random.normal(arg_keys[1], (D,), jnp.float32), 0.5, 1.5).astype(jnp.bfloat16)
    pre_bias = normal_values(arg_keys[2], (D,), 0.3, 1.75)
    in_weight = normal_values(arg_keys[3], (D, 3 * D), D ** -0.5, 0.21875)
    input_projection_bias = normal_values(arg_keys[4], (3 * D,), 0.3, 1.75)
    short_weight = normal_values(arg_keys[5], (3, 3 * D), 0.6, 3.5)
    short_bias = normal_values(arg_keys[6], (3 * D,), 0.3, 1.75)
    pos_weight = normal_values(arg_keys[7], (EMB, FHID), EMB ** -0.5, 1.0)
    pos_bias = normal_values(arg_keys[8], (FHID,), 0.5, 3.0)
    inner_weight = normal_values(arg_keys[9], (FHID, FHID), FHID ** -0.5, 0.75)
    inner_bias = normal_values(arg_keys[10], (FHID,), 0.5, 3.0)
    filter_third_weight = normal_values(arg_keys[11], (FHID, FHID), FHID ** -0.5, 0.75)
    third_bias = normal_values(arg_keys[12], (FHID,), 0.5, 3.0)
    sine_freq = jnp.clip(1.0 + 0.1 * jax.random.normal(arg_keys[13], (FHID,), jnp.float32), 0.5, 1.5).astype(jnp.bfloat16)
    filter_weight = normal_values(arg_keys[14], (2, FHID, D), (FHID * LENGTH // 16) ** -0.5, 0.09375)
    decay_rates = jnp.clip(jnp.exp(jax.random.uniform(arg_keys[15], (2, D), jnp.float32, math.log(0.5), math.log(32.0))), 0.5, 32.0)
    skip_gains = normal_values(arg_keys[16], (2, D), 1.0, 6.0)
    out_weight = normal_values(arg_keys[17], (D, D), D ** -0.5, 0.21875)
    out_bias = normal_values(arg_keys[18], (D,), 0.3, 1.75)
    post_gain = jnp.clip(1.0 + 0.1 * jax.random.normal(arg_keys[19], (D,), jnp.float32), 0.5, 1.5).astype(jnp.bfloat16)
    post_bias = normal_values(arg_keys[20], (D,), 0.3, 1.75)
    up_weight = normal_values(arg_keys[21], (D, FF), D ** -0.5, 0.21875)
    up_bias = normal_values(arg_keys[22], (FF,), 0.3, 1.75)
    down_weight = normal_values(arg_keys[23], (FF, D), FF ** -0.5, 0.109375)
    down_bias = normal_values(arg_keys[24], (D,), 0.3, 1.75)
    cotangent = normal_values(arg_keys[25], (SEQS, LENGTH, D), 1.0, 6.0, ((0, 4), (1, 8)))
    return dict(inputs=inputs, pre_gain=pre_gain, pre_bias=pre_bias, in_weight=in_weight, input_projection_bias=input_projection_bias, short_weight=short_weight, short_bias=short_bias, pos_weight=pos_weight, pos_bias=pos_bias, inner_weight=inner_weight, inner_bias=inner_bias, filter_third_weight=filter_third_weight, third_bias=third_bias, sine_freq=sine_freq, filter_weight=filter_weight, decay_rates=decay_rates, skip_gains=skip_gains, out_weight=out_weight, out_bias=out_bias, post_gain=post_gain, post_bias=post_bias, up_weight=up_weight, up_bias=up_bias, down_weight=down_weight, down_bias=down_bias, cotangent=cotangent)


epsilon = 1e-05
highest_accuracy = lax.Precision.HIGHEST

@jax.custom_vjp
def low(v):
    return lax.optimization_barrier(v.astype(jnp.bfloat16)).astype(jnp.float32)

@jax.custom_vjp
def low_back(v):
    return v

def low_keep(v):
    return (low(v), None)

def low_pass(kept, grad):
    return (grad,)

def back_keep(v):
    return (v, None)

def back_low(kept, grad):
    return (low(grad),)
low.defvjp(low_keep, low_pass)
low_back.defvjp(back_keep, back_low)

def exact_dot(left_side, right_side):
    return jnp.dot(left_side, right_side, precision=highest_accuracy, preferred_element_type=jnp.float32)

def layer_norm(values, gain_vec, shift_vec):
    centre = values - lax.optimization_barrier(jnp.mean(values, axis=-1, keepdims=True))
    spread = lax.optimization_barrier(jnp.mean(centre * centre, axis=-1, keepdims=True))
    return centre * lax.rsqrt(spread + epsilon) * gain_vec + shift_vec

def positions(length, feat_count):
    steps_pos = jnp.arange(length, dtype=jnp.float32)
    time_steps = steps_pos / (length - 1)
    band_count = (feat_count - 1) // 2
    frequency = jnp.linspace(0.0001, band_count - 1, band_count, dtype=jnp.float32)
    angles = (steps_pos * (2.0 * math.pi / length))[:, None] * frequency[None, :]
    features = jnp.concatenate([time_steps[:, None], jnp.cos(angles), -jnp.sin(angles)], axis=1)
    return (features, time_steps)

def make_filters(features, time_steps, pos_weight, pos_bias, inner_weight, inner_bias, filter_third_weight, third_bias, sine_freq, filter_weight, decay_rates):
    hidden = jnp.sin(sine_freq * (exact_dot(features, pos_weight) + pos_bias))
    hidden = jnp.sin(sine_freq * (exact_dot(hidden, inner_weight) + inner_bias))
    hidden = jnp.sin(sine_freq * (exact_dot(hidden, filter_third_weight) + third_bias))
    first_kernel = exact_dot(hidden, filter_weight[0]) * jnp.exp(-time_steps[:, None] * decay_rates[0][None, :])
    second_kernel = exact_dot(hidden, filter_weight[1]) * jnp.exp(-time_steps[:, None] * decay_rates[1][None, :])
    return (first_kernel, second_kernel)

def long_conv(signal, kernel):
    length = signal.shape[0]
    spectrum = jnp.fft.rfft(signal, n=2 * length, axis=0) * jnp.fft.rfft(kernel, n=2 * length, axis=0)
    return jnp.fft.irfft(spectrum, n=2 * length, axis=0)[:length]

def forward(seq_inputs, pre_gain, pre_bias, in_weight, input_projection_bias, short_weight, short_bias, pos_weight, pos_bias, inner_weight, inner_bias, filter_third_weight, third_bias, sine_freq, filter_weight, decay_rates, skip_gains, out_weight, out_bias, post_gain, post_bias, up_weight, up_bias, down_weight, down_bias):
    length = seq_inputs.shape[0]
    model_width = seq_inputs.shape[1]
    normed = low(layer_norm(seq_inputs, pre_gain, pre_bias))
    projected = low_back(exact_dot(normed, in_weight) + input_projection_bias)
    padded = jnp.concatenate([jnp.zeros((2, 3 * model_width), jnp.float32), projected], axis=0)
    mixed_conv = short_weight[0] * padded[:-2] + short_weight[1] * padded[1:-1] + short_weight[2] * padded[2:] + short_bias
    value_part = mixed_conv[:, :model_width]
    gate_one = mixed_conv[:, model_width:2 * model_width]
    gate_two = mixed_conv[:, 2 * model_width:]
    features, time_steps = positions(length, pos_weight.shape[0])
    kernel_one, kernel_two = make_filters(features, time_steps, pos_weight, pos_bias, inner_weight, inner_bias, filter_third_weight, third_bias, sine_freq, filter_weight, decay_rates)
    product = low_back(low(value_part * gate_one))
    after_one = low_back(low(long_conv(product, kernel_one) + skip_gains[0] * product))
    gate_low = low_back(low(gate_two))
    gated_low = low_back(low(after_one * gate_low))
    mixer = low_back(low(long_conv(gated_low, kernel_two) + skip_gains[1] * gated_low))
    branch = low_back(exact_dot(mixer, out_weight) + out_bias)
    residual = seq_inputs + branch
    normed_two = low(layer_norm(residual, post_gain, post_bias))
    upper_pre = low_back(exact_dot(normed_two, up_weight) + up_bias)
    activated = low(jax.nn.gelu(upper_pre, approximate=False))
    return residual + exact_dot(activated, down_weight) + down_bias

def reference(inputs, pre_gain, pre_bias, in_weight, input_projection_bias, short_weight, short_bias, pos_weight, pos_bias, inner_weight, inner_bias, filter_third_weight, third_bias, sine_freq, filter_weight, decay_rates, skip_gains, out_weight, out_bias, post_gain, post_bias, up_weight, up_bias, down_weight, down_bias, cotangent):
    weights = tuple((member.astype(jnp.float32) for member in (pre_gain, pre_bias, in_weight, input_projection_bias, short_weight, short_bias, pos_weight, pos_bias, inner_weight, inner_bias, filter_third_weight, third_bias, sine_freq, filter_weight, decay_rates, skip_gains, out_weight, out_bias, post_gain, post_bias, up_weight, up_bias, down_weight, down_bias)))

    def per_sequence(running, pair):
        seq_inputs, seq_cotangent = pair
        result, pull_back = jax.vjp(forward, seq_inputs.astype(jnp.float32), *weights)
        gradients = pull_back(seq_cotangent.astype(jnp.float32))
        updated = tuple((total_sum + update for total_sum, update in zip(running, gradients[1:])))
        return (updated, (result, gradients[0]))
    zero_sums = tuple((jnp.zeros(member.shape, jnp.float32) for member in weights))
    totals, (outputs, grad_inputs) = lax.scan(per_sequence, zero_sums, (inputs, cotangent))
    return (outputs, grad_inputs, totals[0], totals[1], totals[2], totals[3], totals[4], totals[5], totals[6], totals[7], totals[8], totals[9], totals[10], totals[11], totals[12], totals[13], totals[14], totals[15], totals[16], totals[17], totals[18], totals[19], totals[20], totals[21], totals[22], totals[23])
```

```python
import math

import jax
import jax.numpy as jnp
import numpy as np
from jax import lax
from jax.experimental import pallas as pl
from jax.experimental.pallas import tpu as pltpu
from jax.sharding import PartitionSpec as P

epsilon = 1e-05
highest_accuracy = lax.Precision.HIGHEST


def passed_along(value, axis, steps):
    count = lax.axis_size(axis)
    initial, last = (max(0, -steps), min(count, count - steps))
    return lax.ppermute(value, axis, [(source, source + steps) for source in range(initial, last)])


def plain_dot(left_side, right_side):
    return jnp.dot(left_side, right_side, preferred_element_type=jnp.float32)


def exact_tdot(left_side, right_side):
    return lax.dot_general(
        left_side,
        right_side,
        (((0,), (0,)), ((), ())),
        precision=highest_accuracy,
        preferred_element_type=jnp.float32,
    )


def left_dot(left_side, right_side):
    return lax.dot_general(
        left_side, right_side, (((0,), (0,)), ((), ())), preferred_element_type=jnp.float32
    )


def right_dot(left_side, right_side):
    return lax.dot_general(
        left_side, right_side, (((1,), (1,)), ((), ())), preferred_element_type=jnp.float32
    )


def rounded(values):
    return lax.optimization_barrier(values.astype(jnp.bfloat16)).astype(jnp.float32)


def norm_forward(values, gain_vec, shift_vec):
    centre = values - jnp.mean(values, axis=-1, keepdims=True)
    inv_std = lax.rsqrt(jnp.mean(centre * centre, axis=-1, keepdims=True) + epsilon)
    unit_rows = centre * inv_std
    return (unit_rows * gain_vec + shift_vec, unit_rows, inv_std)


def norm_backward(grad_out, unit_rows, inv_std, gain_vec):
    grad_unit = grad_out * gain_vec
    grad_values = inv_std * (
        grad_unit
        - jnp.mean(grad_unit, axis=-1, keepdims=True)
        - unit_rows * jnp.mean(grad_unit * unit_rows, axis=-1, keepdims=True)
    )
    return (grad_values, jnp.sum(grad_out * unit_rows, axis=0), jnp.sum(grad_out, axis=0))


def position_rows(length, feat_count):
    steps_pos = jnp.arange(length, dtype=jnp.float32)
    time_steps = steps_pos / (length - 1)
    band_count = (feat_count - 1) // 2
    frequency = jnp.linspace(0.0001, band_count - 1, band_count, dtype=jnp.float32)
    angles = frequency[:, None] * (steps_pos * (2.0 * math.pi / length))[None, :]
    features_t = jnp.concatenate([time_steps[None, :], jnp.cos(angles), -jnp.sin(angles)], axis=0)
    return (features_t, time_steps)


def body_filters(
    features_t,
    time_steps,
    pos_weight,
    pos_bias,
    inner_weight,
    inner_bias,
    filter_third_weight,
    third_bias,
    sine_freq,
    weight_local,
    rates_local,
):
    hidden = jnp.sin(sine_freq[:, None] * (exact_tdot(pos_weight, features_t) + pos_bias[:, None]))
    hidden = jnp.sin(sine_freq[:, None] * (exact_tdot(inner_weight, hidden) + inner_bias[:, None]))
    hidden = jnp.sin(
        sine_freq[:, None] * (exact_tdot(filter_third_weight, hidden) + third_bias[:, None])
    )
    first_kernel = exact_tdot(weight_local[0], hidden) * jnp.exp(
        -rates_local[0][:, None] * time_steps[None, :]
    )
    second_kernel = exact_tdot(weight_local[1], hidden) * jnp.exp(
        -rates_local[1][:, None] * time_steps[None, :]
    )
    return (first_kernel, second_kernel)


def split_sizes(extent):
    outer_size = math.gcd(extent // 2, 1 << (extent.bit_length() - 1) // 2)
    return (outer_size, extent // outer_size)


def dft_rect(row_count, col_count, modulus, direction):
    row_ids = jnp.arange(row_count, dtype=jnp.int32)[:, None]
    col_ids = jnp.arange(col_count, dtype=jnp.int32)[None, :]
    angles = (row_ids * col_ids % modulus).astype(jnp.float32) * (2.0 * math.pi / modulus)
    return (jnp.cos(angles), direction * jnp.sin(angles))


def first_section(block_groups, lookup_grid):
    return jnp.einsum(
        "cij,ik->ckj",
        block_groups,
        lookup_grid,
        precision=highest_accuracy,
        preferred_element_type=jnp.float32,
    )


def second_section(block_groups, lookup_grid):
    return jnp.einsum(
        "dhq,qn->dnh",
        block_groups,
        lookup_grid,
        precision=highest_accuracy,
        preferred_element_type=jnp.float32,
    )


def padded_spectrum(signal):
    channels, length = signal.shape
    extent = 2 * length
    outer_size, inner_size = split_sizes(extent)
    block_groups = signal.reshape(channels, inner_size // 2, outer_size)
    cos_inner, sin_inner = dft_rect(inner_size // 2, inner_size, inner_size, -1.0)
    section_real = first_section(block_groups, cos_inner)
    section_imag = first_section(block_groups, sin_inner)
    twist_cos, rotation_sine = dft_rect(inner_size, outer_size, extent, -1.0)
    turned_real = section_real * twist_cos - section_imag * rotation_sine
    turned_imag = section_real * rotation_sine + section_imag * twist_cos
    cos_outer, sin_outer = dft_rect(outer_size, outer_size, outer_size, -1.0)
    out_real = second_section(turned_real, cos_outer) - second_section(turned_imag, sin_outer)
    out_imag = second_section(turned_real, sin_outer) + second_section(turned_imag, cos_outer)
    return (out_real.reshape(channels, extent), out_imag.reshape(channels, extent))


def inverse_real(spec_real, spec_imag):
    channels, extent = spec_real.shape
    outer_size, inner_size = split_sizes(extent)
    blocks_real = spec_real.reshape(channels, inner_size, outer_size)
    blocks_imag = spec_imag.reshape(channels, inner_size, outer_size)
    cos_inner, sin_inner = dft_rect(inner_size, inner_size, inner_size, 1.0)
    section_real = first_section(blocks_real, cos_inner) - first_section(blocks_imag, sin_inner)
    section_imag = first_section(blocks_real, sin_inner) + first_section(blocks_imag, cos_inner)
    twist_cos, rotation_sine = dft_rect(inner_size, outer_size, extent, 1.0)
    turned_real = section_real * twist_cos - section_imag * rotation_sine
    turned_imag = section_real * rotation_sine + section_imag * twist_cos
    cos_outer, sin_outer = dft_rect(outer_size, outer_size // 2, outer_size, 1.0)
    out_real = second_section(turned_real, cos_outer) - second_section(turned_imag, sin_outer)
    return out_real.reshape(channels, extent // 2) / extent


def times_spec(left_real, left_imag, right_real, right_imag):
    return (
        left_real * right_real - left_imag * right_imag,
        left_real * right_imag + left_imag * right_real,
    )


def times_conj(left_real, left_imag, right_real, right_imag):
    return (
        left_real * right_real + left_imag * right_imag,
        left_imag * right_real - left_real * right_imag,
    )


def factored_device(
    inputs,
    pre_gain,
    pre_bias,
    in_weight,
    input_projection_bias,
    short_weight,
    short_bias,
    pos_weight,
    pos_bias,
    inner_weight,
    inner_bias,
    filter_third_weight,
    third_bias,
    sine_freq,
    filter_weight,
    decay_rates,
    skip_gains,
    out_weight,
    out_bias,
    post_gain,
    post_bias,
    up_weight,
    up_bias,
    down_weight,
    down_bias,
    cotangent,
):
    seq_parts = lax.axis_size("seq")
    seq_rank = lax.axis_index("seq")
    tokens = inputs[0]
    tok_count = tokens.shape[0]
    model_width = tokens.shape[1]
    length = tok_count * seq_parts
    channels = model_width // seq_parts
    tokens_wide = tokens.astype(jnp.float32)
    pre_gain_f = pre_gain.astype(jnp.float32)
    pre_bias_f = pre_bias.astype(jnp.float32)
    in_bias_f = input_projection_bias.astype(jnp.float32)
    short_f = short_weight.astype(jnp.float32)
    short_bias_f = short_bias.astype(jnp.float32)
    out_bias_f = out_bias.astype(jnp.float32)
    post_gain_f = post_gain.astype(jnp.float32)
    post_bias_f = post_bias.astype(jnp.float32)
    up_bias_f = up_bias.astype(jnp.float32)
    down_bias_f = down_bias.astype(jnp.float32)
    normed, unit_pre, inv_pre = norm_forward(tokens_wide, pre_gain_f, pre_bias_f)
    normed_low = normed.astype(jnp.bfloat16)
    projected = plain_dot(normed_low, in_weight) + in_bias_f
    previous = passed_along(projected[tok_count - 2 :], "seq", 1)
    extended = jnp.concatenate([previous, projected], axis=0)
    mixed_conv = (
        short_f[0] * extended[:-2]
        + short_f[1] * extended[1:-1]
        + short_f[2] * extended[2:]
        + short_bias_f
    )
    value_part = mixed_conv[:, :model_width]
    gate_one = mixed_conv[:, model_width : 2 * model_width]
    gate_two = mixed_conv[:, 2 * model_width :]
    product_low = (value_part * gate_one).astype(jnp.bfloat16)
    gate_two_low = gate_two.astype(jnp.bfloat16)
    prod_chan, gate_chan = (
        lax.all_to_all(product_low.T, "seq", split_axis=0, concat_axis=1, tiled=True),
        lax.all_to_all(gate_two_low.T, "seq", split_axis=0, concat_axis=1, tiled=True),
    )
    features_t, time_steps = position_rows(length, pos_weight.shape[0])
    chan_start = seq_rank * channels
    weight_local = lax.dynamic_slice_in_dim(
        filter_weight.astype(jnp.float32), chan_start, channels, 2
    )
    rates_local = lax.dynamic_slice_in_dim(decay_rates, chan_start, channels, 1)
    skips_local = lax.dynamic_slice_in_dim(skip_gains.astype(jnp.float32), chan_start, channels, 1)
    skip_one = skips_local[0][:, None]
    skip_two = skips_local[1][:, None]
    shared = tuple(
        (
            member.astype(jnp.float32)
            for member in (
                pos_weight,
                pos_bias,
                inner_weight,
                inner_bias,
                filter_third_weight,
                third_bias,
                sine_freq,
            )
        )
    )

    def local_filters(*params):
        return body_filters(features_t, time_steps, *params)

    (kernel_one, kernel_two), filter_pull = jax.vjp(
        local_filters, *shared, weight_local, rates_local
    )
    prod_wide = prod_chan.astype(jnp.float32)
    gate_wide = gate_chan.astype(jnp.float32)
    prod_real, prod_imag = padded_spectrum(prod_wide)
    kone_real, kone_imag = padded_spectrum(kernel_one)
    convolved_real_part, conv_imag = times_spec(prod_real, prod_imag, kone_real, kone_imag)
    after_one = rounded(inverse_real(convolved_real_part, conv_imag) + skip_one * prod_wide)
    gated_low = rounded(after_one * gate_wide)
    gated_real, gated_imag = padded_spectrum(gated_low)
    ktwo_real, ktwo_imag = padded_spectrum(kernel_two)
    convolved_real_part, conv_imag = times_spec(gated_real, gated_imag, ktwo_real, ktwo_imag)
    mixer_chan = (inverse_real(convolved_real_part, conv_imag) + skip_two * gated_low).astype(
        jnp.bfloat16
    )
    mixer_tok = lax.all_to_all(mixer_chan, "seq", split_axis=1, concat_axis=0, tiled=True).T
    branch = plain_dot(mixer_tok, out_weight) + out_bias_f
    residual = tokens_wide + branch
    normed_two, unit_post, inv_post = norm_forward(residual, post_gain_f, post_bias_f)
    normed_two_low = normed_two.astype(jnp.bfloat16)
    upper_pre = plain_dot(normed_two_low, up_weight) + up_bias_f
    activated = jax.nn.gelu(upper_pre, approximate=False).astype(jnp.bfloat16)
    outputs = residual + plain_dot(activated, down_weight) + down_bias_f
    grad_top = cotangent[0]
    grad_top_wide = grad_top.astype(jnp.float32)
    grad_act = right_dot(grad_top, down_weight)
    grad_down = left_dot(activated, grad_top)
    grad_down_bias = jnp.sum(grad_top_wide, axis=0)
    gelu_slope = (
        0.5 * (1.0 + lax.erf(upper_pre * 0.7071067811865476))
        + upper_pre * jnp.exp(-0.5 * upper_pre * upper_pre) * 0.3989422804014327
    )
    grad_upper = (grad_act * gelu_slope).astype(jnp.bfloat16)
    grad_up = left_dot(normed_two_low, grad_upper)
    grad_up_bias = jnp.sum(grad_upper.astype(jnp.float32), axis=0)
    grad_normed_two = right_dot(grad_upper, up_weight)
    grad_resid_norm, grad_post_gain, grad_post_bias = norm_backward(
        grad_normed_two, unit_post, inv_post, post_gain_f
    )
    grad_residual = grad_top_wide + grad_resid_norm
    grad_branch = grad_residual.astype(jnp.bfloat16)
    grad_out = left_dot(mixer_tok, grad_branch)
    grad_out_bias = jnp.sum(grad_branch.astype(jnp.float32), axis=0)
    grad_mixer = right_dot(grad_branch, out_weight).astype(jnp.bfloat16)
    grad_mixer_chan = lax.all_to_all(
        grad_mixer.T, "seq", split_axis=0, concat_axis=1, tiled=True
    ).astype(jnp.float32)
    gmix_real, gmix_imag = padded_spectrum(grad_mixer_chan)
    corr_real, corr_imag = times_conj(gmix_real, gmix_imag, ktwo_real, ktwo_imag)
    grad_gated = rounded(inverse_real(corr_real, corr_imag) + skip_two * grad_mixer_chan)
    corr_real, corr_imag = times_conj(gmix_real, gmix_imag, gated_real, gated_imag)
    grad_kernel_two = inverse_real(corr_real, corr_imag)
    grad_skip_two = jnp.sum(grad_mixer_chan * gated_low, axis=1)
    grad_after = rounded(grad_gated * gate_wide)
    grad_gate_two = (grad_gated * after_one).astype(jnp.bfloat16)
    gaft_real, gaft_imag = padded_spectrum(grad_after)
    corr_real, corr_imag = times_conj(gaft_real, gaft_imag, kone_real, kone_imag)
    grad_product = (inverse_real(corr_real, corr_imag) + skip_one * grad_after).astype(jnp.bfloat16)
    corr_real, corr_imag = times_conj(gaft_real, gaft_imag, prod_real, prod_imag)
    grad_kernel_one = inverse_real(corr_real, corr_imag)
    grad_skip_one = jnp.sum(grad_after * prod_wide, axis=1)
    filter_grads = filter_pull((grad_kernel_one, grad_kernel_two))
    grad_prod_back, grad_gate_back = (
        lax.all_to_all(grad_product, "seq", split_axis=1, concat_axis=0, tiled=True),
        lax.all_to_all(grad_gate_two, "seq", split_axis=1, concat_axis=0, tiled=True),
    )
    grad_prod_wide = grad_prod_back.T.astype(jnp.float32)
    grad_mixed = jnp.concatenate(
        [
            grad_prod_wide * gate_one,
            grad_prod_wide * value_part,
            grad_gate_back.T.astype(jnp.float32),
        ],
        axis=1,
    )
    grad_short_bias = jnp.sum(grad_mixed, axis=0)
    grad_short = jnp.stack(
        [
            jnp.sum(grad_mixed * extended[0:tok_count], axis=0),
            jnp.sum(grad_mixed * extended[1 : tok_count + 1], axis=0),
            jnp.sum(grad_mixed * extended[2 : tok_count + 2], axis=0),
        ]
    )
    zero_rows = jnp.zeros((2, 3 * model_width), jnp.float32)
    padded_grad = jnp.concatenate([zero_rows, grad_mixed, zero_rows], axis=0)
    grad_extended = (
        short_f[0] * padded_grad[2:]
        + short_f[1] * padded_grad[1:-1]
        + short_f[2] * padded_grad[:-2]
    )
    from_next = passed_along(grad_extended[:2], "seq", -1)
    grad_projected = grad_extended[2:].at[tok_count - 2 :].add(from_next)
    grad_proj_low = grad_projected.astype(jnp.bfloat16)
    grad_in = left_dot(normed_low, grad_proj_low)
    grad_in_bias = jnp.sum(grad_proj_low.astype(jnp.float32), axis=0)
    grad_normed = right_dot(grad_proj_low, in_weight)
    grad_tokens_norm, grad_pre_gain, grad_pre_bias = norm_backward(
        grad_normed, unit_pre, inv_pre, pre_gain_f
    )
    grad_inputs = grad_residual + grad_tokens_norm
    shared_sums = lax.psum(
        (
            grad_pre_gain,
            grad_pre_bias,
            grad_in_bias,
            grad_short,
            grad_short_bias,
            filter_grads[0],
            filter_grads[1],
            filter_grads[2],
            filter_grads[3],
            filter_grads[4],
            filter_grads[5],
            filter_grads[6],
            grad_out_bias,
            grad_post_gain,
            grad_post_bias,
            grad_up_bias,
            grad_down_bias,
        ),
        ("batch", "seq"),
    )
    skip_grads = jnp.stack([grad_skip_one, grad_skip_two])
    weight_shards = (
        lax.psum_scatter(grad_in, "seq", scatter_dimension=0, tiled=True),
        lax.psum_scatter(grad_out, "seq", scatter_dimension=0, tiled=True),
        lax.psum_scatter(grad_up, "seq", scatter_dimension=0, tiled=True),
        lax.psum_scatter(grad_down, "seq", scatter_dimension=0, tiled=True),
    )
    final_in, final_out, final_up, final_down, final_filter, final_rates, final_skips = (
        lax.psum(weight_shards[0].astype(jnp.bfloat16), "batch").astype(jnp.float32),
        lax.psum(weight_shards[1].astype(jnp.bfloat16), "batch").astype(jnp.float32),
        lax.psum(weight_shards[2].astype(jnp.bfloat16), "batch").astype(jnp.float32),
        lax.psum(weight_shards[3].astype(jnp.bfloat16), "batch").astype(jnp.float32),
        lax.psum(filter_grads[7].astype(jnp.bfloat16), "batch").astype(jnp.float32),
        lax.psum(filter_grads[8].astype(jnp.bfloat16), "batch").astype(jnp.float32),
        lax.psum(skip_grads.astype(jnp.bfloat16), "batch").astype(jnp.float32),
    )
    return (
        outputs[None],
        grad_inputs[None],
        shared_sums[0],
        shared_sums[1],
        final_in,
        shared_sums[2],
        shared_sums[3],
        shared_sums[4],
        shared_sums[5],
        shared_sums[6],
        shared_sums[7],
        shared_sums[8],
        shared_sums[9],
        shared_sums[10],
        shared_sums[11],
        final_filter,
        final_rates,
        final_skips,
        final_out,
        shared_sums[12],
        shared_sums[13],
        shared_sums[14],
        final_up,
        shared_sums[15],
        final_down,
        shared_sums[16],
    )


LANES = 128
DENSE_LIMIT = 2048


def vmem_call(kernel, outs, args, flops, scalars=0, name=None):
    specs = [pl.BlockSpec(memory_space=pltpu.SMEM)] * scalars
    specs += [pl.BlockSpec(memory_space=pltpu.VMEM)] * (len(args) - scalars)
    shapes = [jax.ShapeDtypeStruct(shape, dtype) for shape, dtype in outs]
    moved = sum(math.prod(a.shape) * a.dtype.itemsize for a in list(args) + shapes)
    return pl.pallas_call(
        kernel,
        out_shape=shapes,
        in_specs=specs,
        out_specs=[pl.BlockSpec(memory_space=pltpu.VMEM)] * len(shapes),
        compiler_params=pltpu.CompilerParams(vmem_limit_bytes=60 * 1024 * 1024),
        cost_estimate=pl.CostEstimate(flops=flops, transcendentals=0, bytes_accessed=moved),
        name=name,
    )(*args)


def exact_nn(left_side, right_side):
    return jnp.dot(
        left_side, right_side, precision=highest_accuracy, preferred_element_type=jnp.float32
    )


def exact_nt(left_side, right_side):
    return lax.dot_general(
        left_side,
        right_side,
        (((1,), (1,)), ((), ())),
        precision=highest_accuracy,
        preferred_element_type=jnp.float32,
    )


def sine_pair(angle):
    turns = jnp.round(angle * (2.0 / math.pi))
    rest = angle - turns * 1.5703125
    rest = rest - turns * 4.837512969970703125e-4
    rest = rest - turns * 7.549789948768648e-8
    square = rest * rest
    sine = rest + rest * square * (
        -1.6666654611e-1 + square * (8.3321608736e-3 + square * -1.9515295891e-4)
    )
    cosine = (
        1.0
        - 0.5 * square
        + square
        * square
        * (4.166664568298827e-2 + square * (-1.388731625493765e-3 + square * 2.443315711809948e-5))
    )
    quarter = turns.astype(jnp.int32)
    odd = (quarter & 1) == 1
    sine_out = jnp.where(odd, cosine, sine)
    cosine_out = jnp.where(odd, sine, cosine)
    sine_out = jnp.where((quarter & 2) == 2, -sine_out, sine_out)
    cosine_out = jnp.where(((quarter + 1) & 2) == 2, -cosine_out, cosine_out)
    return sine_out, cosine_out


def wave_tables(length):
    step = 32
    count = length // step
    places = np.arange(length)
    coarse = np.arange(count)[:, None]
    fine = np.arange(step)[:, None]
    period = 4 * length
    unit = 2.0 * np.pi / period
    freq_coarse = (2 * step * coarse * places) % period * unit
    freq_fine = ((2 * fine + 1) * places) % period * unit
    place_coarse = ((2 * places + 1) * step * coarse) % period * unit
    place_fine = ((2 * places + 1) * fine) % period * unit
    angles = np.stack([freq_coarse, freq_fine, place_coarse, place_fine])
    return np.stack([np.cos(angles), np.sin(angles)], axis=1).astype(np.float32)


def feature_rows(length, feat_count):
    steps_pos = np.arange(length, dtype=np.float32)
    time_steps = steps_pos / np.float32(length - 1)
    bands = (feat_count - 1) // 2
    frequency = np.linspace(0.0001, bands - 1, bands, dtype=np.float32)
    angles = (steps_pos * np.float32(2.0 * math.pi / length))[:, None] * frequency[None, :]
    rows = [time_steps[:, None], np.cos(angles), -np.sin(angles)]
    return np.concatenate(rows, axis=1).astype(np.float32), time_steps[:, None]


def filter_kernel(
    tables,
    features,
    times,
    pos_weight,
    inner_weight,
    third_weight,
    vectors,
    weights,
    rates,
    wave_out,
    back_out,
    spectrum_out,
    kernel_out,
    hidden_out,
    cosine_out,
    inner_out,
):
    length = features.shape[0]
    step = tables.shape[2]

    def fill(block, carry):
        rows = pl.ds(pl.multiple_of(block * step, step), step)
        low = pl.ds(pl.multiple_of(length + block * step, step), step)
        cos_a, sin_a = tables[0, 0, pl.ds(block, 1), :], tables[0, 1, pl.ds(block, 1), :]
        cos_b, sin_b = tables[1, 0], tables[1, 1]
        wave_out[rows, :] = (cos_a * cos_b - sin_a * sin_b).astype(jnp.bfloat16)
        wave_out[low, :] = (sin_a * cos_b + cos_a * sin_b).astype(jnp.bfloat16)
        cos_a, sin_a = tables[2, 0, pl.ds(block, 1), :], tables[2, 1, pl.ds(block, 1), :]
        cos_b, sin_b = tables[3, 0], tables[3, 1]
        scale = 1.0 / length
        back_out[rows, :length] = ((cos_a * cos_b - sin_a * sin_b) * scale).astype(jnp.bfloat16)
        back_out[rows, length:] = ((sin_a * cos_b + cos_a * sin_b) * scale).astype(jnp.bfloat16)
        return carry

    lax.fori_loop(0, length // step, fill, 0)
    freq = vectors[3:4, :]
    layer_in = features[...]
    for layer, weight in enumerate((pos_weight, inner_weight, third_weight)):
        inner = exact_nn(layer_in, weight[...]) + vectors[layer : layer + 1, :]
        layer_in, cosine = sine_pair(freq * inner)
        inner_out[layer] = inner
        hidden_out[layer] = layer_in
        cosine_out[layer] = cosine
    kernels = exact_nn(layer_in, weights[...]) * jnp.exp(-rates[...] * times[...])
    kernel_out[...] = kernels
    high = kernels.astype(jnp.bfloat16)
    rest = (kernels - high.astype(jnp.float32)).astype(jnp.bfloat16)
    spectrum_out[...] = plain_dot(wave_out[...], high) + plain_dot(wave_out[...], rest)


def forward_wave(wave, signal):
    spectrum = plain_dot(wave[...], signal)
    half = spectrum.shape[0] // 2
    return spectrum[:half], spectrum[half:]


def backward_wave(back, real, imag):
    joined = jnp.concatenate([real.astype(jnp.bfloat16), imag.astype(jnp.bfloat16)], axis=0)
    return plain_dot(back[...], joined)


def shifted_down(rows, count):
    place = lax.broadcasted_iota(jnp.int32, rows.shape, 0)
    return jnp.where(place >= count, pltpu.roll(rows, count, 0), 0.0)


def shifted_up(rows, count):
    length = rows.shape[0]
    place = lax.broadcasted_iota(jnp.int32, rows.shape, 0)
    return jnp.where(place < length - count, pltpu.roll(rows, length - count, 0), 0.0)


def front_kernel(parts, *refs):
    seq_index = refs[0]
    chunks = refs[1 : 1 + parts]
    (gain, bias, weight, in_bias, taps, tap_bias, wave, back, spectrum, skips) = refs[
        1 + parts : 11 + parts
    ]
    (
        normed_out,
        unit_out,
        projected_out,
        product_out,
        gate_out,
        after_out,
        gated_out,
        product_wave,
        gated_wave,
        mixer_out,
    ) = refs[11 + parts :]
    tok_count = chunks[0].shape[0]
    half = wave.shape[1]
    for part in range(parts):
        rows = chunks[part][...].astype(jnp.float32)
        normed, unit, _ = norm_forward(rows, gain[...], bias[...])
        start = pl.multiple_of((seq_index[0] ^ part) * tok_count, tok_count)
        normed_out[pl.ds(start, tok_count), :] = normed.astype(jnp.bfloat16)
        unit_out[pl.ds(start, tok_count), :] = unit.astype(jnp.bfloat16)
    mixed = []
    for group in range(3):
        cols = slice(group * LANES, (group + 1) * LANES)
        projected = plain_dot(normed_out[...], weight[:, cols]) + in_bias[:, cols]
        projected_out[:, cols] = projected
        mixed.append(
            taps[0:1, cols] * shifted_down(projected, 2)
            + taps[1:2, cols] * shifted_down(projected, 1)
            + taps[2:3, cols] * projected
            + tap_bias[:, cols]
        )
    product = (mixed[0] * mixed[1]).astype(jnp.bfloat16)
    gate = mixed[2].astype(jnp.bfloat16)
    product_out[...] = product
    gate_out[...] = gate
    real, imag = forward_wave(wave, product)
    product_wave[:half] = real
    product_wave[half:] = imag
    convolved = backward_wave(
        back,
        *times_spec(real, imag, spectrum[:half, :LANES], spectrum[half:, :LANES]),
    )
    after = (convolved + skips[0:1] * product.astype(jnp.float32)).astype(jnp.bfloat16)
    after_out[...] = after
    gated = (after.astype(jnp.float32) * gate.astype(jnp.float32)).astype(jnp.bfloat16)
    gated_out[...] = gated
    real, imag = forward_wave(wave, gated)
    gated_wave[:half] = real
    gated_wave[half:] = imag
    convolved = backward_wave(
        back,
        *times_spec(real, imag, spectrum[:half, LANES:], spectrum[half:, LANES:]),
    )
    mixer = (convolved + skips[1:2] * gated.astype(jnp.float32)).astype(jnp.bfloat16)
    mixer_out[...] = mixer[:, : mixer_out.shape[1]]


def back_kernel(
    grad_mixer,
    product_ref,
    gate_ref,
    after_ref,
    gated_ref,
    product_wave,
    gated_wave,
    spectrum,
    wave,
    back,
    skips,
    projected,
    taps,
    tap_bias,
    packed_out,
    padded_out,
    grad_kernel_out,
    sums_out,
):
    half = wave.shape[1]
    channels = grad_mixer.shape[1]
    length = grad_mixer.shape[0]
    padding = jnp.zeros((length, LANES - channels), jnp.float32)
    grad_mix = jnp.concatenate([grad_mixer[...].astype(jnp.float32), padding], axis=1)
    real, imag = forward_wave(wave, grad_mix.astype(jnp.bfloat16))
    first = times_conj(real, imag, spectrum[:half, LANES:], spectrum[half:, LANES:])
    second = times_conj(real, imag, gated_wave[:half], gated_wave[half:])
    both = backward_wave(
        back,
        jnp.concatenate([first[0], second[0]], axis=1),
        jnp.concatenate([first[1], second[1]], axis=1),
    )
    grad_kernel_out[:, LANES:] = both[:, LANES:]
    low = jnp.bfloat16
    grad_gated = (both[:, :LANES] + skips[1:2] * grad_mix).astype(low).astype(jnp.float32)
    sums_out[5:6, LANES : 2 * LANES] = jnp.sum(
        grad_mix * gated_ref[...].astype(jnp.float32), axis=0, keepdims=True
    )
    grad_after = (grad_gated * gate_ref[...].astype(jnp.float32)).astype(low)
    grad_gate = (grad_gated * after_ref[...].astype(jnp.float32)).astype(low).astype(jnp.float32)
    real, imag = forward_wave(wave, grad_after)
    first = times_conj(real, imag, spectrum[:half, :LANES], spectrum[half:, :LANES])
    second = times_conj(real, imag, product_wave[:half], product_wave[half:])
    both = backward_wave(
        back,
        jnp.concatenate([first[0], second[0]], axis=1),
        jnp.concatenate([first[1], second[1]], axis=1),
    )
    grad_kernel_out[:, :LANES] = both[:, LANES:]
    grad_after = grad_after.astype(jnp.float32)
    sums_out[5:6, :LANES] = jnp.sum(
        grad_after * product_ref[...].astype(jnp.float32), axis=0, keepdims=True
    )
    sums_out[5:6, 2 * LANES :] = jnp.zeros((1, LANES), jnp.float32)
    sums_out[6:8, :] = jnp.zeros((2, 3 * LANES), jnp.float32)
    grad_product = (both[:, :LANES] + skips[0:1] * grad_after).astype(low).astype(jnp.float32)

    def mixed_of(group):
        cols = slice(group * LANES, (group + 1) * LANES)
        rows = projected[:, cols]
        return (
            taps[0:1, cols] * shifted_down(rows, 2)
            + taps[1:2, cols] * shifted_down(rows, 1)
            + taps[2:3, cols] * rows
            + tap_bias[:, cols]
        )

    pieces = []
    for group in range(3):
        cols = slice(group * LANES, (group + 1) * LANES)
        if group == 2:
            grad_mixed = grad_gate
        else:
            grad_mixed = grad_product * mixed_of(1 - group)
        rows = projected[:, cols]
        sums_out[0:1, cols] = jnp.sum(grad_mixed * shifted_down(rows, 2), axis=0, keepdims=True)
        sums_out[1:2, cols] = jnp.sum(grad_mixed * shifted_down(rows, 1), axis=0, keepdims=True)
        sums_out[2:3, cols] = jnp.sum(grad_mixed * rows, axis=0, keepdims=True)
        sums_out[3:4, cols] = jnp.sum(grad_mixed, axis=0, keepdims=True)
        grad_projected = (
            taps[0:1, cols] * shifted_up(grad_mixed, 2)
            + taps[1:2, cols] * shifted_up(grad_mixed, 1)
            + taps[2:3, cols] * grad_mixed
        ).astype(low)
        padded_out[:, cols] = grad_projected
        wide = grad_projected.astype(jnp.float32)
        sums_out[4:5, cols] = jnp.sum(wide, axis=0, keepdims=True)
        pieces.append(wide[:, :channels])
    packed_out[...] = jnp.concatenate(pieces, axis=1).astype(low)


def chain_kernel(
    grad_kernels,
    kernels,
    features,
    times,
    hidden,
    cosine,
    inner,
    inner_weight,
    third_weight,
    vectors,
    weights,
    rates,
    weights_out,
    rates_out,
    pos_out,
    inner_out,
    third_out,
    vectors_out,
):
    grads = grad_kernels[...]
    rates_out[...] = -jnp.sum(grads * kernels[...] * times[...], axis=0, keepdims=True)
    windowed = grads * jnp.exp(-rates[...] * times[...])
    weights_out[...] = exact_tdot(hidden[2], windowed)
    flow = exact_nt(windowed, weights[...])
    freq = vectors[3:4, :]
    grad_freq = jnp.zeros_like(freq)
    outs = (pos_out, inner_out, third_out)
    for layer in (2, 1, 0):
        slope = flow * cosine[layer]
        grad_freq = grad_freq + jnp.sum(slope * inner[layer], axis=0, keepdims=True)
        slope = slope * freq
        vectors_out[layer : layer + 1, :] = jnp.sum(slope, axis=0, keepdims=True)
        below = features[...] if layer == 0 else hidden[layer - 1]
        outs[layer][...] = exact_tdot(below, slope)
        if layer:
            flow = exact_nt(slope, (inner_weight if layer == 1 else third_weight)[...])
    vectors_out[3:4, :] = grad_freq


def swapped(value, axis, bits):
    count = lax.axis_size(axis)
    return lax.ppermute(value, axis, [(source, source ^ bits) for source in range(count)])


def over_batch(value):
    count = lax.axis_size("batch")
    held = value[None]
    bits = count // 2
    while bits:
        held = jnp.concatenate([held, swapped(held, "batch", bits)], axis=0)
        bits //= 2
    order = []
    for place in range(count):
        index, bits, weight = 0, count // 2, 1
        while bits:
            index += weight if place & bits else 0
            weight *= 2
            bits //= 2
        order.append(index)
    return [held[index] for index in order]


def natural(entries, index):
    stacked = jnp.stack(entries)
    return [
        lax.dynamic_index_in_dim(stacked, index ^ place, 0, keepdims=False)
        for place in range(len(entries))
    ]


def to_batch(quarters):
    count = lax.axis_size("batch")
    mine = lax.axis_index("batch")
    got = [lax.dynamic_index_in_dim(quarters, mine, 0, keepdims=False)]
    for bits in range(1, count):
        sent = lax.dynamic_index_in_dim(quarters, mine ^ bits, 0, keepdims=False)
        got.append(swapped(sent, "batch", bits))
    return got


def halved(total, axis, index, order):
    count = lax.axis_size(axis)
    shape = total.shape[1:]
    left = [bits for bits in (1 << k for k in range(count.bit_length() - 1))]
    for bits in order:
        place = left.index(bits)
        before = 1 << (len(left) - 1 - place)
        after = 1 << place
        view = total.reshape((before, 2, after) + shape)
        bit = (index // bits) % 2
        keep = lax.dynamic_index_in_dim(view, bit, 1, keepdims=False)
        send = lax.dynamic_index_in_dim(view, 1 - bit, 1, keepdims=False).astype(jnp.bfloat16)
        got = swapped(send, axis, bits)
        total = (keep + got.astype(jnp.float32)).reshape((before * after,) + shape)
        left.remove(bits)
    return total.reshape(shape)


def padded_channels(array, start, channels, width):
    rows = array.shape[0]
    groups = array.shape[1] // width
    view = lax.dynamic_slice_in_dim(array.reshape(rows, groups, width), start, channels, 2)
    view = jnp.pad(view, ((0, 0), (0, 0), (0, LANES - channels)))
    return view.reshape(rows, groups * LANES)


def dense_device(
    inputs,
    pre_gain,
    pre_bias,
    in_weight,
    input_projection_bias,
    short_weight,
    short_bias,
    pos_weight,
    pos_bias,
    inner_weight,
    inner_bias,
    filter_third_weight,
    third_bias,
    sine_freq,
    filter_weight,
    decay_rates,
    skip_gains,
    out_weight,
    out_bias,
    post_gain,
    post_bias,
    up_weight,
    up_bias,
    down_weight,
    down_bias,
    cotangent,
):
    seq_parts = lax.axis_size("seq")
    batch_parts = lax.axis_size("batch")
    seq_rank = lax.axis_index("seq")
    batch_rank = lax.axis_index("batch")
    tokens = inputs[0]
    tok_count, width = tokens.shape
    length = tok_count * seq_parts
    channels = width // seq_parts
    hidden_units = up_weight.shape[1]
    f32, low = jnp.float32, jnp.bfloat16
    wide = 3 * LANES
    start = seq_rank * channels

    chunks = {0: tokens}
    for bits in range(2, seq_parts, 2):
        chunks[bits] = swapped(tokens, "seq", bits)
    for bits in range(0, seq_parts, 2):
        chunks[bits + 1] = swapped(chunks[bits], "seq", 1)

    tables = wave_tables(length)
    features, times = feature_rows(length, pos_weight.shape[0])
    vectors = jnp.stack([pos_bias, inner_bias, third_bias, sine_freq]).astype(f32)
    weights_local = padded_channels(
        filter_weight.transpose(1, 0, 2).reshape(-1, 2 * width), start, channels, width
    ).astype(f32)
    rates_local = padded_channels(decay_rates.reshape(1, 2 * width), start, channels, width)
    skips_local = padded_channels(skip_gains, start, channels, width).astype(f32)
    pos_f, inner_f, third_f = (
        member.astype(f32) for member in (pos_weight, inner_weight, filter_third_weight)
    )
    fhid = pos_weight.shape[1]
    tables, features, times = (jnp.asarray(member) for member in (tables, features, times))
    wave, back, spectrum, kernels, hidden, cosine, inner = vmem_call(
        filter_kernel,
        [
            ((2 * length, length), low),
            ((length, 2 * length), low),
            ((2 * length, 2 * LANES), f32),
            ((length, 2 * LANES), f32),
            ((3, length, fhid), f32),
            ((3, length, fhid), f32),
            ((3, length, fhid), f32),
        ],
        [
            tables,
            features,
            times,
            pos_f,
            inner_f,
            third_f,
            vectors,
            weights_local,
            rates_local,
        ],
        flops=4 * 2 * length * length * 2 * LANES,
        name="filters",
    )

    gain_row = pre_gain.astype(f32)[None]
    bias_row = pre_bias.astype(f32)[None]
    in_local = padded_channels(in_weight, start, channels, width)
    in_bias_local = padded_channels(input_projection_bias[None], start, channels, width).astype(f32)
    taps_local = padded_channels(short_weight, start, channels, width).astype(f32)
    tap_bias_local = padded_channels(short_bias[None], start, channels, width).astype(f32)
    (
        normed,
        unit,
        projected,
        product,
        gate,
        after,
        gated,
        product_wave,
        gated_wave,
        mixer_chan,
    ) = vmem_call(
        lambda *refs: front_kernel(seq_parts, *refs),
        [
            ((length, width), low),
            ((length, width), low),
            ((length, wide), f32),
            ((length, LANES), low),
            ((length, LANES), low),
            ((length, LANES), low),
            ((length, LANES), low),
            ((2 * length, LANES), f32),
            ((2 * length, LANES), f32),
            ((length, channels), low),
        ],
        [seq_rank.astype(jnp.int32)[None]]
        + [chunks[part] for part in range(seq_parts)]
        + [
            gain_row,
            bias_row,
            in_local,
            in_bias_local,
            taps_local,
            tap_bias_local,
            wave,
            back,
            spectrum,
            skips_local,
        ],
        flops=2 * length * width * wide + 4 * 4 * length * length * LANES,
        scalars=1,
        name="front",
    )
    mixer_back = lax.all_to_all(
        mixer_chan.reshape(seq_parts, tok_count, channels), "seq", 0, 0, tiled=True
    )
    mixer_tok = mixer_back.transpose(1, 0, 2).reshape(tok_count, width)

    tokens_wide = tokens.astype(f32)
    post_gain_f = post_gain.astype(f32)
    grad_top = cotangent[0]
    grad_top_wide = grad_top.astype(f32)
    residual = tokens_wide + plain_dot(mixer_tok, out_weight) + out_bias.astype(f32)
    normed_two, unit_post, inv_post = norm_forward(residual, post_gain_f, post_bias.astype(f32))
    normed_two_low = normed_two.astype(low)
    upper_pre = plain_dot(normed_two_low, up_weight) + up_bias.astype(f32)
    gauss = 0.5 * (1.0 + lax.erf(upper_pre * 0.7071067811865476))
    activated = (upper_pre * gauss).astype(low)
    outputs = residual + plain_dot(activated, down_weight) + down_bias.astype(f32)
    grad_act = right_dot(grad_top, down_weight)
    gelu_slope = gauss + upper_pre * jnp.exp(-0.5 * upper_pre * upper_pre) * 0.3989422804014327
    grad_upper = (grad_act * gelu_slope).astype(low)
    grad_up_bias = jnp.sum(grad_upper.astype(f32), axis=0)
    grad_down_bias = jnp.sum(grad_top_wide, axis=0)
    grad_normed_two = right_dot(grad_upper, up_weight)
    grad_resid_norm, grad_post_gain, grad_post_bias = norm_backward(
        grad_normed_two, unit_post, inv_post, post_gain_f
    )
    grad_residual = grad_top_wide + grad_resid_norm
    grad_branch = grad_residual.astype(low)
    grad_out_bias = jnp.sum(grad_branch.astype(f32), axis=0)
    grad_mixer = right_dot(grad_branch, out_weight).astype(low)
    grad_mixer_chan = lax.all_to_all(
        grad_mixer.reshape(tok_count, seq_parts, channels).transpose(1, 0, 2),
        "seq",
        0,
        0,
        tiled=True,
    ).reshape(length, channels)

    quarter = hidden_units // batch_parts
    branch_quarter = width // batch_parts
    tops = over_batch(grad_top)
    mixers = over_batch(mixer_tok)
    norms = over_batch(normed_two_low)
    upper_got = to_batch(grad_upper.reshape(tok_count, batch_parts, quarter).transpose(1, 0, 2))
    rows_quarter = hidden_units // (seq_parts * batch_parts)
    act_got = to_batch(
        activated.reshape(tok_count, seq_parts, batch_parts, rows_quarter)
        .transpose(2, 0, 1, 3)
        .reshape(batch_parts, tok_count, seq_parts * rows_quarter)
    )
    branch_got = to_batch(
        grad_branch.reshape(tok_count, batch_parts, branch_quarter).transpose(1, 0, 2)
    )
    cat = lambda members: jnp.concatenate(members, axis=0)
    up_part = left_dot(cat(norms), cat(upper_got)).reshape(seq_parts, -1, quarter)
    down_part = left_dot(cat(act_got), cat(tops)).reshape(seq_parts, -1, width)
    out_part = left_dot(cat(mixers), cat(branch_got)).reshape(seq_parts, -1, branch_quarter)
    bit_list = [1 << k for k in range(seq_parts.bit_length() - 1)]
    swap_list = [bit_list[1], bit_list[0]] + bit_list[2:]
    up_quarter = halved(up_part, "seq", seq_rank, bit_list).astype(low)
    down_quarter = halved(down_part, "seq", seq_rank, swap_list).astype(low)
    out_quarter = halved(out_part, "seq", seq_rank, swap_list).astype(low)
    final_up = jnp.concatenate(natural(over_batch(up_quarter), batch_rank), axis=1).astype(f32)
    final_down = jnp.concatenate(natural(over_batch(down_quarter), batch_rank), axis=0).astype(f32)
    final_out = jnp.concatenate(natural(over_batch(out_quarter), batch_rank), axis=1).astype(f32)

    packed, grad_proj, grad_kernels, sums = vmem_call(
        back_kernel,
        [
            ((length, 3 * channels), low),
            ((length, wide), low),
            ((length, 2 * LANES), f32),
            ((8, wide), f32),
        ],
        [
            grad_mixer_chan,
            product,
            gate,
            after,
            gated,
            product_wave,
            gated_wave,
            spectrum,
            wave,
            back,
            skips_local,
            projected,
            taps_local,
            tap_bias_local,
        ],
        flops=6 * 4 * length * length * LANES,
        name="back",
    )
    proj_back = lax.all_to_all(
        packed.reshape(seq_parts, tok_count, 3 * channels), "seq", 0, 0, tiled=True
    )
    grad_proj_tok = (
        proj_back.reshape(seq_parts, tok_count, 3, channels)
        .transpose(1, 2, 0, 3)
        .reshape(tok_count, 3 * width)
    )
    grad_normed = right_dot(grad_proj_tok, in_weight)
    _, unit_pre, inv_pre = norm_forward(tokens_wide, pre_gain.astype(f32), pre_bias.astype(f32))
    grad_tokens_norm, grad_pre_gain, grad_pre_bias = norm_backward(
        grad_normed, unit_pre, inv_pre, pre_gain.astype(f32)
    )
    grad_inputs = grad_residual + grad_tokens_norm

    in_part = left_dot(normed, grad_proj).reshape(width, 3, LANES)[:, :, :channels]
    in_rows = width // (seq_parts * batch_parts)
    in_part = (
        in_part.reshape(seq_parts, batch_parts, in_rows, 3 * channels)
        .transpose(1, 0, 2, 3)
        .reshape(batch_parts, seq_parts * in_rows, 3 * channels)
    )
    batch_bits = [1 << k for k in range(batch_parts.bit_length() - 1)]
    in_quarter = halved(in_part, "batch", batch_rank, batch_bits).astype(low)
    in_back = lax.all_to_all(
        in_quarter.reshape(seq_parts, in_rows, 3 * channels), "seq", 0, 0, tiled=True
    )
    in_back = (
        in_back.reshape(seq_parts, in_rows, 3, channels)
        .transpose(1, 2, 0, 3)
        .reshape(in_rows, 3 * width)
    )
    final_in = jnp.concatenate(natural(over_batch(in_back), batch_rank), axis=0).astype(f32)

    grad_weights, grad_rates, grad_pos, grad_inner, grad_third, grad_vectors = vmem_call(
        chain_kernel,
        [
            ((fhid, 2 * LANES), f32),
            ((1, 2 * LANES), f32),
            (pos_weight.shape, f32),
            (inner_weight.shape, f32),
            (filter_third_weight.shape, f32),
            ((4, fhid), f32),
        ],
        [
            grad_kernels,
            kernels,
            features,
            times,
            hidden,
            cosine,
            inner,
            inner_f,
            third_f,
            vectors,
            weights_local,
            rates_local,
        ],
        flops=8 * length * fhid * 2 * LANES * 6,
        name="chain",
    )

    local = jnp.concatenate(
        [grad_weights, grad_rates, sums[5:6, : 2 * LANES]], axis=0
    )
    placed = lax.dynamic_update_slice(
        jnp.zeros((5, 3, width), f32),
        sums[:5].reshape(5, 3, LANES)[:, :, :channels],
        (0, 0, start),
    )
    members = [
        grad_pre_gain,
        grad_pre_bias,
        placed,
        grad_pos,
        grad_inner,
        grad_third,
        grad_vectors,
        grad_out_bias,
        grad_post_gain,
        grad_post_bias,
        grad_up_bias,
        grad_down_bias,
    ]
    flat = jnp.concatenate([member.reshape(-1) for member in members])
    size = flat.shape[0]
    rows = -(-size // (8 * LANES)) * 8
    flat = jnp.pad(flat, (0, rows * LANES - size)).reshape(rows, LANES)
    joined = jnp.concatenate([flat, local.reshape(-1, LANES)], axis=0)
    for bits in batch_bits:
        joined = joined + swapped(joined, "batch", bits)
    flat, local = joined[:rows], joined[rows:].reshape(-1, 2 * LANES)
    for bits in bit_list:
        flat = flat + swapped(flat, "seq", bits)
    flat = flat.reshape(-1)
    done, place = [], 0
    for member in members:
        count = math.prod(member.shape)
        done.append(flat[place : place + count].reshape(member.shape))
        place += count
    (
        sum_pre_gain,
        sum_pre_bias,
        sum_placed,
        sum_pos,
        sum_inner,
        sum_third,
        sum_vectors,
        sum_out_bias,
        sum_post_gain,
        sum_post_bias,
        sum_up_bias,
        sum_down_bias,
    ) = done
    sum_placed = sum_placed.reshape(5, 3 * width)
    local = local.reshape(-1, 2, LANES)[:, :, :channels]
    return (
        outputs[None],
        grad_inputs[None],
        sum_pre_gain,
        sum_pre_bias,
        final_in,
        sum_placed[4],
        sum_placed[:3],
        sum_placed[3],
        sum_pos,
        sum_vectors[0],
        sum_inner,
        sum_vectors[1],
        sum_third,
        sum_vectors[2],
        sum_vectors[3],
        local[:fhid].transpose(1, 0, 2),
        local[fhid],
        local[fhid + 1],
        final_out,
        sum_out_bias,
        sum_post_gain,
        sum_post_bias,
        final_up,
        sum_up_bias,
        final_down,
        sum_down_bias,
    )


def per_device(*args):
    length = args[0].shape[1] * lax.axis_size("seq")
    return (dense_device if length <= DENSE_LIMIT else factored_device)(*args)


def solution(mesh):
    in_specs = (
        P("batch", "seq", None),
        P(),
        P(),
        P(),
        P(),
        P(),
        P(),
        P(),
        P(),
        P(),
        P(),
        P(),
        P(),
        P(),
        P(),
        P(),
        P(),
        P(),
        P(),
        P(),
        P(),
        P(),
        P(),
        P(),
        P(),
        P("batch", "seq", None),
    )
    out_specs = (
        P("batch", "seq", None),
        P("batch", "seq", None),
        P(),
        P(),
        P("seq", None),
        P(),
        P(),
        P(),
        P(),
        P(),
        P(),
        P(),
        P(),
        P(),
        P(),
        P(None, None, "seq"),
        P(None, "seq"),
        P(None, "seq"),
        P("seq", None),
        P(),
        P(),
        P(),
        P("seq", None),
        P(),
        P("seq", None),
        P(),
    )
    return jax.shard_map(
        per_device, mesh=mesh, in_specs=in_specs, out_specs=out_specs, check_vma=False
    )
```

```python
import math

import jax
import jax.numpy as jnp
import numpy as np
from jax import lax
from jax.experimental import pallas as pl
from jax.experimental.pallas import tpu as pltpu
from jax.sharding import PartitionSpec as P

epsilon = 1e-05
highest_accuracy = lax.Precision.HIGHEST


def passed_along(value, axis, steps):
    count = lax.axis_size(axis)
    initial, last = (max(0, -steps), min(count, count - steps))
    return lax.ppermute(value, axis, [(source, source + steps) for source in range(initial, last)])


def plain_dot(left_side, right_side):
    return jnp.dot(left_side, right_side, preferred_element_type=jnp.float32)


def exact_tdot(left_side, right_side):
    return lax.dot_general(
        left_side,
        right_side,
        (((0,), (0,)), ((), ())),
        precision=highest_accuracy,
        preferred_element_type=jnp.float32,
    )


def left_dot(left_side, right_side):
    return lax.dot_general(
        left_side, right_side, (((0,), (0,)), ((), ())), preferred_element_type=jnp.float32
    )


def right_dot(left_side, right_side):
    return lax.dot_general(
        left_side, right_side, (((1,), (1,)), ((), ())), preferred_element_type=jnp.float32
    )


def rounded(values):
    return lax.optimization_barrier(values.astype(jnp.bfloat16)).astype(jnp.float32)


def norm_forward(values, gain_vec, shift_vec):
    centre = values - jnp.mean(values, axis=-1, keepdims=True)
    inv_std = lax.rsqrt(jnp.mean(centre * centre, axis=-1, keepdims=True) + epsilon)
    unit_rows = centre * inv_std
    return (unit_rows * gain_vec + shift_vec, unit_rows, inv_std)


def norm_backward(grad_out, unit_rows, inv_std, gain_vec):
    grad_unit = grad_out * gain_vec
    grad_values = inv_std * (
        grad_unit
        - jnp.mean(grad_unit, axis=-1, keepdims=True)
        - unit_rows * jnp.mean(grad_unit * unit_rows, axis=-1, keepdims=True)
    )
    return (grad_values, jnp.sum(grad_out * unit_rows, axis=0), jnp.sum(grad_out, axis=0))


def position_rows(length, feat_count):
    steps_pos = jnp.arange(length, dtype=jnp.float32)
    time_steps = steps_pos / (length - 1)
    band_count = (feat_count - 1) // 2
    frequency = jnp.linspace(0.0001, band_count - 1, band_count, dtype=jnp.float32)
    angles = frequency[:, None] * (steps_pos * (2.0 * math.pi / length))[None, :]
    features_t = jnp.concatenate([time_steps[None, :], jnp.cos(angles), -jnp.sin(angles)], axis=0)
    return (features_t, time_steps)


def body_filters(
    features_t,
    time_steps,
    pos_weight,
    pos_bias,
    inner_weight,
    inner_bias,
    filter_third_weight,
    third_bias,
    sine_freq,
    weight_local,
    rates_local,
):
    hidden = jnp.sin(sine_freq[:, None] * (exact_tdot(pos_weight, features_t) + pos_bias[:, None]))
    hidden = jnp.sin(sine_freq[:, None] * (exact_tdot(inner_weight, hidden) + inner_bias[:, None]))
    hidden = jnp.sin(
        sine_freq[:, None] * (exact_tdot(filter_third_weight, hidden) + third_bias[:, None])
    )
    first_kernel = exact_tdot(weight_local[0], hidden) * jnp.exp(
        -rates_local[0][:, None] * time_steps[None, :]
    )
    second_kernel = exact_tdot(weight_local[1], hidden) * jnp.exp(
        -rates_local[1][:, None] * time_steps[None, :]
    )
    return (first_kernel, second_kernel)


def split_sizes(extent):
    outer_size = math.gcd(extent // 2, 1 << (extent.bit_length() - 1) // 2)
    return (outer_size, extent // outer_size)


def dft_rect(row_count, col_count, modulus, direction):
    row_ids = jnp.arange(row_count, dtype=jnp.int32)[:, None]
    col_ids = jnp.arange(col_count, dtype=jnp.int32)[None, :]
    angles = (row_ids * col_ids % modulus).astype(jnp.float32) * (2.0 * math.pi / modulus)
    return (jnp.cos(angles), direction * jnp.sin(angles))


def first_section(block_groups, lookup_grid):
    return jnp.einsum(
        "cij,ik->ckj",
        block_groups,
        lookup_grid,
        precision=highest_accuracy,
        preferred_element_type=jnp.float32,
    )


def second_section(block_groups, lookup_grid):
    return jnp.einsum(
        "dhq,qn->dnh",
        block_groups,
        lookup_grid,
        precision=highest_accuracy,
        preferred_element_type=jnp.float32,
    )


def padded_spectrum(signal):
    channels, length = signal.shape
    extent = 2 * length
    outer_size, inner_size = split_sizes(extent)
    block_groups = signal.reshape(channels, inner_size // 2, outer_size)
    cos_inner, sin_inner = dft_rect(inner_size // 2, inner_size, inner_size, -1.0)
    section_real = first_section(block_groups, cos_inner)
    section_imag = first_section(block_groups, sin_inner)
    twist_cos, rotation_sine = dft_rect(inner_size, outer_size, extent, -1.0)
    turned_real = section_real * twist_cos - section_imag * rotation_sine
    turned_imag = section_real * rotation_sine + section_imag * twist_cos
    cos_outer, sin_outer = dft_rect(outer_size, outer_size, outer_size, -1.0)
    out_real = second_section(turned_real, cos_outer) - second_section(turned_imag, sin_outer)
    out_imag = second_section(turned_real, sin_outer) + second_section(turned_imag, cos_outer)
    return (out_real.reshape(channels, extent), out_imag.reshape(channels, extent))


def inverse_real(spec_real, spec_imag):
    channels, extent = spec_real.shape
    outer_size, inner_size = split_sizes(extent)
    blocks_real = spec_real.reshape(channels, inner_size, outer_size)
    blocks_imag = spec_imag.reshape(channels, inner_size, outer_size)
    cos_inner, sin_inner = dft_rect(inner_size, inner_size, inner_size, 1.0)
    section_real = first_section(blocks_real, cos_inner) - first_section(blocks_imag, sin_inner)
    section_imag = first_section(blocks_real, sin_inner) + first_section(blocks_imag, cos_inner)
    twist_cos, rotation_sine = dft_rect(inner_size, outer_size, extent, 1.0)
    turned_real = section_real * twist_cos - section_imag * rotation_sine
    turned_imag = section_real * rotation_sine + section_imag * twist_cos
    cos_outer, sin_outer = dft_rect(outer_size, outer_size // 2, outer_size, 1.0)
    out_real = second_section(turned_real, cos_outer) - second_section(turned_imag, sin_outer)
    return out_real.reshape(channels, extent // 2) / extent


def times_spec(left_real, left_imag, right_real, right_imag):
    return (
        left_real * right_real - left_imag * right_imag,
        left_real * right_imag + left_imag * right_real,
    )


def times_conj(left_real, left_imag, right_real, right_imag):
    return (
        left_real * right_real + left_imag * right_imag,
        left_imag * right_real - left_real * right_imag,
    )


def factored_device(
    inputs,
    pre_gain,
    pre_bias,
    in_weight,
    input_projection_bias,
    short_weight,
    short_bias,
    pos_weight,
    pos_bias,
    inner_weight,
    inner_bias,
    filter_third_weight,
    third_bias,
    sine_freq,
    filter_weight,
    decay_rates,
    skip_gains,
    out_weight,
    out_bias,
    post_gain,
    post_bias,
    up_weight,
    up_bias,
    down_weight,
    down_bias,
    cotangent,
):
    seq_parts = lax.axis_size("seq")
    seq_rank = lax.axis_index("seq")
    tokens = inputs[0]
    tok_count = tokens.shape[0]
    model_width = tokens.shape[1]
    length = tok_count * seq_parts
    channels = model_width // seq_parts
    tokens_wide = tokens.astype(jnp.float32)
    pre_gain_f = pre_gain.astype(jnp.float32)
    pre_bias_f = pre_bias.astype(jnp.float32)
    in_bias_f = input_projection_bias.astype(jnp.float32)
    short_f = short_weight.astype(jnp.float32)
    short_bias_f = short_bias.astype(jnp.float32)
    out_bias_f = out_bias.astype(jnp.float32)
    post_gain_f = post_gain.astype(jnp.float32)
    post_bias_f = post_bias.astype(jnp.float32)
    up_bias_f = up_bias.astype(jnp.float32)
    down_bias_f = down_bias.astype(jnp.float32)
    normed, unit_pre, inv_pre = norm_forward(tokens_wide, pre_gain_f, pre_bias_f)
    normed_low = normed.astype(jnp.bfloat16)
    projected = plain_dot(normed_low, in_weight) + in_bias_f
    previous = passed_along(projected[tok_count - 2 :], "seq", 1)
    extended = jnp.concatenate([previous, projected], axis=0)
    mixed_conv = (
        short_f[0] * extended[:-2]
        + short_f[1] * extended[1:-1]
        + short_f[2] * extended[2:]
        + short_bias_f
    )
    value_part = mixed_conv[:, :model_width]
    gate_one = mixed_conv[:, model_width : 2 * model_width]
    gate_two = mixed_conv[:, 2 * model_width :]
    product_low = (value_part * gate_one).astype(jnp.bfloat16)
    gate_two_low = gate_two.astype(jnp.bfloat16)
    prod_chan, gate_chan = (
        lax.all_to_all(product_low.T, "seq", split_axis=0, concat_axis=1, tiled=True),
        lax.all_to_all(gate_two_low.T, "seq", split_axis=0, concat_axis=1, tiled=True),
    )
    features_t, time_steps = position_rows(length, pos_weight.shape[0])
    chan_start = seq_rank * channels
    weight_local = lax.dynamic_slice_in_dim(
        filter_weight.astype(jnp.float32), chan_start, channels, 2
    )
    rates_local = lax.dynamic_slice_in_dim(decay_rates, chan_start, channels, 1)
    skips_local = lax.dynamic_slice_in_dim(skip_gains.astype(jnp.float32), chan_start, channels, 1)
    skip_one = skips_local[0][:, None]
    skip_two = skips_local[1][:, None]
    shared = tuple(
        (
            member.astype(jnp.float32)
            for member in (
                pos_weight,
                pos_bias,
                inner_weight,
                inner_bias,
                filter_third_weight,
                third_bias,
                sine_freq,
            )
        )
    )

    def local_filters(*params):
        return body_filters(features_t, time_steps, *params)

    (kernel_one, kernel_two), filter_pull = jax.vjp(
        local_filters, *shared, weight_local, rates_local
    )
    prod_wide = prod_chan.astype(jnp.float32)
    gate_wide = gate_chan.astype(jnp.float32)
    prod_real, prod_imag = padded_spectrum(prod_wide)
    kone_real, kone_imag = padded_spectrum(kernel_one)
    convolved_real_part, conv_imag = times_spec(prod_real, prod_imag, kone_real, kone_imag)
    after_one = rounded(inverse_real(convolved_real_part, conv_imag) + skip_one * prod_wide)
    gated_low = rounded(after_one * gate_wide)
    gated_real, gated_imag = padded_spectrum(gated_low)
    ktwo_real, ktwo_imag = padded_spectrum(kernel_two)
    convolved_real_part, conv_imag = times_spec(gated_real, gated_imag, ktwo_real, ktwo_imag)
    mixer_chan = (inverse_real(convolved_real_part, conv_imag) + skip_two * gated_low).astype(
        jnp.bfloat16
    )
    mixer_tok = lax.all_to_all(mixer_chan, "seq", split_axis=1, concat_axis=0, tiled=True).T
    branch = plain_dot(mixer_tok, out_weight) + out_bias_f
    residual = tokens_wide + branch
    normed_two, unit_post, inv_post = norm_forward(residual, post_gain_f, post_bias_f)
    normed_two_low = normed_two.astype(jnp.bfloat16)
    upper_pre = plain_dot(normed_two_low, up_weight) + up_bias_f
    activated = jax.nn.gelu(upper_pre, approximate=False).astype(jnp.bfloat16)
    outputs = residual + plain_dot(activated, down_weight) + down_bias_f
    grad_top = cotangent[0]
    grad_top_wide = grad_top.astype(jnp.float32)
    grad_act = right_dot(grad_top, down_weight)
    grad_down = left_dot(activated, grad_top)
    grad_down_bias = jnp.sum(grad_top_wide, axis=0)
    gelu_slope = (
        0.5 * (1.0 + lax.erf(upper_pre * 0.7071067811865476))
        + upper_pre * jnp.exp(-0.5 * upper_pre * upper_pre) * 0.3989422804014327
    )
    grad_upper = (grad_act * gelu_slope).astype(jnp.bfloat16)
    grad_up = left_dot(normed_two_low, grad_upper)
    grad_up_bias = jnp.sum(grad_upper.astype(jnp.float32), axis=0)
    grad_normed_two = right_dot(grad_upper, up_weight)
    grad_resid_norm, grad_post_gain, grad_post_bias = norm_backward(
        grad_normed_two, unit_post, inv_post, post_gain_f
    )
    grad_residual = grad_top_wide + grad_resid_norm
    grad_branch = grad_residual.astype(jnp.bfloat16)
    grad_out = left_dot(mixer_tok, grad_branch)
    grad_out_bias = jnp.sum(grad_branch.astype(jnp.float32), axis=0)
    grad_mixer = right_dot(grad_branch, out_weight).astype(jnp.bfloat16)
    grad_mixer_chan = lax.all_to_all(
        grad_mixer.T, "seq", split_axis=0, concat_axis=1, tiled=True
    ).astype(jnp.float32)
    gmix_real, gmix_imag = padded_spectrum(grad_mixer_chan)
    corr_real, corr_imag = times_conj(gmix_real, gmix_imag, ktwo_real, ktwo_imag)
    grad_gated = rounded(inverse_real(corr_real, corr_imag) + skip_two * grad_mixer_chan)
    corr_real, corr_imag = times_conj(gmix_real, gmix_imag, gated_real, gated_imag)
    grad_kernel_two = inverse_real(corr_real, corr_imag)
    grad_skip_two = jnp.sum(grad_mixer_chan * gated_low, axis=1)
    grad_after = rounded(grad_gated * gate_wide)
    grad_gate_two = (grad_gated * after_one).astype(jnp.bfloat16)
    gaft_real, gaft_imag = padded_spectrum(grad_after)
    corr_real, corr_imag = times_conj(gaft_real, gaft_imag, kone_real, kone_imag)
    grad_product = (inverse_real(corr_real, corr_imag) + skip_one * grad_after).astype(jnp.bfloat16)
    corr_real, corr_imag = times_conj(gaft_real, gaft_imag, prod_real, prod_imag)
    grad_kernel_one = inverse_real(corr_real, corr_imag)
    grad_skip_one = jnp.sum(grad_after * prod_wide, axis=1)
    filter_grads = filter_pull((grad_kernel_one, grad_kernel_two))
    grad_prod_back, grad_gate_back = (
        lax.all_to_all(grad_product, "seq", split_axis=1, concat_axis=0, tiled=True),
        lax.all_to_all(grad_gate_two, "seq", split_axis=1, concat_axis=0, tiled=True),
    )
    grad_prod_wide = grad_prod_back.T.astype(jnp.float32)
    grad_mixed = jnp.concatenate(
        [
            grad_prod_wide * gate_one,
            grad_prod_wide * value_part,
            grad_gate_back.T.astype(jnp.float32),
        ],
        axis=1,
    )
    grad_short_bias = jnp.sum(grad_mixed, axis=0)
    grad_short = jnp.stack(
        [
            jnp.sum(grad_mixed * extended[0:tok_count], axis=0),
            jnp.sum(grad_mixed * extended[1 : tok_count + 1], axis=0),
            jnp.sum(grad_mixed * extended[2 : tok_count + 2], axis=0),
        ]
    )
    zero_rows = jnp.zeros((2, 3 * model_width), jnp.float32)
    padded_grad = jnp.concatenate([zero_rows, grad_mixed, zero_rows], axis=0)
    grad_extended = (
        short_f[0] * padded_grad[2:]
        + short_f[1] * padded_grad[1:-1]
        + short_f[2] * padded_grad[:-2]
    )
    from_next = passed_along(grad_extended[:2], "seq", -1)
    grad_projected = grad_extended[2:].at[tok_count - 2 :].add(from_next)
    grad_proj_low = grad_projected.astype(jnp.bfloat16)
    grad_in = left_dot(normed_low, grad_proj_low)
    grad_in_bias = jnp.sum(grad_proj_low.astype(jnp.float32), axis=0)
    grad_normed = right_dot(grad_proj_low, in_weight)
    grad_tokens_norm, grad_pre_gain, grad_pre_bias = norm_backward(
        grad_normed, unit_pre, inv_pre, pre_gain_f
    )
    grad_inputs = grad_residual + grad_tokens_norm
    shared_sums = lax.psum(
        (
            grad_pre_gain,
            grad_pre_bias,
            grad_in_bias,
            grad_short,
            grad_short_bias,
            filter_grads[0],
            filter_grads[1],
            filter_grads[2],
            filter_grads[3],
            filter_grads[4],
            filter_grads[5],
            filter_grads[6],
            grad_out_bias,
            grad_post_gain,
            grad_post_bias,
            grad_up_bias,
            grad_down_bias,
        ),
        ("batch", "seq"),
    )
    skip_grads = jnp.stack([grad_skip_one, grad_skip_two])
    weight_shards = (
        lax.psum_scatter(grad_in, "seq", scatter_dimension=0, tiled=True),
        lax.psum_scatter(grad_out, "seq", scatter_dimension=0, tiled=True),
        lax.psum_scatter(grad_up, "seq", scatter_dimension=0, tiled=True),
        lax.psum_scatter(grad_down, "seq", scatter_dimension=0, tiled=True),
    )
    final_in, final_out, final_up, final_down, final_filter, final_rates, final_skips = (
        lax.psum(weight_shards[0].astype(jnp.bfloat16), "batch").astype(jnp.float32),
        lax.psum(weight_shards[1].astype(jnp.bfloat16), "batch").astype(jnp.float32),
        lax.psum(weight_shards[2].astype(jnp.bfloat16), "batch").astype(jnp.float32),
        lax.psum(weight_shards[3].astype(jnp.bfloat16), "batch").astype(jnp.float32),
        lax.psum(filter_grads[7].astype(jnp.bfloat16), "batch").astype(jnp.float32),
        lax.psum(filter_grads[8].astype(jnp.bfloat16), "batch").astype(jnp.float32),
        lax.psum(skip_grads.astype(jnp.bfloat16), "batch").astype(jnp.float32),
    )
    return (
        outputs[None],
        grad_inputs[None],
        shared_sums[0],
        shared_sums[1],
        final_in,
        shared_sums[2],
        shared_sums[3],
        shared_sums[4],
        shared_sums[5],
        shared_sums[6],
        shared_sums[7],
        shared_sums[8],
        shared_sums[9],
        shared_sums[10],
        shared_sums[11],
        final_filter,
        final_rates,
        final_skips,
        final_out,
        shared_sums[12],
        shared_sums[13],
        shared_sums[14],
        final_up,
        shared_sums[15],
        final_down,
        shared_sums[16],
    )


LANES = 128
BLOCK = 256
DENSE_LIMIT = 2048
ROW_AT = {
    "pre_gain": 0,
    "pre_bias": 1,
    "in_bias": 2,
    "tap_bias": 5,
    "taps": 8,
    "skips": 17,
    "post_gain": 19,
    "post_bias": 20,
    "out_bias": 21,
    "down_bias": 22,
    "up_bias": 23,
}
ROW_COUNT = 32


def call_kernel(kernel, outs, args, micros, spaces="", scratch=(), limit=60, name=None):
    places = {"v": pltpu.VMEM, "s": pltpu.SMEM, "h": pl.ANY}
    spaces = spaces or "v" * (len(args) + len(outs))
    specs = [pl.BlockSpec(memory_space=places[space]) for space in spaces]
    shapes = [jax.ShapeDtypeStruct(shape, dtype) for shape, dtype in outs]
    return pl.pallas_call(
        kernel,
        out_shape=shapes,
        in_specs=specs[: len(args)],
        out_specs=specs[len(args) :],
        scratch_shapes=[
            pltpu.SemaphoreType.DMA((entry,))
            if isinstance(entry, int)
            else pltpu.VMEM(entry[0], entry[1])
            for entry in scratch
        ],
        compiler_params=pltpu.CompilerParams(vmem_limit_bytes=limit * 1024 * 1024),
        cost_estimate=pl.CostEstimate(
            flops=1, transcendentals=0, bytes_accessed=int(3.0e6 * micros)
        ),
        name=name,
    )(*args)


def row_chunks(source, target, sems, first, count):
    size = source.shape[0] // count
    return [
        pltpu.make_async_copy(
            source.at[pl.ds(place * size, size)],
            target.at[pl.ds(place * size, size)],
            sems.at[first + place],
        )
        for place in range(count)
    ]


def dense_rows(tile):
    tokens, channels = tile.shape
    rows = tokens * channels // LANES
    spare = LANES - channels
    blocks = channels // spare
    pieces = [tile[rows:, block * spare : (block + 1) * spare] for block in range(blocks)]
    return jnp.concatenate([tile[:rows], jnp.concatenate(pieces, axis=0)], axis=1)


def loose_rows(tile, tokens, channels):
    rows = tile.shape[0]
    spare = LANES - channels
    blocks = channels // spare
    rest = tokens - rows
    pieces = [tile[block * rest : (block + 1) * rest, channels:] for block in range(blocks)]
    return jnp.concatenate([tile[:, :channels], jnp.concatenate(pieces, axis=1)], axis=0)


def lays_dense(tokens, channels):
    spare = LANES - channels
    if spare <= 0 or channels % spare or tokens * channels % LANES:
        return False
    rows, blocks = tokens * channels // LANES, channels // spare
    return rows % 8 == 0 and (tokens - rows) * blocks == rows and (tokens - rows) % 8 == 0


def exact_nn(left_side, right_side):
    return jnp.dot(
        left_side, right_side, precision=highest_accuracy, preferred_element_type=jnp.float32
    )


def exact_nt(left_side, right_side):
    return lax.dot_general(
        left_side,
        right_side,
        (((1,), (1,)), ((), ())),
        precision=highest_accuracy,
        preferred_element_type=jnp.float32,
    )


def sine_pair(angle):
    turns = jnp.round(angle * (2.0 / math.pi))
    rest = angle - turns * 1.5703125
    rest = rest - turns * 4.837512969970703125e-4
    rest = rest - turns * 7.549789948768648e-8
    square = rest * rest
    sine = rest + rest * square * (
        -1.6666654611e-1 + square * (8.3321608736e-3 + square * -1.9515295891e-4)
    )
    cosine = (
        1.0
        - 0.5 * square
        + square
        * square
        * (4.166664568298827e-2 + square * (-1.388731625493765e-3 + square * 2.443315711809948e-5))
    )
    quarter = turns.astype(jnp.int32)
    odd = (quarter & 1) == 1
    sine_out = jnp.where(odd, cosine, sine)
    cosine_out = jnp.where(odd, sine, cosine)
    sine_out = jnp.where((quarter & 2) == 2, -sine_out, sine_out)
    cosine_out = jnp.where(((quarter + 1) & 2) == 2, -cosine_out, cosine_out)
    return sine_out, cosine_out


def block_rows(index, size):
    return pl.ds(pl.multiple_of(index * size, size), size)


def wave_pair(index):
    first = index * 2 * BLOCK
    return (
        pl.ds(pl.multiple_of(first, BLOCK), BLOCK),
        pl.ds(pl.multiple_of(first + BLOCK, BLOCK), BLOCK),
    )


def row_of(rows, name, place=0):
    at = ROW_AT[name] + place
    return rows[at : at + 1, :]


def feature_block(first, count, length, feat_count):
    bands = (feat_count - 1) // 2
    place = lax.broadcasted_iota(jnp.int32, (count, feat_count), 0) + first
    lane = lax.broadcasted_iota(jnp.int32, (count, feat_count), 1)
    steps = place.astype(jnp.float32)
    band = jnp.where(lane > bands, lane - 1 - bands, lane - 1).astype(jnp.float32)
    frequency = 0.0001 + band * ((bands - 1 - 0.0001) / (bands - 1))
    sine, cosine = sine_pair(frequency * (steps * (2.0 * math.pi / length)))
    features = jnp.where(lane > bands, -sine, cosine)
    features = jnp.where(lane == 0, steps / (length - 1), features)
    column = lax.broadcasted_iota(jnp.int32, (count, 1), 0) + first
    return features, column.astype(jnp.float32) / (length - 1)


def wave_kernel(channels, start, *refs):
    (
        pre_gain,
        pre_bias,
        in_bias,
        tap_bias,
        taps,
        skips,
        post_gain,
        post_bias,
        out_bias,
        down_bias,
        up_bias,
        pos_bias,
        inner_bias,
        third_bias,
        sine_freq,
        filter_weight,
        decay,
        in_weight_in,
        wave_out,
        back_out,
        rows_out,
        in_out,
        local_out,
        weights_out,
        rates_out,
        vectors_out,
        tables,
        wave,
        back,
        in_weight,
        sems,
    ) = refs
    length = wave.shape[1]
    width = in_weight.shape[0]
    step = tables.shape[1]
    low, f32 = jnp.bfloat16, jnp.float32
    load = pltpu.make_async_copy(in_weight_in, in_weight, sems.at[2])
    load.start()

    def table(which, carry):
        first = which < 2
        at = lax.broadcasted_iota(jnp.int32, (step, length), 0)
        place = lax.broadcasted_iota(jnp.int32, (step, length), 1)
        fine = jnp.where(first, 2, 1)
        scale = jnp.where(which % 2 == 0, fine * step, fine)
        left = at * scale + jnp.where(which == 1, 1, 0)
        right = place * jnp.where(first, 1, 2) + jnp.where(first, 0, 1)
        turn = (left * right) & (4 * length - 1)
        sine, cosine = sine_pair(turn.astype(f32) * (math.pi / (2 * length)))
        tables[2 * which] = cosine
        tables[2 * which + 1] = sine
        return carry

    lax.fori_loop(0, 4, table, 0)
    per_block = BLOCK // step

    def fill(index, carry):
        base = (index // per_block) * (2 * BLOCK) + (index % per_block) * step
        upper = pl.ds(pl.multiple_of(base, step), step)
        lower = pl.ds(pl.multiple_of(base + BLOCK, step), step)
        one = pl.ds(index, 1)
        cos_a, sin_a = tables[0, one, :], tables[1, one, :]
        cos_b, sin_b = tables[2], tables[3]
        wave[upper, :] = (cos_a * cos_b - sin_a * sin_b).astype(low)
        wave[lower, :] = (sin_a * cos_b + cos_a * sin_b).astype(low)
        scale = 1.0 / length
        cos_a, sin_a = tables[4, one, :] * scale, tables[5, one, :] * scale
        cos_b, sin_b = tables[6], tables[7]
        cosine = (cos_a * cos_b - sin_a * sin_b).astype(low)
        sine = (sin_a * cos_b + cos_a * sin_b).astype(low)
        here = block_rows(index, step)
        for part in range(length // BLOCK):
            cols = slice(part * BLOCK, (part + 1) * BLOCK)
            at = part * 2 * BLOCK
            back[here, at : at + BLOCK] = cosine[:, cols]
            back[here, at + BLOCK : at + 2 * BLOCK] = sine[:, cols]
        return carry

    lax.fori_loop(0, length // step, fill, 0)
    sent = [
        pltpu.make_async_copy(wave, wave_out, sems.at[0]),
        pltpu.make_async_copy(back, back_out, sems.at[1]),
    ]
    for copy in sent:
        copy.start()

    rows_out[...] = jnp.zeros_like(rows_out)

    def place_rows(name, vector):
        for number in range(vector.shape[0] // width):
            piece = vector[number * width : (number + 1) * width].astype(f32)
            at = ROW_AT[name] + number
            rows_out[at : at + 1, :] = piece.reshape(1, width)

    for name, vector in (
        ("pre_gain", pre_gain),
        ("pre_bias", pre_bias),
        ("in_bias", in_bias),
        ("tap_bias", tap_bias),
        ("post_gain", post_gain),
        ("post_bias", post_bias),
        ("out_bias", out_bias),
        ("down_bias", down_bias),
        ("up_bias", up_bias),
    ):
        place_rows(name, vector)
    wide_taps = taps[...].astype(f32)
    for tap in range(3):
        for group in range(3):
            at = ROW_AT["taps"] + 3 * tap + group
            rows_out[at : at + 1, :] = wide_taps[tap : tap + 1, group * width : (group + 1) * width]
    at = ROW_AT["skips"]
    rows_out[at : at + 2, :] = skips[...].astype(f32)
    for number, vector in enumerate((pos_bias, inner_bias, third_bias, sine_freq)):
        row = vector[...].astype(f32).reshape(1, vector.shape[0])
        vectors_out[number : number + 1, :] = row

    source = lax.broadcasted_iota(jnp.int32, (width, LANES), 0)
    target = lax.broadcasted_iota(jnp.int32, (width, LANES), 1)
    chosen = (source == start[0] + target) & (target < channels)
    select_wide = jnp.where(chosen, 1.0, 0.0)
    select = select_wide.astype(low)
    local_out[...] = plain_dot(rows_out[...].astype(low), select)
    padded = jnp.concatenate([decay[...], jnp.zeros((6, width), f32)], axis=0)
    rates = exact_nn(padded, select_wide)
    for order in range(2):
        cols = slice(order * LANES, (order + 1) * LANES)
        weights_out[:, cols] = plain_dot(filter_weight[order], select)
        rates_out[:, cols] = rates[order : order + 1]
    load.wait()
    for group in range(3):
        cols = slice(group * LANES, (group + 1) * LANES)
        whole = in_weight[:, group * width : (group + 1) * width]
        in_out[:, cols] = plain_dot(whole, select).astype(low)
    for copy in sent:
        copy.wait()


def filter_kernel(
    pos_weight,
    inner_weight,
    third_weight,
    vectors,
    weights,
    rates,
    wave_in,
    spectrum_out,
    kernel_out,
    waves_out,
    high,
    rest,
    wave,
    sems,
):
    length = wave.shape[1]
    low, f32 = jnp.bfloat16, jnp.float32
    blocks = length // BLOCK
    loads = row_chunks(wave_in, wave, sems, 0, blocks)
    for copy in loads:
        copy.start()
    feat_count, fhid = pos_weight.shape
    freq = vectors[3:4, :]

    def network(index, carry):
        here = block_rows(index, BLOCK)
        features, times = feature_block(index * BLOCK, BLOCK, length, feat_count)
        layer_in = features
        for layer, weight in enumerate((pos_weight, inner_weight, third_weight)):
            inner = exact_nn(layer_in, weight[...].astype(f32)) + vectors[layer : layer + 1, :]
            layer_in, cosine = sine_pair(freq * inner)
            waves_out[layer, here, :] = jnp.concatenate([layer_in, cosine], axis=1)
        kernels = exact_nn(layer_in, weights[...]) * jnp.exp(-rates[...] * times)
        kernel_out[here, :] = kernels
        upper = kernels.astype(low)
        high[here, :] = upper
        rest[here, :] = (kernels - upper.astype(f32)).astype(low)
        return carry

    lax.fori_loop(0, blocks, network, 0)
    for copy in loads:
        copy.wait()

    def spectra(index, carry):
        here = block_rows(index, 2 * BLOCK)
        matrix = wave[here, :]
        spectrum_out[here, :] = plain_dot(matrix, high[...]) + plain_dot(matrix, rest[...])
        return carry

    lax.fori_loop(0, blocks, spectra, 0)


def shifted_down(rows, count):
    place = lax.broadcasted_iota(jnp.int32, rows.shape, 0)
    return jnp.where(place >= count, pltpu.roll(rows, count, 0), 0.0)


def shifted_up(rows, count):
    length = rows.shape[0]
    place = lax.broadcasted_iota(jnp.int32, rows.shape, 0)
    return jnp.where(place < length - count, pltpu.roll(rows, length - count, 0), 0.0)


def short_mix(rows, projected, group):
    taps = [row_of(rows, "taps", 3 * tap + group) for tap in range(3)]
    return (
        taps[0] * shifted_down(projected, 2)
        + taps[1] * shifted_down(projected, 1)
        + taps[2] * projected
        + row_of(rows, "tap_bias", group)
    )


def convolve(wave, back, signal, spectrum, cols, kept, products, finish, arrived=None):
    length = wave.shape[1]
    low = jnp.bfloat16

    def ahead(index, carry):
        both = plain_dot(wave[block_rows(index, 2 * BLOCK), :], signal[...])
        kept[block_rows(index, 2 * BLOCK), :] = both
        upper, lower = wave_pair(index)
        real, imag = times_spec(
            both[:BLOCK], both[BLOCK:], spectrum[upper, cols], spectrum[lower, cols]
        )
        products[upper, :LANES] = real.astype(low)
        products[lower, :LANES] = imag.astype(low)
        return carry

    lax.fori_loop(0, length // BLOCK, ahead, 0)
    if arrived is not None:
        arrived()

    def behind(index, carry):
        here = block_rows(index, 2 * BLOCK)
        finish(here, plain_dot(back[here, :], products[:, :LANES]))
        return carry

    lax.fori_loop(0, length // (2 * BLOCK), behind, 0)


def correlate(wave, back, signal, spectrum, cols, kept, products, finish, arriving=None, arrived=None):
    length = wave.shape[1]
    low = jnp.bfloat16

    def ahead(index, carry):
        if arriving is not None:
            arriving(index)
        both = plain_dot(wave[block_rows(index, 2 * BLOCK), :], signal[...])
        upper, lower = wave_pair(index)
        real, imag = both[:BLOCK], both[BLOCK:]
        first = times_conj(real, imag, spectrum[upper, cols], spectrum[lower, cols])
        second = times_conj(real, imag, kept[upper, :], kept[lower, :])
        products[upper, :LANES] = first[0].astype(low)
        products[lower, :LANES] = first[1].astype(low)
        products[upper, LANES:] = second[0].astype(low)
        products[lower, LANES:] = second[1].astype(low)
        return carry

    lax.fori_loop(0, length // BLOCK, ahead, 0)
    if arrived is not None:
        arrived()

    def behind(index, carry):
        here = block_rows(index, 2 * BLOCK)
        both = plain_dot(back[here, :], products[...])
        return finish(here, both[:, :LANES], both[:, LANES:], carry)

    zero = jnp.zeros((1, LANES), jnp.float32)
    return lax.fori_loop(0, length // (2 * BLOCK), behind, zero)


def front_kernel(parts, index, *refs):
    chunks = refs[:parts]
    (norm_rows, weight, rows, wave_in, back_in, spectrum_in) = refs[parts : 6 + parts]
    (
        pair_out,
        projected_out,
        product_out,
        gate_out,
        after_out,
        gated_out,
        product_wave_out,
        gated_wave_out,
        mixer_out,
        held,
        products,
        wave,
        back,
        spectrum,
        pair,
        projected,
        product_wave,
        gated_wave,
        mixer,
        sems,
    ) = refs[6 + parts :]
    tok_count, width = chunks[0].shape
    length = wave.shape[1]
    channels = width // parts
    low, f32 = jnp.bfloat16, jnp.float32
    loads = [
        pltpu.make_async_copy(source, target, sems.at[place])
        for place, (source, target) in enumerate(
            [(wave_in, wave), (spectrum_in, spectrum), (back_in, back)]
        )
    ]
    stores = [
        pltpu.make_async_copy(source, target, sems.at[3 + place])
        for place, (source, target) in enumerate(
            [
                (pair, pair_out),
                (projected, projected_out),
                (product_wave, product_wave_out),
                (gated_wave, gated_wave_out),
            ]
        )
    ]
    for copy in loads:
        copy.start()
    for part in range(parts):
        held[block_rows(index[0] ^ part, tok_count), :] = chunks[part][...]
    gain = row_of(norm_rows, "pre_gain")
    bias = row_of(norm_rows, "pre_bias")
    in_bias = jnp.concatenate([row_of(rows, "in_bias", group) for group in range(3)], axis=1)

    def project(step, carry):
        here = block_rows(step, BLOCK)
        normed, unit, _ = norm_forward(held[here, :].astype(f32), gain, bias)
        normed = normed.astype(low)
        pair[here, :width] = normed
        pair[here, width:] = unit.astype(low)
        projected[here, :] = plain_dot(normed, weight[...]) + in_bias
        return carry

    lax.fori_loop(0, length // BLOCK, project, 0)
    stores[0].start()
    stores[1].start()
    mixed = [
        short_mix(rows, projected[:, group * LANES : (group + 1) * LANES], group)
        for group in range(2)
    ]
    product_out[...] = (mixed[0] * mixed[1]).astype(low)
    gate_out[...] = short_mix(rows, projected[:, 2 * LANES :], 2).astype(low)

    def first(here, convolved):
        product = product_out[here, :].astype(f32)
        after = (convolved + row_of(rows, "skips", 0) * product).astype(low)
        after_out[here, :] = after
        gated_out[here, :] = (after.astype(f32) * gate_out[here, :].astype(f32)).astype(low)

    def second(here, convolved):
        gated = gated_out[here, :].astype(f32)
        mixer[here, :] = (convolved + row_of(rows, "skips", 1) * gated).astype(low)

    loads[0].wait()
    loads[1].wait()
    cols = [slice(order * LANES, (order + 1) * LANES) for order in range(2)]
    convolve(
        wave,
        back,
        product_out,
        spectrum,
        cols[0],
        product_wave,
        products,
        first,
        arrived=loads[2].wait,
    )
    stores[2].start()
    convolve(wave, back, gated_out, spectrum, cols[1], gated_wave, products, second)
    stores[3].start()
    for part in range(parts):
        tile = mixer[part * tok_count : (part + 1) * tok_count, :channels]
        mixer_out[part] = dense_rows(tile.astype(f32)).astype(low)
    for copy in stores:
        copy.wait()


def back_kernel(
    channels,
    grad_mixer,
    product_ref,
    gate_ref,
    after_ref,
    gated_ref,
    rows,
    product_wave_in,
    gated_wave_in,
    spectrum_in,
    wave_in,
    back_in,
    projected_in,
    packed_out,
    padded_out,
    grad_kernel_out,
    sums_out,
    grad_mix,
    grad_after,
    grad_value,
    grad_gate,
    products,
    wave,
    back,
    spectrum,
    product_wave,
    gated_wave,
    projected,
    sems,
):
    parts = grad_mixer.shape[0]
    length = wave.shape[1]
    tok_count = length // parts
    low, f32 = jnp.bfloat16, jnp.float32
    blocks = length // BLOCK
    loads = [
        (wave_in, wave, blocks),
        (spectrum_in, spectrum, blocks),
        (gated_wave_in, gated_wave, blocks),
    ]
    first_loads = []
    place = 0
    for source, target, count in loads:
        first_loads.append(row_chunks(source, target, sems, place, count))
        place += count
    for block in range(blocks):
        for copies in first_loads:
            copies[block].start()
    later = [
        pltpu.make_async_copy(source, target, sems.at[place + number])
        for number, (source, target) in enumerate(
            [(back_in, back), (product_wave_in, product_wave), (projected_in, projected)]
        )
    ]
    for copy in later:
        copy.start()
    padding = jnp.zeros((tok_count, LANES - channels), f32)
    for part in range(parts):
        tile = loose_rows(grad_mixer[part].astype(f32), tok_count, channels)
        here = slice(part * tok_count, (part + 1) * tok_count)
        grad_mix[here, :] = jnp.concatenate([tile, padding], axis=1).astype(low)

    def arriving(index):
        for number, (source, target, count) in enumerate(loads):
            size = source.shape[0] // count
            part = pl.ds(pl.multiple_of(index * size, size), size)
            pltpu.make_async_copy(
                source.at[part], target.at[part], sems.at[number * blocks + index]
            ).wait()

    def first(here, data, kernel, total):
        grad_kernel_out[here, LANES:] = kernel
        top = grad_mix[here, :].astype(f32)
        grad_gated = (data + row_of(rows, "skips", 1) * top).astype(low).astype(f32)
        grad_after[here, :] = (grad_gated * gate_ref[here, :].astype(f32)).astype(low)
        grad_gate[here, :] = (grad_gated * after_ref[here, :].astype(f32)).astype(low)
        return total + jnp.sum(top * gated_ref[here, :].astype(f32), axis=0, keepdims=True)

    cols = [slice(order * LANES, (order + 1) * LANES) for order in range(2)]
    skip_second = correlate(
        wave,
        back,
        grad_mix,
        spectrum,
        cols[1],
        gated_wave,
        products,
        first,
        arriving=arriving,
        arrived=later[0].wait,
    )

    def second(here, data, kernel, total):
        grad_kernel_out[here, :LANES] = kernel
        top = grad_after[here, :].astype(f32)
        grad_value[here, :] = (data + row_of(rows, "skips", 0) * top).astype(low)
        return total + jnp.sum(top * product_ref[here, :].astype(f32), axis=0, keepdims=True)

    later[1].wait()
    skip_first = correlate(
        wave, back, grad_after, spectrum, cols[0], product_wave, products, second
    )
    sums_out[15:16, :] = skip_first
    sums_out[16:17, :] = skip_second
    sums_out[17:24, :] = jnp.zeros((7, LANES), f32)
    later[2].wait()
    for group in range(3):
        here = slice(group * LANES, (group + 1) * LANES)
        if group == 2:
            grad_mixed = grad_gate[...].astype(f32)
        else:
            other = slice((1 - group) * LANES, (2 - group) * LANES)
            grad_mixed = grad_value[...].astype(f32) * short_mix(
                rows, projected[:, other], 1 - group
            )
        taps = [row_of(rows, "taps", 3 * tap + group) for tap in range(3)]
        plain = projected[:, here]
        for tap in range(3):
            at = 3 * tap + group
            moved = plain if tap == 2 else shifted_down(plain, 2 - tap)
            sums_out[at : at + 1, :] = jnp.sum(grad_mixed * moved, axis=0, keepdims=True)
        sums_out[9 + group : 10 + group, :] = jnp.sum(grad_mixed, axis=0, keepdims=True)
        grad_projected = (
            taps[0] * shifted_up(grad_mixed, 2)
            + taps[1] * shifted_up(grad_mixed, 1)
            + taps[2] * grad_mixed
        ).astype(low)
        padded_out[:, here] = grad_projected
        wide = grad_projected.astype(f32)
        sums_out[12 + group : 13 + group, :] = jnp.sum(wide, axis=0, keepdims=True)
    dense = packed_out.shape[1] // 3

    def pack(part, carry):
        tokens = block_rows(part, tok_count)
        for group in range(3):
            tile = padded_out[tokens, group * LANES : group * LANES + channels]
            packed = dense_rows(tile.astype(f32)).astype(low)
            packed_out[part, group * dense : (group + 1) * dense, :] = packed
        return carry

    lax.fori_loop(0, parts, pack, 0)


def store_rows(target, at, value):
    per = target.shape[1]
    place = 0
    while place < value.shape[0]:
        quarter, inside = divmod(at + place, per)
        count = min(value.shape[0] - place, per - inside)
        target[quarter, inside : inside + count, :] = value[place : place + count]
        place += count


def lane_rows(vector):
    count = vector.shape[1] // LANES
    return jnp.concatenate(
        [vector[:, place * LANES : (place + 1) * LANES] for place in range(count)], axis=0
    )


def middle_kernel(
    parts,
    batch_index,
    received,
    tokens,
    top,
    rows,
    out_in,
    up_in,
    down_in,
    outputs_out,
    residual_out,
    sides_out,
    send_out,
    sums_out,
    *refs,
):
    batch = len(refs) - 12
    got_out = refs[:batch]
    (
        out_w,
        up_w,
        down_w,
        residual,
        total,
        flow,
        act,
        upper_grad,
        act_parts,
        branch_parts,
        up_rows,
        sems,
    ) = refs[batch:]
    tok_count, width = tokens.shape
    channels = width // parts
    f32, low = jnp.float32, jnp.bfloat16
    quarters = up_w.shape[0]
    quarter = up_w.shape[2]
    load_out = pltpu.make_async_copy(out_in, out_w, sems.at[0])
    load_out.start()

    def loads(place):
        cols = pl.ds(pl.multiple_of(place * quarter, quarter), quarter)
        return (
            pltpu.make_async_copy(up_in.at[:, cols], up_w.at[place], sems.at[1 + place]),
            pltpu.make_async_copy(
                down_in.at[cols, :], down_w.at[place], sems.at[1 + quarters + place]
            ),
        )

    for place in range(quarters):
        for copy in loads(place):
            copy.start()
    tiles = [
        loose_rows(received[part].astype(f32), tok_count, channels) for part in range(parts)
    ]
    mixer = jnp.concatenate(tiles, axis=1).astype(low)
    sides_out[:, width : 2 * width] = mixer
    load_out.wait()
    branch = plain_dot(mixer, out_w[...]) + row_of(rows, "out_bias")
    residual[...] = tokens[...].astype(f32) + branch
    gain = row_of(rows, "post_gain")
    bias = row_of(rows, "post_bias")
    normed, _, _ = norm_forward(residual[...], gain, bias)
    sides_out[:, :width] = normed.astype(low)
    for place in range(quarters):
        up_rows[place] = row_of(rows, "up_bias", place)
    total[...] = jnp.zeros_like(total)
    flow[...] = jnp.zeros_like(flow)

    def body(place, carry):
        for copy in loads(place):
            copy.wait()
        upper = plain_dot(sides_out[:, :width], up_w[place]) + up_rows[place]
        gauss = 0.5 * (1.0 + lax.erf(upper * 0.7071067811865476))
        active = (upper * gauss).astype(low)
        act[place] = active
        total[...] += plain_dot(active, down_w[place])
        grad_act = right_dot(top[...], down_w[place])
        slope = gauss + upper * jnp.exp(-0.5 * upper * upper) * 0.3989422804014327
        grad_upper = (grad_act * slope).astype(low)
        upper_grad[place] = grad_upper
        flow[...] += right_dot(grad_upper, up_w[place])
        return carry

    lax.fori_loop(0, quarters, body, 0)
    outputs_out[...] = residual[...] + total[...] + row_of(rows, "down_bias")
    _, unit, inv_std = norm_forward(residual[...], gain, bias)
    grad_norm, grad_gain, grad_bias = norm_backward(flow[...], unit, inv_std, gain)
    grad_residual = top[...].astype(f32) + grad_norm
    residual_out[...] = grad_residual
    grad_branch = grad_residual.astype(low)
    grad_mixer = right_dot(grad_branch, out_w[...])
    for part in range(parts):
        tile = grad_mixer[:, part * channels : (part + 1) * channels]
        send_out[part] = dense_rows(tile).astype(low)
    wide_branch = grad_branch.astype(f32)
    vectors = [
        jnp.sum(wide_branch, axis=0, keepdims=True),
        grad_gain[None],
        grad_bias[None],
        jnp.sum(top[...].astype(f32), axis=0, keepdims=True),
    ]
    vectors += [
        jnp.sum(upper_grad[place].astype(f32), axis=0, keepdims=True) for place in range(quarters)
    ]
    per = width // LANES
    for number, vector in enumerate(vectors):
        sums_out[number * per : (number + 1) * per, :] = lane_rows(vector)
    piece = width // batch
    for place in range(batch):
        branch_parts[place] = wide_branch[:, place * piece : (place + 1) * piece].astype(low)
    step = quarters * quarter // (parts * batch)
    per_part = quarters * quarter // parts
    for place in range(batch):
        tiles = []
        for part in range(parts):
            at = part * per_part + place * step
            inside = at % quarter
            tiles.append(act[at // quarter, :, inside : inside + step].astype(f32))
        act_parts[place] = jnp.concatenate(tiles, axis=1).astype(low)
    for bits in range(batch):
        place = batch_index[0] ^ bits
        got_out[bits][:, :quarter] = upper_grad[place]
        got_out[bits][:, quarter : quarter + parts * step] = act_parts[place]
        got_out[bits][:, quarter + parts * step :] = branch_parts[place]


def weight_kernel(batch, *refs):
    sides, tops, gots = (refs[batch * place : batch * (place + 1)] for place in range(3))
    up_out, rest_out, flipped, columns = refs[3 * batch :]
    tok_count, width = tops[0].shape
    quarter = up_out.shape[1]
    for bits in range(batch):
        here = slice(bits * tok_count, (bits + 1) * tok_count)
        columns[here, :quarter] = gots[bits][:, :quarter]
        columns[here, quarter : quarter + width] = tops[bits][...]
        columns[here, quarter + width :] = gots[bits][:, quarter + width :]
        flipped[:width, here] = sides[bits][:, :width].astype(jnp.float32).T.astype(jnp.bfloat16)
        flipped[width : 2 * width, here] = (
            gots[bits][:, quarter : quarter + width].astype(jnp.float32).T.astype(jnp.bfloat16)
        )
        flipped[2 * width :, here] = (
            sides[bits][:, width : 2 * width].astype(jnp.float32).T.astype(jnp.bfloat16)
        )
    size = width // 3
    for third in range(3):
        rows = slice(third * size, (third + 1) * size)
        up_out[rows, :] = plain_dot(flipped[rows, :], columns[:, :quarter])
        middle = slice(width + third * size, width + (third + 1) * size)
        rest_out[rows, :width] = plain_dot(
            flipped[middle, :], columns[:, quarter : quarter + width]
        )
        last = slice(2 * width + third * size, 2 * width + (third + 1) * size)
        rest_out[rows, width:] = plain_dot(flipped[last, :], columns[:, quarter + width :])


def final_kernel(received, tokens, residual, rows, weight_in, out, weight, joined, sems):
    parts = received.shape[0]
    tok_count, width = tokens.shape
    channels = width // parts
    f32, low = jnp.float32, jnp.bfloat16
    load = pltpu.make_async_copy(weight_in, weight, sems.at[0])
    load.start()
    dense = received.shape[1] // 3
    for group in range(3):
        tiles = [
            loose_rows(
                received[part, group * dense : (group + 1) * dense, :].astype(f32),
                tok_count,
                channels,
            )
            for part in range(parts)
        ]
        joined[:, group * width : (group + 1) * width] = jnp.concatenate(tiles, axis=1).astype(low)
    gain = row_of(rows, "pre_gain")
    bias = row_of(rows, "pre_bias")
    _, unit, inv_std = norm_forward(tokens[...].astype(f32), gain, bias)
    load.wait()
    grad_normed = jnp.zeros((tok_count, width), f32)
    for group in range(3):
        cols = slice(group * width, (group + 1) * width)
        grad_normed = grad_normed + right_dot(joined[:, cols], weight[:, cols])
    grad_tokens, _, _ = norm_backward(grad_normed, unit, inv_std, gain)
    out[...] = residual[...] + grad_tokens


SHARED_ROWS = 48
LAID_ROWS = 8
OWN_ROWS = 40


def chain_kernel(
    in_local,
    sums,
    middle_sums,
    pos_weight,
    inner_weight,
    third_weight,
    vectors,
    weights,
    rates,
    grad_kernels_in,
    kernels_in,
    waves_in,
    pair_in,
    small_out,
    weight_total,
    rate_total,
    shared,
    grad_kernels,
    kernels,
    waves,
    pair_sums,
    sems,
):
    length = kernels.shape[0]
    blocks = length // BLOCK

    def loads(index):
        here = block_rows(index, BLOCK)
        return [
            pltpu.make_async_copy(
                grad_kernels_in.at[here], grad_kernels.at[here], sems.at[index]
            ),
            pltpu.make_async_copy(kernels_in.at[here], kernels.at[here], sems.at[blocks + index]),
            pltpu.make_async_copy(
                waves_in.at[:, here], waves.at[:, here], sems.at[2 * blocks + index]
            ),
        ]

    for block in range(blocks):
        for copy in loads(block):
            copy.start()
    width = in_local.shape[0]
    pair_load = pltpu.make_async_copy(
        pair_in.at[pl.ds(width, width)], pair_sums, sems.at[3 * blocks]
    )
    pair_load.start()
    feat_count, fhid = pos_weight.shape
    f32 = jnp.float32
    freq = vectors[3:4, :]
    weight_total[...] = jnp.zeros_like(weight_total)
    rate_total[...] = jnp.zeros_like(rate_total)
    shared[...] = jnp.zeros_like(shared)

    def body(index, carry):
        here = block_rows(index, BLOCK)
        for copy in loads(index):
            copy.wait()
        features, times = feature_block(index * BLOCK, BLOCK, length, feat_count)
        grads = grad_kernels[here, :]
        decayed = jnp.sum(grads * kernels[here, :] * times, axis=0, keepdims=True)
        rate_total[...] = rate_total[...] - decayed
        windowed = grads * jnp.exp(-rates[...] * times)
        weight_total[...] = weight_total[...] + exact_tdot(waves[2, here, :fhid], windowed)
        flow = exact_nt(windowed, weights[...])
        at, bias_at = 0, 2 * fhid + feat_count
        for layer in (2, 1, 0):
            slope = flow * waves[layer, here, fhid:]
            below = waves[layer - 1, here, :fhid] if layer else features
            count = below.shape[1]
            shared[at : at + count, :] = shared[at : at + count, :] + exact_tdot(below, slope)
            at += count
            row = slice(bias_at + layer, bias_at + layer + 1)
            shared[row, :] = shared[row, :] + jnp.sum(slope, axis=0, keepdims=True)
            if layer:
                weight = inner_weight if layer == 1 else third_weight
                flow = exact_nt(slope * freq, weight[...].astype(f32))
        return carry

    lax.fori_loop(0, blocks, body, 0)
    grad_freq = jnp.zeros_like(freq)
    at, bias_at = 0, 2 * fhid + feat_count
    for layer, weight in ((2, third_weight), (1, inner_weight), (0, pos_weight)):
        count = weight.shape[0]
        matrix = shared[at : at + count, :]
        row = slice(bias_at + layer, bias_at + layer + 1)
        grad_freq = grad_freq + jnp.sum(weight[...].astype(f32) * matrix, axis=0, keepdims=True)
        grad_freq = grad_freq + vectors[layer : layer + 1, :] * shared[row, :]
        shared[at : at + count, :] = matrix * freq
        shared[row, :] = shared[row, :] * freq
        at += count
    shared[bias_at + 3 : bias_at + 4, :] = grad_freq
    pair_load.wait()
    small_out[...] = jnp.zeros_like(small_out)
    ones = jnp.ones((8, in_local.shape[1]), f32)
    in_wide = in_local[...].astype(f32)
    gain = exact_nt(ones, in_wide * pair_sums[...])[0:1]
    column_sums = jnp.concatenate([sums[12 + group : 13 + group, :] for group in range(3)], axis=1)
    bias = exact_nt(jnp.broadcast_to(column_sums, ones.shape), in_wide)[0:1]
    everywhere = small_out.at[:, :SHARED_ROWS, :]
    per = width // LANES
    store_rows(everywhere, 0, lane_rows(gain))
    store_rows(everywhere, per, lane_rows(bias))
    at = 2 * per
    store_rows(everywhere, at, middle_sums[...])
    at += middle_sums.shape[0]
    store_rows(everywhere, at, jnp.concatenate([shared[:fhid, :], shared[fhid : 2 * fhid, :]], axis=1))
    at += fhid
    tail = shared[2 * fhid : 2 * fhid + feat_count + 4, :]
    store_rows(everywhere, at, jnp.concatenate([tail, jnp.zeros_like(tail)], axis=1))
    store_rows(small_out.at[:, SHARED_ROWS : SHARED_ROWS + LAID_ROWS, :], 0, sums[:15, :])
    own = small_out.at[:, SHARED_ROWS + LAID_ROWS :, :]
    for order in range(2):
        cols = slice(order * LANES, (order + 1) * LANES)
        store_rows(own, order * fhid, weight_total[:, cols])
        store_rows(own, 2 * fhid + order, rate_total[:, cols])
    store_rows(own, 2 * fhid + 2, sums[15:17, :])


def spread_kernel(in_keep, in_got, small_keep, small_got, send_out, small_out):
    low, f32 = jnp.bfloat16, jnp.float32
    parts = send_out.shape[0]
    small = small_keep[...] + small_got[...]
    small_out[...] = small
    both = SHARED_ROWS + LAID_ROWS
    high, rest = split_low(small[:both])
    count = in_keep.shape[0] // parts
    for part in range(parts):
        here = slice(part * count, (part + 1) * count)
        send_out[part, :count, :] = (in_keep[here, :] + in_got[here, :].astype(f32)).astype(low)
        send_out[part, count : count + both, :] = high
        send_out[part, count + both :, :] = rest


def merge_kernel(received, small, out):
    f32 = jnp.float32
    parts = received.shape[0]
    both = SHARED_ROWS + LAID_ROWS
    count = received.shape[1] - 2 * both
    total = jnp.zeros((SHARED_ROWS, LANES), f32)
    done = parts * count
    rows = SHARED_ROWS + parts * LAID_ROWS + OWN_ROWS
    for part in range(parts):
        out[part * count : (part + 1) * count, :] = received[part, :count, :]
        high = received[part, count : count + both, :].astype(f32)
        rest = received[part, count + both :, :].astype(f32)
        total = total + high[:SHARED_ROWS] + rest[:SHARED_ROWS]
        at = done + SHARED_ROWS + part * LAID_ROWS
        laid = received[part, count : count + both, :].astype(f32)[SHARED_ROWS:]
        out[at : at + LAID_ROWS, :] = laid.astype(jnp.bfloat16)
        laid = received[part, count + both :, :].astype(f32)[SHARED_ROWS:]
        out[at + rows : at + rows + LAID_ROWS, :] = laid.astype(jnp.bfloat16)
    for at, value in ((0, total), (rows - OWN_ROWS, small[SHARED_ROWS + LAID_ROWS :, :])):
        high, rest = split_low(value)
        count = value.shape[0]
        out[done + at : done + at + count, :] = high
        out[done + rows + at : done + rows + at + count, :] = rest


def take_rows(source, at, count):
    per = source.shape[1]
    pieces = []
    while count:
        quarter, inside = divmod(at, per)
        size = min(count, per - inside)
        pieces.append(source[quarter, inside : inside + size, :])
        at += size
        count -= size
    return pieces[0] if len(pieces) == 1 else jnp.concatenate(pieces, axis=0)


def lane_row(block):
    return jnp.concatenate([block[place : place + 1] for place in range(block.shape[0])], axis=1)


def finish_kernel(batch, channels, batch_index, *refs):
    entries = refs[:batch]
    (
        in_out,
        pre_gain_out,
        pre_bias_out,
        out_bias_out,
        post_gain_out,
        post_bias_out,
        down_bias_out,
        up_bias_out,
        third_out,
        inner_out,
        pos_out,
        pos_bias_out,
        inner_bias_out,
        third_bias_out,
        freq_out,
        taps_out,
        tap_bias_out,
        in_bias_out,
        filter_out,
        rates_out,
        skips_out,
        held,
        small,
    ) = refs[batch:]
    f32 = jnp.float32
    for bits in range(batch):
        held[batch_index[0] ^ bits] = entries[bits][...]
    in_rows = in_out.shape[0] // batch
    width = pre_gain_out.shape[0]
    parts = width // channels
    total = parts * 3 * in_rows
    rows = small.shape[1]
    for place in range(batch):
        small[place] = held[place, total : total + rows, :].astype(f32) + held[
            place, total + rows :, :
        ].astype(f32)

    def gather(place, carry):
        block = held[place, :total, :].astype(f32)
        tiles = []
        for group in range(3):
            for part in range(parts):
                at = (part * 3 + group) * in_rows
                tiles.append(block[at : at + in_rows, :channels])
        in_out[pl.ds(pl.multiple_of(place * in_rows, in_rows), in_rows), :] = jnp.concatenate(
            tiles, axis=1
        )
        return carry

    lax.fori_loop(0, batch, gather, 0)
    everywhere = small.at[:, :SHARED_ROWS, :]
    per = width // LANES
    at = 0
    for target in (
        pre_gain_out,
        pre_bias_out,
        out_bias_out,
        post_gain_out,
        post_bias_out,
        down_bias_out,
        up_bias_out,
    ):
        count = target.shape[0] // LANES
        target[...] = lane_row(take_rows(everywhere, at, count)).reshape(target.shape)
        at += count
    fhid = third_out.shape[0]
    pair = take_rows(everywhere, at, fhid)
    third_out[...] = pair[:, :fhid]
    inner_out[...] = pair[:, fhid : 2 * fhid]
    at += fhid
    tail = take_rows(everywhere, at, pos_out.shape[0] + 4)
    pos_out[...] = tail[: pos_out.shape[0], :fhid]
    for place, target in enumerate((pos_bias_out, inner_bias_out, third_bias_out, freq_out)):
        row = pos_out.shape[0] + place
        target[...] = tail[row : row + 1, :fhid].reshape(target.shape)

    def laid(number):
        place, row = divmod(number, LAID_ROWS)
        return [
            small[place, SHARED_ROWS + part * LAID_ROWS + row :][:1, :channels]
            for part in range(parts)
        ]

    for number in range(5):
        tiles = [tile for group in range(3) for tile in laid(3 * number + group)]
        row = jnp.concatenate(tiles, axis=1)
        if number < 3:
            taps_out[number : number + 1, :] = row
        elif number == 3:
            tap_bias_out[...] = row.reshape(tap_bias_out.shape)
        else:
            in_bias_out[...] = row.reshape(in_bias_out.shape)
    own = small.at[:, SHARED_ROWS + parts * LAID_ROWS :, :]
    for order in range(2):
        filter_out[order] = take_rows(own, order * fhid, fhid)[:, :channels]
    rates_out[...] = take_rows(own, 2 * fhid, 2)[:, :channels]
    skips_out[...] = take_rows(own, 2 * fhid + 2, 2)[:, :channels]


def swapped(value, axis, bits):
    count = lax.axis_size(axis)
    return lax.ppermute(value, axis, [(source, source ^ bits) for source in range(count)])


def over_batch(value):
    held = {0: value}
    bits = lax.axis_size("batch") // 2
    while bits:
        held.update({place ^ bits: swapped(member, "batch", bits) for place, member in held.items()})
        bits //= 2
    return [held[place] for place in range(len(held))]


def natural(entries, index):
    stacked = jnp.stack(entries)
    return [
        lax.dynamic_index_in_dim(stacked, index ^ place, 0, keepdims=False)
        for place in range(len(entries))
    ]


def halves(total, index, bits, left):
    shape = total.shape[1:]
    place = left.index(bits)
    before = 1 << (len(left) - 1 - place)
    after = 1 << place
    view = total.reshape((before, 2, after) + shape)
    bit = (index // bits) % 2
    keep = lax.dynamic_index_in_dim(view, bit, 1, keepdims=False)
    send = lax.dynamic_index_in_dim(view, 1 - bit, 1, keepdims=False)
    return keep.reshape((before * after,) + shape), send.reshape((before * after,) + shape)


def halved(total, axis, index, order):
    count = lax.axis_size(axis)
    left = [1 << k for k in range(count.bit_length() - 1)]
    for bits in order:
        keep, send = halves(total, index, bits, left)
        got = swapped(send.astype(jnp.bfloat16), axis, bits)
        total = keep + got.astype(jnp.float32)
        left.remove(bits)
    return total[0]


def split_low(value):
    high = value.astype(jnp.bfloat16)
    return high, (value - high.astype(jnp.float32)).astype(jnp.bfloat16)


def dense_device(
    inputs,
    pre_gain,
    pre_bias,
    in_weight,
    input_projection_bias,
    short_weight,
    short_bias,
    pos_weight,
    pos_bias,
    inner_weight,
    inner_bias,
    filter_third_weight,
    third_bias,
    sine_freq,
    filter_weight,
    decay_rates,
    skip_gains,
    out_weight,
    out_bias,
    post_gain,
    post_bias,
    up_weight,
    up_bias,
    down_weight,
    down_bias,
    cotangent,
):
    seq_parts = lax.axis_size("seq")
    batch_parts = lax.axis_size("batch")
    seq_rank = lax.axis_index("seq")
    batch_rank = lax.axis_index("batch")
    tokens = inputs[0]
    tok_count, width = tokens.shape
    length = tok_count * seq_parts
    channels = width // seq_parts
    hidden_units = up_weight.shape[1]
    fhid = pos_weight.shape[1]
    f32, low = jnp.float32, jnp.bfloat16
    wide = 3 * LANES
    start = seq_rank * channels
    bit_list = [1 << k for k in range(seq_parts.bit_length() - 1)]
    swap_list = [bit_list[1], bit_list[0]] + bit_list[2:]
    batch_bits = [1 << k for k in range(batch_parts.bit_length() - 1)]

    chunks = {0: tokens}
    for bits in range(2, seq_parts, 2):
        chunks[bits] = swapped(tokens, "seq", bits)

    quarters = hidden_units // width
    seq_scalar = seq_rank.astype(jnp.int32)[None]
    batch_scalar = batch_rank.astype(jnp.int32)[None]
    start_scalar = start.astype(jnp.int32)[None]
    wave, back, rows, in_local, rows_local, weights_local, rates_local, vectors = call_kernel(
        lambda *refs: wave_kernel(channels, *refs),
        [
            ((2 * length, length), low),
            ((length, 2 * length), low),
            ((ROW_COUNT, width), f32),
            ((width, wide), low),
            ((ROW_COUNT, LANES), f32),
            ((fhid, 2 * LANES), f32),
            ((1, 2 * LANES), f32),
            ((4, fhid), f32),
        ],
        [
            start_scalar,
            pre_gain,
            pre_bias,
            input_projection_bias,
            short_bias,
            short_weight,
            skip_gains,
            post_gain,
            post_bias,
            out_bias,
            down_bias,
            up_bias,
            pos_bias,
            inner_bias,
            third_bias,
            sine_freq,
            filter_weight,
            decay_rates,
            in_weight,
        ],
        micros=8.5,
        spaces="s" + "v" * 17 + "h" + "hh" + "v" * 6,
        scratch=[
            ((8, 32, length), f32),
            ((2 * length, length), low),
            ((length, 2 * length), low),
            ((width, 3 * width), low),
            3,
        ],
        name="waves",
    )
    even = [chunks[bits] for bits in range(2, seq_parts, 2)]
    wave, *even = lax.optimization_barrier((wave, *even))
    for bits in range(0, seq_parts, 2):
        if bits:
            chunks[bits] = even[bits // 2 - 1]
        chunks[bits + 1] = swapped(chunks[bits], "seq", 1)
    spectrum, kernels, filter_waves = call_kernel(
        filter_kernel,
        [
            ((2 * length, 2 * LANES), f32),
            ((length, 2 * LANES), f32),
            ((3, length, 2 * fhid), f32),
        ],
        [
            pos_weight,
            inner_weight,
            filter_third_weight,
            vectors,
            weights_local,
            rates_local,
            wave,
        ],
        micros=13,
        spaces="v" * 6 + "h" + "vvv",
        scratch=[
            ((length, 2 * LANES), low),
            ((length, 2 * LANES), low),
            ((2 * length, length), low),
            length // BLOCK,
        ],
        name="filters",
    )
    grad_top = cotangent[0]
    tops = over_batch(grad_top)
    spectrum, *tops = lax.optimization_barrier((spectrum, *tops))

    dense = tok_count * channels // LANES
    (
        norm_pair,
        projected,
        product,
        gate,
        after,
        gated,
        product_wave,
        gated_wave,
        mixer_chan,
    ) = call_kernel(
        lambda *refs: front_kernel(seq_parts, *refs),
        [
            ((length, 2 * width), low),
            ((length, wide), f32),
            ((length, LANES), low),
            ((length, LANES), low),
            ((length, LANES), low),
            ((length, LANES), low),
            ((2 * length, LANES), f32),
            ((2 * length, LANES), f32),
            ((seq_parts, dense, LANES), low),
        ],
        [seq_scalar]
        + [chunks[part] for part in range(seq_parts)]
        + [rows, in_local, rows_local, wave, back, spectrum],
        micros=13,
        spaces="s" + "v" * seq_parts + "vvvhhh" + "hhvvvvhhv",
        scratch=[
            ((length, width), low),
            ((2 * length, LANES), low),
            ((2 * length, length), low),
            ((length, 2 * length), low),
            ((2 * length, 2 * LANES), f32),
            ((length, 2 * width), low),
            ((length, wide), f32),
            ((2 * length, LANES), f32),
            ((2 * length, LANES), f32),
            ((length, LANES), low),
            7,
        ],
        name="front",
    )
    mixer_back = lax.all_to_all(mixer_chan, "seq", 0, 0, tiled=True)

    quarter = hidden_units // batch_parts
    branch_quarter = width // batch_parts
    rows_quarter = hidden_units // (seq_parts * batch_parts)
    assert quarter == width and seq_parts * rows_quarter == width
    got_width = quarter + width + branch_quarter
    outputs, grad_residual, sides, grad_mixer, middle_sums, *gots = call_kernel(
        lambda *refs: middle_kernel(seq_parts, *refs),
        [
            ((tok_count, width), f32),
            ((tok_count, width), f32),
            ((tok_count, 2 * width), low),
            ((seq_parts, dense, LANES), low),
            (((4 * width + hidden_units) // LANES, LANES), f32),
        ]
        + [((tok_count, got_width), low)] * batch_parts,
        [
            batch_scalar,
            mixer_back,
            tokens,
            grad_top,
            rows,
            out_weight,
            up_weight,
            down_weight,
        ],
        micros=11,
        spaces="svvvvhhh" + "v" * (5 + batch_parts),
        scratch=[
            ((width, width), low),
            ((quarters, width, width), low),
            ((quarters, width, width), low),
            ((tok_count, width), f32),
            ((tok_count, width), f32),
            ((tok_count, width), f32),
            ((quarters, tok_count, width), low),
            ((quarters, tok_count, width), low),
            ((batch_parts, tok_count, width), low),
            ((batch_parts, tok_count, branch_quarter), low),
            ((quarters, 1, width), f32),
            1 + 2 * quarters,
        ],
        name="middle",
    )
    grad_mixer_chan = lax.all_to_all(grad_mixer, "seq", 0, 0, tiled=True)

    sides = over_batch(sides)
    gots = [gots[0]] + [swapped(gots[bits], "batch", bits) for bits in range(1, batch_parts)]
    up_part, rest_part = call_kernel(
        lambda *refs: weight_kernel(batch_parts, *refs),
        [((width, quarter), f32), ((width, width + branch_quarter), f32)],
        sides + tops + gots,
        micros=6,
        scratch=[
            ((3 * width, batch_parts * tok_count), low),
            ((batch_parts * tok_count, got_width), low),
        ],
        name="weights",
    )
    blocks = length // BLOCK
    packed, grad_proj, grad_kernels, sums = call_kernel(
        lambda *refs: back_kernel(channels, *refs),
        [
            ((seq_parts, 3 * dense, LANES), low),
            ((length, wide), low),
            ((length, 2 * LANES), f32),
            ((24, LANES), f32),
        ],
        [
            grad_mixer_chan,
            product,
            gate,
            after,
            gated,
            rows_local,
            product_wave,
            gated_wave,
            spectrum,
            wave,
            back,
            projected,
        ],
        micros=15,
        spaces="v" * 6 + "h" * 6 + "vvvv",
        scratch=[((length, LANES), low)] * 4
        + [
            ((2 * length, 2 * LANES), low),
            ((2 * length, length), low),
            ((length, 2 * length), low),
            ((2 * length, 2 * LANES), f32),
            ((2 * length, LANES), f32),
            ((2 * length, LANES), f32),
            ((length, wide), f32),
            3 * blocks + 3,
        ],
        name="back",
    )
    proj_back = lax.all_to_all(packed, "seq", 0, 0, tiled=True)
    pair_part = left_dot(norm_pair, grad_proj)
    in_rows = width // (seq_parts * batch_parts)
    in_count = 3 * in_rows
    in_part = (
        pair_part[:width]
        .reshape(seq_parts, batch_parts, in_rows, 3, LANES)
        .transpose(1, 0, 3, 2, 4)
        .reshape(batch_parts, seq_parts * in_count, LANES)
    )
    small_rows = SHARED_ROWS + LAID_ROWS + OWN_ROWS
    pair_part, in_part, up_part, rest_part = lax.optimization_barrier(
        (pair_part, in_part, up_part, rest_part)
    )
    up_quarter = halved(
        up_part.reshape(seq_parts, -1, quarter), "seq", seq_rank, bit_list
    ).astype(low)
    rest_quarter = halved(
        rest_part.reshape(seq_parts, -1, width + branch_quarter), "seq", seq_rank, swap_list
    ).astype(low)
    weights_all = natural(
        over_batch(jnp.concatenate([up_quarter, rest_quarter], axis=1)), batch_rank
    )
    final_up = jnp.concatenate([part[:, :quarter] for part in weights_all], axis=1).astype(f32)
    final_down = jnp.concatenate(
        [part[:, quarter : quarter + width] for part in weights_all], axis=0
    ).astype(f32)
    final_out = jnp.concatenate(
        [part[:, quarter + width :] for part in weights_all], axis=1
    ).astype(f32)
    (small,) = call_kernel(
        chain_kernel,
        [((batch_parts, small_rows, LANES), f32)],
        [
            in_local,
            sums,
            middle_sums,
            pos_weight,
            inner_weight,
            filter_third_weight,
            vectors,
            weights_local,
            rates_local,
            grad_kernels,
            kernels,
            filter_waves,
            pair_part,
        ],
        micros=12,
        spaces="v" * 9 + "hhhh" + "v",
        scratch=[
            ((fhid, 2 * LANES), f32),
            ((1, 2 * LANES), f32),
            ((2 * fhid + 40, fhid), f32),
            ((length, 2 * LANES), f32),
            ((length, 2 * LANES), f32),
            ((3, length, 2 * fhid), f32),
            ((width, wide), f32),
            3 * blocks + 1,
        ],
        name="chain",
    )
    small, proj_back = lax.optimization_barrier((small, proj_back))
    left = list(batch_bits)
    for bits in batch_bits[:-1]:
        in_keep, in_send = halves(in_part, batch_rank, bits, left)
        small_keep, small_send = halves(small, batch_rank, bits, left)
        in_part = in_keep + swapped(in_send.astype(low), "batch", bits).astype(f32)
        small = small_keep + swapped(small_send, "batch", bits)
        left.remove(bits)
    in_keep, in_send = halves(in_part, batch_rank, batch_bits[-1], left)
    small_keep, small_send = halves(small, batch_rank, batch_bits[-1], left)
    shared_count = in_count + 2 * (SHARED_ROWS + LAID_ROWS)
    mixed_send, small = call_kernel(
        spread_kernel,
        [((seq_parts, shared_count, LANES), low), ((small_rows, LANES), f32)],
        [
            in_keep[0],
            swapped(in_send.astype(low), "batch", batch_bits[-1])[0],
            small_keep[0],
            swapped(small_send, "batch", batch_bits[-1])[0],
        ],
        micros=2,
        name="spread",
    )
    mixed_send, proj_back = lax.optimization_barrier((mixed_send, proj_back))
    mixed_got = lax.all_to_all(mixed_send, "seq", 0, 0, tiled=True)
    (grad_inputs,) = call_kernel(
        final_kernel,
        [((tok_count, width), f32)],
        [proj_back, tokens, grad_residual, rows, in_weight],
        micros=5.5,
        spaces="vvvvhv",
        scratch=[((width, 3 * width), low), ((tok_count, 3 * width), low), 1],
        name="final",
    )
    done_rows = SHARED_ROWS + seq_parts * LAID_ROWS + OWN_ROWS
    (last,) = call_kernel(
        merge_kernel,
        [((seq_parts * in_count + 2 * done_rows, LANES), low)],
        [mixed_got, small],
        micros=2,
        name="merge",
    )
    (
        final_in,
        grad_pre_gain,
        grad_pre_bias,
        grad_out_bias,
        grad_post_gain,
        grad_post_bias,
        grad_down_bias,
        grad_up_bias,
        grad_third,
        grad_inner,
        grad_pos,
        grad_pos_bias,
        grad_inner_bias,
        grad_third_bias,
        grad_freq,
        grad_taps,
        grad_tap_bias,
        grad_in_bias,
        grad_filter,
        grad_rates,
        grad_skips,
    ) = call_kernel(
        lambda *refs: finish_kernel(batch_parts, channels, *refs),
        [
            ((batch_parts * in_rows, 3 * width), f32),
            ((width,), f32),
            ((width,), f32),
            ((width,), f32),
            ((width,), f32),
            ((width,), f32),
            ((width,), f32),
            ((hidden_units,), f32),
            (filter_third_weight.shape, f32),
            (inner_weight.shape, f32),
            (pos_weight.shape, f32),
            ((fhid,), f32),
            ((fhid,), f32),
            ((fhid,), f32),
            ((fhid,), f32),
            ((3, 3 * width), f32),
            ((3 * width,), f32),
            ((3 * width,), f32),
            ((2, fhid, channels), f32),
            ((2, channels), f32),
            ((2, channels), f32),
        ],
        [batch_scalar] + over_batch(last),
        micros=3,
        spaces="s" + "v" * batch_parts + "v" * 21,
        scratch=[
            ((batch_parts,) + last.shape, low),
            ((batch_parts, done_rows, LANES), f32),
        ],
        name="finish",
    )
    return (
        outputs[None],
        grad_inputs[None],
        grad_pre_gain,
        grad_pre_bias,
        final_in,
        grad_in_bias,
        grad_taps,
        grad_tap_bias,
        grad_pos,
        grad_pos_bias,
        grad_inner,
        grad_inner_bias,
        grad_third,
        grad_third_bias,
        grad_freq,
        grad_filter,
        grad_rates,
        grad_skips,
        final_out,
        grad_out_bias,
        grad_post_gain,
        grad_post_bias,
        final_up,
        grad_up_bias,
        final_down,
        grad_down_bias,
    )


def per_device(*args):
    tokens, parts = args[0].shape[1], lax.axis_size("seq")
    channels = args[0].shape[2] // parts
    dense = tokens * parts <= DENSE_LIMIT and lays_dense(tokens, channels)
    return (dense_device if dense else factored_device)(*args)


def solution(mesh):
    in_specs = (
        P("batch", "seq", None),
        P(),
        P(),
        P(),
        P(),
        P(),
        P(),
        P(),
        P(),
        P(),
        P(),
        P(),
        P(),
        P(),
        P(),
        P(),
        P(),
        P(),
        P(),
        P(),
        P(),
        P(),
        P(),
        P(),
        P(),
        P("batch", "seq", None),
    )
    out_specs = (
        P("batch", "seq", None),
        P("batch", "seq", None),
        P(),
        P(),
        P("seq", None),
        P(),
        P(),
        P(),
        P(),
        P(),
        P(),
        P(),
        P(),
        P(),
        P(),
        P(None, None, "seq"),
        P(None, "seq"),
        P(None, "seq"),
        P("seq", None),
        P(),
        P(),
        P(),
        P("seq", None),
        P(),
        P("seq", None),
        P(),
    )
    return jax.shard_map(
        per_device, mesh=mesh, in_specs=in_specs, out_specs=out_specs, check_vma=False
    )
```

```python
import math

import jax
import jax.numpy as jnp
import numpy as np
from jax import lax
from jax.experimental import pallas as pl
from jax.experimental.pallas import tpu as pltpu
from jax.sharding import PartitionSpec as P

epsilon = 1e-05
highest_accuracy = lax.Precision.HIGHEST


def passed_along(value, axis, steps):
    count = lax.axis_size(axis)
    initial, last = (max(0, -steps), min(count, count - steps))
    return lax.ppermute(value, axis, [(source, source + steps) for source in range(initial, last)])


def plain_dot(left_side, right_side):
    return jnp.dot(left_side, right_side, preferred_element_type=jnp.float32)


def exact_tdot(left_side, right_side):
    return lax.dot_general(
        left_side,
        right_side,
        (((0,), (0,)), ((), ())),
        precision=highest_accuracy,
        preferred_element_type=jnp.float32,
    )


def left_dot(left_side, right_side):
    return lax.dot_general(
        left_side, right_side, (((0,), (0,)), ((), ())), preferred_element_type=jnp.float32
    )


def right_dot(left_side, right_side):
    return lax.dot_general(
        left_side, right_side, (((1,), (1,)), ((), ())), preferred_element_type=jnp.float32
    )


def rounded(values):
    return lax.optimization_barrier(values.astype(jnp.bfloat16)).astype(jnp.float32)


def norm_forward(values, gain_vec, shift_vec):
    centre = values - jnp.mean(values, axis=-1, keepdims=True)
    inv_std = lax.rsqrt(jnp.mean(centre * centre, axis=-1, keepdims=True) + epsilon)
    unit_rows = centre * inv_std
    return (unit_rows * gain_vec + shift_vec, unit_rows, inv_std)


def norm_backward(grad_out, unit_rows, inv_std, gain_vec):
    grad_unit = grad_out * gain_vec
    grad_values = inv_std * (
        grad_unit
        - jnp.mean(grad_unit, axis=-1, keepdims=True)
        - unit_rows * jnp.mean(grad_unit * unit_rows, axis=-1, keepdims=True)
    )
    return (grad_values, jnp.sum(grad_out * unit_rows, axis=0), jnp.sum(grad_out, axis=0))


def position_rows(length, feat_count):
    steps_pos = jnp.arange(length, dtype=jnp.float32)
    time_steps = steps_pos / (length - 1)
    band_count = (feat_count - 1) // 2
    frequency = jnp.linspace(0.0001, band_count - 1, band_count, dtype=jnp.float32)
    angles = frequency[:, None] * (steps_pos * (2.0 * math.pi / length))[None, :]
    features_t = jnp.concatenate([time_steps[None, :], jnp.cos(angles), -jnp.sin(angles)], axis=0)
    return (features_t, time_steps)


def body_filters(
    features_t,
    time_steps,
    pos_weight,
    pos_bias,
    inner_weight,
    inner_bias,
    filter_third_weight,
    third_bias,
    sine_freq,
    weight_local,
    rates_local,
):
    hidden = jnp.sin(sine_freq[:, None] * (exact_tdot(pos_weight, features_t) + pos_bias[:, None]))
    hidden = jnp.sin(sine_freq[:, None] * (exact_tdot(inner_weight, hidden) + inner_bias[:, None]))
    hidden = jnp.sin(
        sine_freq[:, None] * (exact_tdot(filter_third_weight, hidden) + third_bias[:, None])
    )
    first_kernel = exact_tdot(weight_local[0], hidden) * jnp.exp(
        -rates_local[0][:, None] * time_steps[None, :]
    )
    second_kernel = exact_tdot(weight_local[1], hidden) * jnp.exp(
        -rates_local[1][:, None] * time_steps[None, :]
    )
    return (first_kernel, second_kernel)


def split_sizes(extent):
    outer_size = math.gcd(extent // 2, 1 << (extent.bit_length() - 1) // 2)
    return (outer_size, extent // outer_size)


def dft_rect(row_count, col_count, modulus, direction):
    row_ids = jnp.arange(row_count, dtype=jnp.int32)[:, None]
    col_ids = jnp.arange(col_count, dtype=jnp.int32)[None, :]
    angles = (row_ids * col_ids % modulus).astype(jnp.float32) * (2.0 * math.pi / modulus)
    return (jnp.cos(angles), direction * jnp.sin(angles))


def first_section(block_groups, lookup_grid):
    return jnp.einsum(
        "cij,ik->ckj",
        block_groups,
        lookup_grid,
        precision=highest_accuracy,
        preferred_element_type=jnp.float32,
    )


def second_section(block_groups, lookup_grid):
    return jnp.einsum(
        "dhq,qn->dnh",
        block_groups,
        lookup_grid,
        precision=highest_accuracy,
        preferred_element_type=jnp.float32,
    )


def padded_spectrum(signal):
    channels, length = signal.shape
    extent = 2 * length
    outer_size, inner_size = split_sizes(extent)
    block_groups = signal.reshape(channels, inner_size // 2, outer_size)
    cos_inner, sin_inner = dft_rect(inner_size // 2, inner_size, inner_size, -1.0)
    section_real = first_section(block_groups, cos_inner)
    section_imag = first_section(block_groups, sin_inner)
    twist_cos, rotation_sine = dft_rect(inner_size, outer_size, extent, -1.0)
    turned_real = section_real * twist_cos - section_imag * rotation_sine
    turned_imag = section_real * rotation_sine + section_imag * twist_cos
    cos_outer, sin_outer = dft_rect(outer_size, outer_size, outer_size, -1.0)
    out_real = second_section(turned_real, cos_outer) - second_section(turned_imag, sin_outer)
    out_imag = second_section(turned_real, sin_outer) + second_section(turned_imag, cos_outer)
    return (out_real.reshape(channels, extent), out_imag.reshape(channels, extent))


def inverse_real(spec_real, spec_imag):
    channels, extent = spec_real.shape
    outer_size, inner_size = split_sizes(extent)
    blocks_real = spec_real.reshape(channels, inner_size, outer_size)
    blocks_imag = spec_imag.reshape(channels, inner_size, outer_size)
    cos_inner, sin_inner = dft_rect(inner_size, inner_size, inner_size, 1.0)
    section_real = first_section(blocks_real, cos_inner) - first_section(blocks_imag, sin_inner)
    section_imag = first_section(blocks_real, sin_inner) + first_section(blocks_imag, cos_inner)
    twist_cos, rotation_sine = dft_rect(inner_size, outer_size, extent, 1.0)
    turned_real = section_real * twist_cos - section_imag * rotation_sine
    turned_imag = section_real * rotation_sine + section_imag * twist_cos
    cos_outer, sin_outer = dft_rect(outer_size, outer_size // 2, outer_size, 1.0)
    out_real = second_section(turned_real, cos_outer) - second_section(turned_imag, sin_outer)
    return out_real.reshape(channels, extent // 2) / extent


def times_spec(left_real, left_imag, right_real, right_imag):
    return (
        left_real * right_real - left_imag * right_imag,
        left_real * right_imag + left_imag * right_real,
    )


def times_conj(left_real, left_imag, right_real, right_imag):
    return (
        left_real * right_real + left_imag * right_imag,
        left_imag * right_real - left_real * right_imag,
    )


def factored_device(
    inputs,
    pre_gain,
    pre_bias,
    in_weight,
    input_projection_bias,
    short_weight,
    short_bias,
    pos_weight,
    pos_bias,
    inner_weight,
    inner_bias,
    filter_third_weight,
    third_bias,
    sine_freq,
    filter_weight,
    decay_rates,
    skip_gains,
    out_weight,
    out_bias,
    post_gain,
    post_bias,
    up_weight,
    up_bias,
    down_weight,
    down_bias,
    cotangent,
):
    seq_parts = lax.axis_size("seq")
    seq_rank = lax.axis_index("seq")
    tokens = inputs[0]
    tok_count = tokens.shape[0]
    model_width = tokens.shape[1]
    length = tok_count * seq_parts
    channels = model_width // seq_parts
    tokens_wide = tokens.astype(jnp.float32)
    pre_gain_f = pre_gain.astype(jnp.float32)
    pre_bias_f = pre_bias.astype(jnp.float32)
    in_bias_f = input_projection_bias.astype(jnp.float32)
    short_f = short_weight.astype(jnp.float32)
    short_bias_f = short_bias.astype(jnp.float32)
    out_bias_f = out_bias.astype(jnp.float32)
    post_gain_f = post_gain.astype(jnp.float32)
    post_bias_f = post_bias.astype(jnp.float32)
    up_bias_f = up_bias.astype(jnp.float32)
    down_bias_f = down_bias.astype(jnp.float32)
    normed, unit_pre, inv_pre = norm_forward(tokens_wide, pre_gain_f, pre_bias_f)
    normed_low = normed.astype(jnp.bfloat16)
    projected = plain_dot(normed_low, in_weight) + in_bias_f
    previous = passed_along(projected[tok_count - 2 :], "seq", 1)
    extended = jnp.concatenate([previous, projected], axis=0)
    mixed_conv = (
        short_f[0] * extended[:-2]
        + short_f[1] * extended[1:-1]
        + short_f[2] * extended[2:]
        + short_bias_f
    )
    value_part = mixed_conv[:, :model_width]
    gate_one = mixed_conv[:, model_width : 2 * model_width]
    gate_two = mixed_conv[:, 2 * model_width :]
    product_low = (value_part * gate_one).astype(jnp.bfloat16)
    gate_two_low = gate_two.astype(jnp.bfloat16)
    prod_chan, gate_chan = (
        lax.all_to_all(product_low.T, "seq", split_axis=0, concat_axis=1, tiled=True),
        lax.all_to_all(gate_two_low.T, "seq", split_axis=0, concat_axis=1, tiled=True),
    )
    features_t, time_steps = position_rows(length, pos_weight.shape[0])
    chan_start = seq_rank * channels
    weight_local = lax.dynamic_slice_in_dim(
        filter_weight.astype(jnp.float32), chan_start, channels, 2
    )
    rates_local = lax.dynamic_slice_in_dim(decay_rates, chan_start, channels, 1)
    skips_local = lax.dynamic_slice_in_dim(skip_gains.astype(jnp.float32), chan_start, channels, 1)
    skip_one = skips_local[0][:, None]
    skip_two = skips_local[1][:, None]
    shared = tuple(
        (
            member.astype(jnp.float32)
            for member in (
                pos_weight,
                pos_bias,
                inner_weight,
                inner_bias,
                filter_third_weight,
                third_bias,
                sine_freq,
            )
        )
    )

    def local_filters(*params):
        return body_filters(features_t, time_steps, *params)

    (kernel_one, kernel_two), filter_pull = jax.vjp(
        local_filters, *shared, weight_local, rates_local
    )
    prod_wide = prod_chan.astype(jnp.float32)
    gate_wide = gate_chan.astype(jnp.float32)
    prod_real, prod_imag = padded_spectrum(prod_wide)
    kone_real, kone_imag = padded_spectrum(kernel_one)
    convolved_real_part, conv_imag = times_spec(prod_real, prod_imag, kone_real, kone_imag)
    after_one = rounded(inverse_real(convolved_real_part, conv_imag) + skip_one * prod_wide)
    gated_low = rounded(after_one * gate_wide)
    gated_real, gated_imag = padded_spectrum(gated_low)
    ktwo_real, ktwo_imag = padded_spectrum(kernel_two)
    convolved_real_part, conv_imag = times_spec(gated_real, gated_imag, ktwo_real, ktwo_imag)
    mixer_chan = (inverse_real(convolved_real_part, conv_imag) + skip_two * gated_low).astype(
        jnp.bfloat16
    )
    mixer_tok = lax.all_to_all(mixer_chan, "seq", split_axis=1, concat_axis=0, tiled=True).T
    branch = plain_dot(mixer_tok, out_weight) + out_bias_f
    residual = tokens_wide + branch
    normed_two, unit_post, inv_post = norm_forward(residual, post_gain_f, post_bias_f)
    normed_two_low = normed_two.astype(jnp.bfloat16)
    upper_pre = plain_dot(normed_two_low, up_weight) + up_bias_f
    activated = jax.nn.gelu(upper_pre, approximate=False).astype(jnp.bfloat16)
    outputs = residual + plain_dot(activated, down_weight) + down_bias_f
    grad_top = cotangent[0]
    grad_top_wide = grad_top.astype(jnp.float32)
    grad_act = right_dot(grad_top, down_weight)
    grad_down = left_dot(activated, grad_top)
    grad_down_bias = jnp.sum(grad_top_wide, axis=0)
    gelu_slope = (
        0.5 * (1.0 + lax.erf(upper_pre * 0.7071067811865476))
        + upper_pre * jnp.exp(-0.5 * upper_pre * upper_pre) * 0.3989422804014327
    )
    grad_upper = (grad_act * gelu_slope).astype(jnp.bfloat16)
    grad_up = left_dot(normed_two_low, grad_upper)
    grad_up_bias = jnp.sum(grad_upper.astype(jnp.float32), axis=0)
    grad_normed_two = right_dot(grad_upper, up_weight)
    grad_resid_norm, grad_post_gain, grad_post_bias = norm_backward(
        grad_normed_two, unit_post, inv_post, post_gain_f
    )
    grad_residual = grad_top_wide + grad_resid_norm
    grad_branch = grad_residual.astype(jnp.bfloat16)
    grad_out = left_dot(mixer_tok, grad_branch)
    grad_out_bias = jnp.sum(grad_branch.astype(jnp.float32), axis=0)
    grad_mixer = right_dot(grad_branch, out_weight).astype(jnp.bfloat16)
    grad_mixer_chan = lax.all_to_all(
        grad_mixer.T, "seq", split_axis=0, concat_axis=1, tiled=True
    ).astype(jnp.float32)
    gmix_real, gmix_imag = padded_spectrum(grad_mixer_chan)
    corr_real, corr_imag = times_conj(gmix_real, gmix_imag, ktwo_real, ktwo_imag)
    grad_gated = rounded(inverse_real(corr_real, corr_imag) + skip_two * grad_mixer_chan)
    corr_real, corr_imag = times_conj(gmix_real, gmix_imag, gated_real, gated_imag)
    grad_kernel_two = inverse_real(corr_real, corr_imag)
    grad_skip_two = jnp.sum(grad_mixer_chan * gated_low, axis=1)
    grad_after = rounded(grad_gated * gate_wide)
    grad_gate_two = (grad_gated * after_one).astype(jnp.bfloat16)
    gaft_real, gaft_imag = padded_spectrum(grad_after)
    corr_real, corr_imag = times_conj(gaft_real, gaft_imag, kone_real, kone_imag)
    grad_product = (inverse_real(corr_real, corr_imag) + skip_one * grad_after).astype(jnp.bfloat16)
    corr_real, corr_imag = times_conj(gaft_real, gaft_imag, prod_real, prod_imag)
    grad_kernel_one = inverse_real(corr_real, corr_imag)
    grad_skip_one = jnp.sum(grad_after * prod_wide, axis=1)
    filter_grads = filter_pull((grad_kernel_one, grad_kernel_two))
    grad_prod_back, grad_gate_back = (
        lax.all_to_all(grad_product, "seq", split_axis=1, concat_axis=0, tiled=True),
        lax.all_to_all(grad_gate_two, "seq", split_axis=1, concat_axis=0, tiled=True),
    )
    grad_prod_wide = grad_prod_back.T.astype(jnp.float32)
    grad_mixed = jnp.concatenate(
        [
            grad_prod_wide * gate_one,
            grad_prod_wide * value_part,
            grad_gate_back.T.astype(jnp.float32),
        ],
        axis=1,
    )
    grad_short_bias = jnp.sum(grad_mixed, axis=0)
    grad_short = jnp.stack(
        [
            jnp.sum(grad_mixed * extended[0:tok_count], axis=0),
            jnp.sum(grad_mixed * extended[1 : tok_count + 1], axis=0),
            jnp.sum(grad_mixed * extended[2 : tok_count + 2], axis=0),
        ]
    )
    zero_rows = jnp.zeros((2, 3 * model_width), jnp.float32)
    padded_grad = jnp.concatenate([zero_rows, grad_mixed, zero_rows], axis=0)
    grad_extended = (
        short_f[0] * padded_grad[2:]
        + short_f[1] * padded_grad[1:-1]
        + short_f[2] * padded_grad[:-2]
    )
    from_next = passed_along(grad_extended[:2], "seq", -1)
    grad_projected = grad_extended[2:].at[tok_count - 2 :].add(from_next)
    grad_proj_low = grad_projected.astype(jnp.bfloat16)
    grad_in = left_dot(normed_low, grad_proj_low)
    grad_in_bias = jnp.sum(grad_proj_low.astype(jnp.float32), axis=0)
    grad_normed = right_dot(grad_proj_low, in_weight)
    grad_tokens_norm, grad_pre_gain, grad_pre_bias = norm_backward(
        grad_normed, unit_pre, inv_pre, pre_gain_f
    )
    grad_inputs = grad_residual + grad_tokens_norm
    shared_sums = lax.psum(
        (
            grad_pre_gain,
            grad_pre_bias,
            grad_in_bias,
            grad_short,
            grad_short_bias,
            filter_grads[0],
            filter_grads[1],
            filter_grads[2],
            filter_grads[3],
            filter_grads[4],
            filter_grads[5],
            filter_grads[6],
            grad_out_bias,
            grad_post_gain,
            grad_post_bias,
            grad_up_bias,
            grad_down_bias,
        ),
        ("batch", "seq"),
    )
    skip_grads = jnp.stack([grad_skip_one, grad_skip_two])
    weight_shards = (
        lax.psum_scatter(grad_in, "seq", scatter_dimension=0, tiled=True),
        lax.psum_scatter(grad_out, "seq", scatter_dimension=0, tiled=True),
        lax.psum_scatter(grad_up, "seq", scatter_dimension=0, tiled=True),
        lax.psum_scatter(grad_down, "seq", scatter_dimension=0, tiled=True),
    )
    final_in, final_out, final_up, final_down, final_filter, final_rates, final_skips = (
        lax.psum(weight_shards[0].astype(jnp.bfloat16), "batch").astype(jnp.float32),
        lax.psum(weight_shards[1].astype(jnp.bfloat16), "batch").astype(jnp.float32),
        lax.psum(weight_shards[2].astype(jnp.bfloat16), "batch").astype(jnp.float32),
        lax.psum(weight_shards[3].astype(jnp.bfloat16), "batch").astype(jnp.float32),
        lax.psum(filter_grads[7].astype(jnp.bfloat16), "batch").astype(jnp.float32),
        lax.psum(filter_grads[8].astype(jnp.bfloat16), "batch").astype(jnp.float32),
        lax.psum(skip_grads.astype(jnp.bfloat16), "batch").astype(jnp.float32),
    )
    return (
        outputs[None],
        grad_inputs[None],
        shared_sums[0],
        shared_sums[1],
        final_in,
        shared_sums[2],
        shared_sums[3],
        shared_sums[4],
        shared_sums[5],
        shared_sums[6],
        shared_sums[7],
        shared_sums[8],
        shared_sums[9],
        shared_sums[10],
        shared_sums[11],
        final_filter,
        final_rates,
        final_skips,
        final_out,
        shared_sums[12],
        shared_sums[13],
        shared_sums[14],
        final_up,
        shared_sums[15],
        final_down,
        shared_sums[16],
    )


LANES = 128
BLOCK = 256
WAVE_BLOCK = 256
PAD = 8
DENSE_LIMIT = 2048
ROW_AT = {
    "pre_gain": 0,
    "pre_bias": 1,
    "in_bias": 2,
    "tap_bias": 5,
    "taps": 8,
    "skips": 17,
    "post_gain": 19,
    "post_bias": 20,
    "out_bias": 21,
    "down_bias": 22,
    "up_bias": 23,
}
ROW_COUNT = 32


def call_kernel(kernel, outs, args, micros, spaces="", scratch=(), limit=60, name=None):
    places = {"v": pltpu.VMEM, "s": pltpu.SMEM, "h": pl.ANY}
    spaces = spaces or "v" * (len(args) + len(outs))
    specs = [pl.BlockSpec(memory_space=places[space]) for space in spaces]
    shapes = [jax.ShapeDtypeStruct(shape, dtype) for shape, dtype in outs]
    return pl.pallas_call(
        kernel,
        out_shape=shapes,
        in_specs=specs[: len(args)],
        out_specs=specs[len(args) :],
        scratch_shapes=[
            pltpu.SemaphoreType.DMA((entry,))
            if isinstance(entry, int)
            else pltpu.VMEM(entry[0], entry[1])
            for entry in scratch
        ],
        compiler_params=pltpu.CompilerParams(vmem_limit_bytes=limit * 1024 * 1024),
        cost_estimate=pl.CostEstimate(
            flops=1, transcendentals=0, bytes_accessed=int(3.0e6 * micros)
        ),
        name=name,
    )(*args)


def row_chunks(source, target, sems, first, count):
    size = source.shape[0] // count
    return [
        pltpu.make_async_copy(
            source.at[pl.ds(place * size, size)],
            target.at[pl.ds(place * size, size)],
            sems.at[first + place],
        )
        for place in range(count)
    ]


def dense_rows(tile):
    tokens, channels = tile.shape
    rows = tokens * channels // LANES
    spare = LANES - channels
    blocks = channels // spare
    pieces = [tile[rows:, block * spare : (block + 1) * spare] for block in range(blocks)]
    return jnp.concatenate([tile[:rows], jnp.concatenate(pieces, axis=0)], axis=1)


def loose_rows(tile, tokens, channels):
    rows = tile.shape[0]
    spare = LANES - channels
    blocks = channels // spare
    rest = tokens - rows
    pieces = [tile[block * rest : (block + 1) * rest, channels:] for block in range(blocks)]
    return jnp.concatenate([tile[:, :channels], jnp.concatenate(pieces, axis=1)], axis=0)


def lays_dense(tokens, channels):
    spare = LANES - channels
    if spare <= 0 or channels % spare or tokens * channels % LANES:
        return False
    rows, blocks = tokens * channels // LANES, channels // spare
    return rows % 8 == 0 and (tokens - rows) * blocks == rows and (tokens - rows) % 8 == 0


def exact_nn(left_side, right_side):
    return jnp.dot(
        left_side, right_side, precision=highest_accuracy, preferred_element_type=jnp.float32
    )


def exact_nt(left_side, right_side):
    return lax.dot_general(
        left_side,
        right_side,
        (((1,), (1,)), ((), ())),
        precision=highest_accuracy,
        preferred_element_type=jnp.float32,
    )


def sine_pair(angle):
    turns = jnp.round(angle * (2.0 / math.pi))
    rest = angle - turns * 1.5703125
    rest = rest - turns * 4.837512969970703125e-4
    rest = rest - turns * 7.549789948768648e-8
    square = rest * rest
    sine = rest + rest * square * (
        -1.6666654611e-1 + square * (8.3321608736e-3 + square * -1.9515295891e-4)
    )
    cosine = (
        1.0
        - 0.5 * square
        + square
        * square
        * (4.166664568298827e-2 + square * (-1.388731625493765e-3 + square * 2.443315711809948e-5))
    )
    quarter = turns.astype(jnp.int32)
    odd = (quarter & 1) == 1
    sine_out = jnp.where(odd, cosine, sine)
    cosine_out = jnp.where(odd, sine, cosine)
    sine_out = jnp.where((quarter & 2) == 2, -sine_out, sine_out)
    cosine_out = jnp.where(((quarter + 1) & 2) == 2, -cosine_out, cosine_out)
    return sine_out, cosine_out


def block_rows(index, size):
    return pl.ds(pl.multiple_of(index * size, size), size)


def wave_pair(index):
    first = index * 2 * WAVE_BLOCK
    return (
        pl.ds(pl.multiple_of(first, WAVE_BLOCK), WAVE_BLOCK),
        pl.ds(pl.multiple_of(first + WAVE_BLOCK, WAVE_BLOCK), WAVE_BLOCK),
    )


def row_of(rows, name, place=0):
    at = ROW_AT[name] + place
    return rows[at : at + 1, :]


def feature_block(first, count, length, feat_count):
    bands = (feat_count - 1) // 2
    place = lax.broadcasted_iota(jnp.int32, (count, 2 * feat_count), 0) + first
    lane = lax.broadcasted_iota(jnp.int32, (count, 2 * feat_count), 1)
    later = lane >= feat_count
    place = jnp.where(later, 2 * place + 1, 2 * place)
    lane = jnp.where(later, lane - feat_count, lane)
    steps = place.astype(jnp.float32)
    band = jnp.where(lane > bands, lane - 1 - bands, lane - 1).astype(jnp.float32)
    frequency = 0.0001 + band * ((bands - 1 - 0.0001) / (bands - 1))
    sine, cosine = sine_pair(frequency * (steps * (2.0 * math.pi / length)))
    features = jnp.where(lane > bands, -sine, cosine)
    features = jnp.where(lane == 0, steps / (length - 1), features)
    column = lax.broadcasted_iota(jnp.int32, (count, 1), 0) + first
    times = [(2 * column + odd).astype(jnp.float32) / (length - 1) for odd in (0, 1)]
    return features, times


def norm_kernel(tokens, top, gain, bias, tokens_out, top_out, normed_out, held):
    low, f32 = jnp.bfloat16, jnp.float32
    count = tokens.shape[0] // 2
    for source, target in ((top, top_out), (tokens, tokens_out)):
        for place in range(held.shape[0]):
            cols = slice(place * LANES, (place + 1) * LANES)
            held[place] = source[:, cols].astype(f32)
            for odd in range(2):
                rows = held[place, pl.ds(odd, count, stride=2), :]
                target[odd * count : (odd + 1) * count, cols] = rows.astype(low)
    rows = [vector[...].astype(f32).reshape(1, vector.shape[0]) for vector in (gain, bias)]
    normed, _, _ = norm_forward(tokens_out[...].astype(f32), *rows)
    normed_out[...] = normed.astype(low)


def wave_kernel(channels, start, *refs):
    (
        pre_gain,
        pre_bias,
        in_bias,
        tap_bias,
        taps,
        skips,
        post_gain,
        post_bias,
        out_bias,
        down_bias,
        up_bias,
        pos_bias,
        inner_bias,
        third_bias,
        sine_freq,
        filter_weight,
        decay,
        in_weight_in,
        wave_out,
        turn_out,
        rows_out,
        in_out,
        local_out,
        weights_out,
        rates_out,
        vectors_out,
        tables,
        wave,
        in_weight,
        sems,
    ) = refs
    half = wave.shape[1]
    width = in_weight.shape[0]
    step = tables.shape[1]
    low, f32 = jnp.bfloat16, jnp.float32
    load = pltpu.make_async_copy(in_weight_in, in_weight, sems.at[1])
    load.start()

    unit = math.pi / (4 * half)

    def table(which, carry):
        at = lax.broadcasted_iota(jnp.int32, (step, half), 0)
        place = lax.broadcasted_iota(jnp.int32, (step, half), 1)
        left = jnp.where(which == 0, 2 * step * at, 2 * at + 1)
        turn = (left * (2 * place + 1)) & (8 * half - 1)
        sine, cosine = sine_pair(turn.astype(f32) * unit)
        tables[2 * which] = cosine
        tables[2 * which + 1] = sine
        return carry

    lax.fori_loop(0, 2, table, 0)
    per_block = WAVE_BLOCK // step

    def fill(index, carry):
        base = (index // per_block) * (2 * WAVE_BLOCK) + (index % per_block) * step
        upper = pl.ds(pl.multiple_of(base, step), step)
        lower = pl.ds(pl.multiple_of(base + WAVE_BLOCK, step), step)
        one = pl.ds(index, 1)
        cos_a, sin_a = tables[0, one, :], tables[1, one, :]
        cos_b, sin_b = tables[2], tables[3]
        wave[upper, :] = (cos_a * cos_b - sin_a * sin_b).astype(low)
        wave[lower, :] = (sin_a * cos_b + cos_a * sin_b).astype(low)
        return carry

    lax.fori_loop(0, half // step, fill, 0)
    sent = [pltpu.make_async_copy(wave, wave_out, sems.at[0])]
    for copy in sent:
        copy.start()

    def turn(index, carry):
        upper, lower = wave_pair(index)
        at = lax.broadcasted_iota(jnp.int32, (WAVE_BLOCK, LANES), 0) + index * WAVE_BLOCK
        sine, cosine = sine_pair((2 * at + 1).astype(f32) * unit)
        turn_out[upper, :] = cosine
        turn_out[lower, :] = sine
        return carry

    lax.fori_loop(0, half // WAVE_BLOCK, turn, 0)
    rows_out[...] = jnp.zeros_like(rows_out)

    def place_rows(name, vector):
        for number in range(vector.shape[0] // width):
            piece = vector[number * width : (number + 1) * width].astype(f32)
            at = ROW_AT[name] + number
            rows_out[at : at + 1, :] = piece.reshape(1, width)

    for name, vector in (
        ("pre_gain", pre_gain),
        ("pre_bias", pre_bias),
        ("in_bias", in_bias),
        ("tap_bias", tap_bias),
        ("post_gain", post_gain),
        ("post_bias", post_bias),
        ("out_bias", out_bias),
        ("down_bias", down_bias),
        ("up_bias", up_bias),
    ):
        place_rows(name, vector)
    wide_taps = taps[...].astype(f32)
    for tap in range(3):
        for group in range(3):
            at = ROW_AT["taps"] + 3 * tap + group
            rows_out[at : at + 1, :] = wide_taps[tap : tap + 1, group * width : (group + 1) * width]
    at = ROW_AT["skips"]
    rows_out[at : at + 2, :] = skips[...].astype(f32)
    for number, vector in enumerate((pos_bias, inner_bias, third_bias, sine_freq)):
        row = vector[...].astype(f32).reshape(1, vector.shape[0])
        vectors_out[number : number + 1, :] = row

    source = lax.broadcasted_iota(jnp.int32, (width, LANES), 0)
    target = lax.broadcasted_iota(jnp.int32, (width, LANES), 1)
    chosen = (source == start[0] + target) & (target < channels)
    select_wide = jnp.where(chosen, 1.0, 0.0)
    select = select_wide.astype(low)
    local_out[...] = plain_dot(rows_out[...].astype(low), select)
    padded = jnp.concatenate([decay[...], jnp.zeros((6, width), f32)], axis=0)
    rates = exact_nn(padded, select_wide)
    for order in range(2):
        cols = slice(order * LANES, (order + 1) * LANES)
        weights_out[:, cols] = plain_dot(filter_weight[order], select)
        rates_out[:, cols] = rates[order : order + 1]
    load.wait()
    for group in range(3):
        cols = slice(group * LANES, (group + 1) * LANES)
        whole = in_weight[:, group * width : (group + 1) * width]
        in_out[:, cols] = plain_dot(whole, select).astype(low)
    for copy in sent:
        copy.wait()


def doubled(weight):
    zero = jnp.zeros_like(weight)
    return jnp.concatenate(
        [jnp.concatenate([weight, zero], axis=1), jnp.concatenate([zero, weight], axis=1)], axis=0
    )


def twice(row):
    return jnp.concatenate([row, row], axis=1)


def filter_kernel(
    pos_weight,
    inner_weight,
    third_weight,
    vectors,
    weights,
    rates,
    turn,
    wave_in,
    spectrum_out,
    kernel_out,
    waves_out,
    high,
    rest,
    wave,
    sems,
):
    half = wave.shape[1]
    length = 2 * half
    low, f32 = jnp.bfloat16, jnp.float32
    loads = row_chunks(wave_in, wave, sems, 0, 1)
    for copy in loads:
        copy.start()
    feat_count = pos_weight.shape[0]
    freq = twice(vectors[3:4, :])

    def network(index, carry):
        here = block_rows(index, BLOCK)
        there = pl.ds(pl.multiple_of(index * BLOCK + half, BLOCK), BLOCK)
        layer_in, times = feature_block(index * BLOCK, BLOCK, length, feat_count)
        for layer, weight in enumerate((pos_weight, inner_weight, third_weight)):
            matrix = doubled(weight[...].astype(f32))
            inner = exact_nn(layer_in, matrix) + twice(vectors[layer : layer + 1, :])
            layer_in, cosine = sine_pair(freq * inner)
            waves_out[layer, here, :] = jnp.concatenate([layer_in, cosine], axis=1)
        both = exact_nn(layer_in, doubled(weights[...]))
        cols = 2 * LANES
        for part, rows in enumerate((here, there)):
            kernels = both[:, part * cols : (part + 1) * cols]
            kernels = kernels * jnp.exp(-rates[...] * times[part])
            kernel_out[rows, :] = kernels
            upper = kernels.astype(low)
            high[rows, :] = upper
            rest[rows, :] = (kernels - upper.astype(f32)).astype(low)
        return carry

    lax.fori_loop(0, half // BLOCK, network, 0)
    for copy in loads:
        copy.wait()

    def spectra(index, carry):
        matrix = wave[block_rows(index, 2 * WAVE_BLOCK), :]
        even, odd = (
            plain_dot(matrix, high[rows, :]) + plain_dot(matrix, rest[rows, :])
            for rows in (slice(0, half), slice(half, length))
        )
        upper, lower = wave_pair(index)
        for order in range(2):
            cols = slice(order * LANES, (order + 1) * LANES)
            parts = butterfly(even[:, cols], odd[:, cols], turn, upper, lower)
            for side, (real, imag) in enumerate(parts):
                spectrum_out[side, upper, cols] = real * (1.0 / length)
                spectrum_out[side, lower, cols] = imag * (1.0 / length)
        return carry

    lax.fori_loop(0, half // WAVE_BLOCK, spectra, 0)


def butterfly(even, odd, turn, upper, lower):
    cosine, sine = turn[upper, :], turn[lower, :]
    even_real, even_imag = even[:WAVE_BLOCK], even[WAVE_BLOCK:]
    odd_real, odd_imag = odd[:WAVE_BLOCK], odd[WAVE_BLOCK:]
    real = even_real * cosine + even_imag * sine
    imag = even_imag * cosine - even_real * sine
    return (real + odd_real, imag + odd_imag), (real - odd_real, odd_imag - imag)


def unbutterfly(first, second, turn, upper, lower):
    cosine, sine = turn[upper, :], turn[lower, :]
    real, imag = first[0] + second[0], first[1] - second[1]
    even = (real * cosine - imag * sine, imag * cosine + real * sine)
    return even, (first[0] - second[0], first[1] + second[1])


def short_mix(rows, projected, group):
    cols = slice(group * LANES, (group + 1) * LANES)
    length = projected.shape[1] - PAD
    now, last = slice(PAD, PAD + length), slice(PAD - 1, PAD - 1 + length)
    taps = [row_of(rows, "taps", 3 * tap + group) for tap in range(3)]
    shift = row_of(rows, "tap_bias", group)
    odd_last = projected[1, last, cols]
    even_now = projected[0, now, cols]
    even = taps[0] * projected[0, last, cols] + taps[1] * odd_last + taps[2] * even_now + shift
    odd = taps[0] * odd_last + taps[1] * even_now + taps[2] * projected[1, now, cols] + shift
    return even, odd


def spread_rows(tile, held, target):
    count = tile.shape[0] // 2
    for place in range(held.shape[0]):
        cols = slice(place * LANES, (place + 1) * LANES)
        for odd in range(2):
            rows = tile[odd * count : (odd + 1) * count, cols]
            held[place, pl.ds(odd, count, stride=2), :] = rows
        target[:, cols] = held[place]


def inverse_block(wave, reals, imags, index):
    upper, lower = wave_pair(index)
    return plain_dot(wave[upper, :], reals[...]) + plain_dot(wave[lower, :], imags[...])


def store_inverse(reals, imags, here, at, parts):
    for place, (real, imag) in enumerate(parts):
        cols = slice((at + place) * LANES, (at + place + 1) * LANES)
        reals[here, cols] = real.astype(jnp.bfloat16)
        imags[here, cols] = imag.astype(jnp.bfloat16)


def convolve(wave, turn, signal, spectrum, cols, kept, reals, imags, finish):
    half = wave.shape[1]

    def ahead(index, carry):
        both = plain_dot(wave[block_rows(index, 2 * WAVE_BLOCK), :], signal[...])
        upper, lower = wave_pair(index)
        sides = butterfly(both[:, :LANES], both[:, LANES:], turn, upper, lower)
        outs = []
        for side, (real, imag) in enumerate(sides):
            kept[side, upper, :], kept[side, lower, :] = real, imag
            outs.append(
                times_spec(real, imag, spectrum[side, upper, cols], spectrum[side, lower, cols])
            )
        parts = unbutterfly(*outs, turn, upper, lower)
        store_inverse(reals, imags, block_rows(index, WAVE_BLOCK), 0, parts)
        return carry

    lax.fori_loop(0, half // WAVE_BLOCK, ahead, 0)

    def behind(index, carry):
        finish(block_rows(index, WAVE_BLOCK), inverse_block(wave, reals, imags, index))
        return carry

    lax.fori_loop(0, half // WAVE_BLOCK, behind, 0)


def correlate(wave, turn, signal, spectrum, cols, kept, reals, imags, finish):
    half = wave.shape[1]
    wide = 2 * LANES

    def ahead(index, carry):
        both = plain_dot(wave[block_rows(index, 2 * WAVE_BLOCK), :], signal[...])
        upper, lower = wave_pair(index)
        sides = butterfly(both[:, :LANES], both[:, LANES:], turn, upper, lower)
        here = block_rows(index, WAVE_BLOCK)
        for number, (other, columns) in enumerate(((spectrum, cols), (kept, slice(0, LANES)))):
            outs = [
                times_conj(*pair, other[side, upper, columns], other[side, lower, columns])
                for side, pair in enumerate(sides)
            ]
            parts = unbutterfly(*outs, turn, upper, lower)
            store_inverse(reals, imags, here, 2 * number, parts)
        return carry

    lax.fori_loop(0, half // WAVE_BLOCK, ahead, 0)

    def behind(index, carry):
        both = inverse_block(wave, reals, imags, index)
        kernel = both[:, wide:] * (0.5 / half)
        return finish(block_rows(index, WAVE_BLOCK), both[:, :wide], kernel, carry)

    zero = jnp.zeros((1, wide), jnp.float32)
    return lax.fori_loop(0, half // WAVE_BLOCK, behind, zero)


def front_kernel(parts, index, *refs):
    chunks = refs[:parts]
    (weight, rows, wave_in, turn_in, spectrum_in) = refs[parts : 5 + parts]
    (
        normed_out,
        projected_out,
        product_out,
        gate_out,
        after_out,
        gated_out,
        product_wave_out,
        gated_wave_out,
        mixer_out,
        held,
        reals,
        imags,
        wave,
        turn,
        spectrum,
        projected,
        product_wave,
        gated_wave,
        mixer,
        sems,
    ) = refs[5 + parts :]
    tok_count, width = chunks[0].shape
    half = wave.shape[1]
    channels = width // parts
    low, f32 = jnp.bfloat16, jnp.float32
    loads = [
        pltpu.make_async_copy(source, target, sems.at[place])
        for place, (source, target) in enumerate(
            [(wave_in, wave), (turn_in, turn), (spectrum_in, spectrum)]
        )
    ]
    stores = [
        pltpu.make_async_copy(source, target, sems.at[3 + place])
        for place, (source, target) in enumerate(
            [
                (held, normed_out),
                (projected, projected_out),
                (product_wave, product_wave_out),
                (gated_wave, gated_wave_out),
            ]
        )
    ]
    for copy in loads:
        copy.start()
    count = tok_count // 2
    for part in range(parts):
        place = index[0] ^ part
        for odd in range(2):
            at = pl.ds(pl.multiple_of(odd * half + place * count, count), count)
            held[at, :] = chunks[part][odd * count : (odd + 1) * count, :]
    stores[0].start()
    in_bias = jnp.concatenate([row_of(rows, "in_bias", group) for group in range(3)], axis=1)
    projected[:, :PAD, :] = jnp.zeros((2, PAD, projected.shape[2]), f32)

    def project(odd, carry):
        projected[odd, PAD:, :] = plain_dot(held[block_rows(odd, half), :], weight[...]) + in_bias
        return carry

    lax.fori_loop(0, 2, project, 0)
    stores[1].start()
    mixed = [short_mix(rows, projected, group) for group in range(3)]
    for odd in range(2):
        cols = slice(odd * LANES, (odd + 1) * LANES)
        product_out[:, cols] = (mixed[0][odd] * mixed[1][odd]).astype(low)
        gate_out[:, cols] = mixed[2][odd].astype(low)
    skips = [twice(row_of(rows, "skips", order)) for order in range(2)]

    def first(here, convolved):
        product = product_out[here, :].astype(f32)
        after = (convolved + skips[0] * product).astype(low)
        after_out[here, :] = after
        gated_out[here, :] = (after.astype(f32) * gate_out[here, :].astype(f32)).astype(low)

    def second(here, convolved):
        gated = gated_out[here, :].astype(f32)
        mixer[here, :] = (convolved + skips[1] * gated).astype(low)

    for copy in loads:
        copy.wait()
    cols = [slice(order * LANES, (order + 1) * LANES) for order in range(2)]
    convolve(wave, turn, product_out, spectrum, cols[0], product_wave, reals, imags, first)
    stores[2].start()
    convolve(wave, turn, gated_out, spectrum, cols[1], gated_wave, reals, imags, second)
    stores[3].start()
    for part in range(parts):
        at = slice(part * count, (part + 1) * count)
        tiles = [mixer[at, odd * LANES : odd * LANES + channels].astype(f32) for odd in range(2)]
        mixer_out[part] = dense_rows(jnp.concatenate(tiles, axis=0)).astype(low)
    for copy in stores:
        copy.wait()


def back_kernel(
    channels,
    grad_mixer,
    product_ref,
    gate_ref,
    after_ref,
    gated_ref,
    rows,
    turn,
    product_wave_in,
    gated_wave_in,
    spectrum_in,
    wave_in,
    projected_in,
    packed_out,
    padded_out,
    grad_kernel_out,
    sums_out,
    grad_mix,
    grad_after,
    grad_value,
    grad_gate,
    reals,
    imags,
    wave,
    spectrum,
    product_wave,
    gated_wave,
    projected,
    shifted,
    sems,
):
    parts = grad_mixer.shape[0]
    half = wave.shape[1]
    count = half // parts
    low, f32 = jnp.bfloat16, jnp.float32
    loads = [
        pltpu.make_async_copy(source, target, sems.at[place])
        for place, (source, target) in enumerate(
            [
                (wave_in, wave),
                (spectrum_in, spectrum),
                (gated_wave_in, gated_wave),
                (product_wave_in, product_wave),
                (projected_in, projected),
            ]
        )
    ]
    for copy in loads:
        copy.start()
    padding = jnp.zeros((count, LANES - channels), f32)
    for part in range(parts):
        tile = loose_rows(grad_mixer[part].astype(f32), 2 * count, channels)
        here = slice(part * count, (part + 1) * count)
        pieces = [tile[:count], padding, tile[count:], padding]
        grad_mix[here, :] = jnp.concatenate(pieces, axis=1).astype(low)
    skips = [twice(row_of(rows, "skips", order)) for order in range(2)]

    def store_kernel(here, order, kernel):
        cols = slice(order * LANES, (order + 1) * LANES)
        grad_kernel_out[0, here, cols] = kernel[:, :LANES]
        grad_kernel_out[1, here, cols] = kernel[:, LANES:]

    def first(here, data, kernel, total):
        store_kernel(here, 1, kernel)
        top = grad_mix[here, :].astype(f32)
        grad_gated = (data + skips[1] * top).astype(low).astype(f32)
        grad_after[here, :] = (grad_gated * gate_ref[here, :].astype(f32)).astype(low)
        grad_gate[here, :] = (grad_gated * after_ref[here, :].astype(f32)).astype(low)
        return total + jnp.sum(top * gated_ref[here, :].astype(f32), axis=0, keepdims=True)

    def second(here, data, kernel, total):
        store_kernel(here, 0, kernel)
        top = grad_after[here, :].astype(f32)
        grad_value[here, :] = (data + skips[0] * top).astype(low)
        return total + jnp.sum(top * product_ref[here, :].astype(f32), axis=0, keepdims=True)

    cols = [slice(order * LANES, (order + 1) * LANES) for order in range(2)]
    for copy in loads[:3]:
        copy.wait()
    skip_second = correlate(
        wave, turn, grad_mix, spectrum, cols[1], gated_wave, reals, imags, first
    )
    loads[3].wait()
    skip_first = correlate(
        wave, turn, grad_after, spectrum, cols[0], product_wave, reals, imags, second
    )
    sums_out[15:16, :] = skip_first[:, :LANES] + skip_first[:, LANES:]
    sums_out[16:17, :] = skip_second[:, :LANES] + skip_second[:, LANES:]
    sums_out[17:24, :] = jnp.zeros((7, LANES), f32)
    loads[4].wait()
    now, last, after = slice(PAD, PAD + half), slice(PAD - 1, PAD - 1 + half), slice(1, 1 + half)

    def total(value):
        return jnp.sum(value, axis=0, keepdims=True)

    shifted[:, half:, :] = jnp.zeros((2, PAD, LANES), f32)
    for group in range(3):
        here = slice(group * LANES, (group + 1) * LANES)
        sides = [slice(odd * LANES, (odd + 1) * LANES) for odd in range(2)]
        if group == 2:
            mixed = [grad_gate[:, side].astype(f32) for side in sides]
        else:
            others = short_mix(rows, projected, 1 - group)
            mixed = [grad_value[:, side].astype(f32) * other for side, other in zip(sides, others)]
        shifted[0, :half, :], shifted[1, :half, :] = mixed
        even, odd = mixed
        taps = [row_of(rows, "taps", 3 * tap + group) for tap in range(3)]
        odd_last, even_now = projected[1, last, here], projected[0, now, here]
        moved = (
            total(even * projected[0, last, here] + odd * odd_last),
            total(even * odd_last + odd * even_now),
            total(even * even_now + odd * projected[1, now, here]),
        )
        for tap in range(3):
            at = 3 * tap + group
            sums_out[at : at + 1, :] = moved[tap]
        sums_out[9 + group : 10 + group, :] = total(even + odd)
        even_next, odd_next = shifted[0, after, :], shifted[1, after, :]
        grads = (
            taps[0] * even_next + taps[1] * odd + taps[2] * even,
            taps[0] * odd_next + taps[1] * even_next + taps[2] * odd,
        )
        grads = [grad.astype(low) for grad in grads]
        for place, grad in enumerate(grads):
            padded_out[place * half : (place + 1) * half, here] = grad
        sums_out[12 + group : 13 + group, :] = total(grads[0].astype(f32) + grads[1].astype(f32))
    dense = packed_out.shape[1] // 3

    def pack(part, carry):
        for group in range(3):
            cols = slice(group * LANES, group * LANES + channels)
            tiles = [
                padded_out[
                    pl.ds(pl.multiple_of(odd * half + part * count, count), count), cols
                ].astype(f32)
                for odd in range(2)
            ]
            packed = dense_rows(jnp.concatenate(tiles, axis=0)).astype(low)
            packed_out[part, group * dense : (group + 1) * dense, :] = packed
        return carry

    lax.fori_loop(0, parts, pack, 0)


def store_rows(target, at, value):
    per = target.shape[1]
    place = 0
    while place < value.shape[0]:
        quarter, inside = divmod(at + place, per)
        count = min(value.shape[0] - place, per - inside)
        target[quarter, inside : inside + count, :] = value[place : place + count]
        place += count


def lane_rows(vector):
    count = vector.shape[1] // LANES
    return jnp.concatenate(
        [vector[:, place * LANES : (place + 1) * LANES] for place in range(count)], axis=0
    )


def middle_kernel(
    parts,
    batch_index,
    received,
    tokens,
    top,
    rows,
    out_in,
    up_in,
    down_in,
    outputs_out,
    residual_out,
    send_out,
    sums_out,
    *refs,
):
    batch = len(refs) - 14
    sides, parts_out = refs[0], refs[1 : 1 + batch]
    (
        out_w,
        up_w,
        down_w,
        residual,
        total,
        flow,
        act,
        upper_grad,
        act_parts,
        branch_parts,
        up_rows,
        held,
        sems,
    ) = refs[1 + batch :]
    tok_count, width = tokens.shape
    channels = width // parts
    f32, low = jnp.float32, jnp.bfloat16
    quarters = up_w.shape[0]
    quarter = up_w.shape[2]
    load_out = pltpu.make_async_copy(out_in, out_w, sems.at[0])
    load_out.start()

    def loads(place):
        cols = pl.ds(pl.multiple_of(place * quarter, quarter), quarter)
        return (
            pltpu.make_async_copy(up_in.at[:, cols], up_w.at[place], sems.at[1 + place]),
            pltpu.make_async_copy(
                down_in.at[cols, :], down_w.at[place], sems.at[1 + quarters + place]
            ),
        )

    for place in range(quarters):
        for copy in loads(place):
            copy.start()
    tiles = [
        loose_rows(received[part].astype(f32), tok_count, channels) for part in range(parts)
    ]
    mixer = jnp.concatenate(tiles, axis=1).astype(low)
    load_out.wait()
    branch = plain_dot(mixer, out_w[...]) + row_of(rows, "out_bias")
    residual[...] = tokens[...].astype(f32) + branch
    gain = row_of(rows, "post_gain")
    bias = row_of(rows, "post_bias")
    normed, _, _ = norm_forward(residual[...], gain, bias)
    sides[:, :width] = normed.astype(low)
    sides[:, width:] = mixer
    for place in range(quarters):
        up_rows[place] = row_of(rows, "up_bias", place)
    total[...] = jnp.zeros_like(total)
    flow[...] = jnp.zeros_like(flow)

    def body(place, carry):
        for copy in loads(place):
            copy.wait()
        upper = plain_dot(sides[:, :width], up_w[place]) + up_rows[place]
        gauss = 0.5 * (1.0 + lax.erf(upper * 0.7071067811865476))
        active = (upper * gauss).astype(low)
        act[place] = active
        total[...] += plain_dot(active, down_w[place])
        grad_act = right_dot(top[...], down_w[place])
        slope = gauss + upper * jnp.exp(-0.5 * upper * upper) * 0.3989422804014327
        grad_upper = (grad_act * slope).astype(low)
        upper_grad[place] = grad_upper
        flow[...] += right_dot(grad_upper, up_w[place])
        return carry

    lax.fori_loop(0, quarters, body, 0)
    spread_rows(residual[...] + total[...] + row_of(rows, "down_bias"), held, outputs_out)
    _, unit, inv_std = norm_forward(residual[...], gain, bias)
    grad_norm, grad_gain, grad_bias = norm_backward(flow[...], unit, inv_std, gain)
    grad_residual = top[...].astype(f32) + grad_norm
    residual_out[...] = grad_residual
    grad_branch = grad_residual.astype(low)
    grad_mixer = right_dot(grad_branch, out_w[...])
    for part in range(parts):
        tile = grad_mixer[:, part * channels : (part + 1) * channels]
        send_out[part] = dense_rows(tile).astype(low)
    wide_branch = grad_branch.astype(f32)
    vectors = [
        jnp.sum(wide_branch, axis=0, keepdims=True),
        grad_gain[None],
        grad_bias[None],
        jnp.sum(top[...].astype(f32), axis=0, keepdims=True),
    ]
    vectors += [
        jnp.sum(upper_grad[place].astype(f32), axis=0, keepdims=True) for place in range(quarters)
    ]
    per = width // LANES
    for number, vector in enumerate(vectors):
        sums_out[number * per : (number + 1) * per, :] = lane_rows(vector)
    piece = width // batch
    for place in range(batch):
        part = wide_branch[:, place * piece : (place + 1) * piece]
        spare = branch_parts.shape[2] - piece
        part = jnp.concatenate([part, jnp.zeros((tok_count, spare), f32)], axis=1)
        branch_parts[place] = part.astype(low)
    step = quarters * quarter // (parts * batch)
    per_part = quarters * quarter // parts
    for place in range(batch):
        tiles = []
        for part in range(parts):
            at = part * per_part + place * step
            inside = at % quarter
            tiles.append(act[at // quarter, :, inside : inside + step].astype(f32))
        act_parts[place] = jnp.concatenate(tiles, axis=1).astype(low)
    for bits in range(batch):
        place = batch_index[0] ^ bits
        parts_out[bits][:, :quarter] = upper_grad[place]
        parts_out[bits][:, quarter : 2 * quarter] = act_parts[place]
        parts_out[bits][:, 2 * quarter :] = branch_parts[place]


def store_halves(part, bit, bits, keep_out, send_out):
    count = keep_out.shape[0]
    size = keep_out.shape[1]
    for entry in range(count):
        lower, upper = entry % bits, entry // bits
        base = upper * 2 * bits + lower
        mine = pl.ds(pl.multiple_of((base + bit * bits) * size, size), size)
        other = pl.ds(pl.multiple_of((base + (1 - bit) * bits) * size, size), size)
        keep_out[entry] = part[mine, :]
        send_out[entry] = part[other, :].astype(jnp.bfloat16)


def flip(tile):
    return tile.astype(jnp.float32).T.astype(jnp.bfloat16)


def weight_kernel(batch, orders, index, *refs):
    sides, tops, gots = (refs[batch * place : batch * (place + 1)] for place in range(3))
    up_keep, up_send, rest_keep, rest_send, flipped, columns, part, rest = refs[3 * batch :]
    tok_count, width = tops[0].shape
    for entry in range(batch):
        here = slice(entry * tok_count, (entry + 1) * tok_count)
        columns[here, :width] = gots[entry][:, :width]
        columns[here, width : 2 * width] = tops[entry][...]
        columns[here, 2 * width :] = gots[entry][:, 2 * width :]
        flipped[:width, here] = flip(sides[entry][:, :width])
        flipped[width : 2 * width, here] = flip(gots[entry][:, width : 2 * width])
        flipped[2 * width :, here] = flip(sides[entry][:, width:])
    part[...] = plain_dot(flipped[:width, :], columns[:, :width])
    store_halves(part, index[0], orders[0], up_keep, up_send)
    rest[:, :width] = plain_dot(flipped[width : 2 * width, :], columns[:, width : 2 * width])
    last = plain_dot(flipped[2 * width :, :], columns[:, 2 * width :])
    rest[:, width:] = last[:, : rest.shape[1] - width]
    store_halves(rest, index[1], orders[1], rest_keep, rest_send)


def fold_kernel(bits, bit, keep, got, keep_out, send_out):
    for entry in range(keep_out.shape[0]):
        lower, upper = entry % bits, entry // bits
        base = upper * 2 * bits + lower
        mine, other = base + bit[0] * bits, base + (1 - bit[0]) * bits
        keep_out[entry] = keep[mine] + got[mine].astype(jnp.float32)
        send_out[entry] = (keep[other] + got[other].astype(jnp.float32)).astype(jnp.bfloat16)


def collect_kernel(batch, batch_index, *refs):
    entries = refs[:batch]
    down_out, up_out, out_out, held = refs[batch:]
    rows, total = entries[0].shape
    width = down_out.shape[1]
    piece = width // batch
    f32 = jnp.float32
    for entry in range(batch):
        held[batch_index[0] ^ entry] = entries[entry][...]
    for place in range(batch):
        up_out[:, place * width : (place + 1) * width] = held[place, :, :width].astype(f32)
        down = held[place, :, width : 2 * width].astype(f32)
        down_out[place * rows : (place + 1) * rows, :] = down
    tiles = [held[place, :, 2 * width : 2 * width + piece].astype(f32) for place in range(batch)]
    out_out[...] = jnp.concatenate(tiles, axis=1)


def final_kernel(received, tokens, residual, rows, weight_in, out, weight, joined, held, sems):
    parts = received.shape[0]
    tok_count, width = tokens.shape
    channels = width // parts
    f32, low = jnp.float32, jnp.bfloat16
    load = pltpu.make_async_copy(weight_in, weight, sems.at[0])
    load.start()
    dense = received.shape[1] // 3
    for group in range(3):
        tiles = [
            loose_rows(
                received[part, group * dense : (group + 1) * dense, :].astype(f32),
                tok_count,
                channels,
            )
            for part in range(parts)
        ]
        joined[:, group * width : (group + 1) * width] = jnp.concatenate(tiles, axis=1).astype(low)
    gain = row_of(rows, "pre_gain")
    bias = row_of(rows, "pre_bias")
    _, unit, inv_std = norm_forward(tokens[...].astype(f32), gain, bias)
    load.wait()
    grad_normed = jnp.zeros((tok_count, width), f32)
    for group in range(3):
        cols = slice(group * width, (group + 1) * width)
        grad_normed = grad_normed + right_dot(joined[:, cols], weight[:, cols])
    grad_tokens, _, _ = norm_backward(grad_normed, unit, inv_std, gain)
    spread_rows(residual[...] + grad_tokens, held, out)


SHARED_ROWS = 48
LAID_ROWS = 8
OWN_ROWS = 40


def chain_kernel(
    norm_rows,
    in_local,
    sums,
    middle_sums,
    pos_weight,
    inner_weight,
    third_weight,
    vectors,
    weights,
    rates,
    grad_kernels_in,
    kernels_in,
    waves_in,
    pair_in,
    small_out,
    weight_total,
    rate_total,
    shared,
    pairs,
    grad_kernels,
    kernels,
    waves,
    pair_sums,
    sems,
):
    length = kernels.shape[0]
    blocks = length // BLOCK

    def loads(index):
        here = block_rows(index, BLOCK)
        later = pl.ds(pl.multiple_of(index * BLOCK + length // 2, BLOCK), BLOCK)
        pieces = [
            (source.at[rows], target.at[rows])
            for source, target in ((grad_kernels_in, grad_kernels), (kernels_in, kernels))
            for rows in (here, later)
        ]
        pieces.append((waves_in.at[:, here], waves.at[:, here]))
        return [
            pltpu.make_async_copy(source, target, sems.at[number * (blocks // 2) + index])
            for number, (source, target) in enumerate(pieces)
        ]

    for block in range(blocks // 2):
        for copy in loads(block):
            copy.start()
    width = in_local.shape[0]
    pair_load = pltpu.make_async_copy(pair_in, pair_sums, sems.at[5 * (blocks // 2)])
    pair_load.start()
    feat_count, fhid = pos_weight.shape
    f32 = jnp.float32
    freq = vectors[3:4, :]
    weight_total[...] = jnp.zeros_like(weight_total)
    rate_total[...] = jnp.zeros_like(rate_total)
    pairs[...] = jnp.zeros_like(pairs)

    half = length // 2
    cols = 2 * LANES
    weight_pair = doubled(weights[...])
    freq_pair = twice(freq)

    def body(index, carry):
        here = block_rows(index, BLOCK)
        there = pl.ds(pl.multiple_of(index * BLOCK + half, BLOCK), BLOCK)
        for copy in loads(index):
            copy.wait()
        features, times = feature_block(index * BLOCK, BLOCK, length, feat_count)
        windowed = []
        for rows, time in zip((here, there), times):
            grads = grad_kernels[rows, :]
            decayed = jnp.sum(grads * kernels[rows, :] * time, axis=0, keepdims=True)
            rate_total[...] = rate_total[...] - decayed
            windowed.append(grads * jnp.exp(-rates[...] * time))
        windowed = jnp.concatenate(windowed, axis=1)
        weight_total[...] = weight_total[...] + exact_tdot(waves[2, here, :LANES], windowed)
        flow = exact_nt(windowed, weight_pair)
        for layer in (2, 1, 0):
            slope = flow * waves[layer, here, LANES:]
            below = waves[layer - 1, here, :LANES] if layer else features
            count = below.shape[1]
            pairs[layer, :count, :] = pairs[layer, :count, :] + exact_tdot(below, slope)
            row = slice(LANES, LANES + 1)
            pairs[layer, row, :] = pairs[layer, row, :] + jnp.sum(slope, axis=0, keepdims=True)
            if layer:
                weight = inner_weight if layer == 1 else third_weight
                flow = exact_nt(slope * freq_pair, doubled(weight[...].astype(f32)))
        return carry

    lax.fori_loop(0, blocks // 2, body, 0)
    grad_freq = jnp.zeros_like(freq)
    at, bias_at = 0, 2 * fhid + feat_count
    for layer, weight in ((2, third_weight), (1, inner_weight), (0, pos_weight)):
        count = weight.shape[0]
        matrix = pairs[layer, :count, :fhid] + pairs[layer, count : 2 * count, fhid:]
        both = pairs[layer, LANES : LANES + 1, :]
        vector = both[:, :fhid] + both[:, fhid:]
        grad_freq = grad_freq + jnp.sum(weight[...].astype(f32) * matrix, axis=0, keepdims=True)
        grad_freq = grad_freq + vectors[layer : layer + 1, :] * vector
        shared[at : at + count, :] = matrix * freq
        shared[bias_at + layer : bias_at + layer + 1, :] = vector * freq
        at += count
    shared[bias_at + 3 : bias_at + 4, :] = grad_freq
    pair_load.wait()
    small_out[...] = jnp.zeros_like(small_out)
    ones = jnp.ones((8, in_local.shape[1]), f32)
    in_wide = in_local[...].astype(f32)
    gain = exact_nt(ones, in_wide * pair_sums[...])[0:1]
    column_sums = jnp.concatenate([sums[12 + group : 13 + group, :] for group in range(3)], axis=1)
    bias = exact_nt(jnp.broadcast_to(column_sums, ones.shape), in_wide)[0:1]
    everywhere = small_out.at[:, :SHARED_ROWS, :]
    per = width // LANES
    gain = (gain - row_of(norm_rows, "pre_bias") * bias) / row_of(norm_rows, "pre_gain")
    store_rows(everywhere, 0, lane_rows(gain))
    store_rows(everywhere, per, lane_rows(bias))
    at = 2 * per
    store_rows(everywhere, at, middle_sums[...])
    at += middle_sums.shape[0]
    store_rows(everywhere, at, jnp.concatenate([shared[:fhid, :], shared[fhid : 2 * fhid, :]], axis=1))
    at += fhid
    tail = shared[2 * fhid : 2 * fhid + feat_count + 4, :]
    store_rows(everywhere, at, jnp.concatenate([tail, jnp.zeros_like(tail)], axis=1))
    store_rows(small_out.at[:, SHARED_ROWS : SHARED_ROWS + LAID_ROWS, :], 0, sums[:15, :])
    own = small_out.at[:, SHARED_ROWS + LAID_ROWS :, :]
    for order in range(2):
        first = slice(order * LANES, (order + 1) * LANES)
        second = slice(cols + order * LANES, cols + (order + 1) * LANES)
        both = weight_total[:fhid, first] + weight_total[fhid:, second]
        store_rows(own, order * fhid, both)
        store_rows(own, 2 * fhid + order, rate_total[:, first])
    store_rows(own, 2 * fhid + 2, sums[15:17, :])


def spread_kernel(in_keep, in_got, small_keep, small_got, send_out, small_out):
    low, f32 = jnp.bfloat16, jnp.float32
    parts = send_out.shape[0]
    small = small_keep[...] + small_got[...]
    small_out[...] = small
    both = SHARED_ROWS + LAID_ROWS
    high, rest = split_low(small[:both])
    count = in_keep.shape[0] // parts
    for part in range(parts):
        here = slice(part * count, (part + 1) * count)
        send_out[part, :count, :] = (in_keep[here, :] + in_got[here, :].astype(f32)).astype(low)
        send_out[part, count : count + both, :] = high
        send_out[part, count + both :, :] = rest


def merge_kernel(received, small, out):
    f32 = jnp.float32
    parts = received.shape[0]
    both = SHARED_ROWS + LAID_ROWS
    count = received.shape[1] - 2 * both
    total = jnp.zeros((SHARED_ROWS, LANES), f32)
    done = parts * count
    rows = SHARED_ROWS + parts * LAID_ROWS + OWN_ROWS
    for part in range(parts):
        out[part * count : (part + 1) * count, :] = received[part, :count, :]
        high = received[part, count : count + both, :].astype(f32)
        rest = received[part, count + both :, :].astype(f32)
        total = total + high[:SHARED_ROWS] + rest[:SHARED_ROWS]
        at = done + SHARED_ROWS + part * LAID_ROWS
        laid = received[part, count : count + both, :].astype(f32)[SHARED_ROWS:]
        out[at : at + LAID_ROWS, :] = laid.astype(jnp.bfloat16)
        laid = received[part, count + both :, :].astype(f32)[SHARED_ROWS:]
        out[at + rows : at + rows + LAID_ROWS, :] = laid.astype(jnp.bfloat16)
    for at, value in ((0, total), (rows - OWN_ROWS, small[SHARED_ROWS + LAID_ROWS :, :])):
        high, rest = split_low(value)
        count = value.shape[0]
        out[done + at : done + at + count, :] = high
        out[done + rows + at : done + rows + at + count, :] = rest


def take_rows(source, at, count):
    per = source.shape[1]
    pieces = []
    while count:
        quarter, inside = divmod(at, per)
        size = min(count, per - inside)
        pieces.append(source[quarter, inside : inside + size, :])
        at += size
        count -= size
    return pieces[0] if len(pieces) == 1 else jnp.concatenate(pieces, axis=0)


def lane_row(block):
    return jnp.concatenate([block[place : place + 1] for place in range(block.shape[0])], axis=1)


def last_fold_kernel(up_keep, up_got, rest_keep, rest_got, out):
    f32, low = jnp.float32, jnp.bfloat16
    width = up_keep.shape[2]
    wide = width + rest_keep.shape[2]
    out[:, :width] = (up_keep[0] + up_got[0].astype(f32)).astype(low)
    out[:, width:wide] = (rest_keep[0] + rest_got[0].astype(f32)).astype(low)
    out[:, wide:] = jnp.zeros((out.shape[0], out.shape[1] - wide), low)


def finish_kernel(batch, channels, batch_index, *refs):
    entries = refs[:batch]
    (
        in_out,
        pre_gain_out,
        pre_bias_out,
        out_bias_out,
        post_gain_out,
        post_bias_out,
        down_bias_out,
        up_bias_out,
        third_out,
        inner_out,
        pos_out,
        pos_bias_out,
        inner_bias_out,
        third_bias_out,
        freq_out,
        taps_out,
        tap_bias_out,
        in_bias_out,
        filter_out,
        rates_out,
        skips_out,
        held,
        small,
    ) = refs[batch:]
    f32 = jnp.float32
    for bits in range(batch):
        held[batch_index[0] ^ bits] = entries[bits][...]
    in_rows = in_out.shape[0] // batch
    width = pre_gain_out.shape[0]
    parts = width // channels
    total = parts * 3 * in_rows
    rows = small.shape[1]
    for place in range(batch):
        small[place] = held[place, total : total + rows, :].astype(f32) + held[
            place, total + rows :, :
        ].astype(f32)

    def gather(place, carry):
        block = held[place, :total, :].astype(f32)
        tiles = []
        for group in range(3):
            for part in range(parts):
                at = (part * 3 + group) * in_rows
                tiles.append(block[at : at + in_rows, :channels])
        in_out[pl.ds(pl.multiple_of(place * in_rows, in_rows), in_rows), :] = jnp.concatenate(
            tiles, axis=1
        )
        return carry

    lax.fori_loop(0, batch, gather, 0)
    everywhere = small.at[:, :SHARED_ROWS, :]
    per = width // LANES
    at = 0
    for target in (
        pre_gain_out,
        pre_bias_out,
        out_bias_out,
        post_gain_out,
        post_bias_out,
        down_bias_out,
        up_bias_out,
    ):
        count = target.shape[0] // LANES
        target[...] = lane_row(take_rows(everywhere, at, count)).reshape(target.shape)
        at += count
    fhid = third_out.shape[0]
    pair = take_rows(everywhere, at, fhid)
    third_out[...] = pair[:, :fhid]
    inner_out[...] = pair[:, fhid : 2 * fhid]
    at += fhid
    tail = take_rows(everywhere, at, pos_out.shape[0] + 4)
    pos_out[...] = tail[: pos_out.shape[0], :fhid]
    for place, target in enumerate((pos_bias_out, inner_bias_out, third_bias_out, freq_out)):
        row = pos_out.shape[0] + place
        target[...] = tail[row : row + 1, :fhid].reshape(target.shape)

    def laid(number):
        place, row = divmod(number, LAID_ROWS)
        return [
            small[place, SHARED_ROWS + part * LAID_ROWS + row :][:1, :channels]
            for part in range(parts)
        ]

    for number in range(5):
        tiles = [tile for group in range(3) for tile in laid(3 * number + group)]
        row = jnp.concatenate(tiles, axis=1)
        if number < 3:
            taps_out[number : number + 1, :] = row
        elif number == 3:
            tap_bias_out[...] = row.reshape(tap_bias_out.shape)
        else:
            in_bias_out[...] = row.reshape(in_bias_out.shape)
    own = small.at[:, SHARED_ROWS + parts * LAID_ROWS :, :]
    for order in range(2):
        filter_out[order] = take_rows(own, order * fhid, fhid)[:, :channels]
    rates_out[...] = take_rows(own, 2 * fhid, 2)[:, :channels]
    skips_out[...] = take_rows(own, 2 * fhid + 2, 2)[:, :channels]


def swapped(value, axis, bits):
    count = lax.axis_size(axis)
    return lax.ppermute(value, axis, [(source, source ^ bits) for source in range(count)])


def over_batch(value):
    held = {0: value}
    bits = lax.axis_size("batch") // 2
    while bits:
        held.update({place ^ bits: swapped(member, "batch", bits) for place, member in held.items()})
        bits //= 2
    return [held[place] for place in range(len(held))]


def natural(entries, index):
    stacked = jnp.stack(entries)
    return [
        lax.dynamic_index_in_dim(stacked, index ^ place, 0, keepdims=False)
        for place in range(len(entries))
    ]


def halves(total, index, bits, left):
    shape = total.shape[1:]
    place = left.index(bits)
    before = 1 << (len(left) - 1 - place)
    after = 1 << place
    view = total.reshape((before, 2, after) + shape)
    bit = (index // bits) % 2
    keep = lax.dynamic_index_in_dim(view, bit, 1, keepdims=False)
    send = lax.dynamic_index_in_dim(view, 1 - bit, 1, keepdims=False)
    return keep.reshape((before * after,) + shape), send.reshape((before * after,) + shape)


def halved(total, axis, index, order):
    count = lax.axis_size(axis)
    left = [1 << k for k in range(count.bit_length() - 1)]
    for bits in order:
        keep, send = halves(total, index, bits, left)
        got = swapped(send.astype(jnp.bfloat16), axis, bits)
        total = keep + got.astype(jnp.float32)
        left.remove(bits)
    return total[0]


def split_low(value):
    high = value.astype(jnp.bfloat16)
    return high, (value - high.astype(jnp.float32)).astype(jnp.bfloat16)


def dense_device(
    inputs,
    pre_gain,
    pre_bias,
    in_weight,
    input_projection_bias,
    short_weight,
    short_bias,
    pos_weight,
    pos_bias,
    inner_weight,
    inner_bias,
    filter_third_weight,
    third_bias,
    sine_freq,
    filter_weight,
    decay_rates,
    skip_gains,
    out_weight,
    out_bias,
    post_gain,
    post_bias,
    up_weight,
    up_bias,
    down_weight,
    down_bias,
    cotangent,
):
    seq_parts = lax.axis_size("seq")
    batch_parts = lax.axis_size("batch")
    seq_rank = lax.axis_index("seq")
    batch_rank = lax.axis_index("batch")
    tokens = inputs[0]
    tok_count, width = tokens.shape
    length = tok_count * seq_parts
    channels = width // seq_parts
    hidden_units = up_weight.shape[1]
    fhid = pos_weight.shape[1]
    f32, low = jnp.float32, jnp.bfloat16
    wide = 3 * LANES
    start = seq_rank * channels
    bit_list = [1 << k for k in range(seq_parts.bit_length() - 1)]
    swap_list = [bit_list[1], bit_list[0]] + bit_list[2:]
    batch_bits = [1 << k for k in range(batch_parts.bit_length() - 1)]

    tokens, grad_top, own_normed = call_kernel(
        norm_kernel,
        [((tok_count, width), low)] * 3,
        [tokens, cotangent[0], pre_gain, pre_bias],
        micros=1,
        scratch=[((width // LANES, tok_count, LANES), f32)],
        name="norm",
    )
    chunks = {0: own_normed}
    for bits in range(2, seq_parts, 2):
        chunks[bits] = swapped(own_normed, "seq", bits)

    quarters = hidden_units // width
    half = length // 2
    seq_scalar = seq_rank.astype(jnp.int32)[None]
    batch_scalar = batch_rank.astype(jnp.int32)[None]
    start_scalar = start.astype(jnp.int32)[None]
    wave, turn, rows, in_local, rows_local, weights_local, rates_local, vectors = call_kernel(
        lambda *refs: wave_kernel(channels, *refs),
        [
            ((length, half), low),
            ((length, LANES), f32),
            ((ROW_COUNT, width), f32),
            ((width, wide), low),
            ((ROW_COUNT, LANES), f32),
            ((fhid, 2 * LANES), f32),
            ((1, 2 * LANES), f32),
            ((4, fhid), f32),
        ],
        [
            start_scalar,
            pre_gain,
            pre_bias,
            input_projection_bias,
            short_bias,
            short_weight,
            skip_gains,
            post_gain,
            post_bias,
            out_bias,
            down_bias,
            up_bias,
            pos_bias,
            inner_bias,
            third_bias,
            sine_freq,
            filter_weight,
            decay_rates,
            in_weight,
        ],
        micros=8.5,
        spaces="s" + "v" * 17 + "h" + "h" + "v" * 7,
        scratch=[
            ((4, 32, half), f32),
            ((length, half), low),
            ((width, 3 * width), low),
            2,
        ],
        name="waves",
    )
    even = [chunks[bits] for bits in range(2, seq_parts, 2)]
    wave, *even = lax.optimization_barrier((wave, *even))
    for bits in range(0, seq_parts, 2):
        if bits:
            chunks[bits] = even[bits // 2 - 1]
        chunks[bits + 1] = swapped(chunks[bits], "seq", 1)
    spectrum, kernels, filter_waves = call_kernel(
        filter_kernel,
        [
            ((2, length, 2 * LANES), f32),
            ((length, 2 * LANES), f32),
            ((3, half, 4 * fhid), f32),
        ],
        [
            pos_weight,
            inner_weight,
            filter_third_weight,
            vectors,
            weights_local,
            rates_local,
            turn,
            wave,
        ],
        micros=13,
        spaces="v" * 7 + "h" + "vvv",
        scratch=[
            ((length, 2 * LANES), low),
            ((length, 2 * LANES), low),
            ((length, half), low),
            1,
        ],
        name="filters",
    )
    tops = over_batch(grad_top)
    spectrum, *tops = lax.optimization_barrier((spectrum, *tops))

    dense = tok_count * channels // LANES
    (
        normed,
        projected,
        product,
        gate,
        after,
        gated,
        product_wave,
        gated_wave,
        mixer_chan,
    ) = call_kernel(
        lambda *refs: front_kernel(seq_parts, *refs),
        [
            ((length, width), low),
            ((2, PAD + half, wide), f32),
            ((half, 2 * LANES), low),
            ((half, 2 * LANES), low),
            ((half, 2 * LANES), low),
            ((half, 2 * LANES), low),
            ((2, length, LANES), f32),
            ((2, length, LANES), f32),
            ((seq_parts, dense, LANES), low),
        ],
        [seq_scalar]
        + [chunks[part] for part in range(seq_parts)]
        + [in_local, rows_local, wave, turn, spectrum],
        micros=13,
        spaces="s" + "v" * seq_parts + "vvhhh" + "hhvvvvhhv",
        scratch=[
            ((length, width), low),
            ((half, 2 * LANES), low),
            ((half, 2 * LANES), low),
            ((length, half), low),
            ((length, LANES), f32),
            ((2, length, 2 * LANES), f32),
            ((2, PAD + half, wide), f32),
            ((2, length, LANES), f32),
            ((2, length, LANES), f32),
            ((half, 2 * LANES), low),
            7,
        ],
        name="front",
    )
    mixer_back = lax.all_to_all(mixer_chan, "seq", 0, 0, tiled=True)

    quarter = hidden_units // batch_parts
    branch_quarter = width // batch_parts
    rows_quarter = hidden_units // (seq_parts * batch_parts)
    assert quarter == width and seq_parts * rows_quarter == width
    up_width = quarter + branch_quarter
    padded = quarter + -(-branch_quarter // LANES) * LANES
    message = padded + width
    outputs, grad_residual, grad_mixer, middle_sums, sides, *gots = call_kernel(
        lambda *refs: middle_kernel(seq_parts, *refs),
        [
            ((tok_count, width), f32),
            ((tok_count, width), f32),
            ((seq_parts, dense, LANES), low),
            (((4 * width + hidden_units) // LANES, LANES), f32),
        ]
        + [((tok_count, 2 * width), low)]
        + [((tok_count, message), low)] * batch_parts,
        [
            batch_scalar,
            mixer_back,
            tokens,
            grad_top,
            rows,
            out_weight,
            up_weight,
            down_weight,
        ],
        micros=11,
        spaces="svvvvhhh" + "v" * (5 + batch_parts),
        scratch=[
            ((width, width), low),
            ((quarters, width, width), low),
            ((quarters, width, width), low),
            ((tok_count, width), f32),
            ((tok_count, width), f32),
            ((tok_count, width), f32),
            ((quarters, tok_count, width), low),
            ((quarters, tok_count, width), low),
            ((batch_parts, tok_count, width), low),
            ((batch_parts, tok_count, padded - quarter), low),
            ((quarters, 1, width), f32),
            ((width // LANES, tok_count, LANES), f32),
            1 + 2 * quarters,
        ],
        name="middle",
    )
    grad_mixer_chan = lax.all_to_all(grad_mixer, "seq", 0, 0, tiled=True)

    def bit_of(bits):
        return ((seq_rank // bits) % 2).astype(jnp.int32)[None]

    def fold(keep, got, bits, left):
        size = keep.shape[0] // 2
        block = keep.shape[1:]
        place = left.index(bits)
        return call_kernel(
            lambda *refs: fold_kernel(1 << place, *refs),
            [((size,) + block, f32), ((size,) + block, low)],
            [bit_of(bits), keep, got],
            micros=1,
            spaces="svvvv",
            name="fold",
        )

    grad_mixer_chan = lax.all_to_all(grad_mixer, "seq", 0, 0, tiled=True)
    sides = over_batch(sides)
    gots = [gots[0]] + [swapped(gots[bits], "batch", bits) for bits in range(1, batch_parts)]
    rows_each = width // seq_parts

    blocks = length // BLOCK
    packed, grad_proj, grad_kernels, sums = call_kernel(
        lambda *refs: back_kernel(channels, *refs),
        [
            ((seq_parts, 3 * dense, LANES), low),
            ((length, wide), low),
            ((2, half, 2 * LANES), f32),
            ((24, LANES), f32),
        ],
        [
            grad_mixer_chan,
            product,
            gate,
            after,
            gated,
            rows_local,
            turn,
            product_wave,
            gated_wave,
            spectrum,
            wave,
            projected,
        ],
        micros=15,
        spaces="v" * 7 + "h" * 5 + "vvvv",
        scratch=[((half, 2 * LANES), low)] * 4
        + [
            ((half, 4 * LANES), low),
            ((half, 4 * LANES), low),
            ((length, half), low),
            ((2, length, 2 * LANES), f32),
            ((2, length, LANES), f32),
            ((2, length, LANES), f32),
            ((2, PAD + half, wide), f32),
            ((2, half + PAD, LANES), f32),
            5,
        ],
        name="back",
    )
    proj_back = lax.all_to_all(packed, "seq", 0, 0, tiled=True)
    orders = (bit_list, swap_list)
    halves_of = [
        ((seq_parts // 2, rows_each, columns), dtype)
        for columns in (width, width + branch_quarter)
        for dtype in (f32, low)
    ]
    up_keep, up_send, rest_keep, rest_send = call_kernel(
        lambda *refs: weight_kernel(batch_parts, (orders[0][0], orders[1][0]), *refs),
        halves_of,
        [jnp.concatenate([bit_of(order[0]) for order in orders])] + sides + tops + gots,
        micros=6,
        spaces="s" + "v" * (3 * batch_parts + 4),
        scratch=[
            ((3 * width, batch_parts * tok_count), low),
            ((batch_parts * tok_count, width + padded), low),
            ((width, width), f32),
            ((width, width + branch_quarter), f32),
        ],
        name="weights",
    )
    up_got = swapped(up_send, "seq", orders[0][0])
    rest_got = swapped(rest_send, "seq", orders[1][0])

    pair_part = left_dot(normed, grad_proj)
    in_rows = width // (seq_parts * batch_parts)
    in_count = 3 * in_rows
    in_part = (
        pair_part.reshape(seq_parts, batch_parts, in_rows, 3, LANES)
        .transpose(1, 0, 3, 2, 4)
        .reshape(batch_parts, seq_parts * in_count, LANES)
    )
    small_rows = SHARED_ROWS + LAID_ROWS + OWN_ROWS
    in_part, pair_part, up_keep, rest_keep = lax.optimization_barrier(
        (in_part, pair_part, up_keep, rest_keep)
    )
    (small,) = call_kernel(
        chain_kernel,
        [((batch_parts, small_rows, LANES), f32)],
        [
            rows,
            in_local,
            sums,
            middle_sums,
            pos_weight,
            inner_weight,
            filter_third_weight,
            vectors,
            weights_local,
            rates_local,
            grad_kernels.reshape(length, 2 * LANES),
            kernels,
            filter_waves,
            pair_part,
        ],
        micros=12,
        spaces="v" * 10 + "hhhh" + "v",
        scratch=[
            ((2 * fhid, 4 * LANES), f32),
            ((1, 2 * LANES), f32),
            ((2 * fhid + 40, fhid), f32),
            ((3, LANES + 8, 2 * fhid), f32),
            ((length, 2 * LANES), f32),
            ((length, 2 * LANES), f32),
            ((3, length // 2, 4 * fhid), f32),
            ((width, wide), f32),
            5 * (blocks // 2) + 1,
        ],
        name="chain",
    )
    small, proj_back = lax.optimization_barrier((small, proj_back))

    def next_fold(keep, got, order, step):
        left = [bits for bits in bit_list if bits not in order[:step]]
        return fold(keep, got, order[step], left)

    left = list(batch_bits)
    for bits in batch_bits[:-1]:
        in_keep, in_send = halves(in_part, batch_rank, bits, left)
        small_keep, small_send = halves(small, batch_rank, bits, left)
        in_part = in_keep + swapped(in_send.astype(low), "batch", bits).astype(f32)
        small = small_keep + swapped(small_send, "batch", bits)
        left.remove(bits)
    in_keep, in_send = halves(in_part, batch_rank, batch_bits[-1], left)
    small_keep, small_send = halves(small, batch_rank, batch_bits[-1], left)
    shared_count = in_count + 2 * (SHARED_ROWS + LAID_ROWS)
    mixed_send, small = call_kernel(
        spread_kernel,
        [((seq_parts, shared_count, LANES), low), ((small_rows, LANES), f32)],
        [
            in_keep[0],
            swapped(in_send.astype(low), "batch", batch_bits[-1])[0],
            small_keep[0],
            swapped(small_send, "batch", batch_bits[-1])[0],
        ],
        micros=2,
        name="spread",
    )
    up_keep, up_send = next_fold(up_keep, up_got, orders[0], 1)
    rest_keep, rest_send = next_fold(rest_keep, rest_got, orders[1], 1)
    up_got = swapped(up_send, "seq", orders[0][1])
    rest_got = swapped(rest_send, "seq", orders[1][1])
    mixed_send, proj_back = lax.optimization_barrier((mixed_send, proj_back))
    mixed_got = lax.all_to_all(mixed_send, "seq", 0, 0, tiled=True)
    (grad_inputs,) = call_kernel(
        final_kernel,
        [((tok_count, width), f32)],
        [proj_back, tokens, grad_residual, rows, in_weight],
        micros=5.5,
        spaces="vvvvhv",
        scratch=[
            ((width, 3 * width), low),
            ((tok_count, 3 * width), low),
            ((width // LANES, tok_count, LANES), f32),
            1,
        ],
        name="final",
    )
    done_rows = SHARED_ROWS + seq_parts * LAID_ROWS + OWN_ROWS
    (last,) = call_kernel(
        merge_kernel,
        [((seq_parts * in_count + 2 * done_rows, LANES), low)],
        [mixed_got, small],
        micros=2,
        name="merge",
    )
    up_keep, up_send = next_fold(up_keep, up_got, orders[0], 2)
    rest_keep, rest_send = next_fold(rest_keep, rest_got, orders[1], 2)
    up_got = swapped(up_send, "seq", orders[0][2])
    rest_got = swapped(rest_send, "seq", orders[1][2])
    lasts = over_batch(last)
    up_got, grad_inputs, last = lax.optimization_barrier((up_got, grad_inputs, last))
    total = -(-(2 * width + branch_quarter) // LANES) * LANES
    (weights_done,) = call_kernel(
        last_fold_kernel,
        [((rows_each, total), low)],
        [up_keep, up_got, rest_keep, rest_got],
        micros=1,
        name="last_fold",
    )
    final_down, final_up, final_out = call_kernel(
        lambda *refs: collect_kernel(batch_parts, *refs),
        [
            ((batch_parts * rows_each, width), f32),
            ((rows_each, hidden_units), f32),
            ((rows_each, width), f32),
        ],
        [batch_scalar] + over_batch(weights_done),
        micros=3,
        spaces="s" + "v" * (batch_parts + 3),
        scratch=[((batch_parts, rows_each, total), low)],
        name="collect",
    )
    (
        final_in,
        grad_pre_gain,
        grad_pre_bias,
        grad_out_bias,
        grad_post_gain,
        grad_post_bias,
        grad_down_bias,
        grad_up_bias,
        grad_third,
        grad_inner,
        grad_pos,
        grad_pos_bias,
        grad_inner_bias,
        grad_third_bias,
        grad_freq,
        grad_taps,
        grad_tap_bias,
        grad_in_bias,
        grad_filter,
        grad_rates,
        grad_skips,
    ) = call_kernel(
        lambda *refs: finish_kernel(batch_parts, channels, *refs),
        [
            ((batch_parts * in_rows, 3 * width), f32),
            ((width,), f32),
            ((width,), f32),
            ((width,), f32),
            ((width,), f32),
            ((width,), f32),
            ((width,), f32),
            ((hidden_units,), f32),
            (filter_third_weight.shape, f32),
            (inner_weight.shape, f32),
            (pos_weight.shape, f32),
            ((fhid,), f32),
            ((fhid,), f32),
            ((fhid,), f32),
            ((fhid,), f32),
            ((3, 3 * width), f32),
            ((3 * width,), f32),
            ((3 * width,), f32),
            ((2, fhid, channels), f32),
            ((2, channels), f32),
            ((2, channels), f32),
        ],
        [batch_scalar] + lasts,
        micros=3,
        spaces="s" + "v" * batch_parts + "v" * 21,
        scratch=[
            ((batch_parts,) + last.shape, low),
            ((batch_parts, done_rows, LANES), f32),
        ],
        name="finish",
    )
    return (
        outputs[None],
        grad_inputs[None],
        grad_pre_gain,
        grad_pre_bias,
        final_in,
        grad_in_bias,
        grad_taps,
        grad_tap_bias,
        grad_pos,
        grad_pos_bias,
        grad_inner,
        grad_inner_bias,
        grad_third,
        grad_third_bias,
        grad_freq,
        grad_filter,
        grad_rates,
        grad_skips,
        final_out,
        grad_out_bias,
        grad_post_gain,
        grad_post_bias,
        final_up,
        grad_up_bias,
        final_down,
        grad_down_bias,
    )


def per_device(*args):
    tokens, parts = args[0].shape[1], lax.axis_size("seq")
    channels = args[0].shape[2] // parts
    dense = tokens * parts <= DENSE_LIMIT and lays_dense(tokens, channels)
    return (dense_device if dense else factored_device)(*args)


def solution(mesh):
    in_specs = (
        P("batch", "seq", None),
        P(),
        P(),
        P(),
        P(),
        P(),
        P(),
        P(),
        P(),
        P(),
        P(),
        P(),
        P(),
        P(),
        P(),
        P(),
        P(),
        P(),
        P(),
        P(),
        P(),
        P(),
        P(),
        P(),
        P(),
        P("batch", "seq", None),
    )
    out_specs = (
        P("batch", "seq", None),
        P("batch", "seq", None),
        P(),
        P(),
        P("seq", None),
        P(),
        P(),
        P(),
        P(),
        P(),
        P(),
        P(),
        P(),
        P(),
        P(),
        P(None, None, "seq"),
        P(None, "seq"),
        P(None, "seq"),
        P("seq", None),
        P(),
        P(),
        P(),
        P("seq", None),
        P(),
        P("seq", None),
        P(),
    )
    return jax.shard_map(
        per_device, mesh=mesh, in_specs=in_specs, out_specs=out_specs, check_vma=False
    )
```

```python
import math

import jax
import jax.numpy as jnp
import numpy as np
from jax import lax
from jax.experimental import pallas as pl
from jax.experimental.pallas import tpu as pltpu
from jax.sharding import PartitionSpec as P

epsilon = 1e-05
highest_accuracy = lax.Precision.HIGHEST


def passed_along(value, axis, steps):
    count = lax.axis_size(axis)
    initial, last = (max(0, -steps), min(count, count - steps))
    return lax.ppermute(value, axis, [(source, source + steps) for source in range(initial, last)])


def plain_dot(left_side, right_side):
    return jnp.dot(left_side, right_side, preferred_element_type=jnp.float32)


def exact_tdot(left_side, right_side):
    return lax.dot_general(
        left_side,
        right_side,
        (((0,), (0,)), ((), ())),
        precision=highest_accuracy,
        preferred_element_type=jnp.float32,
    )


def left_dot(left_side, right_side):
    return lax.dot_general(
        left_side, right_side, (((0,), (0,)), ((), ())), preferred_element_type=jnp.float32
    )


def right_dot(left_side, right_side):
    return lax.dot_general(
        left_side, right_side, (((1,), (1,)), ((), ())), preferred_element_type=jnp.float32
    )


def rounded(values):
    return lax.optimization_barrier(values.astype(jnp.bfloat16)).astype(jnp.float32)


def norm_forward(values, gain_vec, shift_vec):
    centre = values - jnp.mean(values, axis=-1, keepdims=True)
    inv_std = lax.rsqrt(jnp.mean(centre * centre, axis=-1, keepdims=True) + epsilon)
    unit_rows = centre * inv_std
    return (unit_rows * gain_vec + shift_vec, unit_rows, inv_std)


def norm_backward(grad_out, unit_rows, inv_std, gain_vec):
    grad_unit = grad_out * gain_vec
    grad_values = inv_std * (
        grad_unit
        - jnp.mean(grad_unit, axis=-1, keepdims=True)
        - unit_rows * jnp.mean(grad_unit * unit_rows, axis=-1, keepdims=True)
    )
    return (grad_values, jnp.sum(grad_out * unit_rows, axis=0), jnp.sum(grad_out, axis=0))


def position_rows(length, feat_count):
    steps_pos = jnp.arange(length, dtype=jnp.float32)
    time_steps = steps_pos / (length - 1)
    band_count = (feat_count - 1) // 2
    frequency = jnp.linspace(0.0001, band_count - 1, band_count, dtype=jnp.float32)
    angles = frequency[:, None] * (steps_pos * (2.0 * math.pi / length))[None, :]
    features_t = jnp.concatenate([time_steps[None, :], jnp.cos(angles), -jnp.sin(angles)], axis=0)
    return (features_t, time_steps)


def body_filters(
    features_t,
    time_steps,
    pos_weight,
    pos_bias,
    inner_weight,
    inner_bias,
    filter_third_weight,
    third_bias,
    sine_freq,
    weight_local,
    rates_local,
):
    hidden = jnp.sin(sine_freq[:, None] * (exact_tdot(pos_weight, features_t) + pos_bias[:, None]))
    hidden = jnp.sin(sine_freq[:, None] * (exact_tdot(inner_weight, hidden) + inner_bias[:, None]))
    hidden = jnp.sin(
        sine_freq[:, None] * (exact_tdot(filter_third_weight, hidden) + third_bias[:, None])
    )
    first_kernel = exact_tdot(weight_local[0], hidden) * jnp.exp(
        -rates_local[0][:, None] * time_steps[None, :]
    )
    second_kernel = exact_tdot(weight_local[1], hidden) * jnp.exp(
        -rates_local[1][:, None] * time_steps[None, :]
    )
    return (first_kernel, second_kernel)


def split_sizes(extent):
    outer_size = math.gcd(extent // 2, 1 << (extent.bit_length() - 1) // 2)
    return (outer_size, extent // outer_size)


def dft_rect(row_count, col_count, modulus, direction):
    row_ids = jnp.arange(row_count, dtype=jnp.int32)[:, None]
    col_ids = jnp.arange(col_count, dtype=jnp.int32)[None, :]
    angles = (row_ids * col_ids % modulus).astype(jnp.float32) * (2.0 * math.pi / modulus)
    return (jnp.cos(angles), direction * jnp.sin(angles))


def first_section(block_groups, lookup_grid):
    return jnp.einsum(
        "cij,ik->ckj",
        block_groups,
        lookup_grid,
        precision=highest_accuracy,
        preferred_element_type=jnp.float32,
    )


def second_section(block_groups, lookup_grid):
    return jnp.einsum(
        "dhq,qn->dnh",
        block_groups,
        lookup_grid,
        precision=highest_accuracy,
        preferred_element_type=jnp.float32,
    )


def padded_spectrum(signal):
    channels, length = signal.shape
    extent = 2 * length
    outer_size, inner_size = split_sizes(extent)
    block_groups = signal.reshape(channels, inner_size // 2, outer_size)
    cos_inner, sin_inner = dft_rect(inner_size // 2, inner_size, inner_size, -1.0)
    section_real = first_section(block_groups, cos_inner)
    section_imag = first_section(block_groups, sin_inner)
    twist_cos, rotation_sine = dft_rect(inner_size, outer_size, extent, -1.0)
    turned_real = section_real * twist_cos - section_imag * rotation_sine
    turned_imag = section_real * rotation_sine + section_imag * twist_cos
    cos_outer, sin_outer = dft_rect(outer_size, outer_size, outer_size, -1.0)
    out_real = second_section(turned_real, cos_outer) - second_section(turned_imag, sin_outer)
    out_imag = second_section(turned_real, sin_outer) + second_section(turned_imag, cos_outer)
    return (out_real.reshape(channels, extent), out_imag.reshape(channels, extent))


def inverse_real(spec_real, spec_imag):
    channels, extent = spec_real.shape
    outer_size, inner_size = split_sizes(extent)
    blocks_real = spec_real.reshape(channels, inner_size, outer_size)
    blocks_imag = spec_imag.reshape(channels, inner_size, outer_size)
    cos_inner, sin_inner = dft_rect(inner_size, inner_size, inner_size, 1.0)
    section_real = first_section(blocks_real, cos_inner) - first_section(blocks_imag, sin_inner)
    section_imag = first_section(blocks_real, sin_inner) + first_section(blocks_imag, cos_inner)
    twist_cos, rotation_sine = dft_rect(inner_size, outer_size, extent, 1.0)
    turned_real = section_real * twist_cos - section_imag * rotation_sine
    turned_imag = section_real * rotation_sine + section_imag * twist_cos
    cos_outer, sin_outer = dft_rect(outer_size, outer_size // 2, outer_size, 1.0)
    out_real = second_section(turned_real, cos_outer) - second_section(turned_imag, sin_outer)
    return out_real.reshape(channels, extent // 2) / extent


def times_spec(left_real, left_imag, right_real, right_imag):
    return (
        left_real * right_real - left_imag * right_imag,
        left_real * right_imag + left_imag * right_real,
    )


def times_conj(left_real, left_imag, right_real, right_imag):
    return (
        left_real * right_real + left_imag * right_imag,
        left_imag * right_real - left_real * right_imag,
    )


def factored_device(
    inputs,
    pre_gain,
    pre_bias,
    in_weight,
    input_projection_bias,
    short_weight,
    short_bias,
    pos_weight,
    pos_bias,
    inner_weight,
    inner_bias,
    filter_third_weight,
    third_bias,
    sine_freq,
    filter_weight,
    decay_rates,
    skip_gains,
    out_weight,
    out_bias,
    post_gain,
    post_bias,
    up_weight,
    up_bias,
    down_weight,
    down_bias,
    cotangent,
):
    seq_parts = lax.axis_size("seq")
    seq_rank = lax.axis_index("seq")
    tokens = inputs[0]
    tok_count = tokens.shape[0]
    model_width = tokens.shape[1]
    length = tok_count * seq_parts
    channels = model_width // seq_parts
    tokens_wide = tokens.astype(jnp.float32)
    pre_gain_f = pre_gain.astype(jnp.float32)
    pre_bias_f = pre_bias.astype(jnp.float32)
    in_bias_f = input_projection_bias.astype(jnp.float32)
    short_f = short_weight.astype(jnp.float32)
    short_bias_f = short_bias.astype(jnp.float32)
    out_bias_f = out_bias.astype(jnp.float32)
    post_gain_f = post_gain.astype(jnp.float32)
    post_bias_f = post_bias.astype(jnp.float32)
    up_bias_f = up_bias.astype(jnp.float32)
    down_bias_f = down_bias.astype(jnp.float32)
    normed, unit_pre, inv_pre = norm_forward(tokens_wide, pre_gain_f, pre_bias_f)
    normed_low = normed.astype(jnp.bfloat16)
    projected = plain_dot(normed_low, in_weight) + in_bias_f
    previous = passed_along(projected[tok_count - 2 :], "seq", 1)
    extended = jnp.concatenate([previous, projected], axis=0)
    mixed_conv = (
        short_f[0] * extended[:-2]
        + short_f[1] * extended[1:-1]
        + short_f[2] * extended[2:]
        + short_bias_f
    )
    value_part = mixed_conv[:, :model_width]
    gate_one = mixed_conv[:, model_width : 2 * model_width]
    gate_two = mixed_conv[:, 2 * model_width :]
    product_low = (value_part * gate_one).astype(jnp.bfloat16)
    gate_two_low = gate_two.astype(jnp.bfloat16)
    prod_chan, gate_chan = (
        lax.all_to_all(product_low.T, "seq", split_axis=0, concat_axis=1, tiled=True),
        lax.all_to_all(gate_two_low.T, "seq", split_axis=0, concat_axis=1, tiled=True),
    )
    features_t, time_steps = position_rows(length, pos_weight.shape[0])
    chan_start = seq_rank * channels
    weight_local = lax.dynamic_slice_in_dim(
        filter_weight.astype(jnp.float32), chan_start, channels, 2
    )
    rates_local = lax.dynamic_slice_in_dim(decay_rates, chan_start, channels, 1)
    skips_local = lax.dynamic_slice_in_dim(skip_gains.astype(jnp.float32), chan_start, channels, 1)
    skip_one = skips_local[0][:, None]
    skip_two = skips_local[1][:, None]
    shared = tuple(
        (
            member.astype(jnp.float32)
            for member in (
                pos_weight,
                pos_bias,
                inner_weight,
                inner_bias,
                filter_third_weight,
                third_bias,
                sine_freq,
            )
        )
    )

    def local_filters(*params):
        return body_filters(features_t, time_steps, *params)

    (kernel_one, kernel_two), filter_pull = jax.vjp(
        local_filters, *shared, weight_local, rates_local
    )
    prod_wide = prod_chan.astype(jnp.float32)
    gate_wide = gate_chan.astype(jnp.float32)
    prod_real, prod_imag = padded_spectrum(prod_wide)
    kone_real, kone_imag = padded_spectrum(kernel_one)
    convolved_real_part, conv_imag = times_spec(prod_real, prod_imag, kone_real, kone_imag)
    after_one = rounded(inverse_real(convolved_real_part, conv_imag) + skip_one * prod_wide)
    gated_low = rounded(after_one * gate_wide)
    gated_real, gated_imag = padded_spectrum(gated_low)
    ktwo_real, ktwo_imag = padded_spectrum(kernel_two)
    convolved_real_part, conv_imag = times_spec(gated_real, gated_imag, ktwo_real, ktwo_imag)
    mixer_chan = (inverse_real(convolved_real_part, conv_imag) + skip_two * gated_low).astype(
        jnp.bfloat16
    )
    mixer_tok = lax.all_to_all(mixer_chan, "seq", split_axis=1, concat_axis=0, tiled=True).T
    branch = plain_dot(mixer_tok, out_weight) + out_bias_f
    residual = tokens_wide + branch
    normed_two, unit_post, inv_post = norm_forward(residual, post_gain_f, post_bias_f)
    normed_two_low = normed_two.astype(jnp.bfloat16)
    upper_pre = plain_dot(normed_two_low, up_weight) + up_bias_f
    activated = jax.nn.gelu(upper_pre, approximate=False).astype(jnp.bfloat16)
    outputs = residual + plain_dot(activated, down_weight) + down_bias_f
    grad_top = cotangent[0]
    grad_top_wide = grad_top.astype(jnp.float32)
    grad_act = right_dot(grad_top, down_weight)
    grad_down = left_dot(activated, grad_top)
    grad_down_bias = jnp.sum(grad_top_wide, axis=0)
    gelu_slope = (
        0.5 * (1.0 + lax.erf(upper_pre * 0.7071067811865476))
        + upper_pre * jnp.exp(-0.5 * upper_pre * upper_pre) * 0.3989422804014327
    )
    grad_upper = (grad_act * gelu_slope).astype(jnp.bfloat16)
    grad_up = left_dot(normed_two_low, grad_upper)
    grad_up_bias = jnp.sum(grad_upper.astype(jnp.float32), axis=0)
    grad_normed_two = right_dot(grad_upper, up_weight)
    grad_resid_norm, grad_post_gain, grad_post_bias = norm_backward(
        grad_normed_two, unit_post, inv_post, post_gain_f
    )
    grad_residual = grad_top_wide + grad_resid_norm
    grad_branch = grad_residual.astype(jnp.bfloat16)
    grad_out = left_dot(mixer_tok, grad_branch)
    grad_out_bias = jnp.sum(grad_branch.astype(jnp.float32), axis=0)
    grad_mixer = right_dot(grad_branch, out_weight).astype(jnp.bfloat16)
    grad_mixer_chan = lax.all_to_all(
        grad_mixer.T, "seq", split_axis=0, concat_axis=1, tiled=True
    ).astype(jnp.float32)
    gmix_real, gmix_imag = padded_spectrum(grad_mixer_chan)
    corr_real, corr_imag = times_conj(gmix_real, gmix_imag, ktwo_real, ktwo_imag)
    grad_gated = rounded(inverse_real(corr_real, corr_imag) + skip_two * grad_mixer_chan)
    corr_real, corr_imag = times_conj(gmix_real, gmix_imag, gated_real, gated_imag)
    grad_kernel_two = inverse_real(corr_real, corr_imag)
    grad_skip_two = jnp.sum(grad_mixer_chan * gated_low, axis=1)
    grad_after = rounded(grad_gated * gate_wide)
    grad_gate_two = (grad_gated * after_one).astype(jnp.bfloat16)
    gaft_real, gaft_imag = padded_spectrum(grad_after)
    corr_real, corr_imag = times_conj(gaft_real, gaft_imag, kone_real, kone_imag)
    grad_product = (inverse_real(corr_real, corr_imag) + skip_one * grad_after).astype(jnp.bfloat16)
    corr_real, corr_imag = times_conj(gaft_real, gaft_imag, prod_real, prod_imag)
    grad_kernel_one = inverse_real(corr_real, corr_imag)
    grad_skip_one = jnp.sum(grad_after * prod_wide, axis=1)
    filter_grads = filter_pull((grad_kernel_one, grad_kernel_two))
    grad_prod_back, grad_gate_back = (
        lax.all_to_all(grad_product, "seq", split_axis=1, concat_axis=0, tiled=True),
        lax.all_to_all(grad_gate_two, "seq", split_axis=1, concat_axis=0, tiled=True),
    )
    grad_prod_wide = grad_prod_back.T.astype(jnp.float32)
    grad_mixed = jnp.concatenate(
        [
            grad_prod_wide * gate_one,
            grad_prod_wide * value_part,
            grad_gate_back.T.astype(jnp.float32),
        ],
        axis=1,
    )
    grad_short_bias = jnp.sum(grad_mixed, axis=0)
    grad_short = jnp.stack(
        [
            jnp.sum(grad_mixed * extended[0:tok_count], axis=0),
            jnp.sum(grad_mixed * extended[1 : tok_count + 1], axis=0),
            jnp.sum(grad_mixed * extended[2 : tok_count + 2], axis=0),
        ]
    )
    zero_rows = jnp.zeros((2, 3 * model_width), jnp.float32)
    padded_grad = jnp.concatenate([zero_rows, grad_mixed, zero_rows], axis=0)
    grad_extended = (
        short_f[0] * padded_grad[2:]
        + short_f[1] * padded_grad[1:-1]
        + short_f[2] * padded_grad[:-2]
    )
    from_next = passed_along(grad_extended[:2], "seq", -1)
    grad_projected = grad_extended[2:].at[tok_count - 2 :].add(from_next)
    grad_proj_low = grad_projected.astype(jnp.bfloat16)
    grad_in = left_dot(normed_low, grad_proj_low)
    grad_in_bias = jnp.sum(grad_proj_low.astype(jnp.float32), axis=0)
    grad_normed = right_dot(grad_proj_low, in_weight)
    grad_tokens_norm, grad_pre_gain, grad_pre_bias = norm_backward(
        grad_normed, unit_pre, inv_pre, pre_gain_f
    )
    grad_inputs = grad_residual + grad_tokens_norm
    shared_sums = lax.psum(
        (
            grad_pre_gain,
            grad_pre_bias,
            grad_in_bias,
            grad_short,
            grad_short_bias,
            filter_grads[0],
            filter_grads[1],
            filter_grads[2],
            filter_grads[3],
            filter_grads[4],
            filter_grads[5],
            filter_grads[6],
            grad_out_bias,
            grad_post_gain,
            grad_post_bias,
            grad_up_bias,
            grad_down_bias,
        ),
        ("batch", "seq"),
    )
    skip_grads = jnp.stack([grad_skip_one, grad_skip_two])
    weight_shards = (
        lax.psum_scatter(grad_in, "seq", scatter_dimension=0, tiled=True),
        lax.psum_scatter(grad_out, "seq", scatter_dimension=0, tiled=True),
        lax.psum_scatter(grad_up, "seq", scatter_dimension=0, tiled=True),
        lax.psum_scatter(grad_down, "seq", scatter_dimension=0, tiled=True),
    )
    final_in, final_out, final_up, final_down, final_filter, final_rates, final_skips = (
        lax.psum(weight_shards[0].astype(jnp.bfloat16), "batch").astype(jnp.float32),
        lax.psum(weight_shards[1].astype(jnp.bfloat16), "batch").astype(jnp.float32),
        lax.psum(weight_shards[2].astype(jnp.bfloat16), "batch").astype(jnp.float32),
        lax.psum(weight_shards[3].astype(jnp.bfloat16), "batch").astype(jnp.float32),
        lax.psum(filter_grads[7].astype(jnp.bfloat16), "batch").astype(jnp.float32),
        lax.psum(filter_grads[8].astype(jnp.bfloat16), "batch").astype(jnp.float32),
        lax.psum(skip_grads.astype(jnp.bfloat16), "batch").astype(jnp.float32),
    )
    return (
        outputs[None],
        grad_inputs[None],
        shared_sums[0],
        shared_sums[1],
        final_in,
        shared_sums[2],
        shared_sums[3],
        shared_sums[4],
        shared_sums[5],
        shared_sums[6],
        shared_sums[7],
        shared_sums[8],
        shared_sums[9],
        shared_sums[10],
        shared_sums[11],
        final_filter,
        final_rates,
        final_skips,
        final_out,
        shared_sums[12],
        shared_sums[13],
        shared_sums[14],
        final_up,
        shared_sums[15],
        final_down,
        shared_sums[16],
    )


LANES = 128
BLOCK = 256
WAVE_BLOCK = 256
PAD = 8
CHUNK = 64
DENSE_LIMIT = 2048
ROW_AT = {
    "pre_gain": 0,
    "pre_bias": 1,
    "in_bias": 2,
    "tap_bias": 5,
    "taps": 8,
    "skips": 17,
    "post_gain": 19,
    "post_bias": 20,
    "out_bias": 21,
    "down_bias": 22,
    "up_bias": 23,
}
ROW_COUNT = 32


def call_kernel(kernel, outs, args, micros, spaces="", scratch=(), limit=60, name=None):
    places = {"v": pltpu.VMEM, "s": pltpu.SMEM, "h": pl.ANY}
    spaces = spaces or "v" * (len(args) + len(outs))
    specs = [pl.BlockSpec(memory_space=places[space]) for space in spaces]
    shapes = [jax.ShapeDtypeStruct(shape, dtype) for shape, dtype in outs]
    return pl.pallas_call(
        kernel,
        out_shape=shapes,
        in_specs=specs[: len(args)],
        out_specs=specs[len(args) :],
        scratch_shapes=[
            pltpu.SemaphoreType.DMA((entry,))
            if isinstance(entry, int)
            else pltpu.VMEM(entry[0], entry[1])
            for entry in scratch
        ],
        compiler_params=pltpu.CompilerParams(vmem_limit_bytes=limit * 1024 * 1024),
        cost_estimate=pl.CostEstimate(
            flops=1, transcendentals=0, bytes_accessed=int(3.0e6 * micros)
        ),
        name=name,
    )(*args)


def row_chunks(source, target, sems, first, count):
    size = source.shape[0] // count
    return [
        pltpu.make_async_copy(
            source.at[pl.ds(place * size, size)],
            target.at[pl.ds(place * size, size)],
            sems.at[first + place],
        )
        for place in range(count)
    ]


def dense_rows(tile):
    tokens, channels = tile.shape
    rows = tokens * channels // LANES
    spare = LANES - channels
    blocks = channels // spare
    pieces = [tile[rows:, block * spare : (block + 1) * spare] for block in range(blocks)]
    return jnp.concatenate([tile[:rows], jnp.concatenate(pieces, axis=0)], axis=1)


def loose_rows(tile, tokens, channels):
    rows = tile.shape[0]
    spare = LANES - channels
    blocks = channels // spare
    rest = tokens - rows
    pieces = [tile[block * rest : (block + 1) * rest, channels:] for block in range(blocks)]
    return jnp.concatenate([tile[:, :channels], jnp.concatenate(pieces, axis=1)], axis=0)


def lays_dense(tokens, channels):
    spare = LANES - channels
    if spare <= 0 or channels % spare or tokens * channels % LANES:
        return False
    rows, blocks = tokens * channels // LANES, channels // spare
    return rows % 8 == 0 and (tokens - rows) * blocks == rows and (tokens - rows) % 8 == 0


def split_low(value):
    high = value.astype(jnp.bfloat16)
    return high, (value - high.astype(jnp.float32)).astype(jnp.bfloat16)


def three_products(dot, left_side, right_side):
    left_high, left_rest = split_low(left_side)
    right_high, right_rest = split_low(right_side)
    return dot(left_high, right_high) + dot(left_high, right_rest) + dot(left_rest, right_high)


def fine_nn(left_side, right_side):
    return three_products(plain_dot, left_side, right_side)


def fine_nt(left_side, right_side):
    return three_products(right_dot, left_side, right_side)


def fine_tn(left_side, right_side):
    return three_products(left_dot, left_side, right_side)


def exact_nn(left_side, right_side):
    return jnp.dot(
        left_side, right_side, precision=highest_accuracy, preferred_element_type=jnp.float32
    )


def sine_pair(angle):
    turns = jnp.round(angle * (2.0 / math.pi))
    rest = angle - turns * 1.5703125
    rest = rest - turns * 4.837512969970703125e-4
    rest = rest - turns * 7.549789948768648e-8
    square = rest * rest
    sine = rest + rest * square * (
        -1.6666654611e-1 + square * (8.3321608736e-3 + square * -1.9515295891e-4)
    )
    cosine = (
        1.0
        - 0.5 * square
        + square
        * square
        * (4.166664568298827e-2 + square * (-1.388731625493765e-3 + square * 2.443315711809948e-5))
    )
    quarter = turns.astype(jnp.int32)
    odd = (quarter & 1) == 1
    sine_out = jnp.where(odd, cosine, sine)
    cosine_out = jnp.where(odd, sine, cosine)
    sine_out = jnp.where((quarter & 2) == 2, -sine_out, sine_out)
    cosine_out = jnp.where(((quarter + 1) & 2) == 2, -cosine_out, cosine_out)
    return sine_out, cosine_out


def block_rows(index, size):
    return pl.ds(pl.multiple_of(index * size, size), size)


def wave_pair(index):
    first = index * 2 * WAVE_BLOCK
    return (
        pl.ds(pl.multiple_of(first, WAVE_BLOCK), WAVE_BLOCK),
        pl.ds(pl.multiple_of(first + WAVE_BLOCK, WAVE_BLOCK), WAVE_BLOCK),
    )


def row_of(rows, name, place=0):
    at = ROW_AT[name] + place
    return rows[at : at + 1, :]


def feature_block(first, count, length, feat_count):
    bands = (feat_count - 1) // 2
    place = lax.broadcasted_iota(jnp.int32, (count, 2 * feat_count), 0) + first
    lane = lax.broadcasted_iota(jnp.int32, (count, 2 * feat_count), 1)
    later = lane >= feat_count
    place = jnp.where(later, 2 * place + 1, 2 * place)
    lane = jnp.where(later, lane - feat_count, lane)
    steps = place.astype(jnp.float32)
    band = jnp.where(lane > bands, lane - 1 - bands, lane - 1).astype(jnp.float32)
    frequency = 0.0001 + band * ((bands - 1 - 0.0001) / (bands - 1))
    sine, cosine = sine_pair(frequency * (steps * (2.0 * math.pi / length)))
    features = jnp.where(lane > bands, -sine, cosine)
    features = jnp.where(lane == 0, steps / (length - 1), features)
    column = lax.broadcasted_iota(jnp.int32, (count, 1), 0) + first
    times = [(2 * column + odd).astype(jnp.float32) / (length - 1) for odd in (0, 1)]
    return features, times


def norm_kernel(tokens, top, gain, bias, tokens_out, top_out, normed_out, held):
    low, f32 = jnp.bfloat16, jnp.float32
    count = tokens.shape[0] // 2
    for source, target in ((top, top_out), (tokens, tokens_out)):
        for place in range(held.shape[0]):
            cols = slice(place * LANES, (place + 1) * LANES)
            held[place] = source[:, cols].astype(f32)
            for odd in range(2):
                rows = held[place, pl.ds(odd, count, stride=2), :]
                target[odd * count : (odd + 1) * count, cols] = rows.astype(low)
    rows = [vector[...].astype(f32).reshape(1, vector.shape[0]) for vector in (gain, bias)]
    normed, _, _ = norm_forward(tokens_out[...].astype(f32), *rows)
    normed_out[...] = normed.astype(low)


def wave_kernel(channels, start, *refs):
    (
        pre_gain,
        pre_bias,
        in_bias,
        tap_bias,
        taps,
        skips,
        post_gain,
        post_bias,
        out_bias,
        down_bias,
        up_bias,
        pos_bias,
        inner_bias,
        third_bias,
        sine_freq,
        filter_weight,
        decay,
        in_weight_in,
        wave_out,
        turn_out,
        rows_out,
        in_out,
        local_out,
        weights_out,
        rates_out,
        vectors_out,
        tables,
        wave,
        in_weight,
        sems,
    ) = refs
    half = wave.shape[1]
    width = in_weight.shape[0]
    step = tables.shape[1]
    low, f32 = jnp.bfloat16, jnp.float32
    load = pltpu.make_async_copy(in_weight_in, in_weight, sems.at[1])
    load.start()

    unit = math.pi / (4 * half)

    def table(which, carry):
        at = lax.broadcasted_iota(jnp.int32, (step, half), 0)
        place = lax.broadcasted_iota(jnp.int32, (step, half), 1)
        left = jnp.where(which == 0, 2 * step * at, 2 * at + 1)
        turn = (left * (2 * place + 1)) & (8 * half - 1)
        sine, cosine = sine_pair(turn.astype(f32) * unit)
        tables[2 * which] = cosine
        tables[2 * which + 1] = sine
        return carry

    lax.fori_loop(0, 2, table, 0)
    per_block = WAVE_BLOCK // step

    def fill(index, carry):
        base = (index // per_block) * (2 * WAVE_BLOCK) + (index % per_block) * step
        upper = pl.ds(pl.multiple_of(base, step), step)
        lower = pl.ds(pl.multiple_of(base + WAVE_BLOCK, step), step)
        one = pl.ds(index, 1)
        cos_a, sin_a = tables[0, one, :], tables[1, one, :]
        cos_b, sin_b = tables[2], tables[3]
        wave[upper, :] = (cos_a * cos_b - sin_a * sin_b).astype(low)
        wave[lower, :] = (sin_a * cos_b + cos_a * sin_b).astype(low)
        return carry

    lax.fori_loop(0, half // step, fill, 0)
    sent = [pltpu.make_async_copy(wave, wave_out, sems.at[0])]
    for copy in sent:
        copy.start()

    def turn(index, carry):
        upper, lower = wave_pair(index)
        at = lax.broadcasted_iota(jnp.int32, (WAVE_BLOCK, LANES), 0) + index * WAVE_BLOCK
        sine, cosine = sine_pair((2 * at + 1).astype(f32) * unit)
        turn_out[upper, :] = cosine
        turn_out[lower, :] = sine
        return carry

    lax.fori_loop(0, half // WAVE_BLOCK, turn, 0)
    rows_out[...] = jnp.zeros_like(rows_out)

    def place_rows(name, vector):
        for number in range(vector.shape[0] // width):
            piece = vector[number * width : (number + 1) * width].astype(f32)
            at = ROW_AT[name] + number
            rows_out[at : at + 1, :] = piece.reshape(1, width)

    for name, vector in (
        ("pre_gain", pre_gain),
        ("pre_bias", pre_bias),
        ("in_bias", in_bias),
        ("tap_bias", tap_bias),
        ("post_gain", post_gain),
        ("post_bias", post_bias),
        ("out_bias", out_bias),
        ("down_bias", down_bias),
        ("up_bias", up_bias),
    ):
        place_rows(name, vector)
    wide_taps = taps[...].astype(f32)
    for tap in range(3):
        for group in range(3):
            at = ROW_AT["taps"] + 3 * tap + group
            rows_out[at : at + 1, :] = wide_taps[tap : tap + 1, group * width : (group + 1) * width]
    at = ROW_AT["skips"]
    rows_out[at : at + 2, :] = skips[...].astype(f32)
    for number, vector in enumerate((pos_bias, inner_bias, third_bias, sine_freq)):
        row = vector[...].astype(f32).reshape(1, vector.shape[0])
        vectors_out[number : number + 1, :] = row

    source = lax.broadcasted_iota(jnp.int32, (width, LANES), 0)
    target = lax.broadcasted_iota(jnp.int32, (width, LANES), 1)
    chosen = (source == start[0] + target) & (target < channels)
    select_wide = jnp.where(chosen, 1.0, 0.0)
    select = select_wide.astype(low)
    local_out[...] = plain_dot(rows_out[...].astype(low), select)
    padded = jnp.concatenate([decay[...], jnp.zeros((6, width), f32)], axis=0)
    rates = exact_nn(padded, select_wide)
    for order in range(2):
        cols = slice(order * LANES, (order + 1) * LANES)
        weights_out[:, cols] = plain_dot(filter_weight[order], select)
        rates_out[:, cols] = rates[order : order + 1]
    load.wait()
    for group in range(3):
        cols = slice(group * LANES, (group + 1) * LANES)
        whole = in_weight[:, group * width : (group + 1) * width]
        in_out[:, cols] = plain_dot(whole, select).astype(low)
    for copy in sent:
        copy.wait()


def doubled(weight):
    zero = jnp.zeros_like(weight)
    return jnp.concatenate(
        [jnp.concatenate([weight, zero], axis=1), jnp.concatenate([zero, weight], axis=1)], axis=0
    )


def twice(row):
    return jnp.concatenate([row, row], axis=1)


def filter_kernel(
    pos_weight,
    inner_weight,
    third_weight,
    vectors,
    weights,
    rates,
    turn,
    wave_in,
    spectrum_out,
    kernel_out,
    waves_out,
    high,
    rest,
    wave,
    sems,
):
    half = wave.shape[1]
    length = 2 * half
    low, f32 = jnp.bfloat16, jnp.float32
    loads = row_chunks(wave_in, wave, sems, 0, 1)
    for copy in loads:
        copy.start()
    feat_count = pos_weight.shape[0]
    freq = twice(vectors[3:4, :])

    def network(index, carry):
        here = block_rows(index, BLOCK)
        there = pl.ds(pl.multiple_of(index * BLOCK + half, BLOCK), BLOCK)
        layer_in, times = feature_block(index * BLOCK, BLOCK, length, feat_count)
        for layer, weight in enumerate((pos_weight, inner_weight, third_weight)):
            matrix = doubled(weight[...].astype(f32))
            inner = fine_nn(layer_in, matrix) + twice(vectors[layer : layer + 1, :])
            layer_in, cosine = sine_pair(freq * inner)
            waves_out[layer, here, :] = jnp.concatenate([layer_in, cosine], axis=1)
        both = fine_nn(layer_in, doubled(weights[...]))
        cols = 2 * LANES
        for part, rows in enumerate((here, there)):
            kernels = both[:, part * cols : (part + 1) * cols]
            kernels = kernels * jnp.exp(-rates[...] * times[part])
            kernel_out[rows, :] = kernels
            upper = kernels.astype(low)
            high[rows, :] = upper
            rest[rows, :] = (kernels - upper.astype(f32)).astype(low)
        return carry

    lax.fori_loop(0, half // BLOCK, network, 0, unroll=True)
    for copy in loads:
        copy.wait()

    def spectra(index, carry):
        matrix = wave[block_rows(index, 2 * WAVE_BLOCK), :]
        even, odd = (
            plain_dot(matrix, high[rows, :]) + plain_dot(matrix, rest[rows, :])
            for rows in (slice(0, half), slice(half, length))
        )
        upper, lower = wave_pair(index)
        for order in range(2):
            cols = slice(order * LANES, (order + 1) * LANES)
            parts = butterfly(even[:, cols], odd[:, cols], turn, upper, lower)
            for side, (real, imag) in enumerate(parts):
                spectrum_out[side, upper, cols] = real * (1.0 / length)
                spectrum_out[side, lower, cols] = imag * (1.0 / length)
        return carry

    lax.fori_loop(0, half // WAVE_BLOCK, spectra, 0, unroll=True)


def butterfly(even, odd, turn, upper, lower):
    cosine, sine = turn[upper, :], turn[lower, :]
    even_real, even_imag = even[:WAVE_BLOCK], even[WAVE_BLOCK:]
    odd_real, odd_imag = odd[:WAVE_BLOCK], odd[WAVE_BLOCK:]
    real = even_real * cosine + even_imag * sine
    imag = even_imag * cosine - even_real * sine
    return (real + odd_real, imag + odd_imag), (real - odd_real, odd_imag - imag)


def unbutterfly(first, second, turn, upper, lower):
    cosine, sine = turn[upper, :], turn[lower, :]
    real, imag = first[0] + second[0], first[1] - second[1]
    even = (real * cosine - imag * sine, imag * cosine + real * sine)
    return even, (first[0] - second[0], first[1] + second[1])


def short_mix(rows, projected, index, group):
    cols = slice(group * LANES, (group + 1) * LANES)
    here = pl.ds(pl.multiple_of(index * CHUNK, CHUNK), CHUNK + PAD)
    even, odd = projected[0, here, cols], projected[1, here, cols]
    taps = [row_of(rows, "taps", 3 * tap + group) for tap in range(3)]
    shift = row_of(rows, "tap_bias", group)
    last = slice(PAD - 1, PAD - 1 + CHUNK)
    return (
        taps[0] * even[last] + taps[1] * odd[last] + taps[2] * even[PAD:] + shift,
        taps[0] * odd[last] + taps[1] * even[PAD:] + taps[2] * odd[PAD:] + shift,
    )


def spread_rows(tile, held, target):
    count = tile.shape[0] // 2
    for place in range(held.shape[0]):
        cols = slice(place * LANES, (place + 1) * LANES)
        for odd in range(2):
            rows = tile[odd * count : (odd + 1) * count, cols]
            held[place, pl.ds(odd, count, stride=2), :] = rows
        target[:, cols] = held[place]


def inverse_block(wave, reals, imags, index):
    upper, lower = wave_pair(index)
    return plain_dot(wave[upper, :], reals[...]) + plain_dot(wave[lower, :], imags[...])


def store_inverse(reals, imags, here, at, parts):
    for place, (real, imag) in enumerate(parts):
        cols = slice((at + place) * LANES, (at + place + 1) * LANES)
        reals[here, cols] = real.astype(jnp.bfloat16)
        imags[here, cols] = imag.astype(jnp.bfloat16)


def convolve(wave, turn, signal, spectrum, cols, kept, reals, imags, finish):
    half = wave.shape[1]

    def ahead(index, carry):
        both = plain_dot(wave[block_rows(index, 2 * WAVE_BLOCK), :], signal[...])
        upper, lower = wave_pair(index)
        sides = butterfly(both[:, :LANES], both[:, LANES:], turn, upper, lower)
        outs = []
        for side, (real, imag) in enumerate(sides):
            kept[side, upper, :], kept[side, lower, :] = real, imag
            outs.append(
                times_spec(real, imag, spectrum[side, upper, cols], spectrum[side, lower, cols])
            )
        parts = unbutterfly(*outs, turn, upper, lower)
        store_inverse(reals, imags, block_rows(index, WAVE_BLOCK), 0, parts)
        return carry

    lax.fori_loop(0, half // WAVE_BLOCK, ahead, 0, unroll=True)

    def behind(index, carry):
        finish(block_rows(index, WAVE_BLOCK), inverse_block(wave, reals, imags, index))
        return carry

    lax.fori_loop(0, half // WAVE_BLOCK, behind, 0, unroll=True)


def correlate(wave, turn, signal, spectrum, cols, kept, reals, imags, finish):
    half = wave.shape[1]
    wide = 2 * LANES

    def ahead(index, carry):
        both = plain_dot(wave[block_rows(index, 2 * WAVE_BLOCK), :], signal[...])
        upper, lower = wave_pair(index)
        sides = butterfly(both[:, :LANES], both[:, LANES:], turn, upper, lower)
        here = block_rows(index, WAVE_BLOCK)
        for number, (other, columns) in enumerate(((spectrum, cols), (kept, slice(0, LANES)))):
            outs = [
                times_conj(*pair, other[side, upper, columns], other[side, lower, columns])
                for side, pair in enumerate(sides)
            ]
            parts = unbutterfly(*outs, turn, upper, lower)
            store_inverse(reals, imags, here, 2 * number, parts)
        return carry

    lax.fori_loop(0, half // WAVE_BLOCK, ahead, 0, unroll=True)

    def behind(index, carry):
        both = inverse_block(wave, reals, imags, index)
        kernel = both[:, wide:] * (0.5 / half)
        return finish(block_rows(index, WAVE_BLOCK), both[:, :wide], kernel, carry)

    zero = jnp.zeros((1, wide), jnp.float32)
    return lax.fori_loop(0, half // WAVE_BLOCK, behind, zero, unroll=True)


def front_kernel(parts, index, *refs):
    chunks = refs[:parts]
    (weight, rows, wave_in, turn_in, spectrum_in) = refs[parts : 5 + parts]
    (
        normed_out,
        projected_out,
        product_out,
        gate_out,
        after_out,
        gated_out,
        product_wave_out,
        gated_wave_out,
        mixed_out,
        mixer_out,
        held,
        reals,
        imags,
        wave,
        turn,
        spectrum,
        projected,
        product_wave,
        gated_wave,
        mixed,
        mixer,
        sems,
    ) = refs[5 + parts :]
    tok_count, width = chunks[0].shape
    half = wave.shape[1]
    channels = width // parts
    low, f32 = jnp.bfloat16, jnp.float32
    loads = [
        pltpu.make_async_copy(source, target, sems.at[place])
        for place, (source, target) in enumerate(
            [(wave_in, wave), (turn_in, turn), (spectrum_in, spectrum)]
        )
    ]
    stores = [
        pltpu.make_async_copy(source, target, sems.at[3 + place])
        for place, (source, target) in enumerate(
            [
                (held, normed_out),
                (projected, projected_out),
                (product_wave, product_wave_out),
                (gated_wave, gated_wave_out),
                (mixed, mixed_out),
            ]
        )
    ]
    for copy in loads:
        copy.start()
    count = tok_count // 2
    for part in range(parts):
        place = index[0] ^ part
        for odd in range(2):
            at = pl.ds(pl.multiple_of(odd * half + place * count, count), count)
            held[at, :] = chunks[part][odd * count : (odd + 1) * count, :]
    stores[0].start()
    in_bias = jnp.concatenate([row_of(rows, "in_bias", group) for group in range(3)], axis=1)
    projected[:, :PAD, :] = jnp.zeros((2, PAD, projected.shape[2]), f32)

    def project(odd, carry):
        projected[odd, PAD:, :] = plain_dot(held[block_rows(odd, half), :], weight[...]) + in_bias
        return carry

    lax.fori_loop(0, 2, project, 0, unroll=True)
    stores[1].start()

    def mix(step, carry):
        here = block_rows(step, CHUNK)
        value, gate_one, gate_two = (short_mix(rows, projected, step, group) for group in range(3))
        for odd in range(2):
            cols = slice(odd * LANES, (odd + 1) * LANES)
            mixed[0, here, cols] = value[odd]
            mixed[1, here, cols] = gate_one[odd]
            product_out[here, cols] = (value[odd] * gate_one[odd]).astype(low)
            gate_out[here, cols] = gate_two[odd].astype(low)
        return carry

    lax.fori_loop(0, half // CHUNK, mix, 0)
    stores[4].start()
    skips = [twice(row_of(rows, "skips", order)) for order in range(2)]

    def first(here, convolved):
        product = product_out[here, :].astype(f32)
        after = (convolved + skips[0] * product).astype(low)
        after_out[here, :] = after
        gated_out[here, :] = (after.astype(f32) * gate_out[here, :].astype(f32)).astype(low)

    def second(here, convolved):
        gated = gated_out[here, :].astype(f32)
        mixer[here, :] = (convolved + skips[1] * gated).astype(low)

    for copy in loads:
        copy.wait()
    cols = [slice(order * LANES, (order + 1) * LANES) for order in range(2)]
    convolve(wave, turn, product_out, spectrum, cols[0], product_wave, reals, imags, first)
    stores[2].start()
    convolve(wave, turn, gated_out, spectrum, cols[1], gated_wave, reals, imags, second)
    stores[3].start()
    for part in range(parts):
        at = slice(part * count, (part + 1) * count)
        tiles = [mixer[at, odd * LANES : odd * LANES + channels] for odd in range(2)]
        mixer_out[part] = dense_rows(jnp.concatenate(tiles, axis=0))
    for copy in stores:
        copy.wait()


def back_kernel(
    channels,
    grad_mixer,
    product_ref,
    gate_ref,
    after_ref,
    gated_ref,
    rows,
    turn,
    product_wave_in,
    gated_wave_in,
    spectrum_in,
    wave_in,
    projected_in,
    mixed_in,
    packed_out,
    padded_out,
    grad_kernel_out,
    sums_out,
    grad_mix,
    grad_after,
    grad_value,
    grad_gate,
    reals,
    imags,
    wave,
    spectrum,
    product_wave,
    gated_wave,
    projected,
    mixed,
    shifted,
    sems,
):
    parts = grad_mixer.shape[0]
    half = wave.shape[1]
    count = half // parts
    low, f32 = jnp.bfloat16, jnp.float32
    loads = [
        pltpu.make_async_copy(source, target, sems.at[place])
        for place, (source, target) in enumerate(
            [
                (wave_in, wave),
                (spectrum_in, spectrum),
                (gated_wave_in, gated_wave),
                (product_wave_in, product_wave),
                (projected_in, projected),
                (mixed_in, mixed),
            ]
        )
    ]
    for copy in loads:
        copy.start()
    padding = jnp.zeros((count, LANES - channels), low)
    for part in range(parts):
        tile = loose_rows(grad_mixer[part], 2 * count, channels)
        here = slice(part * count, (part + 1) * count)
        pieces = [tile[:count], padding, tile[count:], padding]
        grad_mix[here, :] = jnp.concatenate(pieces, axis=1)
    skips = [twice(row_of(rows, "skips", order)) for order in range(2)]

    def store_kernel(here, order, kernel):
        cols = slice(order * LANES, (order + 1) * LANES)
        grad_kernel_out[0, here, cols] = kernel[:, :LANES]
        grad_kernel_out[1, here, cols] = kernel[:, LANES:]

    def first(here, data, kernel, total):
        store_kernel(here, 1, kernel)
        top = grad_mix[here, :].astype(f32)
        grad_gated = (data + skips[1] * top).astype(low).astype(f32)
        grad_after[here, :] = (grad_gated * gate_ref[here, :].astype(f32)).astype(low)
        grad_gate[here, :] = (grad_gated * after_ref[here, :].astype(f32)).astype(low)
        return total + jnp.sum(top * gated_ref[here, :].astype(f32), axis=0, keepdims=True)

    def second(here, data, kernel, total):
        store_kernel(here, 0, kernel)
        top = grad_after[here, :].astype(f32)
        grad_value[here, :] = (data + skips[0] * top).astype(low)
        return total + jnp.sum(top * product_ref[here, :].astype(f32), axis=0, keepdims=True)

    cols = [slice(order * LANES, (order + 1) * LANES) for order in range(2)]
    for copy in loads[:3]:
        copy.wait()
    skip_second = correlate(
        wave, turn, grad_mix, spectrum, cols[1], gated_wave, reals, imags, first
    )
    loads[3].wait()
    skip_first = correlate(
        wave, turn, grad_after, spectrum, cols[0], product_wave, reals, imags, second
    )
    sums_out[15:16, :] = skip_first[:, :LANES] + skip_first[:, LANES:]
    sums_out[16:17, :] = skip_second[:, :LANES] + skip_second[:, LANES:]
    sums_out[17:24, :] = jnp.zeros((7, LANES), f32)
    for copy in loads[4:]:
        copy.wait()
    shifted[:, :, half:, :] = jnp.zeros((3, 2, PAD, LANES), f32)
    sides = [slice(odd * LANES, (odd + 1) * LANES) for odd in range(2)]

    def folded(value):
        return jnp.sum(value.reshape(CHUNK // 8, 8, LANES), axis=0)

    def taps_back(step, totals):
        here = block_rows(step, CHUNK)
        window = pl.ds(pl.multiple_of(step * CHUNK, CHUNK), CHUNK + PAD)
        last = slice(PAD - 1, PAD - 1 + CHUNK)
        totals = list(totals)
        for group in range(3):
            cols = slice(group * LANES, (group + 1) * LANES)
            if group == 2:
                even, odd = (grad_gate[here, side].astype(f32) for side in sides)
            else:
                even, odd = (
                    grad_value[here, side].astype(f32) * mixed[1 - group, here, side]
                    for side in sides
                )
            shifted[group, 0, here, :], shifted[group, 1, here, :] = even, odd
            even_rows, odd_rows = projected[0, window, cols], projected[1, window, cols]
            terms = (
                even * even_rows[last] + odd * odd_rows[last],
                even * odd_rows[last] + odd * even_rows[PAD:],
                even * even_rows[PAD:] + odd * odd_rows[PAD:],
                even + odd,
            )
            for number, term in enumerate(terms):
                totals[3 * number + group] = totals[3 * number + group] + folded(term)
        return tuple(totals)

    zero = jnp.zeros((8, LANES), f32)
    totals = lax.fori_loop(0, half // CHUNK, taps_back, (zero,) * 12)

    def project_back(step, totals):
        window = pl.ds(pl.multiple_of(step * CHUNK, CHUNK), CHUNK + PAD)
        following = slice(1, 1 + CHUNK)
        totals = list(totals)
        for group in range(3):
            cols = slice(group * LANES, (group + 1) * LANES)
            even, odd = shifted[group, 0, window, :], shifted[group, 1, window, :]
            taps = [row_of(rows, "taps", 3 * tap + group) for tap in range(3)]
            now = slice(0, CHUNK)
            grads = (
                taps[0] * even[following] + taps[1] * odd[now] + taps[2] * even[now],
                taps[0] * odd[following] + taps[1] * even[following] + taps[2] * odd[now],
            )
            grads = [grad.astype(low) for grad in grads]
            for place, grad in enumerate(grads):
                at = pl.ds(pl.multiple_of(place * half + step * CHUNK, CHUNK), CHUNK)
                padded_out[at, cols] = grad
            wide = grads[0].astype(f32) + grads[1].astype(f32)
            totals[group] = totals[group] + folded(wide)
        return tuple(totals)

    totals = totals + lax.fori_loop(0, half // CHUNK, project_back, (zero,) * 3)
    for number, value in enumerate(totals):
        sums_out[number : number + 1, :] = jnp.sum(value, axis=0, keepdims=True)
    dense = packed_out.shape[1] // 3

    def pack(part, carry):
        for group in range(3):
            cols = slice(group * LANES, group * LANES + channels)
            tiles = [
                padded_out[
                    pl.ds(pl.multiple_of(odd * half + part * count, count), count), cols
                ]
                for odd in range(2)
            ]
            packed = dense_rows(jnp.concatenate(tiles, axis=0))
            packed_out[part, group * dense : (group + 1) * dense, :] = packed
        return carry

    lax.fori_loop(0, parts, pack, 0)


def store_rows(target, at, value):
    per = target.shape[1]
    place = 0
    while place < value.shape[0]:
        quarter, inside = divmod(at + place, per)
        count = min(value.shape[0] - place, per - inside)
        target[quarter, inside : inside + count, :] = value[place : place + count]
        place += count


def lane_rows(vector):
    count = vector.shape[1] // LANES
    return jnp.concatenate(
        [vector[:, place * LANES : (place + 1) * LANES] for place in range(count)], axis=0
    )


def middle_kernel(
    parts,
    batch_index,
    received,
    tokens,
    top,
    rows,
    out_in,
    up_in,
    down_in,
    outputs_out,
    residual_out,
    send_out,
    sums_out,
    *refs,
):
    batch = len(refs) - 14
    sides, parts_out = refs[0], refs[1 : 1 + batch]
    (
        out_w,
        up_w,
        down_w,
        residual,
        total,
        flow,
        act,
        upper_grad,
        act_parts,
        branch_parts,
        up_rows,
        held,
        sems,
    ) = refs[1 + batch :]
    tok_count, width = tokens.shape
    channels = width // parts
    f32, low = jnp.float32, jnp.bfloat16
    quarters = up_w.shape[0]
    quarter = up_w.shape[2]
    load_out = pltpu.make_async_copy(out_in, out_w, sems.at[0])
    load_out.start()

    def loads(place):
        cols = pl.ds(pl.multiple_of(place * quarter, quarter), quarter)
        return (
            pltpu.make_async_copy(up_in.at[:, cols], up_w.at[place], sems.at[1 + place]),
            pltpu.make_async_copy(
                down_in.at[cols, :], down_w.at[place], sems.at[1 + quarters + place]
            ),
        )

    for place in range(quarters):
        for copy in loads(place):
            copy.start()
    tiles = [
        loose_rows(received[part], tok_count, channels) for part in range(parts)
    ]
    mixer = jnp.concatenate(tiles, axis=1)
    load_out.wait()
    branch = plain_dot(mixer, out_w[...]) + row_of(rows, "out_bias")
    residual[...] = tokens[...].astype(f32) + branch
    gain = row_of(rows, "post_gain")
    bias = row_of(rows, "post_bias")
    normed, _, _ = norm_forward(residual[...], gain, bias)
    sides[:, :width] = normed.astype(low)
    sides[:, width:] = mixer
    for place in range(quarters):
        up_rows[place] = row_of(rows, "up_bias", place)
    total[...] = jnp.zeros_like(total)
    flow[...] = jnp.zeros_like(flow)

    def body(place, carry):
        for copy in loads(place):
            copy.wait()
        upper = plain_dot(sides[:, :width], up_w[place]) + up_rows[place]
        gauss = 0.5 * (1.0 + lax.erf(upper * 0.7071067811865476))
        active = (upper * gauss).astype(low)
        act[place] = active
        total[...] += plain_dot(active, down_w[place])
        grad_act = right_dot(top[...], down_w[place])
        slope = gauss + upper * jnp.exp(-0.5 * upper * upper) * 0.3989422804014327
        grad_upper = (grad_act * slope).astype(low)
        upper_grad[place] = grad_upper
        flow[...] += right_dot(grad_upper, up_w[place])
        return carry

    lax.fori_loop(0, quarters, body, 0, unroll=2)
    spread_rows(residual[...] + total[...] + row_of(rows, "down_bias"), held, outputs_out)
    _, unit, inv_std = norm_forward(residual[...], gain, bias)
    grad_norm, grad_gain, grad_bias = norm_backward(flow[...], unit, inv_std, gain)
    grad_residual = top[...].astype(f32) + grad_norm
    residual_out[...] = grad_residual
    grad_branch = grad_residual.astype(low)
    grad_mixer = right_dot(grad_branch, out_w[...]).astype(low)
    for part in range(parts):
        tile = grad_mixer[:, part * channels : (part + 1) * channels]
        send_out[part] = dense_rows(tile)
    wide_branch = grad_branch.astype(f32)
    vectors = [
        jnp.sum(wide_branch, axis=0, keepdims=True),
        grad_gain[None],
        grad_bias[None],
        jnp.sum(top[...].astype(f32), axis=0, keepdims=True),
    ]
    vectors += [
        jnp.sum(upper_grad[place].astype(f32), axis=0, keepdims=True) for place in range(quarters)
    ]
    per = width // LANES
    for number, vector in enumerate(vectors):
        sums_out[number * per : (number + 1) * per, :] = lane_rows(vector)
    piece = width // batch
    for place in range(batch):
        part = wide_branch[:, place * piece : (place + 1) * piece]
        spare = branch_parts.shape[2] - piece
        part = jnp.concatenate([part, jnp.zeros((tok_count, spare), f32)], axis=1)
        branch_parts[place] = part.astype(low)
    step = quarters * quarter // (parts * batch)
    per_part = quarters * quarter // parts
    for place in range(batch):
        tiles = []
        for part in range(parts):
            at = part * per_part + place * step
            inside = at % quarter
            tiles.append(act[at // quarter, :, inside : inside + step])
        act_parts[place] = jnp.concatenate(tiles, axis=1)
    for bits in range(batch):
        place = batch_index[0] ^ bits
        parts_out[bits][:, :quarter] = upper_grad[place]
        parts_out[bits][:, quarter : 2 * quarter] = act_parts[place]
        parts_out[bits][:, 2 * quarter :] = branch_parts[place]


def store_halves(part, bit, bits, keep_out, send_out):
    count = keep_out.shape[0]
    size = keep_out.shape[1]
    for entry in range(count):
        lower, upper = entry % bits, entry // bits
        base = upper * 2 * bits + lower
        mine = pl.ds(pl.multiple_of((base + bit * bits) * size, size), size)
        other = pl.ds(pl.multiple_of((base + (1 - bit) * bits) * size, size), size)
        keep_out[entry] = part[mine, :]
        send_out[entry] = part[other, :].astype(jnp.bfloat16)


def flip(tile):
    return tile.T


def weight_kernel(batch, orders, index, *refs):
    sides, tops, gots = (refs[batch * place : batch * (place + 1)] for place in range(3))
    up_keep, up_send, rest_keep, rest_send, flipped, columns, part, rest = refs[3 * batch :]
    tok_count, width = tops[0].shape
    for entry in range(batch):
        here = slice(entry * tok_count, (entry + 1) * tok_count)
        columns[here, :width] = gots[entry][:, :width]
        columns[here, width : 2 * width] = tops[entry][...]
        columns[here, 2 * width :] = gots[entry][:, 2 * width :]
        flipped[:width, here] = flip(sides[entry][:, :width])
        flipped[width : 2 * width, here] = flip(gots[entry][:, width : 2 * width])
        flipped[2 * width :, here] = flip(sides[entry][:, width:])
    part[...] = plain_dot(flipped[:width, :], columns[:, :width])
    store_halves(part, index[0], orders[0], up_keep, up_send)
    rest[:, :width] = plain_dot(flipped[width : 2 * width, :], columns[:, width : 2 * width])
    last = plain_dot(flipped[2 * width :, :], columns[:, 2 * width :])
    rest[:, width:] = last[:, : rest.shape[1] - width]
    store_halves(rest, index[1], orders[1], rest_keep, rest_send)


def fold_kernel(bits, bit, keep, got, keep_out, send_out):
    for entry in range(keep_out.shape[0]):
        lower, upper = entry % bits, entry // bits
        base = upper * 2 * bits + lower
        mine, other = base + bit[0] * bits, base + (1 - bit[0]) * bits
        keep_out[entry] = keep[mine] + got[mine].astype(jnp.float32)
        send_out[entry] = (keep[other] + got[other].astype(jnp.float32)).astype(jnp.bfloat16)


def collect_kernel(batch, batch_index, *refs):
    entries = refs[:batch]
    down_out, up_out, out_out, held = refs[batch:]
    rows, total = entries[0].shape
    width = down_out.shape[1]
    piece = width // batch
    f32 = jnp.float32
    for entry in range(batch):
        held[batch_index[0] ^ entry] = entries[entry][...]
    for place in range(batch):
        up_out[:, place * width : (place + 1) * width] = held[place, :, :width].astype(f32)
        down = held[place, :, width : 2 * width].astype(f32)
        down_out[place * rows : (place + 1) * rows, :] = down
    tiles = [held[place, :, 2 * width : 2 * width + piece].astype(f32) for place in range(batch)]
    out_out[...] = jnp.concatenate(tiles, axis=1)


def final_kernel(received, tokens, residual, rows, weight_in, out, weight, joined, held, sems):
    parts = received.shape[0]
    tok_count, width = tokens.shape
    channels = width // parts
    f32, low = jnp.float32, jnp.bfloat16
    load = pltpu.make_async_copy(weight_in, weight, sems.at[0])
    load.start()
    dense = received.shape[1] // 3
    for group in range(3):
        tiles = [
            loose_rows(
                received[part, group * dense : (group + 1) * dense, :],
                tok_count,
                channels,
            )
            for part in range(parts)
        ]
        joined[:, group * width : (group + 1) * width] = jnp.concatenate(tiles, axis=1)
    gain = row_of(rows, "pre_gain")
    bias = row_of(rows, "pre_bias")
    _, unit, inv_std = norm_forward(tokens[...].astype(f32), gain, bias)
    load.wait()
    grad_normed = jnp.zeros((tok_count, width), f32)
    for group in range(3):
        cols = slice(group * width, (group + 1) * width)
        grad_normed = grad_normed + right_dot(joined[:, cols], weight[:, cols])
    grad_tokens, _, _ = norm_backward(grad_normed, unit, inv_std, gain)
    spread_rows(residual[...] + grad_tokens, held, out)


SHARED_ROWS = 48
LAID_ROWS = 8
OWN_ROWS = 40


def chain_kernel(
    norm_rows,
    in_local,
    sums,
    middle_sums,
    pos_weight,
    inner_weight,
    third_weight,
    vectors,
    weights,
    rates,
    grad_kernels_in,
    kernels_in,
    waves_in,
    pair_in,
    small_out,
    weight_total,
    rate_total,
    shared,
    pairs,
    grad_kernels,
    kernels,
    waves,
    pair_sums,
    sems,
):
    length = kernels.shape[0]
    blocks = length // BLOCK

    def loads(index):
        here = block_rows(index, BLOCK)
        later = pl.ds(pl.multiple_of(index * BLOCK + length // 2, BLOCK), BLOCK)
        pieces = [
            (source.at[rows], target.at[rows])
            for source, target in ((grad_kernels_in, grad_kernels), (kernels_in, kernels))
            for rows in (here, later)
        ]
        pieces.append((waves_in.at[:, here], waves.at[:, here]))
        return [
            pltpu.make_async_copy(source, target, sems.at[number * (blocks // 2) + index])
            for number, (source, target) in enumerate(pieces)
        ]

    for block in range(blocks // 2):
        for copy in loads(block):
            copy.start()
    width = in_local.shape[0]
    pair_load = pltpu.make_async_copy(pair_in, pair_sums, sems.at[5 * (blocks // 2)])
    pair_load.start()
    feat_count, fhid = pos_weight.shape
    f32 = jnp.float32
    freq = vectors[3:4, :]
    weight_total[...] = jnp.zeros_like(weight_total)
    rate_total[...] = jnp.zeros_like(rate_total)
    pairs[...] = jnp.zeros_like(pairs)

    half = length // 2
    cols = 2 * LANES
    weight_pair = doubled(weights[...])
    freq_pair = twice(freq)

    def body(index, carry):
        here = block_rows(index, BLOCK)
        there = pl.ds(pl.multiple_of(index * BLOCK + half, BLOCK), BLOCK)
        for copy in loads(index):
            copy.wait()
        features, times = feature_block(index * BLOCK, BLOCK, length, feat_count)
        windowed = []
        for rows, time in zip((here, there), times):
            grads = grad_kernels[rows, :]
            decayed = jnp.sum(grads * kernels[rows, :] * time, axis=0, keepdims=True)
            rate_total[...] = rate_total[...] - decayed
            windowed.append(grads * jnp.exp(-rates[...] * time))
        windowed = jnp.concatenate(windowed, axis=1)
        weight_total[...] = weight_total[...] + fine_tn(waves[2, here, :LANES], windowed)
        flow = fine_nt(windowed, weight_pair)
        for layer in (2, 1, 0):
            slope = flow * waves[layer, here, LANES:]
            below = waves[layer - 1, here, :LANES] if layer else features
            count = below.shape[1]
            pairs[layer, :count, :] = pairs[layer, :count, :] + fine_tn(below, slope)
            row = slice(LANES, LANES + 1)
            pairs[layer, row, :] = pairs[layer, row, :] + jnp.sum(slope, axis=0, keepdims=True)
            if layer:
                weight = inner_weight if layer == 1 else third_weight
                flow = fine_nt(slope * freq_pair, doubled(weight[...].astype(f32)))
        return carry

    lax.fori_loop(0, blocks // 2, body, 0, unroll=True)
    grad_freq = jnp.zeros_like(freq)
    at, bias_at = 0, 2 * fhid + feat_count
    for layer, weight in ((2, third_weight), (1, inner_weight), (0, pos_weight)):
        count = weight.shape[0]
        matrix = pairs[layer, :count, :fhid] + pairs[layer, count : 2 * count, fhid:]
        both = pairs[layer, LANES : LANES + 1, :]
        vector = both[:, :fhid] + both[:, fhid:]
        grad_freq = grad_freq + jnp.sum(weight[...].astype(f32) * matrix, axis=0, keepdims=True)
        grad_freq = grad_freq + vectors[layer : layer + 1, :] * vector
        shared[at : at + count, :] = matrix * freq
        shared[bias_at + layer : bias_at + layer + 1, :] = vector * freq
        at += count
    shared[bias_at + 3 : bias_at + 4, :] = grad_freq
    pair_load.wait()
    small_out[...] = jnp.zeros_like(small_out)
    ones = jnp.ones((16, in_local.shape[1]), jnp.bfloat16)
    high, rest = split_low(in_local[...].astype(f32) * pair_sums[...])
    gain = (right_dot(ones, high) + right_dot(ones, rest))[0:1]
    column_sums = jnp.concatenate([sums[12 + group : 13 + group, :] for group in range(3)], axis=1)
    high, rest = split_low(jnp.broadcast_to(column_sums, ones.shape))
    bias = (right_dot(high, in_local[...]) + right_dot(rest, in_local[...]))[0:1]
    everywhere = small_out.at[:, :SHARED_ROWS, :]
    per = width // LANES
    gain = (gain - row_of(norm_rows, "pre_bias") * bias) / row_of(norm_rows, "pre_gain")
    store_rows(everywhere, 0, lane_rows(gain))
    store_rows(everywhere, per, lane_rows(bias))
    at = 2 * per
    store_rows(everywhere, at, middle_sums[...])
    at += middle_sums.shape[0]
    store_rows(everywhere, at, jnp.concatenate([shared[:fhid, :], shared[fhid : 2 * fhid, :]], axis=1))
    at += fhid
    tail = shared[2 * fhid : 2 * fhid + feat_count + 4, :]
    store_rows(everywhere, at, jnp.concatenate([tail, jnp.zeros_like(tail)], axis=1))
    store_rows(small_out.at[:, SHARED_ROWS : SHARED_ROWS + LAID_ROWS, :], 0, sums[:15, :])
    own = small_out.at[:, SHARED_ROWS + LAID_ROWS :, :]
    for order in range(2):
        first = slice(order * LANES, (order + 1) * LANES)
        second = slice(cols + order * LANES, cols + (order + 1) * LANES)
        both = weight_total[:fhid, first] + weight_total[fhid:, second]
        store_rows(own, order * fhid, both)
        store_rows(own, 2 * fhid + order, rate_total[:, first])
    store_rows(own, 2 * fhid + 2, sums[15:17, :])


def spread_kernel(in_keep, in_got, small_keep, small_got, send_out, small_out):
    low, f32 = jnp.bfloat16, jnp.float32
    parts = send_out.shape[0]
    small = small_keep[...] + small_got[...]
    small_out[...] = small
    both = SHARED_ROWS + LAID_ROWS
    high, rest = split_low(small[:both])
    count = in_keep.shape[0] // parts
    for part in range(parts):
        here = slice(part * count, (part + 1) * count)
        send_out[part, :count, :] = (in_keep[here, :] + in_got[here, :].astype(f32)).astype(low)
        send_out[part, count : count + both, :] = high
        send_out[part, count + both :, :] = rest


def merge_kernel(received, small, out):
    f32 = jnp.float32
    parts = received.shape[0]
    both = SHARED_ROWS + LAID_ROWS
    count = received.shape[1] - 2 * both
    total = jnp.zeros((SHARED_ROWS, LANES), f32)
    done = parts * count
    rows = SHARED_ROWS + parts * LAID_ROWS + OWN_ROWS
    for part in range(parts):
        out[part * count : (part + 1) * count, :] = received[part, :count, :]
        high = received[part, count : count + both, :].astype(f32)
        rest = received[part, count + both :, :].astype(f32)
        total = total + high[:SHARED_ROWS] + rest[:SHARED_ROWS]
        at = done + SHARED_ROWS + part * LAID_ROWS
        laid = received[part, count : count + both, :].astype(f32)[SHARED_ROWS:]
        out[at : at + LAID_ROWS, :] = laid.astype(jnp.bfloat16)
        laid = received[part, count + both :, :].astype(f32)[SHARED_ROWS:]
        out[at + rows : at + rows + LAID_ROWS, :] = laid.astype(jnp.bfloat16)
    for at, value in ((0, total), (rows - OWN_ROWS, small[SHARED_ROWS + LAID_ROWS :, :])):
        high, rest = split_low(value)
        count = value.shape[0]
        out[done + at : done + at + count, :] = high
        out[done + rows + at : done + rows + at + count, :] = rest


def take_rows(source, at, count):
    per = source.shape[1]
    pieces = []
    while count:
        quarter, inside = divmod(at, per)
        size = min(count, per - inside)
        pieces.append(source[quarter, inside : inside + size, :])
        at += size
        count -= size
    return pieces[0] if len(pieces) == 1 else jnp.concatenate(pieces, axis=0)


def lane_row(block):
    return jnp.concatenate([block[place : place + 1] for place in range(block.shape[0])], axis=1)


def last_fold_kernel(up_keep, up_got, rest_keep, rest_got, out):
    f32, low = jnp.float32, jnp.bfloat16
    width = up_keep.shape[2]
    wide = width + rest_keep.shape[2]
    out[:, :width] = (up_keep[0] + up_got[0].astype(f32)).astype(low)
    out[:, width:wide] = (rest_keep[0] + rest_got[0].astype(f32)).astype(low)
    out[:, wide:] = jnp.zeros((out.shape[0], out.shape[1] - wide), low)


def finish_kernel(batch, channels, batch_index, *refs):
    entries = refs[:batch]
    (
        in_out,
        pre_gain_out,
        pre_bias_out,
        out_bias_out,
        post_gain_out,
        post_bias_out,
        down_bias_out,
        up_bias_out,
        third_out,
        inner_out,
        pos_out,
        pos_bias_out,
        inner_bias_out,
        third_bias_out,
        freq_out,
        taps_out,
        tap_bias_out,
        in_bias_out,
        filter_out,
        rates_out,
        skips_out,
        held,
        small,
    ) = refs[batch:]
    f32 = jnp.float32
    for bits in range(batch):
        held[batch_index[0] ^ bits] = entries[bits][...]
    in_rows = in_out.shape[0] // batch
    width = pre_gain_out.shape[0]
    parts = width // channels
    total = parts * 3 * in_rows
    rows = small.shape[1]
    for place in range(batch):
        small[place] = held[place, total : total + rows, :].astype(f32) + held[
            place, total + rows :, :
        ].astype(f32)

    def gather(place, carry):
        block = held[place, :total, :].astype(f32)
        tiles = []
        for group in range(3):
            for part in range(parts):
                at = (part * 3 + group) * in_rows
                tiles.append(block[at : at + in_rows, :channels])
        in_out[pl.ds(pl.multiple_of(place * in_rows, in_rows), in_rows), :] = jnp.concatenate(
            tiles, axis=1
        )
        return carry

    lax.fori_loop(0, batch, gather, 0)
    everywhere = small.at[:, :SHARED_ROWS, :]
    per = width // LANES
    at = 0
    for target in (
        pre_gain_out,
        pre_bias_out,
        out_bias_out,
        post_gain_out,
        post_bias_out,
        down_bias_out,
        up_bias_out,
    ):
        count = target.shape[0] // LANES
        target[...] = lane_row(take_rows(everywhere, at, count)).reshape(target.shape)
        at += count
    fhid = third_out.shape[0]
    pair = take_rows(everywhere, at, fhid)
    third_out[...] = pair[:, :fhid]
    inner_out[...] = pair[:, fhid : 2 * fhid]
    at += fhid
    tail = take_rows(everywhere, at, pos_out.shape[0] + 4)
    pos_out[...] = tail[: pos_out.shape[0], :fhid]
    for place, target in enumerate((pos_bias_out, inner_bias_out, third_bias_out, freq_out)):
        row = pos_out.shape[0] + place
        target[...] = tail[row : row + 1, :fhid].reshape(target.shape)

    def laid(number):
        place, row = divmod(number, LAID_ROWS)
        return [
            small[place, SHARED_ROWS + part * LAID_ROWS + row :][:1, :channels]
            for part in range(parts)
        ]

    for number in range(5):
        tiles = [tile for group in range(3) for tile in laid(3 * number + group)]
        row = jnp.concatenate(tiles, axis=1)
        if number < 3:
            taps_out[number : number + 1, :] = row
        elif number == 3:
            tap_bias_out[...] = row.reshape(tap_bias_out.shape)
        else:
            in_bias_out[...] = row.reshape(in_bias_out.shape)
    own = small.at[:, SHARED_ROWS + parts * LAID_ROWS :, :]
    for order in range(2):
        filter_out[order] = take_rows(own, order * fhid, fhid)[:, :channels]
    rates_out[...] = take_rows(own, 2 * fhid, 2)[:, :channels]
    skips_out[...] = take_rows(own, 2 * fhid + 2, 2)[:, :channels]


def swapped(value, axis, bits):
    count = lax.axis_size(axis)
    return lax.ppermute(value, axis, [(source, source ^ bits) for source in range(count)])


def over_batch(value):
    held = {0: value}
    bits = lax.axis_size("batch") // 2
    while bits:
        held.update({place ^ bits: swapped(member, "batch", bits) for place, member in held.items()})
        bits //= 2
    return [held[place] for place in range(len(held))]


def natural(entries, index):
    stacked = jnp.stack(entries)
    return [
        lax.dynamic_index_in_dim(stacked, index ^ place, 0, keepdims=False)
        for place in range(len(entries))
    ]


def halves(total, index, bits, left):
    shape = total.shape[1:]
    place = left.index(bits)
    before = 1 << (len(left) - 1 - place)
    after = 1 << place
    view = total.reshape((before, 2, after) + shape)
    bit = (index // bits) % 2
    keep = lax.dynamic_index_in_dim(view, bit, 1, keepdims=False)
    send = lax.dynamic_index_in_dim(view, 1 - bit, 1, keepdims=False)
    return keep.reshape((before * after,) + shape), send.reshape((before * after,) + shape)


def halved(total, axis, index, order):
    count = lax.axis_size(axis)
    left = [1 << k for k in range(count.bit_length() - 1)]
    for bits in order:
        keep, send = halves(total, index, bits, left)
        got = swapped(send.astype(jnp.bfloat16), axis, bits)
        total = keep + got.astype(jnp.float32)
        left.remove(bits)
    return total[0]


def dense_device(
    inputs,
    pre_gain,
    pre_bias,
    in_weight,
    input_projection_bias,
    short_weight,
    short_bias,
    pos_weight,
    pos_bias,
    inner_weight,
    inner_bias,
    filter_third_weight,
    third_bias,
    sine_freq,
    filter_weight,
    decay_rates,
    skip_gains,
    out_weight,
    out_bias,
    post_gain,
    post_bias,
    up_weight,
    up_bias,
    down_weight,
    down_bias,
    cotangent,
):
    seq_parts = lax.axis_size("seq")
    batch_parts = lax.axis_size("batch")
    seq_rank = lax.axis_index("seq")
    batch_rank = lax.axis_index("batch")
    tokens = inputs[0]
    tok_count, width = tokens.shape
    length = tok_count * seq_parts
    channels = width // seq_parts
    hidden_units = up_weight.shape[1]
    fhid = pos_weight.shape[1]
    f32, low = jnp.float32, jnp.bfloat16
    wide = 3 * LANES
    start = seq_rank * channels
    bit_list = [1 << k for k in range(seq_parts.bit_length() - 1)]
    swap_list = [bit_list[1], bit_list[0]] + bit_list[2:]
    batch_bits = [1 << k for k in range(batch_parts.bit_length() - 1)]

    tokens, grad_top, own_normed = call_kernel(
        norm_kernel,
        [((tok_count, width), low)] * 3,
        [tokens, cotangent[0], pre_gain, pre_bias],
        micros=1,
        scratch=[((width // LANES, tok_count, LANES), f32)],
        name="norm",
    )
    chunks = {0: own_normed}
    for bits in range(2, seq_parts, 2):
        chunks[bits] = swapped(own_normed, "seq", bits)

    quarters = hidden_units // width
    half = length // 2
    seq_scalar = seq_rank.astype(jnp.int32)[None]
    batch_scalar = batch_rank.astype(jnp.int32)[None]
    start_scalar = start.astype(jnp.int32)[None]
    wave, turn, rows, in_local, rows_local, weights_local, rates_local, vectors = call_kernel(
        lambda *refs: wave_kernel(channels, *refs),
        [
            ((length, half), low),
            ((length, LANES), f32),
            ((ROW_COUNT, width), f32),
            ((width, wide), low),
            ((ROW_COUNT, LANES), f32),
            ((fhid, 2 * LANES), f32),
            ((1, 2 * LANES), f32),
            ((4, fhid), f32),
        ],
        [
            start_scalar,
            pre_gain,
            pre_bias,
            input_projection_bias,
            short_bias,
            short_weight,
            skip_gains,
            post_gain,
            post_bias,
            out_bias,
            down_bias,
            up_bias,
            pos_bias,
            inner_bias,
            third_bias,
            sine_freq,
            filter_weight,
            decay_rates,
            in_weight,
        ],
        micros=8.5,
        spaces="s" + "v" * 17 + "h" + "h" + "v" * 7,
        scratch=[
            ((4, 32, half), f32),
            ((length, half), low),
            ((width, 3 * width), low),
            2,
        ],
        name="waves",
    )
    even = [chunks[bits] for bits in range(2, seq_parts, 2)]
    wave, *even = lax.optimization_barrier((wave, *even))
    for bits in range(0, seq_parts, 2):
        if bits:
            chunks[bits] = even[bits // 2 - 1]
        chunks[bits + 1] = swapped(chunks[bits], "seq", 1)
    spectrum, kernels, filter_waves = call_kernel(
        filter_kernel,
        [
            ((2, length, 2 * LANES), f32),
            ((length, 2 * LANES), f32),
            ((3, half, 4 * fhid), f32),
        ],
        [
            pos_weight,
            inner_weight,
            filter_third_weight,
            vectors,
            weights_local,
            rates_local,
            turn,
            wave,
        ],
        micros=13,
        spaces="v" * 7 + "h" + "vvv",
        scratch=[
            ((length, 2 * LANES), low),
            ((length, 2 * LANES), low),
            ((length, half), low),
            1,
        ],
        name="filters",
    )
    dense = tok_count * channels // LANES
    (
        normed,
        projected,
        product,
        gate,
        after,
        gated,
        product_wave,
        gated_wave,
        mixed,
        mixer_chan,
    ) = call_kernel(
        lambda *refs: front_kernel(seq_parts, *refs),
        [
            ((length, width), low),
            ((2, PAD + half, wide), f32),
            ((half, 2 * LANES), low),
            ((half, 2 * LANES), low),
            ((half, 2 * LANES), low),
            ((half, 2 * LANES), low),
            ((2, length, LANES), f32),
            ((2, length, LANES), f32),
            ((2, half, 2 * LANES), f32),
            ((seq_parts, dense, LANES), low),
        ],
        [seq_scalar]
        + [chunks[part] for part in range(seq_parts)]
        + [in_local, rows_local, wave, turn, spectrum],
        micros=13,
        spaces="s" + "v" * seq_parts + "vvhhh" + "hhvvvvhhhv",
        scratch=[
            ((length, width), low),
            ((half, 2 * LANES), low),
            ((half, 2 * LANES), low),
            ((length, half), low),
            ((length, LANES), f32),
            ((2, length, 2 * LANES), f32),
            ((2, PAD + half, wide), f32),
            ((2, length, LANES), f32),
            ((2, length, LANES), f32),
            ((2, half, 2 * LANES), f32),
            ((half, 2 * LANES), low),
            8,
        ],
        name="front",
    )
    tops = over_batch(grad_top)
    mixer_back = lax.all_to_all(mixer_chan, "seq", 0, 0, tiled=True)
    mixer_back, *tops = lax.optimization_barrier((mixer_back, *tops))

    quarter = hidden_units // batch_parts
    branch_quarter = width // batch_parts
    rows_quarter = hidden_units // (seq_parts * batch_parts)
    assert quarter == width and seq_parts * rows_quarter == width
    up_width = quarter + branch_quarter
    padded = quarter + -(-branch_quarter // LANES) * LANES
    message = padded + width
    outputs, grad_residual, grad_mixer, middle_sums, sides, *gots = call_kernel(
        lambda *refs: middle_kernel(seq_parts, *refs),
        [
            ((tok_count, width), f32),
            ((tok_count, width), f32),
            ((seq_parts, dense, LANES), low),
            (((4 * width + hidden_units) // LANES, LANES), f32),
        ]
        + [((tok_count, 2 * width), low)]
        + [((tok_count, message), low)] * batch_parts,
        [
            batch_scalar,
            mixer_back,
            tokens,
            grad_top,
            rows,
            out_weight,
            up_weight,
            down_weight,
        ],
        micros=11,
        spaces="svvvvhhh" + "v" * (5 + batch_parts),
        scratch=[
            ((width, width), low),
            ((quarters, width, width), low),
            ((quarters, width, width), low),
            ((tok_count, width), f32),
            ((tok_count, width), f32),
            ((tok_count, width), f32),
            ((quarters, tok_count, width), low),
            ((quarters, tok_count, width), low),
            ((batch_parts, tok_count, width), low),
            ((batch_parts, tok_count, padded - quarter), low),
            ((quarters, 1, width), f32),
            ((width // LANES, tok_count, LANES), f32),
            1 + 2 * quarters,
        ],
        name="middle",
    )
    grad_mixer_chan = lax.all_to_all(grad_mixer, "seq", 0, 0, tiled=True)

    def bit_of(bits):
        return ((seq_rank // bits) % 2).astype(jnp.int32)[None]

    def fold(keep, got, bits, left):
        size = keep.shape[0] // 2
        block = keep.shape[1:]
        place = left.index(bits)
        return call_kernel(
            lambda *refs: fold_kernel(1 << place, *refs),
            [((size,) + block, f32), ((size,) + block, low)],
            [bit_of(bits), keep, got],
            micros=1,
            spaces="svvvv",
            name="fold",
        )

    grad_mixer_chan = lax.all_to_all(grad_mixer, "seq", 0, 0, tiled=True)
    sides = over_batch(sides)
    gots = [gots[0]] + [swapped(gots[bits], "batch", bits) for bits in range(1, batch_parts)]
    rows_each = width // seq_parts

    blocks = length // BLOCK
    packed, grad_proj, grad_kernels, sums = call_kernel(
        lambda *refs: back_kernel(channels, *refs),
        [
            ((seq_parts, 3 * dense, LANES), low),
            ((length, wide), low),
            ((2, half, 2 * LANES), f32),
            ((24, LANES), f32),
        ],
        [
            grad_mixer_chan,
            product,
            gate,
            after,
            gated,
            rows_local,
            turn,
            product_wave,
            gated_wave,
            spectrum,
            wave,
            projected,
            mixed,
        ],
        micros=15,
        spaces="v" * 7 + "h" * 6 + "vvvv",
        scratch=[((half, 2 * LANES), low)] * 4
        + [
            ((half, 4 * LANES), low),
            ((half, 4 * LANES), low),
            ((length, half), low),
            ((2, length, 2 * LANES), f32),
            ((2, length, LANES), f32),
            ((2, length, LANES), f32),
            ((2, PAD + half, wide), f32),
            ((2, half, 2 * LANES), f32),
            ((3, 2, half + PAD, LANES), f32),
            6,
        ],
        name="back",
    )
    proj_back = lax.all_to_all(packed, "seq", 0, 0, tiled=True)
    orders = (bit_list, swap_list)
    halves_of = [
        ((seq_parts // 2, rows_each, columns), dtype)
        for columns in (width, width + branch_quarter)
        for dtype in (f32, low)
    ]
    up_keep, up_send, rest_keep, rest_send = call_kernel(
        lambda *refs: weight_kernel(batch_parts, (orders[0][0], orders[1][0]), *refs),
        halves_of,
        [jnp.concatenate([bit_of(order[0]) for order in orders])] + sides + tops + gots,
        micros=6,
        spaces="s" + "v" * (3 * batch_parts + 4),
        scratch=[
            ((3 * width, batch_parts * tok_count), low),
            ((batch_parts * tok_count, width + padded), low),
            ((width, width), f32),
            ((width, width + branch_quarter), f32),
        ],
        name="weights",
    )
    up_got = swapped(up_send, "seq", orders[0][0])
    rest_got = swapped(rest_send, "seq", orders[1][0])

    pair_part = left_dot(normed, grad_proj)
    in_rows = width // (seq_parts * batch_parts)
    in_count = 3 * in_rows
    in_part = (
        pair_part.reshape(seq_parts, batch_parts, in_rows, 3, LANES)
        .transpose(1, 0, 3, 2, 4)
        .reshape(batch_parts, seq_parts * in_count, LANES)
    )
    small_rows = SHARED_ROWS + LAID_ROWS + OWN_ROWS
    in_part, pair_part, up_keep, rest_keep = lax.optimization_barrier(
        (in_part, pair_part, up_keep, rest_keep)
    )
    (small,) = call_kernel(
        chain_kernel,
        [((batch_parts, small_rows, LANES), f32)],
        [
            rows,
            in_local,
            sums,
            middle_sums,
            pos_weight,
            inner_weight,
            filter_third_weight,
            vectors,
            weights_local,
            rates_local,
            grad_kernels.reshape(length, 2 * LANES),
            kernels,
            filter_waves,
            pair_part,
        ],
        micros=12,
        spaces="v" * 10 + "hhhh" + "v",
        scratch=[
            ((2 * fhid, 4 * LANES), f32),
            ((1, 2 * LANES), f32),
            ((2 * fhid + 40, fhid), f32),
            ((3, LANES + 8, 2 * fhid), f32),
            ((length, 2 * LANES), f32),
            ((length, 2 * LANES), f32),
            ((3, length // 2, 4 * fhid), f32),
            ((width, wide), f32),
            5 * (blocks // 2) + 1,
        ],
        name="chain",
    )
    small, proj_back = lax.optimization_barrier((small, proj_back))

    def next_fold(keep, got, order, step):
        left = [bits for bits in bit_list if bits not in order[:step]]
        return fold(keep, got, order[step], left)

    left = list(batch_bits)
    for bits in batch_bits[:-1]:
        in_keep, in_send = halves(in_part, batch_rank, bits, left)
        small_keep, small_send = halves(small, batch_rank, bits, left)
        in_part = in_keep + swapped(in_send.astype(low), "batch", bits).astype(f32)
        small = small_keep + swapped(small_send, "batch", bits)
        left.remove(bits)
    in_keep, in_send = halves(in_part, batch_rank, batch_bits[-1], left)
    small_keep, small_send = halves(small, batch_rank, batch_bits[-1], left)
    shared_count = in_count + 2 * (SHARED_ROWS + LAID_ROWS)
    mixed_send, small = call_kernel(
        spread_kernel,
        [((seq_parts, shared_count, LANES), low), ((small_rows, LANES), f32)],
        [
            in_keep[0],
            swapped(in_send.astype(low), "batch", batch_bits[-1])[0],
            small_keep[0],
            swapped(small_send, "batch", batch_bits[-1])[0],
        ],
        micros=2,
        name="spread",
    )
    up_keep, up_send = next_fold(up_keep, up_got, orders[0], 1)
    rest_keep, rest_send = next_fold(rest_keep, rest_got, orders[1], 1)
    up_got = swapped(up_send, "seq", orders[0][1])
    rest_got = swapped(rest_send, "seq", orders[1][1])
    mixed_send, proj_back = lax.optimization_barrier((mixed_send, proj_back))
    mixed_got = lax.all_to_all(mixed_send, "seq", 0, 0, tiled=True)
    (grad_inputs,) = call_kernel(
        final_kernel,
        [((tok_count, width), f32)],
        [proj_back, tokens, grad_residual, rows, in_weight],
        micros=5.5,
        spaces="vvvvhv",
        scratch=[
            ((width, 3 * width), low),
            ((tok_count, 3 * width), low),
            ((width // LANES, tok_count, LANES), f32),
            1,
        ],
        name="final",
    )
    done_rows = SHARED_ROWS + seq_parts * LAID_ROWS + OWN_ROWS
    (last,) = call_kernel(
        merge_kernel,
        [((seq_parts * in_count + 2 * done_rows, LANES), low)],
        [mixed_got, small],
        micros=2,
        name="merge",
    )
    up_keep, up_send = next_fold(up_keep, up_got, orders[0], 2)
    rest_keep, rest_send = next_fold(rest_keep, rest_got, orders[1], 2)
    up_got = swapped(up_send, "seq", orders[0][2])
    rest_got = swapped(rest_send, "seq", orders[1][2])
    lasts = over_batch(last)
    up_got, grad_inputs, last = lax.optimization_barrier((up_got, grad_inputs, last))
    total = -(-(2 * width + branch_quarter) // LANES) * LANES
    (weights_done,) = call_kernel(
        last_fold_kernel,
        [((rows_each, total), low)],
        [up_keep, up_got, rest_keep, rest_got],
        micros=1,
        name="last_fold",
    )
    (
        final_in,
        grad_pre_gain,
        grad_pre_bias,
        grad_out_bias,
        grad_post_gain,
        grad_post_bias,
        grad_down_bias,
        grad_up_bias,
        grad_third,
        grad_inner,
        grad_pos,
        grad_pos_bias,
        grad_inner_bias,
        grad_third_bias,
        grad_freq,
        grad_taps,
        grad_tap_bias,
        grad_in_bias,
        grad_filter,
        grad_rates,
        grad_skips,
    ) = call_kernel(
        lambda *refs: finish_kernel(batch_parts, channels, *refs),
        [
            ((batch_parts * in_rows, 3 * width), f32),
            ((width,), f32),
            ((width,), f32),
            ((width,), f32),
            ((width,), f32),
            ((width,), f32),
            ((width,), f32),
            ((hidden_units,), f32),
            (filter_third_weight.shape, f32),
            (inner_weight.shape, f32),
            (pos_weight.shape, f32),
            ((fhid,), f32),
            ((fhid,), f32),
            ((fhid,), f32),
            ((fhid,), f32),
            ((3, 3 * width), f32),
            ((3 * width,), f32),
            ((3 * width,), f32),
            ((2, fhid, channels), f32),
            ((2, channels), f32),
            ((2, channels), f32),
        ],
        [batch_scalar] + lasts,
        micros=3,
        spaces="s" + "v" * batch_parts + "v" * 21,
        scratch=[
            ((batch_parts,) + last.shape, low),
            ((batch_parts, done_rows, LANES), f32),
        ],
        name="finish",
    )
    entries = {0: weights_done, batch_parts // 2: swapped(weights_done, "batch", batch_parts // 2)}
    entries[batch_parts // 2], final_in = lax.optimization_barrier(
        (entries[batch_parts // 2], final_in)
    )
    bits = batch_parts // 4
    while bits:
        entries.update(
            {place ^ bits: swapped(member, "batch", bits) for place, member in entries.items()}
        )
        bits //= 2
    entries = [entries[place] for place in range(batch_parts)]
    final_down, final_up, final_out = call_kernel(
        lambda *refs: collect_kernel(batch_parts, *refs),
        [
            ((batch_parts * rows_each, width), f32),
            ((rows_each, hidden_units), f32),
            ((rows_each, width), f32),
        ],
        [batch_scalar] + entries,
        micros=3,
        spaces="s" + "v" * (batch_parts + 3),
        scratch=[((batch_parts, rows_each, total), low)],
        name="collect",
    )
    return (
        outputs[None],
        grad_inputs[None],
        grad_pre_gain,
        grad_pre_bias,
        final_in,
        grad_in_bias,
        grad_taps,
        grad_tap_bias,
        grad_pos,
        grad_pos_bias,
        grad_inner,
        grad_inner_bias,
        grad_third,
        grad_third_bias,
        grad_freq,
        grad_filter,
        grad_rates,
        grad_skips,
        final_out,
        grad_out_bias,
        grad_post_gain,
        grad_post_bias,
        final_up,
        grad_up_bias,
        final_down,
        grad_down_bias,
    )


def per_device(*args):
    tokens, parts = args[0].shape[1], lax.axis_size("seq")
    channels = args[0].shape[2] // parts
    dense = tokens * parts <= DENSE_LIMIT and lays_dense(tokens, channels)
    return (dense_device if dense else factored_device)(*args)


def solution(mesh):
    in_specs = (
        P("batch", "seq", None),
        P(),
        P(),
        P(),
        P(),
        P(),
        P(),
        P(),
        P(),
        P(),
        P(),
        P(),
        P(),
        P(),
        P(),
        P(),
        P(),
        P(),
        P(),
        P(),
        P(),
        P(),
        P(),
        P(),
        P(),
        P("batch", "seq", None),
    )
    out_specs = (
        P("batch", "seq", None),
        P("batch", "seq", None),
        P(),
        P(),
        P("seq", None),
        P(),
        P(),
        P(),
        P(),
        P(),
        P(),
        P(),
        P(),
        P(),
        P(),
        P(None, None, "seq"),
        P(None, "seq"),
        P(None, "seq"),
        P("seq", None),
        P(),
        P(),
        P(),
        P("seq", None),
        P(),
        P("seq", None),
        P(),
    )
    return jax.shard_map(
        per_device, mesh=mesh, in_specs=in_specs, out_specs=out_specs, check_vma=False
    )
```

```python
import math

import jax
import jax.numpy as jnp
import numpy as np
from jax import lax
from jax.experimental import pallas as pl
from jax.experimental.pallas import tpu as pltpu
from jax.sharding import PartitionSpec as P

epsilon = 1e-05
highest_accuracy = lax.Precision.HIGHEST


def passed_along(value, axis, steps):
    count = lax.axis_size(axis)
    initial, last = (max(0, -steps), min(count, count - steps))
    return lax.ppermute(value, axis, [(source, source + steps) for source in range(initial, last)])


def plain_dot(left_side, right_side):
    return jnp.dot(left_side, right_side, preferred_element_type=jnp.float32)


def exact_tdot(left_side, right_side):
    return lax.dot_general(
        left_side,
        right_side,
        (((0,), (0,)), ((), ())),
        precision=highest_accuracy,
        preferred_element_type=jnp.float32,
    )


def left_dot(left_side, right_side):
    return lax.dot_general(
        left_side, right_side, (((0,), (0,)), ((), ())), preferred_element_type=jnp.float32
    )


def right_dot(left_side, right_side):
    return lax.dot_general(
        left_side, right_side, (((1,), (1,)), ((), ())), preferred_element_type=jnp.float32
    )


def rounded(values):
    return lax.optimization_barrier(values.astype(jnp.bfloat16)).astype(jnp.float32)


def norm_forward(values, gain_vec, shift_vec):
    centre = values - jnp.mean(values, axis=-1, keepdims=True)
    inv_std = lax.rsqrt(jnp.mean(centre * centre, axis=-1, keepdims=True) + epsilon)
    unit_rows = centre * inv_std
    return (unit_rows * gain_vec + shift_vec, unit_rows, inv_std)


def norm_backward(grad_out, unit_rows, inv_std, gain_vec):
    grad_unit = grad_out * gain_vec
    grad_values = inv_std * (
        grad_unit
        - jnp.mean(grad_unit, axis=-1, keepdims=True)
        - unit_rows * jnp.mean(grad_unit * unit_rows, axis=-1, keepdims=True)
    )
    return (grad_values, jnp.sum(grad_out * unit_rows, axis=0), jnp.sum(grad_out, axis=0))


def position_rows(length, feat_count):
    steps_pos = jnp.arange(length, dtype=jnp.float32)
    time_steps = steps_pos / (length - 1)
    band_count = (feat_count - 1) // 2
    frequency = jnp.linspace(0.0001, band_count - 1, band_count, dtype=jnp.float32)
    angles = frequency[:, None] * (steps_pos * (2.0 * math.pi / length))[None, :]
    features_t = jnp.concatenate([time_steps[None, :], jnp.cos(angles), -jnp.sin(angles)], axis=0)
    return (features_t, time_steps)


def body_filters(
    features_t,
    time_steps,
    pos_weight,
    pos_bias,
    inner_weight,
    inner_bias,
    filter_third_weight,
    third_bias,
    sine_freq,
    weight_local,
    rates_local,
):
    hidden = jnp.sin(sine_freq[:, None] * (exact_tdot(pos_weight, features_t) + pos_bias[:, None]))
    hidden = jnp.sin(sine_freq[:, None] * (exact_tdot(inner_weight, hidden) + inner_bias[:, None]))
    hidden = jnp.sin(
        sine_freq[:, None] * (exact_tdot(filter_third_weight, hidden) + third_bias[:, None])
    )
    first_kernel = exact_tdot(weight_local[0], hidden) * jnp.exp(
        -rates_local[0][:, None] * time_steps[None, :]
    )
    second_kernel = exact_tdot(weight_local[1], hidden) * jnp.exp(
        -rates_local[1][:, None] * time_steps[None, :]
    )
    return (first_kernel, second_kernel)


def split_sizes(extent):
    outer_size = math.gcd(extent // 2, 1 << (extent.bit_length() - 1) // 2)
    return (outer_size, extent // outer_size)


def dft_rect(row_count, col_count, modulus, direction):
    row_ids = jnp.arange(row_count, dtype=jnp.int32)[:, None]
    col_ids = jnp.arange(col_count, dtype=jnp.int32)[None, :]
    angles = (row_ids * col_ids % modulus).astype(jnp.float32) * (2.0 * math.pi / modulus)
    return (jnp.cos(angles), direction * jnp.sin(angles))


def first_section(block_groups, lookup_grid):
    return jnp.einsum(
        "cij,ik->ckj",
        block_groups,
        lookup_grid,
        precision=highest_accuracy,
        preferred_element_type=jnp.float32,
    )


def second_section(block_groups, lookup_grid):
    return jnp.einsum(
        "dhq,qn->dnh",
        block_groups,
        lookup_grid,
        precision=highest_accuracy,
        preferred_element_type=jnp.float32,
    )


def padded_spectrum(signal):
    channels, length = signal.shape
    extent = 2 * length
    outer_size, inner_size = split_sizes(extent)
    block_groups = signal.reshape(channels, inner_size // 2, outer_size)
    cos_inner, sin_inner = dft_rect(inner_size // 2, inner_size, inner_size, -1.0)
    section_real = first_section(block_groups, cos_inner)
    section_imag = first_section(block_groups, sin_inner)
    twist_cos, rotation_sine = dft_rect(inner_size, outer_size, extent, -1.0)
    turned_real = section_real * twist_cos - section_imag * rotation_sine
    turned_imag = section_real * rotation_sine + section_imag * twist_cos
    cos_outer, sin_outer = dft_rect(outer_size, outer_size, outer_size, -1.0)
    out_real = second_section(turned_real, cos_outer) - second_section(turned_imag, sin_outer)
    out_imag = second_section(turned_real, sin_outer) + second_section(turned_imag, cos_outer)
    return (out_real.reshape(channels, extent), out_imag.reshape(channels, extent))


def inverse_real(spec_real, spec_imag):
    channels, extent = spec_real.shape
    outer_size, inner_size = split_sizes(extent)
    blocks_real = spec_real.reshape(channels, inner_size, outer_size)
    blocks_imag = spec_imag.reshape(channels, inner_size, outer_size)
    cos_inner, sin_inner = dft_rect(inner_size, inner_size, inner_size, 1.0)
    section_real = first_section(blocks_real, cos_inner) - first_section(blocks_imag, sin_inner)
    section_imag = first_section(blocks_real, sin_inner) + first_section(blocks_imag, cos_inner)
    twist_cos, rotation_sine = dft_rect(inner_size, outer_size, extent, 1.0)
    turned_real = section_real * twist_cos - section_imag * rotation_sine
    turned_imag = section_real * rotation_sine + section_imag * twist_cos
    cos_outer, sin_outer = dft_rect(outer_size, outer_size // 2, outer_size, 1.0)
    out_real = second_section(turned_real, cos_outer) - second_section(turned_imag, sin_outer)
    return out_real.reshape(channels, extent // 2) / extent


def times_spec(left_real, left_imag, right_real, right_imag):
    return (
        left_real * right_real - left_imag * right_imag,
        left_real * right_imag + left_imag * right_real,
    )


def times_conj(left_real, left_imag, right_real, right_imag):
    return (
        left_real * right_real + left_imag * right_imag,
        left_imag * right_real - left_real * right_imag,
    )


def factored_device(
    inputs,
    pre_gain,
    pre_bias,
    in_weight,
    input_projection_bias,
    short_weight,
    short_bias,
    pos_weight,
    pos_bias,
    inner_weight,
    inner_bias,
    filter_third_weight,
    third_bias,
    sine_freq,
    filter_weight,
    decay_rates,
    skip_gains,
    out_weight,
    out_bias,
    post_gain,
    post_bias,
    up_weight,
    up_bias,
    down_weight,
    down_bias,
    cotangent,
):
    seq_parts = lax.axis_size("seq")
    seq_rank = lax.axis_index("seq")
    tokens = inputs[0]
    tok_count = tokens.shape[0]
    model_width = tokens.shape[1]
    length = tok_count * seq_parts
    channels = model_width // seq_parts
    tokens_wide = tokens.astype(jnp.float32)
    pre_gain_f = pre_gain.astype(jnp.float32)
    pre_bias_f = pre_bias.astype(jnp.float32)
    in_bias_f = input_projection_bias.astype(jnp.float32)
    short_f = short_weight.astype(jnp.float32)
    short_bias_f = short_bias.astype(jnp.float32)
    out_bias_f = out_bias.astype(jnp.float32)
    post_gain_f = post_gain.astype(jnp.float32)
    post_bias_f = post_bias.astype(jnp.float32)
    up_bias_f = up_bias.astype(jnp.float32)
    down_bias_f = down_bias.astype(jnp.float32)
    normed, unit_pre, inv_pre = norm_forward(tokens_wide, pre_gain_f, pre_bias_f)
    normed_low = normed.astype(jnp.bfloat16)
    projected = plain_dot(normed_low, in_weight) + in_bias_f
    previous = passed_along(projected[tok_count - 2 :], "seq", 1)
    extended = jnp.concatenate([previous, projected], axis=0)
    mixed_conv = (
        short_f[0] * extended[:-2]
        + short_f[1] * extended[1:-1]
        + short_f[2] * extended[2:]
        + short_bias_f
    )
    value_part = mixed_conv[:, :model_width]
    gate_one = mixed_conv[:, model_width : 2 * model_width]
    gate_two = mixed_conv[:, 2 * model_width :]
    product_low = (value_part * gate_one).astype(jnp.bfloat16)
    gate_two_low = gate_two.astype(jnp.bfloat16)
    prod_chan, gate_chan = (
        lax.all_to_all(product_low.T, "seq", split_axis=0, concat_axis=1, tiled=True),
        lax.all_to_all(gate_two_low.T, "seq", split_axis=0, concat_axis=1, tiled=True),
    )
    features_t, time_steps = position_rows(length, pos_weight.shape[0])
    chan_start = seq_rank * channels
    weight_local = lax.dynamic_slice_in_dim(
        filter_weight.astype(jnp.float32), chan_start, channels, 2
    )
    rates_local = lax.dynamic_slice_in_dim(decay_rates, chan_start, channels, 1)
    skips_local = lax.dynamic_slice_in_dim(skip_gains.astype(jnp.float32), chan_start, channels, 1)
    skip_one = skips_local[0][:, None]
    skip_two = skips_local[1][:, None]
    shared = tuple(
        (
            member.astype(jnp.float32)
            for member in (
                pos_weight,
                pos_bias,
                inner_weight,
                inner_bias,
                filter_third_weight,
                third_bias,
                sine_freq,
            )
        )
    )

    def local_filters(*params):
        return body_filters(features_t, time_steps, *params)

    (kernel_one, kernel_two), filter_pull = jax.vjp(
        local_filters, *shared, weight_local, rates_local
    )
    prod_wide = prod_chan.astype(jnp.float32)
    gate_wide = gate_chan.astype(jnp.float32)
    prod_real, prod_imag = padded_spectrum(prod_wide)
    kone_real, kone_imag = padded_spectrum(kernel_one)
    convolved_real_part, conv_imag = times_spec(prod_real, prod_imag, kone_real, kone_imag)
    after_one = rounded(inverse_real(convolved_real_part, conv_imag) + skip_one * prod_wide)
    gated_low = rounded(after_one * gate_wide)
    gated_real, gated_imag = padded_spectrum(gated_low)
    ktwo_real, ktwo_imag = padded_spectrum(kernel_two)
    convolved_real_part, conv_imag = times_spec(gated_real, gated_imag, ktwo_real, ktwo_imag)
    mixer_chan = (inverse_real(convolved_real_part, conv_imag) + skip_two * gated_low).astype(
        jnp.bfloat16
    )
    mixer_tok = lax.all_to_all(mixer_chan, "seq", split_axis=1, concat_axis=0, tiled=True).T
    branch = plain_dot(mixer_tok, out_weight) + out_bias_f
    residual = tokens_wide + branch
    normed_two, unit_post, inv_post = norm_forward(residual, post_gain_f, post_bias_f)
    normed_two_low = normed_two.astype(jnp.bfloat16)
    upper_pre = plain_dot(normed_two_low, up_weight) + up_bias_f
    activated = jax.nn.gelu(upper_pre, approximate=False).astype(jnp.bfloat16)
    outputs = residual + plain_dot(activated, down_weight) + down_bias_f
    grad_top = cotangent[0]
    grad_top_wide = grad_top.astype(jnp.float32)
    grad_act = right_dot(grad_top, down_weight)
    grad_down = left_dot(activated, grad_top)
    grad_down_bias = jnp.sum(grad_top_wide, axis=0)
    gelu_slope = (
        0.5 * (1.0 + lax.erf(upper_pre * 0.7071067811865476))
        + upper_pre * jnp.exp(-0.5 * upper_pre * upper_pre) * 0.3989422804014327
    )
    grad_upper = (grad_act * gelu_slope).astype(jnp.bfloat16)
    grad_up = left_dot(normed_two_low, grad_upper)
    grad_up_bias = jnp.sum(grad_upper.astype(jnp.float32), axis=0)
    grad_normed_two = right_dot(grad_upper, up_weight)
    grad_resid_norm, grad_post_gain, grad_post_bias = norm_backward(
        grad_normed_two, unit_post, inv_post, post_gain_f
    )
    grad_residual = grad_top_wide + grad_resid_norm
    grad_branch = grad_residual.astype(jnp.bfloat16)
    grad_out = left_dot(mixer_tok, grad_branch)
    grad_out_bias = jnp.sum(grad_branch.astype(jnp.float32), axis=0)
    grad_mixer = right_dot(grad_branch, out_weight).astype(jnp.bfloat16)
    grad_mixer_chan = lax.all_to_all(
        grad_mixer.T, "seq", split_axis=0, concat_axis=1, tiled=True
    ).astype(jnp.float32)
    gmix_real, gmix_imag = padded_spectrum(grad_mixer_chan)
    corr_real, corr_imag = times_conj(gmix_real, gmix_imag, ktwo_real, ktwo_imag)
    grad_gated = rounded(inverse_real(corr_real, corr_imag) + skip_two * grad_mixer_chan)
    corr_real, corr_imag = times_conj(gmix_real, gmix_imag, gated_real, gated_imag)
    grad_kernel_two = inverse_real(corr_real, corr_imag)
    grad_skip_two = jnp.sum(grad_mixer_chan * gated_low, axis=1)
    grad_after = rounded(grad_gated * gate_wide)
    grad_gate_two = (grad_gated * after_one).astype(jnp.bfloat16)
    gaft_real, gaft_imag = padded_spectrum(grad_after)
    corr_real, corr_imag = times_conj(gaft_real, gaft_imag, kone_real, kone_imag)
    grad_product = (inverse_real(corr_real, corr_imag) + skip_one * grad_after).astype(jnp.bfloat16)
    corr_real, corr_imag = times_conj(gaft_real, gaft_imag, prod_real, prod_imag)
    grad_kernel_one = inverse_real(corr_real, corr_imag)
    grad_skip_one = jnp.sum(grad_after * prod_wide, axis=1)
    filter_grads = filter_pull((grad_kernel_one, grad_kernel_two))
    grad_prod_back, grad_gate_back = (
        lax.all_to_all(grad_product, "seq", split_axis=1, concat_axis=0, tiled=True),
        lax.all_to_all(grad_gate_two, "seq", split_axis=1, concat_axis=0, tiled=True),
    )
    grad_prod_wide = grad_prod_back.T.astype(jnp.float32)
    grad_mixed = jnp.concatenate(
        [
            grad_prod_wide * gate_one,
            grad_prod_wide * value_part,
            grad_gate_back.T.astype(jnp.float32),
        ],
        axis=1,
    )
    grad_short_bias = jnp.sum(grad_mixed, axis=0)
    grad_short = jnp.stack(
        [
            jnp.sum(grad_mixed * extended[0:tok_count], axis=0),
            jnp.sum(grad_mixed * extended[1 : tok_count + 1], axis=0),
            jnp.sum(grad_mixed * extended[2 : tok_count + 2], axis=0),
        ]
    )
    zero_rows = jnp.zeros((2, 3 * model_width), jnp.float32)
    padded_grad = jnp.concatenate([zero_rows, grad_mixed, zero_rows], axis=0)
    grad_extended = (
        short_f[0] * padded_grad[2:]
        + short_f[1] * padded_grad[1:-1]
        + short_f[2] * padded_grad[:-2]
    )
    from_next = passed_along(grad_extended[:2], "seq", -1)
    grad_projected = grad_extended[2:].at[tok_count - 2 :].add(from_next)
    grad_proj_low = grad_projected.astype(jnp.bfloat16)
    grad_in = left_dot(normed_low, grad_proj_low)
    grad_in_bias = jnp.sum(grad_proj_low.astype(jnp.float32), axis=0)
    grad_normed = right_dot(grad_proj_low, in_weight)
    grad_tokens_norm, grad_pre_gain, grad_pre_bias = norm_backward(
        grad_normed, unit_pre, inv_pre, pre_gain_f
    )
    grad_inputs = grad_residual + grad_tokens_norm
    shared_sums = lax.psum(
        (
            grad_pre_gain,
            grad_pre_bias,
            grad_in_bias,
            grad_short,
            grad_short_bias,
            filter_grads[0],
            filter_grads[1],
            filter_grads[2],
            filter_grads[3],
            filter_grads[4],
            filter_grads[5],
            filter_grads[6],
            grad_out_bias,
            grad_post_gain,
            grad_post_bias,
            grad_up_bias,
            grad_down_bias,
        ),
        ("batch", "seq"),
    )
    skip_grads = jnp.stack([grad_skip_one, grad_skip_two])
    weight_shards = (
        lax.psum_scatter(grad_in, "seq", scatter_dimension=0, tiled=True),
        lax.psum_scatter(grad_out, "seq", scatter_dimension=0, tiled=True),
        lax.psum_scatter(grad_up, "seq", scatter_dimension=0, tiled=True),
        lax.psum_scatter(grad_down, "seq", scatter_dimension=0, tiled=True),
    )
    final_in, final_out, final_up, final_down, final_filter, final_rates, final_skips = (
        lax.psum(weight_shards[0].astype(jnp.bfloat16), "batch").astype(jnp.float32),
        lax.psum(weight_shards[1].astype(jnp.bfloat16), "batch").astype(jnp.float32),
        lax.psum(weight_shards[2].astype(jnp.bfloat16), "batch").astype(jnp.float32),
        lax.psum(weight_shards[3].astype(jnp.bfloat16), "batch").astype(jnp.float32),
        lax.psum(filter_grads[7].astype(jnp.bfloat16), "batch").astype(jnp.float32),
        lax.psum(filter_grads[8].astype(jnp.bfloat16), "batch").astype(jnp.float32),
        lax.psum(skip_grads.astype(jnp.bfloat16), "batch").astype(jnp.float32),
    )
    return (
        outputs[None],
        grad_inputs[None],
        shared_sums[0],
        shared_sums[1],
        final_in,
        shared_sums[2],
        shared_sums[3],
        shared_sums[4],
        shared_sums[5],
        shared_sums[6],
        shared_sums[7],
        shared_sums[8],
        shared_sums[9],
        shared_sums[10],
        shared_sums[11],
        final_filter,
        final_rates,
        final_skips,
        final_out,
        shared_sums[12],
        shared_sums[13],
        shared_sums[14],
        final_up,
        shared_sums[15],
        final_down,
        shared_sums[16],
    )


LANES = 128
BLOCK = 256
WAVE_BLOCK = 256
PAD = 8
CHUNK = 64
DENSE_LIMIT = 2048
ROW_AT = {
    "pre_gain": 0,
    "pre_bias": 1,
    "in_bias": 2,
    "tap_bias": 5,
    "taps": 8,
    "skips": 17,
    "post_gain": 19,
    "post_bias": 20,
    "out_bias": 21,
    "down_bias": 22,
    "up_bias": 23,
}
ROW_COUNT = 32


def call_kernel(kernel, outs, args, micros, spaces="", scratch=(), limit=60, name=None):
    places = {"v": pltpu.VMEM, "s": pltpu.SMEM, "h": pl.ANY}
    spaces = spaces or "v" * (len(args) + len(outs))
    specs = [pl.BlockSpec(memory_space=places[space]) for space in spaces]
    shapes = [jax.ShapeDtypeStruct(shape, dtype) for shape, dtype in outs]
    return pl.pallas_call(
        kernel,
        out_shape=shapes,
        in_specs=specs[: len(args)],
        out_specs=specs[len(args) :],
        scratch_shapes=[
            pltpu.SemaphoreType.DMA((entry,))
            if isinstance(entry, int)
            else pltpu.VMEM(entry[0], entry[1])
            for entry in scratch
        ],
        compiler_params=pltpu.CompilerParams(vmem_limit_bytes=limit * 1024 * 1024),
        cost_estimate=pl.CostEstimate(
            flops=1, transcendentals=0, bytes_accessed=int(3.0e6 * micros)
        ),
        name=name,
    )(*args)


def row_chunks(source, target, sems, first, count):
    size = source.shape[0] // count
    return [
        pltpu.make_async_copy(
            source.at[pl.ds(place * size, size)],
            target.at[pl.ds(place * size, size)],
            sems.at[first + place],
        )
        for place in range(count)
    ]


def dense_rows(tile):
    tokens, channels = tile.shape
    rows = tokens * channels // LANES
    spare = LANES - channels
    blocks = channels // spare
    pieces = [tile[rows:, block * spare : (block + 1) * spare] for block in range(blocks)]
    return jnp.concatenate([tile[:rows], jnp.concatenate(pieces, axis=0)], axis=1)


def loose_rows(tile, tokens, channels):
    rows = tile.shape[0]
    spare = LANES - channels
    blocks = channels // spare
    rest = tokens - rows
    pieces = [tile[block * rest : (block + 1) * rest, channels:] for block in range(blocks)]
    return jnp.concatenate([tile[:, :channels], jnp.concatenate(pieces, axis=1)], axis=0)


def lays_dense(tokens, channels):
    spare = LANES - channels
    if spare <= 0 or channels % spare or tokens * channels % LANES:
        return False
    rows, blocks = tokens * channels // LANES, channels // spare
    return rows % 8 == 0 and (tokens - rows) * blocks == rows and (tokens - rows) % 8 == 0


def split_low(value):
    high = value.astype(jnp.bfloat16)
    return high, (value - high.astype(jnp.float32)).astype(jnp.bfloat16)


def three_products(dot, left_side, right_side):
    left_high, left_rest = split_low(left_side)
    right_high, right_rest = split_low(right_side)
    return dot(left_high, right_high) + dot(left_high, right_rest) + dot(left_rest, right_high)


def fine_nn(left_side, right_side):
    return three_products(plain_dot, left_side, right_side)


def fine_nt(left_side, right_side):
    return three_products(right_dot, left_side, right_side)


def fine_tn(left_side, right_side):
    return three_products(left_dot, left_side, right_side)


def exact_nn(left_side, right_side):
    return jnp.dot(
        left_side, right_side, precision=highest_accuracy, preferred_element_type=jnp.float32
    )


def sine_pair(angle):
    turns = jnp.round(angle * (2.0 / math.pi))
    rest = angle - turns * 1.5703125
    rest = rest - turns * 4.837512969970703125e-4
    rest = rest - turns * 7.549789948768648e-8
    square = rest * rest
    sine = rest + rest * square * (
        -1.6666654611e-1 + square * (8.3321608736e-3 + square * -1.9515295891e-4)
    )
    cosine = (
        1.0
        - 0.5 * square
        + square
        * square
        * (4.166664568298827e-2 + square * (-1.388731625493765e-3 + square * 2.443315711809948e-5))
    )
    quarter = turns.astype(jnp.int32)
    odd = (quarter & 1) == 1
    sine_out = jnp.where(odd, cosine, sine)
    cosine_out = jnp.where(odd, sine, cosine)
    sine_out = jnp.where((quarter & 2) == 2, -sine_out, sine_out)
    cosine_out = jnp.where(((quarter + 1) & 2) == 2, -cosine_out, cosine_out)
    return sine_out, cosine_out


def block_rows(index, size):
    return pl.ds(pl.multiple_of(index * size, size), size)


def wave_pair(index):
    first = index * 2 * WAVE_BLOCK
    return (
        pl.ds(pl.multiple_of(first, WAVE_BLOCK), WAVE_BLOCK),
        pl.ds(pl.multiple_of(first + WAVE_BLOCK, WAVE_BLOCK), WAVE_BLOCK),
    )


def row_of(rows, name, place=0):
    at = ROW_AT[name] + place
    return rows[at : at + 1, :]


def feature_block(first, count, length, feat_count):
    bands = (feat_count - 1) // 2
    place = lax.broadcasted_iota(jnp.int32, (count, 2 * feat_count), 0) + first
    lane = lax.broadcasted_iota(jnp.int32, (count, 2 * feat_count), 1)
    later = lane >= feat_count
    place = jnp.where(later, 2 * place + 1, 2 * place)
    lane = jnp.where(later, lane - feat_count, lane)
    steps = place.astype(jnp.float32)
    band = jnp.where(lane > bands, lane - 1 - bands, lane - 1).astype(jnp.float32)
    frequency = 0.0001 + band * ((bands - 1 - 0.0001) / (bands - 1))
    sine, cosine = sine_pair(frequency * (steps * (2.0 * math.pi / length)))
    features = jnp.where(lane > bands, -sine, cosine)
    features = jnp.where(lane == 0, steps / (length - 1), features)
    column = lax.broadcasted_iota(jnp.int32, (count, 1), 0) + first
    times = [(2 * column + odd).astype(jnp.float32) / (length - 1) for odd in (0, 1)]
    return features, times


def norm_kernel(tokens, top, gain, bias, tokens_out, top_out, normed_out, held):
    low, f32 = jnp.bfloat16, jnp.float32
    count = tokens.shape[0] // 2
    for source, target in ((top, top_out), (tokens, tokens_out)):
        for place in range(held.shape[0]):
            cols = slice(place * LANES, (place + 1) * LANES)
            held[place] = source[:, cols].astype(f32)
            for odd in range(2):
                rows = held[place, pl.ds(odd, count, stride=2), :]
                target[odd * count : (odd + 1) * count, cols] = rows.astype(low)
    rows = [vector[...].astype(f32).reshape(1, vector.shape[0]) for vector in (gain, bias)]
    normed, _, _ = norm_forward(tokens_out[...].astype(f32), *rows)
    normed_out[...] = normed.astype(low)


def wave_kernel(channels, start, *refs):
    (
        pre_gain,
        pre_bias,
        in_bias,
        tap_bias,
        taps,
        skips,
        post_gain,
        post_bias,
        out_bias,
        down_bias,
        up_bias,
        pos_bias,
        inner_bias,
        third_bias,
        sine_freq,
        filter_weight,
        decay,
        in_weight_in,
        wave_out,
        turn_out,
        rows_out,
        in_out,
        local_out,
        weights_out,
        rates_out,
        vectors_out,
        tables,
        wave,
        in_weight,
        sems,
    ) = refs
    half = wave.shape[1]
    width = in_weight.shape[0]
    step = tables.shape[1]
    low, f32 = jnp.bfloat16, jnp.float32
    load = pltpu.make_async_copy(in_weight_in, in_weight, sems.at[1])
    load.start()

    unit = math.pi / (4 * half)

    def table(which, carry):
        at = lax.broadcasted_iota(jnp.int32, (step, half), 0)
        place = lax.broadcasted_iota(jnp.int32, (step, half), 1)
        left = jnp.where(which == 0, 2 * step * at, 2 * at + 1)
        turn = (left * (2 * place + 1)) & (8 * half - 1)
        sine, cosine = sine_pair(turn.astype(f32) * unit)
        tables[2 * which] = cosine
        tables[2 * which + 1] = sine
        return carry

    lax.fori_loop(0, 2, table, 0)
    per_block = WAVE_BLOCK // step

    def fill(index, carry):
        base = (index // per_block) * (2 * WAVE_BLOCK) + (index % per_block) * step
        upper = pl.ds(pl.multiple_of(base, step), step)
        lower = pl.ds(pl.multiple_of(base + WAVE_BLOCK, step), step)
        one = pl.ds(index, 1)
        cos_a, sin_a = tables[0, one, :], tables[1, one, :]
        cos_b, sin_b = tables[2], tables[3]
        wave[upper, :] = (cos_a * cos_b - sin_a * sin_b).astype(low)
        wave[lower, :] = (sin_a * cos_b + cos_a * sin_b).astype(low)
        return carry

    lax.fori_loop(0, half // step, fill, 0)
    sent = [pltpu.make_async_copy(wave, wave_out, sems.at[0])]
    for copy in sent:
        copy.start()

    def turn(index, carry):
        upper, lower = wave_pair(index)
        at = lax.broadcasted_iota(jnp.int32, (WAVE_BLOCK, LANES), 0) + index * WAVE_BLOCK
        sine, cosine = sine_pair((2 * at + 1).astype(f32) * unit)
        turn_out[upper, :] = cosine
        turn_out[lower, :] = sine
        return carry

    lax.fori_loop(0, half // WAVE_BLOCK, turn, 0)
    rows_out[...] = jnp.zeros_like(rows_out)

    def place_rows(name, vector):
        for number in range(vector.shape[0] // width):
            piece = vector[number * width : (number + 1) * width].astype(f32)
            at = ROW_AT[name] + number
            rows_out[at : at + 1, :] = piece.reshape(1, width)

    for name, vector in (
        ("pre_gain", pre_gain),
        ("pre_bias", pre_bias),
        ("in_bias", in_bias),
        ("tap_bias", tap_bias),
        ("post_gain", post_gain),
        ("post_bias", post_bias),
        ("out_bias", out_bias),
        ("down_bias", down_bias),
        ("up_bias", up_bias),
    ):
        place_rows(name, vector)
    wide_taps = taps[...].astype(f32)
    for tap in range(3):
        for group in range(3):
            at = ROW_AT["taps"] + 3 * tap + group
            rows_out[at : at + 1, :] = wide_taps[tap : tap + 1, group * width : (group + 1) * width]
    at = ROW_AT["skips"]
    rows_out[at : at + 2, :] = skips[...].astype(f32)
    for number, vector in enumerate((pos_bias, inner_bias, third_bias, sine_freq)):
        row = vector[...].astype(f32).reshape(1, vector.shape[0])
        vectors_out[number : number + 1, :] = row

    source = lax.broadcasted_iota(jnp.int32, (width, LANES), 0)
    target = lax.broadcasted_iota(jnp.int32, (width, LANES), 1)
    chosen = (source == start[0] + target) & (target < channels)
    select_wide = jnp.where(chosen, 1.0, 0.0)
    select = select_wide.astype(low)
    local_out[...] = plain_dot(rows_out[...].astype(low), select)
    padded = jnp.concatenate([decay[...], jnp.zeros((6, width), f32)], axis=0)
    rates = exact_nn(padded, select_wide)
    for order in range(2):
        cols = slice(order * LANES, (order + 1) * LANES)
        weights_out[:, cols] = plain_dot(filter_weight[order], select)
        rates_out[:, cols] = rates[order : order + 1]
    load.wait()
    for group in range(3):
        cols = slice(group * LANES, (group + 1) * LANES)
        whole = in_weight[:, group * width : (group + 1) * width]
        in_out[:, cols] = plain_dot(whole, select).astype(low)
    for copy in sent:
        copy.wait()


def doubled(weight):
    zero = jnp.zeros_like(weight)
    return jnp.concatenate(
        [jnp.concatenate([weight, zero], axis=1), jnp.concatenate([zero, weight], axis=1)], axis=0
    )


def twice(row):
    return jnp.concatenate([row, row], axis=1)


def filter_kernel(
    pos_weight,
    inner_weight,
    third_weight,
    vectors,
    weights,
    rates,
    turn,
    wave_in,
    spectrum_out,
    kernel_out,
    waves_out,
    high,
    rest,
    wave,
    sems,
):
    half = wave.shape[1]
    length = 2 * half
    low, f32 = jnp.bfloat16, jnp.float32
    loads = row_chunks(wave_in, wave, sems, 0, 1)
    for copy in loads:
        copy.start()
    feat_count = pos_weight.shape[0]
    freq = twice(vectors[3:4, :])

    def network(index, carry):
        here = block_rows(index, BLOCK)
        there = pl.ds(pl.multiple_of(index * BLOCK + half, BLOCK), BLOCK)
        layer_in, times = feature_block(index * BLOCK, BLOCK, length, feat_count)
        for layer, weight in enumerate((pos_weight, inner_weight, third_weight)):
            matrix = doubled(weight[...].astype(f32))
            inner = fine_nn(layer_in, matrix) + twice(vectors[layer : layer + 1, :])
            layer_in, cosine = sine_pair(freq * inner)
            waves_out[layer, here, :] = jnp.concatenate([layer_in, cosine], axis=1)
        both = fine_nn(layer_in, doubled(weights[...]))
        cols = 2 * LANES
        for part, rows in enumerate((here, there)):
            kernels = both[:, part * cols : (part + 1) * cols]
            kernels = kernels * jnp.exp(-rates[...] * times[part])
            kernel_out[rows, :] = kernels
            upper = kernels.astype(low)
            high[rows, :] = upper
            rest[rows, :] = (kernels - upper.astype(f32)).astype(low)
        return carry

    lax.fori_loop(0, half // BLOCK, network, 0, unroll=True)
    for copy in loads:
        copy.wait()

    def spectra(index, carry):
        matrix = wave[block_rows(index, 2 * WAVE_BLOCK), :]
        even, odd = (
            plain_dot(matrix, high[rows, :]) + plain_dot(matrix, rest[rows, :])
            for rows in (slice(0, half), slice(half, length))
        )
        upper, lower = wave_pair(index)
        for order in range(2):
            cols = slice(order * LANES, (order + 1) * LANES)
            parts = butterfly(even[:, cols], odd[:, cols], turn, upper, lower)
            for side, (real, imag) in enumerate(parts):
                spectrum_out[side, upper, cols] = real * (1.0 / length)
                spectrum_out[side, lower, cols] = imag * (1.0 / length)
        return carry

    lax.fori_loop(0, half // WAVE_BLOCK, spectra, 0, unroll=True)


def butterfly(even, odd, turn, upper, lower):
    cosine, sine = turn[upper, :], turn[lower, :]
    even_real, even_imag = even[:WAVE_BLOCK], even[WAVE_BLOCK:]
    odd_real, odd_imag = odd[:WAVE_BLOCK], odd[WAVE_BLOCK:]
    real = even_real * cosine + even_imag * sine
    imag = even_imag * cosine - even_real * sine
    return (real + odd_real, imag + odd_imag), (real - odd_real, odd_imag - imag)


def unbutterfly(first, second, turn, upper, lower):
    cosine, sine = turn[upper, :], turn[lower, :]
    real, imag = first[0] + second[0], first[1] - second[1]
    even = (real * cosine - imag * sine, imag * cosine + real * sine)
    return even, (first[0] - second[0], first[1] + second[1])


def short_mix(rows, projected, index, group):
    cols = slice(group * LANES, (group + 1) * LANES)
    here = pl.ds(pl.multiple_of(index * CHUNK, CHUNK), CHUNK + PAD)
    even, odd = projected[0, here, cols], projected[1, here, cols]
    taps = [row_of(rows, "taps", 3 * tap + group) for tap in range(3)]
    shift = row_of(rows, "tap_bias", group)
    last = slice(PAD - 1, PAD - 1 + CHUNK)
    return (
        taps[0] * even[last] + taps[1] * odd[last] + taps[2] * even[PAD:] + shift,
        taps[0] * odd[last] + taps[1] * even[PAD:] + taps[2] * odd[PAD:] + shift,
    )


def spread_rows(tile, held, target):
    count = tile.shape[0] // 2
    for place in range(held.shape[0]):
        cols = slice(place * LANES, (place + 1) * LANES)
        for odd in range(2):
            rows = tile[odd * count : (odd + 1) * count, cols]
            held[place, pl.ds(odd, count, stride=2), :] = rows
        target[:, cols] = held[place]


def inverse_block(wave, reals, imags, index):
    upper, lower = wave_pair(index)
    return plain_dot(wave[upper, :], reals[...]) + plain_dot(wave[lower, :], imags[...])


def store_inverse(reals, imags, here, at, parts):
    for place, (real, imag) in enumerate(parts):
        cols = slice((at + place) * LANES, (at + place + 1) * LANES)
        reals[here, cols] = real.astype(jnp.bfloat16)
        imags[here, cols] = imag.astype(jnp.bfloat16)


def convolve(wave, turn, signal, spectrum, cols, kept, reals, imags, finish):
    half = wave.shape[1]

    def ahead(index, carry):
        both = plain_dot(wave[block_rows(index, 2 * WAVE_BLOCK), :], signal[...])
        upper, lower = wave_pair(index)
        sides = butterfly(both[:, :LANES], both[:, LANES:], turn, upper, lower)
        outs = []
        for side, (real, imag) in enumerate(sides):
            kept[side, upper, :], kept[side, lower, :] = real, imag
            outs.append(
                times_spec(real, imag, spectrum[side, upper, cols], spectrum[side, lower, cols])
            )
        parts = unbutterfly(*outs, turn, upper, lower)
        store_inverse(reals, imags, block_rows(index, WAVE_BLOCK), 0, parts)
        return carry

    lax.fori_loop(0, half // WAVE_BLOCK, ahead, 0, unroll=True)

    def behind(index, carry):
        finish(block_rows(index, WAVE_BLOCK), inverse_block(wave, reals, imags, index))
        return carry

    lax.fori_loop(0, half // WAVE_BLOCK, behind, 0, unroll=True)


def correlate(wave, turn, signal, spectrum, cols, kept, reals, imags, finish):
    half = wave.shape[1]
    wide = 2 * LANES

    def ahead(index, carry):
        both = plain_dot(wave[block_rows(index, 2 * WAVE_BLOCK), :], signal[...])
        upper, lower = wave_pair(index)
        sides = butterfly(both[:, :LANES], both[:, LANES:], turn, upper, lower)
        here = block_rows(index, WAVE_BLOCK)
        for number, (other, columns) in enumerate(((spectrum, cols), (kept, slice(0, LANES)))):
            outs = [
                times_conj(*pair, other[side, upper, columns], other[side, lower, columns])
                for side, pair in enumerate(sides)
            ]
            parts = unbutterfly(*outs, turn, upper, lower)
            store_inverse(reals, imags, here, 2 * number, parts)
        return carry

    lax.fori_loop(0, half // WAVE_BLOCK, ahead, 0, unroll=True)

    def behind(index, carry):
        both = inverse_block(wave, reals, imags, index)
        kernel = both[:, wide:] * (0.5 / half)
        return finish(block_rows(index, WAVE_BLOCK), both[:, :wide], kernel, carry)

    zero = jnp.zeros((1, wide), jnp.float32)
    return lax.fori_loop(0, half // WAVE_BLOCK, behind, zero, unroll=True)


def front_kernel(parts, index, *refs):
    chunks = refs[:parts]
    (weight, rows, wave_in, turn_in, spectrum_in) = refs[parts : 5 + parts]
    (
        normed_out,
        projected_out,
        product_out,
        gate_out,
        after_out,
        gated_out,
        product_wave_out,
        gated_wave_out,
        mixed_out,
        mixer_out,
        held,
        reals,
        imags,
        wave,
        turn,
        spectrum,
        projected,
        product_wave,
        gated_wave,
        mixed,
        mixer,
        sems,
    ) = refs[5 + parts :]
    tok_count, width = chunks[0].shape
    half = wave.shape[1]
    channels = width // parts
    low, f32 = jnp.bfloat16, jnp.float32
    loads = [
        pltpu.make_async_copy(source, target, sems.at[place])
        for place, (source, target) in enumerate(
            [(wave_in, wave), (turn_in, turn), (spectrum_in, spectrum)]
        )
    ]
    stores = [
        pltpu.make_async_copy(source, target, sems.at[3 + place])
        for place, (source, target) in enumerate(
            [
                (held, normed_out),
                (projected, projected_out),
                (product_wave, product_wave_out),
                (gated_wave, gated_wave_out),
                (mixed, mixed_out),
            ]
        )
    ]
    for copy in loads:
        copy.start()
    count = tok_count // 2
    for part in range(parts):
        place = index[0] ^ part
        for odd in range(2):
            at = pl.ds(pl.multiple_of(odd * half + place * count, count), count)
            held[at, :] = chunks[part][odd * count : (odd + 1) * count, :]
    stores[0].start()
    in_bias = jnp.concatenate([row_of(rows, "in_bias", group) for group in range(3)], axis=1)
    projected[:, :PAD, :] = jnp.zeros((2, PAD, projected.shape[2]), f32)

    def project(odd, carry):
        projected[odd, PAD:, :] = plain_dot(held[block_rows(odd, half), :], weight[...]) + in_bias
        return carry

    lax.fori_loop(0, 2, project, 0, unroll=True)
    stores[1].start()

    def mix(step, carry):
        here = block_rows(step, CHUNK)
        value, gate_one, gate_two = (short_mix(rows, projected, step, group) for group in range(3))
        for odd in range(2):
            cols = slice(odd * LANES, (odd + 1) * LANES)
            mixed[0, here, cols] = value[odd]
            mixed[1, here, cols] = gate_one[odd]
            product_out[here, cols] = (value[odd] * gate_one[odd]).astype(low)
            gate_out[here, cols] = gate_two[odd].astype(low)
        return carry

    lax.fori_loop(0, half // CHUNK, mix, 0)
    stores[4].start()
    skips = [twice(row_of(rows, "skips", order)) for order in range(2)]

    def first(here, convolved):
        product = product_out[here, :].astype(f32)
        after = (convolved + skips[0] * product).astype(low)
        after_out[here, :] = after
        gated_out[here, :] = (after.astype(f32) * gate_out[here, :].astype(f32)).astype(low)

    def second(here, convolved):
        gated = gated_out[here, :].astype(f32)
        mixer[here, :] = (convolved + skips[1] * gated).astype(low)

    for copy in loads:
        copy.wait()
    cols = [slice(order * LANES, (order + 1) * LANES) for order in range(2)]
    convolve(wave, turn, product_out, spectrum, cols[0], product_wave, reals, imags, first)
    stores[2].start()
    convolve(wave, turn, gated_out, spectrum, cols[1], gated_wave, reals, imags, second)
    stores[3].start()
    for part in range(parts):
        at = slice(part * count, (part + 1) * count)
        tiles = [mixer[at, odd * LANES : odd * LANES + channels] for odd in range(2)]
        mixer_out[part] = dense_rows(jnp.concatenate(tiles, axis=0))
    for copy in stores:
        copy.wait()


def back_kernel(
    channels,
    grad_mixer,
    product_ref,
    gate_ref,
    after_ref,
    gated_ref,
    rows,
    turn,
    product_wave_in,
    gated_wave_in,
    spectrum_in,
    wave_in,
    projected_in,
    mixed_in,
    packed_out,
    padded_out,
    grad_kernel_out,
    sums_out,
    grad_mix,
    grad_after,
    grad_value,
    grad_gate,
    reals,
    imags,
    wave,
    spectrum,
    product_wave,
    gated_wave,
    projected,
    mixed,
    shifted,
    sems,
):
    parts = grad_mixer.shape[0]
    half = wave.shape[1]
    count = half // parts
    low, f32 = jnp.bfloat16, jnp.float32
    loads = [
        pltpu.make_async_copy(source, target, sems.at[place])
        for place, (source, target) in enumerate(
            [
                (wave_in, wave),
                (spectrum_in, spectrum),
                (gated_wave_in, gated_wave),
                (product_wave_in, product_wave),
                (projected_in, projected),
                (mixed_in, mixed),
            ]
        )
    ]
    for copy in loads:
        copy.start()
    padding = jnp.zeros((count, LANES - channels), low)
    for part in range(parts):
        tile = loose_rows(grad_mixer[part], 2 * count, channels)
        here = slice(part * count, (part + 1) * count)
        pieces = [tile[:count], padding, tile[count:], padding]
        grad_mix[here, :] = jnp.concatenate(pieces, axis=1)
    skips = [twice(row_of(rows, "skips", order)) for order in range(2)]

    def store_kernel(here, order, kernel):
        cols = slice(order * LANES, (order + 1) * LANES)
        grad_kernel_out[0, here, cols] = kernel[:, :LANES]
        grad_kernel_out[1, here, cols] = kernel[:, LANES:]

    def first(here, data, kernel, total):
        store_kernel(here, 1, kernel)
        top = grad_mix[here, :].astype(f32)
        grad_gated = (data + skips[1] * top).astype(low).astype(f32)
        grad_after[here, :] = (grad_gated * gate_ref[here, :].astype(f32)).astype(low)
        grad_gate[here, :] = (grad_gated * after_ref[here, :].astype(f32)).astype(low)
        return total + jnp.sum(top * gated_ref[here, :].astype(f32), axis=0, keepdims=True)

    def second(here, data, kernel, total):
        store_kernel(here, 0, kernel)
        top = grad_after[here, :].astype(f32)
        grad_value[here, :] = (data + skips[0] * top).astype(low)
        return total + jnp.sum(top * product_ref[here, :].astype(f32), axis=0, keepdims=True)

    cols = [slice(order * LANES, (order + 1) * LANES) for order in range(2)]
    for copy in loads[:3]:
        copy.wait()
    skip_second = correlate(
        wave, turn, grad_mix, spectrum, cols[1], gated_wave, reals, imags, first
    )
    loads[3].wait()
    skip_first = correlate(
        wave, turn, grad_after, spectrum, cols[0], product_wave, reals, imags, second
    )
    sums_out[15:16, :] = skip_first[:, :LANES] + skip_first[:, LANES:]
    sums_out[16:17, :] = skip_second[:, :LANES] + skip_second[:, LANES:]
    sums_out[17:24, :] = jnp.zeros((7, LANES), f32)
    for copy in loads[4:]:
        copy.wait()
    shifted[:, :, half:, :] = jnp.zeros((3, 2, PAD, LANES), f32)
    sides = [slice(odd * LANES, (odd + 1) * LANES) for odd in range(2)]

    def folded(value):
        return jnp.sum(value.reshape(CHUNK // 8, 8, LANES), axis=0)

    def taps_back(step, totals):
        here = block_rows(step, CHUNK)
        window = pl.ds(pl.multiple_of(step * CHUNK, CHUNK), CHUNK + PAD)
        last = slice(PAD - 1, PAD - 1 + CHUNK)
        totals = list(totals)
        for group in range(3):
            cols = slice(group * LANES, (group + 1) * LANES)
            if group == 2:
                even, odd = (grad_gate[here, side].astype(f32) for side in sides)
            else:
                even, odd = (
                    grad_value[here, side].astype(f32) * mixed[1 - group, here, side]
                    for side in sides
                )
            shifted[group, 0, here, :], shifted[group, 1, here, :] = even, odd
            even_rows, odd_rows = projected[0, window, cols], projected[1, window, cols]
            terms = (
                even * even_rows[last] + odd * odd_rows[last],
                even * odd_rows[last] + odd * even_rows[PAD:],
                even * even_rows[PAD:] + odd * odd_rows[PAD:],
                even + odd,
            )
            for number, term in enumerate(terms):
                totals[3 * number + group] = totals[3 * number + group] + folded(term)
        return tuple(totals)

    zero = jnp.zeros((8, LANES), f32)
    totals = lax.fori_loop(0, half // CHUNK, taps_back, (zero,) * 12)

    def project_back(step, totals):
        window = pl.ds(pl.multiple_of(step * CHUNK, CHUNK), CHUNK + PAD)
        following = slice(1, 1 + CHUNK)
        totals = list(totals)
        for group in range(3):
            cols = slice(group * LANES, (group + 1) * LANES)
            even, odd = shifted[group, 0, window, :], shifted[group, 1, window, :]
            taps = [row_of(rows, "taps", 3 * tap + group) for tap in range(3)]
            now = slice(0, CHUNK)
            grads = (
                taps[0] * even[following] + taps[1] * odd[now] + taps[2] * even[now],
                taps[0] * odd[following] + taps[1] * even[following] + taps[2] * odd[now],
            )
            grads = [grad.astype(low) for grad in grads]
            for place, grad in enumerate(grads):
                at = pl.ds(pl.multiple_of(place * half + step * CHUNK, CHUNK), CHUNK)
                padded_out[at, cols] = grad
            wide = grads[0].astype(f32) + grads[1].astype(f32)
            totals[group] = totals[group] + folded(wide)
        return tuple(totals)

    totals = totals + lax.fori_loop(0, half // CHUNK, project_back, (zero,) * 3)
    for number, value in enumerate(totals):
        sums_out[number : number + 1, :] = jnp.sum(value, axis=0, keepdims=True)
    dense = packed_out.shape[1] // 3

    def pack(part, carry):
        for group in range(3):
            cols = slice(group * LANES, group * LANES + channels)
            tiles = [
                padded_out[
                    pl.ds(pl.multiple_of(odd * half + part * count, count), count), cols
                ]
                for odd in range(2)
            ]
            packed = dense_rows(jnp.concatenate(tiles, axis=0))
            packed_out[part, group * dense : (group + 1) * dense, :] = packed
        return carry

    lax.fori_loop(0, parts, pack, 0)


def store_rows(target, at, value):
    per = target.shape[1]
    place = 0
    while place < value.shape[0]:
        quarter, inside = divmod(at + place, per)
        count = min(value.shape[0] - place, per - inside)
        target[quarter, inside : inside + count, :] = value[place : place + count]
        place += count


def lane_rows(vector):
    count = vector.shape[1] // LANES
    return jnp.concatenate(
        [vector[:, place * LANES : (place + 1) * LANES] for place in range(count)], axis=0
    )


def middle_kernel(
    parts,
    batch_index,
    received,
    tokens,
    top,
    rows,
    out_in,
    up_in,
    down_in,
    outputs_out,
    residual_out,
    send_out,
    sums_out,
    *refs,
):
    batch = len(refs) - 14
    sides, parts_out = refs[0], refs[1 : 1 + batch]
    (
        out_w,
        up_w,
        down_w,
        residual,
        total,
        flow,
        act,
        upper_grad,
        act_parts,
        branch_parts,
        up_rows,
        held,
        sems,
    ) = refs[1 + batch :]
    tok_count, width = tokens.shape
    channels = width // parts
    f32, low = jnp.float32, jnp.bfloat16
    quarters = up_w.shape[0]
    quarter = up_w.shape[2]
    load_out = pltpu.make_async_copy(out_in, out_w, sems.at[0])
    load_out.start()

    def loads(place):
        cols = pl.ds(pl.multiple_of(place * quarter, quarter), quarter)
        return (
            pltpu.make_async_copy(up_in.at[:, cols], up_w.at[place], sems.at[1 + place]),
            pltpu.make_async_copy(
                down_in.at[cols, :], down_w.at[place], sems.at[1 + quarters + place]
            ),
        )

    for place in range(quarters):
        for copy in loads(place):
            copy.start()
    tiles = [
        loose_rows(received[part], tok_count, channels) for part in range(parts)
    ]
    mixer = jnp.concatenate(tiles, axis=1)
    load_out.wait()
    branch = plain_dot(mixer, out_w[...]) + row_of(rows, "out_bias")
    residual[...] = tokens[...].astype(f32) + branch
    gain = row_of(rows, "post_gain")
    bias = row_of(rows, "post_bias")
    normed, _, _ = norm_forward(residual[...], gain, bias)
    sides[:, :width] = normed.astype(low)
    sides[:, width:] = mixer
    for place in range(quarters):
        up_rows[place] = row_of(rows, "up_bias", place)
    total[...] = jnp.zeros_like(total)
    flow[...] = jnp.zeros_like(flow)

    def body(place, carry):
        for copy in loads(place):
            copy.wait()
        upper = plain_dot(sides[:, :width], up_w[place]) + up_rows[place]
        gauss = 0.5 * (1.0 + lax.erf(upper * 0.7071067811865476))
        active = (upper * gauss).astype(low)
        act[place] = active
        total[...] += plain_dot(active, down_w[place])
        grad_act = right_dot(top[...], down_w[place])
        slope = gauss + upper * jnp.exp(-0.5 * upper * upper) * 0.3989422804014327
        grad_upper = (grad_act * slope).astype(low)
        upper_grad[place] = grad_upper
        flow[...] += right_dot(grad_upper, up_w[place])
        return carry

    lax.fori_loop(0, quarters, body, 0, unroll=2)
    spread_rows(residual[...] + total[...] + row_of(rows, "down_bias"), held, outputs_out)
    _, unit, inv_std = norm_forward(residual[...], gain, bias)
    grad_norm, grad_gain, grad_bias = norm_backward(flow[...], unit, inv_std, gain)
    grad_residual = top[...].astype(f32) + grad_norm
    residual_out[...] = grad_residual
    grad_branch = grad_residual.astype(low)
    grad_mixer = right_dot(grad_branch, out_w[...]).astype(low)
    for part in range(parts):
        tile = grad_mixer[:, part * channels : (part + 1) * channels]
        send_out[part] = dense_rows(tile)
    wide_branch = grad_branch.astype(f32)
    vectors = [
        jnp.sum(wide_branch, axis=0, keepdims=True),
        grad_gain[None],
        grad_bias[None],
        jnp.sum(top[...].astype(f32), axis=0, keepdims=True),
    ]
    vectors += [
        jnp.sum(upper_grad[place].astype(f32), axis=0, keepdims=True) for place in range(quarters)
    ]
    per = width // LANES
    for number, vector in enumerate(vectors):
        sums_out[number * per : (number + 1) * per, :] = lane_rows(vector)
    piece = width // batch
    for place in range(batch):
        part = wide_branch[:, place * piece : (place + 1) * piece]
        spare = branch_parts.shape[2] - piece
        part = jnp.concatenate([part, jnp.zeros((tok_count, spare), f32)], axis=1)
        branch_parts[place] = part.astype(low)
    step = quarters * quarter // (parts * batch)
    per_part = quarters * quarter // parts
    for place in range(batch):
        tiles = []
        for part in range(parts):
            at = part * per_part + place * step
            inside = at % quarter
            tiles.append(act[at // quarter, :, inside : inside + step])
        act_parts[place] = jnp.concatenate(tiles, axis=1)
    for bits in range(batch):
        place = batch_index[0] ^ bits
        parts_out[bits][:, :quarter] = upper_grad[place]
        parts_out[bits][:, quarter : 2 * quarter] = act_parts[place]
        parts_out[bits][:, 2 * quarter :] = branch_parts[place]


def store_halves(part, bit, bits, keep_out, send_out):
    count = keep_out.shape[0]
    size = keep_out.shape[1]
    for entry in range(count):
        lower, upper = entry % bits, entry // bits
        base = upper * 2 * bits + lower
        mine = pl.ds(pl.multiple_of((base + bit * bits) * size, size), size)
        other = pl.ds(pl.multiple_of((base + (1 - bit) * bits) * size, size), size)
        keep_out[entry] = part[mine, :]
        send_out[entry] = part[other, :].astype(jnp.bfloat16)


def flip(tile):
    return tile.T


def weight_kernel(batch, orders, index, *refs):
    sides, tops, gots = (refs[batch * place : batch * (place + 1)] for place in range(3))
    up_keep, up_send, rest_keep, rest_send, flipped, columns, part, rest = refs[3 * batch :]
    tok_count, width = tops[0].shape
    for entry in range(batch):
        here = slice(entry * tok_count, (entry + 1) * tok_count)
        columns[here, :width] = gots[entry][:, :width]
        columns[here, width : 2 * width] = tops[entry][...]
        columns[here, 2 * width :] = gots[entry][:, 2 * width :]
        flipped[:width, here] = flip(sides[entry][:, :width])
        flipped[width : 2 * width, here] = flip(gots[entry][:, width : 2 * width])
        flipped[2 * width :, here] = flip(sides[entry][:, width:])
    part[...] = plain_dot(flipped[:width, :], columns[:, :width])
    store_halves(part, index[0], orders[0], up_keep, up_send)
    rest[:, :width] = plain_dot(flipped[width : 2 * width, :], columns[:, width : 2 * width])
    last = plain_dot(flipped[2 * width :, :], columns[:, 2 * width :])
    rest[:, width:] = last[:, : rest.shape[1] - width]
    store_halves(rest, index[1], orders[1], rest_keep, rest_send)


def fold_kernel(bits, bit, keep, got, keep_out, send_out):
    for entry in range(keep_out.shape[0]):
        lower, upper = entry % bits, entry // bits
        base = upper * 2 * bits + lower
        mine, other = base + bit[0] * bits, base + (1 - bit[0]) * bits
        keep_out[entry] = keep[mine] + got[mine].astype(jnp.float32)
        send_out[entry] = (keep[other] + got[other].astype(jnp.float32)).astype(jnp.bfloat16)


def collect_kernel(batch, batch_index, *refs):
    entries = refs[:batch]
    down_out, up_out, out_out, held = refs[batch:]
    rows, total = entries[0].shape
    width = down_out.shape[1]
    piece = width // batch
    f32 = jnp.float32
    for entry in range(batch):
        held[batch_index[0] ^ entry] = entries[entry][...]
    for place in range(batch):
        up_out[:, place * width : (place + 1) * width] = held[place, :, :width].astype(f32)
        down = held[place, :, width : 2 * width].astype(f32)
        down_out[place * rows : (place + 1) * rows, :] = down
    tiles = [held[place, :, 2 * width : 2 * width + piece].astype(f32) for place in range(batch)]
    out_out[...] = jnp.concatenate(tiles, axis=1)


def final_kernel(received, tokens, residual, rows, weight_in, out, weight, joined, held, sems):
    parts = received.shape[0]
    tok_count, width = tokens.shape
    channels = width // parts
    f32, low = jnp.float32, jnp.bfloat16
    load = pltpu.make_async_copy(weight_in, weight, sems.at[0])
    load.start()
    dense = received.shape[1] // 3
    for group in range(3):
        tiles = [
            loose_rows(
                received[part, group * dense : (group + 1) * dense, :],
                tok_count,
                channels,
            )
            for part in range(parts)
        ]
        joined[:, group * width : (group + 1) * width] = jnp.concatenate(tiles, axis=1)
    gain = row_of(rows, "pre_gain")
    bias = row_of(rows, "pre_bias")
    _, unit, inv_std = norm_forward(tokens[...].astype(f32), gain, bias)
    load.wait()
    grad_normed = jnp.zeros((tok_count, width), f32)
    for group in range(3):
        cols = slice(group * width, (group + 1) * width)
        grad_normed = grad_normed + right_dot(joined[:, cols], weight[:, cols])
    grad_tokens, _, _ = norm_backward(grad_normed, unit, inv_std, gain)
    spread_rows(residual[...] + grad_tokens, held, out)


SHARED_ROWS = 48
LAID_ROWS = 8
OWN_ROWS = 40


def chain_kernel(
    norm_rows,
    in_local,
    sums,
    middle_sums,
    pos_weight,
    inner_weight,
    third_weight,
    vectors,
    weights,
    rates,
    grad_kernels_in,
    kernels_in,
    waves_in,
    pair_in,
    small_out,
    weight_total,
    rate_total,
    shared,
    pairs,
    grad_kernels,
    kernels,
    waves,
    pair_sums,
    sems,
):
    length = kernels.shape[0]
    blocks = length // BLOCK

    def loads(index):
        here = block_rows(index, BLOCK)
        later = pl.ds(pl.multiple_of(index * BLOCK + length // 2, BLOCK), BLOCK)
        pieces = [
            (source.at[rows], target.at[rows])
            for source, target in ((grad_kernels_in, grad_kernels), (kernels_in, kernels))
            for rows in (here, later)
        ]
        pieces.append((waves_in.at[:, here], waves.at[:, here]))
        return [
            pltpu.make_async_copy(source, target, sems.at[number * (blocks // 2) + index])
            for number, (source, target) in enumerate(pieces)
        ]

    for block in range(blocks // 2):
        for copy in loads(block):
            copy.start()
    width = in_local.shape[0]
    pair_load = pltpu.make_async_copy(pair_in, pair_sums, sems.at[5 * (blocks // 2)])
    pair_load.start()
    feat_count, fhid = pos_weight.shape
    f32 = jnp.float32
    freq = vectors[3:4, :]
    weight_total[...] = jnp.zeros_like(weight_total)
    rate_total[...] = jnp.zeros_like(rate_total)
    pairs[...] = jnp.zeros_like(pairs)

    half = length // 2
    cols = 2 * LANES
    weight_pair = doubled(weights[...])
    freq_pair = twice(freq)

    def body(index, carry):
        here = block_rows(index, BLOCK)
        there = pl.ds(pl.multiple_of(index * BLOCK + half, BLOCK), BLOCK)
        for copy in loads(index):
            copy.wait()
        features, times = feature_block(index * BLOCK, BLOCK, length, feat_count)
        windowed = []
        for rows, time in zip((here, there), times):
            grads = grad_kernels[rows, :]
            decayed = jnp.sum(grads * kernels[rows, :] * time, axis=0, keepdims=True)
            rate_total[...] = rate_total[...] - decayed
            windowed.append(grads * jnp.exp(-rates[...] * time))
        windowed = jnp.concatenate(windowed, axis=1)
        weight_total[...] = weight_total[...] + fine_tn(waves[2, here, :LANES], windowed)
        flow = fine_nt(windowed, weight_pair)
        for layer in (2, 1, 0):
            slope = flow * waves[layer, here, LANES:]
            below = waves[layer - 1, here, :LANES] if layer else features
            count = below.shape[1]
            pairs[layer, :count, :] = pairs[layer, :count, :] + fine_tn(below, slope)
            row = slice(LANES, LANES + 1)
            pairs[layer, row, :] = pairs[layer, row, :] + jnp.sum(slope, axis=0, keepdims=True)
            if layer:
                weight = inner_weight if layer == 1 else third_weight
                flow = fine_nt(slope * freq_pair, doubled(weight[...].astype(f32)))
        return carry

    lax.fori_loop(0, blocks // 2, body, 0, unroll=True)
    grad_freq = jnp.zeros_like(freq)
    at, bias_at = 0, 2 * fhid + feat_count
    for layer, weight in ((2, third_weight), (1, inner_weight), (0, pos_weight)):
        count = weight.shape[0]
        matrix = pairs[layer, :count, :fhid] + pairs[layer, count : 2 * count, fhid:]
        both = pairs[layer, LANES : LANES + 1, :]
        vector = both[:, :fhid] + both[:, fhid:]
        grad_freq = grad_freq + jnp.sum(weight[...].astype(f32) * matrix, axis=0, keepdims=True)
        grad_freq = grad_freq + vectors[layer : layer + 1, :] * vector
        shared[at : at + count, :] = matrix * freq
        shared[bias_at + layer : bias_at + layer + 1, :] = vector * freq
        at += count
    shared[bias_at + 3 : bias_at + 4, :] = grad_freq
    pair_load.wait()
    small_out[...] = jnp.zeros_like(small_out)
    ones = jnp.ones((16, in_local.shape[1]), jnp.bfloat16)
    high, rest = split_low(in_local[...].astype(f32) * pair_sums[...])
    gain = (right_dot(ones, high) + right_dot(ones, rest))[0:1]
    column_sums = jnp.concatenate([sums[12 + group : 13 + group, :] for group in range(3)], axis=1)
    high, rest = split_low(jnp.broadcast_to(column_sums, ones.shape))
    bias = (right_dot(high, in_local[...]) + right_dot(rest, in_local[...]))[0:1]
    everywhere = small_out.at[:, :SHARED_ROWS, :]
    per = width // LANES
    gain = (gain - row_of(norm_rows, "pre_bias") * bias) / row_of(norm_rows, "pre_gain")
    store_rows(everywhere, 0, lane_rows(gain))
    store_rows(everywhere, per, lane_rows(bias))
    at = 2 * per
    store_rows(everywhere, at, middle_sums[...])
    at += middle_sums.shape[0]
    store_rows(everywhere, at, jnp.concatenate([shared[:fhid, :], shared[fhid : 2 * fhid, :]], axis=1))
    at += fhid
    tail = shared[2 * fhid : 2 * fhid + feat_count + 4, :]
    store_rows(everywhere, at, jnp.concatenate([tail, jnp.zeros_like(tail)], axis=1))
    store_rows(small_out.at[:, SHARED_ROWS : SHARED_ROWS + LAID_ROWS, :], 0, sums[:15, :])
    own = small_out.at[:, SHARED_ROWS + LAID_ROWS :, :]
    for order in range(2):
        first = slice(order * LANES, (order + 1) * LANES)
        second = slice(cols + order * LANES, cols + (order + 1) * LANES)
        both = weight_total[:fhid, first] + weight_total[fhid:, second]
        store_rows(own, order * fhid, both)
        store_rows(own, 2 * fhid + order, rate_total[:, first])
    store_rows(own, 2 * fhid + 2, sums[15:17, :])


def spread_kernel(in_keep, in_got, small_keep, small_got, send_out, small_out):
    low, f32 = jnp.bfloat16, jnp.float32
    parts = send_out.shape[0]
    small = small_keep[...] + small_got[...]
    small_out[...] = small
    both = SHARED_ROWS + LAID_ROWS
    high, rest = split_low(small[:both])
    count = in_keep.shape[0] // parts
    for part in range(parts):
        here = slice(part * count, (part + 1) * count)
        send_out[part, :count, :] = (in_keep[here, :] + in_got[here, :].astype(f32)).astype(low)
        send_out[part, count : count + both, :] = high
        send_out[part, count + both :, :] = rest


def merge_kernel(received, small, out):
    f32 = jnp.float32
    parts = received.shape[0]
    both = SHARED_ROWS + LAID_ROWS
    count = received.shape[1] - 2 * both
    total = jnp.zeros((SHARED_ROWS, LANES), f32)
    done = parts * count
    rows = SHARED_ROWS + parts * LAID_ROWS + OWN_ROWS
    for part in range(parts):
        out[part * count : (part + 1) * count, :] = received[part, :count, :]
        high = received[part, count : count + both, :].astype(f32)
        rest = received[part, count + both :, :].astype(f32)
        total = total + high[:SHARED_ROWS] + rest[:SHARED_ROWS]
        at = done + SHARED_ROWS + part * LAID_ROWS
        laid = received[part, count : count + both, :].astype(f32)[SHARED_ROWS:]
        out[at : at + LAID_ROWS, :] = laid.astype(jnp.bfloat16)
        laid = received[part, count + both :, :].astype(f32)[SHARED_ROWS:]
        out[at + rows : at + rows + LAID_ROWS, :] = laid.astype(jnp.bfloat16)
    for at, value in ((0, total), (rows - OWN_ROWS, small[SHARED_ROWS + LAID_ROWS :, :])):
        high, rest = split_low(value)
        count = value.shape[0]
        out[done + at : done + at + count, :] = high
        out[done + rows + at : done + rows + at + count, :] = rest


def take_rows(source, at, count):
    per = source.shape[1]
    pieces = []
    while count:
        quarter, inside = divmod(at, per)
        size = min(count, per - inside)
        pieces.append(source[quarter, inside : inside + size, :])
        at += size
        count -= size
    return pieces[0] if len(pieces) == 1 else jnp.concatenate(pieces, axis=0)


def lane_row(block):
    return jnp.concatenate([block[place : place + 1] for place in range(block.shape[0])], axis=1)


def last_fold_kernel(up_keep, up_got, rest_keep, rest_got, out):
    f32, low = jnp.float32, jnp.bfloat16
    width = up_keep.shape[2]
    wide = width + rest_keep.shape[2]
    out[:, :width] = (up_keep[0] + up_got[0].astype(f32)).astype(low)
    out[:, width:wide] = (rest_keep[0] + rest_got[0].astype(f32)).astype(low)
    out[:, wide:] = jnp.zeros((out.shape[0], out.shape[1] - wide), low)


def finish_kernel(batch, channels, batch_index, *refs):
    entries = refs[:batch]
    (
        in_out,
        pre_gain_out,
        pre_bias_out,
        out_bias_out,
        post_gain_out,
        post_bias_out,
        down_bias_out,
        up_bias_out,
        third_out,
        inner_out,
        pos_out,
        pos_bias_out,
        inner_bias_out,
        third_bias_out,
        freq_out,
        taps_out,
        tap_bias_out,
        in_bias_out,
        filter_out,
        rates_out,
        skips_out,
        held,
        small,
    ) = refs[batch:]
    f32 = jnp.float32
    for bits in range(batch):
        held[batch_index[0] ^ bits] = entries[bits][...]
    in_rows = in_out.shape[0] // batch
    width = pre_gain_out.shape[0]
    parts = width // channels
    total = parts * 3 * in_rows
    rows = small.shape[1]
    for place in range(batch):
        small[place] = held[place, total : total + rows, :].astype(f32) + held[
            place, total + rows :, :
        ].astype(f32)

    def gather(place, carry):
        block = held[place, :total, :].astype(f32)
        tiles = []
        for group in range(3):
            for part in range(parts):
                at = (part * 3 + group) * in_rows
                tiles.append(block[at : at + in_rows, :channels])
        in_out[pl.ds(pl.multiple_of(place * in_rows, in_rows), in_rows), :] = jnp.concatenate(
            tiles, axis=1
        )
        return carry

    lax.fori_loop(0, batch, gather, 0)
    everywhere = small.at[:, :SHARED_ROWS, :]
    per = width // LANES
    at = 0
    for target in (
        pre_gain_out,
        pre_bias_out,
        out_bias_out,
        post_gain_out,
        post_bias_out,
        down_bias_out,
        up_bias_out,
    ):
        count = target.shape[0] // LANES
        target[...] = lane_row(take_rows(everywhere, at, count)).reshape(target.shape)
        at += count
    fhid = third_out.shape[0]
    pair = take_rows(everywhere, at, fhid)
    third_out[...] = pair[:, :fhid]
    inner_out[...] = pair[:, fhid : 2 * fhid]
    at += fhid
    tail = take_rows(everywhere, at, pos_out.shape[0] + 4)
    pos_out[...] = tail[: pos_out.shape[0], :fhid]
    for place, target in enumerate((pos_bias_out, inner_bias_out, third_bias_out, freq_out)):
        row = pos_out.shape[0] + place
        target[...] = tail[row : row + 1, :fhid].reshape(target.shape)

    def laid(number):
        place, row = divmod(number, LAID_ROWS)
        return [
            small[place, SHARED_ROWS + part * LAID_ROWS + row :][:1, :channels]
            for part in range(parts)
        ]

    for number in range(5):
        tiles = [tile for group in range(3) for tile in laid(3 * number + group)]
        row = jnp.concatenate(tiles, axis=1)
        if number < 3:
            taps_out[number : number + 1, :] = row
        elif number == 3:
            tap_bias_out[...] = row.reshape(tap_bias_out.shape)
        else:
            in_bias_out[...] = row.reshape(in_bias_out.shape)
    own = small.at[:, SHARED_ROWS + parts * LAID_ROWS :, :]
    for order in range(2):
        filter_out[order] = take_rows(own, order * fhid, fhid)[:, :channels]
    rates_out[...] = take_rows(own, 2 * fhid, 2)[:, :channels]
    skips_out[...] = take_rows(own, 2 * fhid + 2, 2)[:, :channels]


def swapped(value, axis, bits):
    count = lax.axis_size(axis)
    return lax.ppermute(value, axis, [(source, source ^ bits) for source in range(count)])


def over_batch(value):
    held = {0: value}
    bits = lax.axis_size("batch") // 2
    while bits:
        held.update({place ^ bits: swapped(member, "batch", bits) for place, member in held.items()})
        bits //= 2
    return [held[place] for place in range(len(held))]


def natural(entries, index):
    stacked = jnp.stack(entries)
    return [
        lax.dynamic_index_in_dim(stacked, index ^ place, 0, keepdims=False)
        for place in range(len(entries))
    ]


def halves(total, index, bits, left):
    shape = total.shape[1:]
    place = left.index(bits)
    before = 1 << (len(left) - 1 - place)
    after = 1 << place
    view = total.reshape((before, 2, after) + shape)
    bit = (index // bits) % 2
    keep = lax.dynamic_index_in_dim(view, bit, 1, keepdims=False)
    send = lax.dynamic_index_in_dim(view, 1 - bit, 1, keepdims=False)
    return keep.reshape((before * after,) + shape), send.reshape((before * after,) + shape)


def halved(total, axis, index, order):
    count = lax.axis_size(axis)
    left = [1 << k for k in range(count.bit_length() - 1)]
    for bits in order:
        keep, send = halves(total, index, bits, left)
        got = swapped(send.astype(jnp.bfloat16), axis, bits)
        total = keep + got.astype(jnp.float32)
        left.remove(bits)
    return total[0]


def dense_device(
    inputs,
    pre_gain,
    pre_bias,
    in_weight,
    input_projection_bias,
    short_weight,
    short_bias,
    pos_weight,
    pos_bias,
    inner_weight,
    inner_bias,
    filter_third_weight,
    third_bias,
    sine_freq,
    filter_weight,
    decay_rates,
    skip_gains,
    out_weight,
    out_bias,
    post_gain,
    post_bias,
    up_weight,
    up_bias,
    down_weight,
    down_bias,
    cotangent,
):
    seq_parts = lax.axis_size("seq")
    batch_parts = lax.axis_size("batch")
    seq_rank = lax.axis_index("seq")
    batch_rank = lax.axis_index("batch")
    tokens = inputs[0]
    tok_count, width = tokens.shape
    length = tok_count * seq_parts
    channels = width // seq_parts
    hidden_units = up_weight.shape[1]
    fhid = pos_weight.shape[1]
    f32, low = jnp.float32, jnp.bfloat16
    wide = 3 * LANES
    start = seq_rank * channels
    bit_list = [1 << k for k in range(seq_parts.bit_length() - 1)]
    swap_list = [bit_list[1], bit_list[0]] + bit_list[2:]
    batch_bits = [1 << k for k in range(batch_parts.bit_length() - 1)]

    tokens, grad_top, own_normed = call_kernel(
        norm_kernel,
        [((tok_count, width), low)] * 3,
        [tokens, cotangent[0], pre_gain, pre_bias],
        micros=1,
        scratch=[((width // LANES, tok_count, LANES), f32)],
        name="norm",
    )
    chunks = {0: own_normed}
    for bits in range(2, seq_parts, 2):
        chunks[bits] = swapped(own_normed, "seq", bits)

    quarters = hidden_units // width
    half = length // 2
    seq_scalar = seq_rank.astype(jnp.int32)[None]
    batch_scalar = batch_rank.astype(jnp.int32)[None]
    start_scalar = start.astype(jnp.int32)[None]
    wave, turn, rows, in_local, rows_local, weights_local, rates_local, vectors = call_kernel(
        lambda *refs: wave_kernel(channels, *refs),
        [
            ((length, half), low),
            ((length, LANES), f32),
            ((ROW_COUNT, width), f32),
            ((width, wide), low),
            ((ROW_COUNT, LANES), f32),
            ((fhid, 2 * LANES), f32),
            ((1, 2 * LANES), f32),
            ((4, fhid), f32),
        ],
        [
            start_scalar,
            pre_gain,
            pre_bias,
            input_projection_bias,
            short_bias,
            short_weight,
            skip_gains,
            post_gain,
            post_bias,
            out_bias,
            down_bias,
            up_bias,
            pos_bias,
            inner_bias,
            third_bias,
            sine_freq,
            filter_weight,
            decay_rates,
            in_weight,
        ],
        micros=8.5,
        spaces="s" + "v" * 17 + "h" + "h" + "v" * 7,
        scratch=[
            ((4, 32, half), f32),
            ((length, half), low),
            ((width, 3 * width), low),
            2,
        ],
        name="waves",
    )
    even = [chunks[bits] for bits in range(2, seq_parts, 2)]
    wave, *even = lax.optimization_barrier((wave, *even))
    for bits in range(0, seq_parts, 2):
        if bits:
            chunks[bits] = even[bits // 2 - 1]
        chunks[bits + 1] = swapped(chunks[bits], "seq", 1)
    spectrum, kernels, filter_waves = call_kernel(
        filter_kernel,
        [
            ((2, length, 2 * LANES), f32),
            ((length, 2 * LANES), f32),
            ((3, half, 4 * fhid), f32),
        ],
        [
            pos_weight,
            inner_weight,
            filter_third_weight,
            vectors,
            weights_local,
            rates_local,
            turn,
            wave,
        ],
        micros=13,
        spaces="v" * 7 + "h" + "vvv",
        scratch=[
            ((length, 2 * LANES), low),
            ((length, 2 * LANES), low),
            ((length, half), low),
            1,
        ],
        name="filters",
    )
    dense = tok_count * channels // LANES
    (
        normed,
        projected,
        product,
        gate,
        after,
        gated,
        product_wave,
        gated_wave,
        mixed,
        mixer_chan,
    ) = call_kernel(
        lambda *refs: front_kernel(seq_parts, *refs),
        [
            ((length, width), low),
            ((2, PAD + half, wide), f32),
            ((half, 2 * LANES), low),
            ((half, 2 * LANES), low),
            ((half, 2 * LANES), low),
            ((half, 2 * LANES), low),
            ((2, length, LANES), f32),
            ((2, length, LANES), f32),
            ((2, half, 2 * LANES), f32),
            ((seq_parts, dense, LANES), low),
        ],
        [seq_scalar]
        + [chunks[part] for part in range(seq_parts)]
        + [in_local, rows_local, wave, turn, spectrum],
        micros=13,
        spaces="s" + "v" * seq_parts + "vvhhh" + "hhvvvvhhhv",
        scratch=[
            ((length, width), low),
            ((half, 2 * LANES), low),
            ((half, 2 * LANES), low),
            ((length, half), low),
            ((length, LANES), f32),
            ((2, length, 2 * LANES), f32),
            ((2, PAD + half, wide), f32),
            ((2, length, LANES), f32),
            ((2, length, LANES), f32),
            ((2, half, 2 * LANES), f32),
            ((half, 2 * LANES), low),
            8,
        ],
        name="front",
    )
    tops = over_batch(grad_top)
    mixer_back = lax.all_to_all(mixer_chan, "seq", 0, 0, tiled=True)
    mixer_back, *tops = lax.optimization_barrier((mixer_back, *tops))

    quarter = hidden_units // batch_parts
    branch_quarter = width // batch_parts
    rows_quarter = hidden_units // (seq_parts * batch_parts)
    assert quarter == width and seq_parts * rows_quarter == width
    up_width = quarter + branch_quarter
    padded = quarter + -(-branch_quarter // LANES) * LANES
    message = padded + width
    outputs, grad_residual, grad_mixer, middle_sums, sides, *gots = call_kernel(
        lambda *refs: middle_kernel(seq_parts, *refs),
        [
            ((tok_count, width), f32),
            ((tok_count, width), f32),
            ((seq_parts, dense, LANES), low),
            (((4 * width + hidden_units) // LANES, LANES), f32),
        ]
        + [((tok_count, 2 * width), low)]
        + [((tok_count, message), low)] * batch_parts,
        [
            batch_scalar,
            mixer_back,
            tokens,
            grad_top,
            rows,
            out_weight,
            up_weight,
            down_weight,
        ],
        micros=11,
        spaces="svvvvhhh" + "v" * (5 + batch_parts),
        scratch=[
            ((width, width), low),
            ((quarters, width, width), low),
            ((quarters, width, width), low),
            ((tok_count, width), f32),
            ((tok_count, width), f32),
            ((tok_count, width), f32),
            ((quarters, tok_count, width), low),
            ((quarters, tok_count, width), low),
            ((batch_parts, tok_count, width), low),
            ((batch_parts, tok_count, padded - quarter), low),
            ((quarters, 1, width), f32),
            ((width // LANES, tok_count, LANES), f32),
            1 + 2 * quarters,
        ],
        name="middle",
    )
    grad_mixer_chan = lax.all_to_all(grad_mixer, "seq", 0, 0, tiled=True)

    def bit_of(bits):
        return ((seq_rank // bits) % 2).astype(jnp.int32)[None]

    def fold(keep, got, bits, left):
        size = keep.shape[0] // 2
        block = keep.shape[1:]
        place = left.index(bits)
        return call_kernel(
            lambda *refs: fold_kernel(1 << place, *refs),
            [((size,) + block, f32), ((size,) + block, low)],
            [bit_of(bits), keep, got],
            micros=1,
            spaces="svvvv",
            limit=12,
        name="fold",
        )

    grad_mixer_chan = lax.all_to_all(grad_mixer, "seq", 0, 0, tiled=True)
    sides = over_batch(sides)
    gots = [gots[0]] + [swapped(gots[bits], "batch", bits) for bits in range(1, batch_parts)]
    rows_each = width // seq_parts

    blocks = length // BLOCK
    packed, grad_proj, grad_kernels, sums = call_kernel(
        lambda *refs: back_kernel(channels, *refs),
        [
            ((seq_parts, 3 * dense, LANES), low),
            ((length, wide), low),
            ((2, half, 2 * LANES), f32),
            ((24, LANES), f32),
        ],
        [
            grad_mixer_chan,
            product,
            gate,
            after,
            gated,
            rows_local,
            turn,
            product_wave,
            gated_wave,
            spectrum,
            wave,
            projected,
            mixed,
        ],
        micros=15,
        spaces="v" * 7 + "h" * 6 + "vvvv",
        scratch=[((half, 2 * LANES), low)] * 4
        + [
            ((half, 4 * LANES), low),
            ((half, 4 * LANES), low),
            ((length, half), low),
            ((2, length, 2 * LANES), f32),
            ((2, length, LANES), f32),
            ((2, length, LANES), f32),
            ((2, PAD + half, wide), f32),
            ((2, half, 2 * LANES), f32),
            ((3, 2, half + PAD, LANES), f32),
            6,
        ],
        name="back",
    )
    proj_back = lax.all_to_all(packed, "seq", 0, 0, tiled=True)
    orders = (bit_list, swap_list)
    halves_of = [
        ((seq_parts // 2, rows_each, columns), dtype)
        for columns in (width, width + branch_quarter)
        for dtype in (f32, low)
    ]
    up_keep, up_send, rest_keep, rest_send = call_kernel(
        lambda *refs: weight_kernel(batch_parts, (orders[0][0], orders[1][0]), *refs),
        halves_of,
        [jnp.concatenate([bit_of(order[0]) for order in orders])] + sides + tops + gots,
        micros=6,
        spaces="s" + "v" * (3 * batch_parts + 4),
        scratch=[
            ((3 * width, batch_parts * tok_count), low),
            ((batch_parts * tok_count, width + padded), low),
            ((width, width), f32),
            ((width, width + branch_quarter), f32),
        ],
        name="weights",
    )
    up_got = swapped(up_send, "seq", orders[0][0])
    rest_got = swapped(rest_send, "seq", orders[1][0])

    pair_part = left_dot(normed, grad_proj)
    in_rows = width // (seq_parts * batch_parts)
    in_count = 3 * in_rows
    in_part = (
        pair_part.reshape(seq_parts, batch_parts, in_rows, 3, LANES)
        .transpose(1, 0, 3, 2, 4)
        .reshape(batch_parts, seq_parts * in_count, LANES)
    )
    small_rows = SHARED_ROWS + LAID_ROWS + OWN_ROWS
    in_part, pair_part, up_keep, rest_keep = lax.optimization_barrier(
        (in_part, pair_part, up_keep, rest_keep)
    )
    (small,) = call_kernel(
        chain_kernel,
        [((batch_parts, small_rows, LANES), f32)],
        [
            rows,
            in_local,
            sums,
            middle_sums,
            pos_weight,
            inner_weight,
            filter_third_weight,
            vectors,
            weights_local,
            rates_local,
            grad_kernels.reshape(length, 2 * LANES),
            kernels,
            filter_waves,
            pair_part,
        ],
        micros=12,
        spaces="v" * 10 + "hhhh" + "v",
        scratch=[
            ((2 * fhid, 4 * LANES), f32),
            ((1, 2 * LANES), f32),
            ((2 * fhid + 40, fhid), f32),
            ((3, LANES + 8, 2 * fhid), f32),
            ((length, 2 * LANES), f32),
            ((length, 2 * LANES), f32),
            ((3, length // 2, 4 * fhid), f32),
            ((width, wide), f32),
            5 * (blocks // 2) + 1,
        ],
        name="chain",
    )
    small, proj_back = lax.optimization_barrier((small, proj_back))

    def next_fold(keep, got, order, step):
        left = [bits for bits in bit_list if bits not in order[:step]]
        return fold(keep, got, order[step], left)

    left = list(batch_bits)
    for bits in batch_bits[:-1]:
        in_keep, in_send = halves(in_part, batch_rank, bits, left)
        small_keep, small_send = halves(small, batch_rank, bits, left)
        in_part = in_keep + swapped(in_send.astype(low), "batch", bits).astype(f32)
        small = small_keep + swapped(small_send, "batch", bits)
        left.remove(bits)
    in_keep, in_send = halves(in_part, batch_rank, batch_bits[-1], left)
    small_keep, small_send = halves(small, batch_rank, batch_bits[-1], left)
    shared_count = in_count + 2 * (SHARED_ROWS + LAID_ROWS)
    mixed_send, small = call_kernel(
        spread_kernel,
        [((seq_parts, shared_count, LANES), low), ((small_rows, LANES), f32)],
        [
            in_keep[0],
            swapped(in_send.astype(low), "batch", batch_bits[-1])[0],
            small_keep[0],
            swapped(small_send, "batch", batch_bits[-1])[0],
        ],
        micros=2,
        limit=12,
        name="spread",
    )
    up_keep, up_send = next_fold(up_keep, up_got, orders[0], 1)
    rest_keep, rest_send = next_fold(rest_keep, rest_got, orders[1], 1)
    up_got = swapped(up_send, "seq", orders[0][1])
    rest_got = swapped(rest_send, "seq", orders[1][1])
    mixed_send, proj_back = lax.optimization_barrier((mixed_send, proj_back))
    mixed_got = lax.all_to_all(mixed_send, "seq", 0, 0, tiled=True)
    (grad_inputs,) = call_kernel(
        final_kernel,
        [((tok_count, width), f32)],
        [proj_back, tokens, grad_residual, rows, in_weight],
        micros=5.5,
        spaces="vvvvhv",
        scratch=[
            ((width, 3 * width), low),
            ((tok_count, 3 * width), low),
            ((width // LANES, tok_count, LANES), f32),
            1,
        ],
        name="final",
    )
    done_rows = SHARED_ROWS + seq_parts * LAID_ROWS + OWN_ROWS
    (last,) = call_kernel(
        merge_kernel,
        [((seq_parts * in_count + 2 * done_rows, LANES), low)],
        [mixed_got, small],
        micros=2,
        limit=12,
        name="merge",
    )
    up_keep, up_send = next_fold(up_keep, up_got, orders[0], 2)
    rest_keep, rest_send = next_fold(rest_keep, rest_got, orders[1], 2)
    up_got = swapped(up_send, "seq", orders[0][2])
    rest_got = swapped(rest_send, "seq", orders[1][2])
    lasts = over_batch(last)
    up_got, grad_inputs, last = lax.optimization_barrier((up_got, grad_inputs, last))
    total = -(-(2 * width + branch_quarter) // LANES) * LANES
    (weights_done,) = call_kernel(
        last_fold_kernel,
        [((rows_each, total), low)],
        [up_keep, up_got, rest_keep, rest_got],
        micros=1,
        limit=12,
        name="last_fold",
    )
    (
        final_in,
        grad_pre_gain,
        grad_pre_bias,
        grad_out_bias,
        grad_post_gain,
        grad_post_bias,
        grad_down_bias,
        grad_up_bias,
        grad_third,
        grad_inner,
        grad_pos,
        grad_pos_bias,
        grad_inner_bias,
        grad_third_bias,
        grad_freq,
        grad_taps,
        grad_tap_bias,
        grad_in_bias,
        grad_filter,
        grad_rates,
        grad_skips,
    ) = call_kernel(
        lambda *refs: finish_kernel(batch_parts, channels, *refs),
        [
            ((batch_parts * in_rows, 3 * width), f32),
            ((width,), f32),
            ((width,), f32),
            ((width,), f32),
            ((width,), f32),
            ((width,), f32),
            ((width,), f32),
            ((hidden_units,), f32),
            (filter_third_weight.shape, f32),
            (inner_weight.shape, f32),
            (pos_weight.shape, f32),
            ((fhid,), f32),
            ((fhid,), f32),
            ((fhid,), f32),
            ((fhid,), f32),
            ((3, 3 * width), f32),
            ((3 * width,), f32),
            ((3 * width,), f32),
            ((2, fhid, channels), f32),
            ((2, channels), f32),
            ((2, channels), f32),
        ],
        [batch_scalar] + lasts,
        micros=3,
        spaces="s" + "v" * batch_parts + "v" * 21,
        scratch=[
            ((batch_parts,) + last.shape, low),
            ((batch_parts, done_rows, LANES), f32),
        ],
        limit=12,
        name="finish",
    )
    entries = {0: weights_done, batch_parts // 2: swapped(weights_done, "batch", batch_parts // 2)}
    entries[batch_parts // 2], final_in = lax.optimization_barrier(
        (entries[batch_parts // 2], final_in)
    )
    bits = batch_parts // 4
    while bits:
        entries.update(
            {place ^ bits: swapped(member, "batch", bits) for place, member in entries.items()}
        )
        bits //= 2
    entries = [entries[place] for place in range(batch_parts)]
    final_down, final_up, final_out = call_kernel(
        lambda *refs: collect_kernel(batch_parts, *refs),
        [
            ((batch_parts * rows_each, width), f32),
            ((rows_each, hidden_units), f32),
            ((rows_each, width), f32),
        ],
        [batch_scalar] + entries,
        micros=3,
        spaces="s" + "v" * (batch_parts + 3),
        scratch=[((batch_parts, rows_each, total), low)],
        limit=12,
        name="collect",
    )
    return (
        outputs[None],
        grad_inputs[None],
        grad_pre_gain,
        grad_pre_bias,
        final_in,
        grad_in_bias,
        grad_taps,
        grad_tap_bias,
        grad_pos,
        grad_pos_bias,
        grad_inner,
        grad_inner_bias,
        grad_third,
        grad_third_bias,
        grad_freq,
        grad_filter,
        grad_rates,
        grad_skips,
        final_out,
        grad_out_bias,
        grad_post_gain,
        grad_post_bias,
        final_up,
        grad_up_bias,
        final_down,
        grad_down_bias,
    )


def per_device(*args):
    tokens, parts = args[0].shape[1], lax.axis_size("seq")
    channels = args[0].shape[2] // parts
    dense = tokens * parts <= DENSE_LIMIT and lays_dense(tokens, channels)
    return (dense_device if dense else factored_device)(*args)


def solution(mesh):
    in_specs = (
        P("batch", "seq", None),
        P(),
        P(),
        P(),
        P(),
        P(),
        P(),
        P(),
        P(),
        P(),
        P(),
        P(),
        P(),
        P(),
        P(),
        P(),
        P(),
        P(),
        P(),
        P(),
        P(),
        P(),
        P(),
        P(),
        P(),
        P("batch", "seq", None),
    )
    out_specs = (
        P("batch", "seq", None),
        P("batch", "seq", None),
        P(),
        P(),
        P("seq", None),
        P(),
        P(),
        P(),
        P(),
        P(),
        P(),
        P(),
        P(),
        P(),
        P(),
        P(None, None, "seq"),
        P(None, "seq"),
        P(None, "seq"),
        P("seq", None),
        P(),
        P(),
        P(),
        P("seq", None),
        P(),
        P("seq", None),
        P(),
    )
    return jax.shard_map(
        per_device, mesh=mesh, in_specs=in_specs, out_specs=out_specs, check_vma=False
    )
```

```python
import math

import jax
import jax.numpy as jnp
import numpy as np
from jax import lax
from jax.experimental import pallas as pl
from jax.experimental.pallas import tpu as pltpu
from jax.sharding import PartitionSpec as P

epsilon = 1e-05
highest_accuracy = lax.Precision.HIGHEST


def passed_along(value, axis, steps):
    count = lax.axis_size(axis)
    initial, last = (max(0, -steps), min(count, count - steps))
    return lax.ppermute(value, axis, [(source, source + steps) for source in range(initial, last)])


def plain_dot(left_side, right_side):
    return jnp.dot(left_side, right_side, preferred_element_type=jnp.float32)


def exact_tdot(left_side, right_side):
    return lax.dot_general(
        left_side,
        right_side,
        (((0,), (0,)), ((), ())),
        precision=highest_accuracy,
        preferred_element_type=jnp.float32,
    )


def left_dot(left_side, right_side):
    return lax.dot_general(
        left_side, right_side, (((0,), (0,)), ((), ())), preferred_element_type=jnp.float32
    )


def right_dot(left_side, right_side):
    return lax.dot_general(
        left_side, right_side, (((1,), (1,)), ((), ())), preferred_element_type=jnp.float32
    )


def rounded(values):
    return lax.optimization_barrier(values.astype(jnp.bfloat16)).astype(jnp.float32)


def norm_forward(values, gain_vec, shift_vec):
    centre = values - jnp.mean(values, axis=-1, keepdims=True)
    inv_std = lax.rsqrt(jnp.mean(centre * centre, axis=-1, keepdims=True) + epsilon)
    unit_rows = centre * inv_std
    return (unit_rows * gain_vec + shift_vec, unit_rows, inv_std)


def norm_backward(grad_out, unit_rows, inv_std, gain_vec):
    grad_unit = grad_out * gain_vec
    grad_values = inv_std * (
        grad_unit
        - jnp.mean(grad_unit, axis=-1, keepdims=True)
        - unit_rows * jnp.mean(grad_unit * unit_rows, axis=-1, keepdims=True)
    )
    return (grad_values, jnp.sum(grad_out * unit_rows, axis=0), jnp.sum(grad_out, axis=0))


def position_rows(length, feat_count):
    steps_pos = jnp.arange(length, dtype=jnp.float32)
    time_steps = steps_pos / (length - 1)
    band_count = (feat_count - 1) // 2
    frequency = jnp.linspace(0.0001, band_count - 1, band_count, dtype=jnp.float32)
    angles = frequency[:, None] * (steps_pos * (2.0 * math.pi / length))[None, :]
    features_t = jnp.concatenate([time_steps[None, :], jnp.cos(angles), -jnp.sin(angles)], axis=0)
    return (features_t, time_steps)


def body_filters(
    features_t,
    time_steps,
    pos_weight,
    pos_bias,
    inner_weight,
    inner_bias,
    filter_third_weight,
    third_bias,
    sine_freq,
    weight_local,
    rates_local,
):
    hidden = jnp.sin(sine_freq[:, None] * (exact_tdot(pos_weight, features_t) + pos_bias[:, None]))
    hidden = jnp.sin(sine_freq[:, None] * (exact_tdot(inner_weight, hidden) + inner_bias[:, None]))
    hidden = jnp.sin(
        sine_freq[:, None] * (exact_tdot(filter_third_weight, hidden) + third_bias[:, None])
    )
    first_kernel = exact_tdot(weight_local[0], hidden) * jnp.exp(
        -rates_local[0][:, None] * time_steps[None, :]
    )
    second_kernel = exact_tdot(weight_local[1], hidden) * jnp.exp(
        -rates_local[1][:, None] * time_steps[None, :]
    )
    return (first_kernel, second_kernel)


def split_sizes(extent):
    outer_size = math.gcd(extent // 2, 1 << (extent.bit_length() - 1) // 2)
    return (outer_size, extent // outer_size)


def dft_rect(row_count, col_count, modulus, direction):
    row_ids = jnp.arange(row_count, dtype=jnp.int32)[:, None]
    col_ids = jnp.arange(col_count, dtype=jnp.int32)[None, :]
    angles = (row_ids * col_ids % modulus).astype(jnp.float32) * (2.0 * math.pi / modulus)
    return (jnp.cos(angles), direction * jnp.sin(angles))


def first_section(block_groups, lookup_grid):
    return jnp.einsum(
        "cij,ik->ckj",
        block_groups,
        lookup_grid,
        precision=highest_accuracy,
        preferred_element_type=jnp.float32,
    )


def second_section(block_groups, lookup_grid):
    return jnp.einsum(
        "dhq,qn->dnh",
        block_groups,
        lookup_grid,
        precision=highest_accuracy,
        preferred_element_type=jnp.float32,
    )


def padded_spectrum(signal):
    channels, length = signal.shape
    extent = 2 * length
    outer_size, inner_size = split_sizes(extent)
    block_groups = signal.reshape(channels, inner_size // 2, outer_size)
    cos_inner, sin_inner = dft_rect(inner_size // 2, inner_size, inner_size, -1.0)
    section_real = first_section(block_groups, cos_inner)
    section_imag = first_section(block_groups, sin_inner)
    twist_cos, rotation_sine = dft_rect(inner_size, outer_size, extent, -1.0)
    turned_real = section_real * twist_cos - section_imag * rotation_sine
    turned_imag = section_real * rotation_sine + section_imag * twist_cos
    cos_outer, sin_outer = dft_rect(outer_size, outer_size, outer_size, -1.0)
    out_real = second_section(turned_real, cos_outer) - second_section(turned_imag, sin_outer)
    out_imag = second_section(turned_real, sin_outer) + second_section(turned_imag, cos_outer)
    return (out_real.reshape(channels, extent), out_imag.reshape(channels, extent))


def inverse_real(spec_real, spec_imag):
    channels, extent = spec_real.shape
    outer_size, inner_size = split_sizes(extent)
    blocks_real = spec_real.reshape(channels, inner_size, outer_size)
    blocks_imag = spec_imag.reshape(channels, inner_size, outer_size)
    cos_inner, sin_inner = dft_rect(inner_size, inner_size, inner_size, 1.0)
    section_real = first_section(blocks_real, cos_inner) - first_section(blocks_imag, sin_inner)
    section_imag = first_section(blocks_real, sin_inner) + first_section(blocks_imag, cos_inner)
    twist_cos, rotation_sine = dft_rect(inner_size, outer_size, extent, 1.0)
    turned_real = section_real * twist_cos - section_imag * rotation_sine
    turned_imag = section_real * rotation_sine + section_imag * twist_cos
    cos_outer, sin_outer = dft_rect(outer_size, outer_size // 2, outer_size, 1.0)
    out_real = second_section(turned_real, cos_outer) - second_section(turned_imag, sin_outer)
    return out_real.reshape(channels, extent // 2) / extent


def times_spec(left_real, left_imag, right_real, right_imag):
    return (
        left_real * right_real - left_imag * right_imag,
        left_real * right_imag + left_imag * right_real,
    )


def times_conj(left_real, left_imag, right_real, right_imag):
    return (
        left_real * right_real + left_imag * right_imag,
        left_imag * right_real - left_real * right_imag,
    )


def factored_device(
    inputs,
    pre_gain,
    pre_bias,
    in_weight,
    input_projection_bias,
    short_weight,
    short_bias,
    pos_weight,
    pos_bias,
    inner_weight,
    inner_bias,
    filter_third_weight,
    third_bias,
    sine_freq,
    filter_weight,
    decay_rates,
    skip_gains,
    out_weight,
    out_bias,
    post_gain,
    post_bias,
    up_weight,
    up_bias,
    down_weight,
    down_bias,
    cotangent,
):
    seq_parts = lax.axis_size("seq")
    seq_rank = lax.axis_index("seq")
    tokens = inputs[0]
    tok_count = tokens.shape[0]
    model_width = tokens.shape[1]
    length = tok_count * seq_parts
    channels = model_width // seq_parts
    tokens_wide = tokens.astype(jnp.float32)
    pre_gain_f = pre_gain.astype(jnp.float32)
    pre_bias_f = pre_bias.astype(jnp.float32)
    in_bias_f = input_projection_bias.astype(jnp.float32)
    short_f = short_weight.astype(jnp.float32)
    short_bias_f = short_bias.astype(jnp.float32)
    out_bias_f = out_bias.astype(jnp.float32)
    post_gain_f = post_gain.astype(jnp.float32)
    post_bias_f = post_bias.astype(jnp.float32)
    up_bias_f = up_bias.astype(jnp.float32)
    down_bias_f = down_bias.astype(jnp.float32)
    normed, unit_pre, inv_pre = norm_forward(tokens_wide, pre_gain_f, pre_bias_f)
    normed_low = normed.astype(jnp.bfloat16)
    projected = plain_dot(normed_low, in_weight) + in_bias_f
    previous = passed_along(projected[tok_count - 2 :], "seq", 1)
    extended = jnp.concatenate([previous, projected], axis=0)
    mixed_conv = (
        short_f[0] * extended[:-2]
        + short_f[1] * extended[1:-1]
        + short_f[2] * extended[2:]
        + short_bias_f
    )
    value_part = mixed_conv[:, :model_width]
    gate_one = mixed_conv[:, model_width : 2 * model_width]
    gate_two = mixed_conv[:, 2 * model_width :]
    product_low = (value_part * gate_one).astype(jnp.bfloat16)
    gate_two_low = gate_two.astype(jnp.bfloat16)
    prod_chan, gate_chan = (
        lax.all_to_all(product_low.T, "seq", split_axis=0, concat_axis=1, tiled=True),
        lax.all_to_all(gate_two_low.T, "seq", split_axis=0, concat_axis=1, tiled=True),
    )
    features_t, time_steps = position_rows(length, pos_weight.shape[0])
    chan_start = seq_rank * channels
    weight_local = lax.dynamic_slice_in_dim(
        filter_weight.astype(jnp.float32), chan_start, channels, 2
    )
    rates_local = lax.dynamic_slice_in_dim(decay_rates, chan_start, channels, 1)
    skips_local = lax.dynamic_slice_in_dim(skip_gains.astype(jnp.float32), chan_start, channels, 1)
    skip_one = skips_local[0][:, None]
    skip_two = skips_local[1][:, None]
    shared = tuple(
        (
            member.astype(jnp.float32)
            for member in (
                pos_weight,
                pos_bias,
                inner_weight,
                inner_bias,
                filter_third_weight,
                third_bias,
                sine_freq,
            )
        )
    )

    def local_filters(*params):
        return body_filters(features_t, time_steps, *params)

    (kernel_one, kernel_two), filter_pull = jax.vjp(
        local_filters, *shared, weight_local, rates_local
    )
    prod_wide = prod_chan.astype(jnp.float32)
    gate_wide = gate_chan.astype(jnp.float32)
    prod_real, prod_imag = padded_spectrum(prod_wide)
    kone_real, kone_imag = padded_spectrum(kernel_one)
    convolved_real_part, conv_imag = times_spec(prod_real, prod_imag, kone_real, kone_imag)
    after_one = rounded(inverse_real(convolved_real_part, conv_imag) + skip_one * prod_wide)
    gated_low = rounded(after_one * gate_wide)
    gated_real, gated_imag = padded_spectrum(gated_low)
    ktwo_real, ktwo_imag = padded_spectrum(kernel_two)
    convolved_real_part, conv_imag = times_spec(gated_real, gated_imag, ktwo_real, ktwo_imag)
    mixer_chan = (inverse_real(convolved_real_part, conv_imag) + skip_two * gated_low).astype(
        jnp.bfloat16
    )
    mixer_tok = lax.all_to_all(mixer_chan, "seq", split_axis=1, concat_axis=0, tiled=True).T
    branch = plain_dot(mixer_tok, out_weight) + out_bias_f
    residual = tokens_wide + branch
    normed_two, unit_post, inv_post = norm_forward(residual, post_gain_f, post_bias_f)
    normed_two_low = normed_two.astype(jnp.bfloat16)
    upper_pre = plain_dot(normed_two_low, up_weight) + up_bias_f
    activated = jax.nn.gelu(upper_pre, approximate=False).astype(jnp.bfloat16)
    outputs = residual + plain_dot(activated, down_weight) + down_bias_f
    grad_top = cotangent[0]
    grad_top_wide = grad_top.astype(jnp.float32)
    grad_act = right_dot(grad_top, down_weight)
    grad_down = left_dot(activated, grad_top)
    grad_down_bias = jnp.sum(grad_top_wide, axis=0)
    gelu_slope = (
        0.5 * (1.0 + lax.erf(upper_pre * 0.7071067811865476))
        + upper_pre * jnp.exp(-0.5 * upper_pre * upper_pre) * 0.3989422804014327
    )
    grad_upper = (grad_act * gelu_slope).astype(jnp.bfloat16)
    grad_up = left_dot(normed_two_low, grad_upper)
    grad_up_bias = jnp.sum(grad_upper.astype(jnp.float32), axis=0)
    grad_normed_two = right_dot(grad_upper, up_weight)
    grad_resid_norm, grad_post_gain, grad_post_bias = norm_backward(
        grad_normed_two, unit_post, inv_post, post_gain_f
    )
    grad_residual = grad_top_wide + grad_resid_norm
    grad_branch = grad_residual.astype(jnp.bfloat16)
    grad_out = left_dot(mixer_tok, grad_branch)
    grad_out_bias = jnp.sum(grad_branch.astype(jnp.float32), axis=0)
    grad_mixer = right_dot(grad_branch, out_weight).astype(jnp.bfloat16)
    grad_mixer_chan = lax.all_to_all(
        grad_mixer.T, "seq", split_axis=0, concat_axis=1, tiled=True
    ).astype(jnp.float32)
    gmix_real, gmix_imag = padded_spectrum(grad_mixer_chan)
    corr_real, corr_imag = times_conj(gmix_real, gmix_imag, ktwo_real, ktwo_imag)
    grad_gated = rounded(inverse_real(corr_real, corr_imag) + skip_two * grad_mixer_chan)
    corr_real, corr_imag = times_conj(gmix_real, gmix_imag, gated_real, gated_imag)
    grad_kernel_two = inverse_real(corr_real, corr_imag)
    grad_skip_two = jnp.sum(grad_mixer_chan * gated_low, axis=1)
    grad_after = rounded(grad_gated * gate_wide)
    grad_gate_two = (grad_gated * after_one).astype(jnp.bfloat16)
    gaft_real, gaft_imag = padded_spectrum(grad_after)
    corr_real, corr_imag = times_conj(gaft_real, gaft_imag, kone_real, kone_imag)
    grad_product = (inverse_real(corr_real, corr_imag) + skip_one * grad_after).astype(jnp.bfloat16)
    corr_real, corr_imag = times_conj(gaft_real, gaft_imag, prod_real, prod_imag)
    grad_kernel_one = inverse_real(corr_real, corr_imag)
    grad_skip_one = jnp.sum(grad_after * prod_wide, axis=1)
    filter_grads = filter_pull((grad_kernel_one, grad_kernel_two))
    grad_prod_back, grad_gate_back = (
        lax.all_to_all(grad_product, "seq", split_axis=1, concat_axis=0, tiled=True),
        lax.all_to_all(grad_gate_two, "seq", split_axis=1, concat_axis=0, tiled=True),
    )
    grad_prod_wide = grad_prod_back.T.astype(jnp.float32)
    grad_mixed = jnp.concatenate(
        [
            grad_prod_wide * gate_one,
            grad_prod_wide * value_part,
            grad_gate_back.T.astype(jnp.float32),
        ],
        axis=1,
    )
    grad_short_bias = jnp.sum(grad_mixed, axis=0)
    grad_short = jnp.stack(
        [
            jnp.sum(grad_mixed * extended[0:tok_count], axis=0),
            jnp.sum(grad_mixed * extended[1 : tok_count + 1], axis=0),
            jnp.sum(grad_mixed * extended[2 : tok_count + 2], axis=0),
        ]
    )
    zero_rows = jnp.zeros((2, 3 * model_width), jnp.float32)
    padded_grad = jnp.concatenate([zero_rows, grad_mixed, zero_rows], axis=0)
    grad_extended = (
        short_f[0] * padded_grad[2:]
        + short_f[1] * padded_grad[1:-1]
        + short_f[2] * padded_grad[:-2]
    )
    from_next = passed_along(grad_extended[:2], "seq", -1)
    grad_projected = grad_extended[2:].at[tok_count - 2 :].add(from_next)
    grad_proj_low = grad_projected.astype(jnp.bfloat16)
    grad_in = left_dot(normed_low, grad_proj_low)
    grad_in_bias = jnp.sum(grad_proj_low.astype(jnp.float32), axis=0)
    grad_normed = right_dot(grad_proj_low, in_weight)
    grad_tokens_norm, grad_pre_gain, grad_pre_bias = norm_backward(
        grad_normed, unit_pre, inv_pre, pre_gain_f
    )
    grad_inputs = grad_residual + grad_tokens_norm
    shared_sums = lax.psum(
        (
            grad_pre_gain,
            grad_pre_bias,
            grad_in_bias,
            grad_short,
            grad_short_bias,
            filter_grads[0],
            filter_grads[1],
            filter_grads[2],
            filter_grads[3],
            filter_grads[4],
            filter_grads[5],
            filter_grads[6],
            grad_out_bias,
            grad_post_gain,
            grad_post_bias,
            grad_up_bias,
            grad_down_bias,
        ),
        ("batch", "seq"),
    )
    skip_grads = jnp.stack([grad_skip_one, grad_skip_two])
    weight_shards = (
        lax.psum_scatter(grad_in, "seq", scatter_dimension=0, tiled=True),
        lax.psum_scatter(grad_out, "seq", scatter_dimension=0, tiled=True),
        lax.psum_scatter(grad_up, "seq", scatter_dimension=0, tiled=True),
        lax.psum_scatter(grad_down, "seq", scatter_dimension=0, tiled=True),
    )
    final_in, final_out, final_up, final_down, final_filter, final_rates, final_skips = (
        lax.psum(weight_shards[0].astype(jnp.bfloat16), "batch").astype(jnp.float32),
        lax.psum(weight_shards[1].astype(jnp.bfloat16), "batch").astype(jnp.float32),
        lax.psum(weight_shards[2].astype(jnp.bfloat16), "batch").astype(jnp.float32),
        lax.psum(weight_shards[3].astype(jnp.bfloat16), "batch").astype(jnp.float32),
        lax.psum(filter_grads[7].astype(jnp.bfloat16), "batch").astype(jnp.float32),
        lax.psum(filter_grads[8].astype(jnp.bfloat16), "batch").astype(jnp.float32),
        lax.psum(skip_grads.astype(jnp.bfloat16), "batch").astype(jnp.float32),
    )
    return (
        outputs[None],
        grad_inputs[None],
        shared_sums[0],
        shared_sums[1],
        final_in,
        shared_sums[2],
        shared_sums[3],
        shared_sums[4],
        shared_sums[5],
        shared_sums[6],
        shared_sums[7],
        shared_sums[8],
        shared_sums[9],
        shared_sums[10],
        shared_sums[11],
        final_filter,
        final_rates,
        final_skips,
        final_out,
        shared_sums[12],
        shared_sums[13],
        shared_sums[14],
        final_up,
        shared_sums[15],
        final_down,
        shared_sums[16],
    )


LANES = 128
BLOCK = 256
WAVE_BLOCK = 256
PAD = 8
CHUNK = 64
DENSE_LIMIT = 2048
ROW_AT = {
    "pre_gain": 0,
    "pre_bias": 1,
    "in_bias": 2,
    "tap_bias": 5,
    "taps": 8,
    "skips": 17,
    "post_gain": 19,
    "post_bias": 20,
    "out_bias": 21,
    "down_bias": 22,
    "up_bias": 23,
}
ROW_COUNT = 32


def call_kernel(kernel, outs, args, micros, spaces="", scratch=(), limit=60, name=None):
    places = {"v": pltpu.VMEM, "s": pltpu.SMEM, "h": pl.ANY}
    spaces = spaces or "v" * (len(args) + len(outs))
    specs = [pl.BlockSpec(memory_space=places[space]) for space in spaces]
    shapes = [jax.ShapeDtypeStruct(shape, dtype) for shape, dtype in outs]
    return pl.pallas_call(
        kernel,
        out_shape=shapes,
        in_specs=specs[: len(args)],
        out_specs=specs[len(args) :],
        scratch_shapes=[
            pltpu.SemaphoreType.DMA((entry,))
            if isinstance(entry, int)
            else pltpu.VMEM(entry[0], entry[1])
            for entry in scratch
        ],
        compiler_params=pltpu.CompilerParams(vmem_limit_bytes=limit * 1024 * 1024),
        cost_estimate=pl.CostEstimate(
            flops=1, transcendentals=0, bytes_accessed=int(3.0e6 * micros)
        ),
        name=name,
    )(*args)


def row_chunks(source, target, sems, first, count):
    size = source.shape[0] // count
    return [
        pltpu.make_async_copy(
            source.at[pl.ds(place * size, size)],
            target.at[pl.ds(place * size, size)],
            sems.at[first + place],
        )
        for place in range(count)
    ]


def dense_rows(tile):
    tokens, channels = tile.shape
    rows = tokens * channels // LANES
    spare = LANES - channels
    blocks = channels // spare
    pieces = [tile[rows:, block * spare : (block + 1) * spare] for block in range(blocks)]
    return jnp.concatenate([tile[:rows], jnp.concatenate(pieces, axis=0)], axis=1)


def loose_rows(tile, tokens, channels):
    rows = tile.shape[0]
    spare = LANES - channels
    blocks = channels // spare
    rest = tokens - rows
    pieces = [tile[block * rest : (block + 1) * rest, channels:] for block in range(blocks)]
    return jnp.concatenate([tile[:, :channels], jnp.concatenate(pieces, axis=1)], axis=0)


def lays_dense(tokens, channels):
    spare = LANES - channels
    if spare <= 0 or channels % spare or tokens * channels % LANES:
        return False
    rows, blocks = tokens * channels // LANES, channels // spare
    return rows % 8 == 0 and (tokens - rows) * blocks == rows and (tokens - rows) % 8 == 0


def split_low(value):
    high = value.astype(jnp.bfloat16)
    return high, (value - high.astype(jnp.float32)).astype(jnp.bfloat16)


def three_products(dot, left_side, right_side):
    left_high, left_rest = split_low(left_side)
    right_high, right_rest = split_low(right_side)
    return dot(left_high, right_high) + dot(left_high, right_rest) + dot(left_rest, right_high)


def fine_nn(left_side, right_side):
    return three_products(plain_dot, left_side, right_side)


def fine_nt(left_side, right_side):
    return three_products(right_dot, left_side, right_side)


def fine_tn(left_side, right_side):
    return three_products(left_dot, left_side, right_side)


def exact_nn(left_side, right_side):
    return jnp.dot(
        left_side, right_side, precision=highest_accuracy, preferred_element_type=jnp.float32
    )


def sine_pair(angle):
    turns = jnp.round(angle * (2.0 / math.pi))
    rest = angle - turns * 1.5703125
    rest = rest - turns * 4.837512969970703125e-4
    rest = rest - turns * 7.549789948768648e-8
    square = rest * rest
    sine = rest + rest * square * (
        -1.6666654611e-1 + square * (8.3321608736e-3 + square * -1.9515295891e-4)
    )
    cosine = (
        1.0
        - 0.5 * square
        + square
        * square
        * (4.166664568298827e-2 + square * (-1.388731625493765e-3 + square * 2.443315711809948e-5))
    )
    quarter = turns.astype(jnp.int32)
    odd = (quarter & 1) == 1
    sine_out = jnp.where(odd, cosine, sine)
    cosine_out = jnp.where(odd, sine, cosine)
    sine_out = jnp.where((quarter & 2) == 2, -sine_out, sine_out)
    cosine_out = jnp.where(((quarter + 1) & 2) == 2, -cosine_out, cosine_out)
    return sine_out, cosine_out


def block_rows(index, size):
    return pl.ds(pl.multiple_of(index * size, size), size)


def wave_pair(index):
    first = index * 2 * WAVE_BLOCK
    return (
        pl.ds(pl.multiple_of(first, WAVE_BLOCK), WAVE_BLOCK),
        pl.ds(pl.multiple_of(first + WAVE_BLOCK, WAVE_BLOCK), WAVE_BLOCK),
    )


def row_of(rows, name, place=0):
    at = ROW_AT[name] + place
    return rows[at : at + 1, :]


def feature_block(first, count, length, feat_count):
    bands = (feat_count - 1) // 2
    place = lax.broadcasted_iota(jnp.int32, (count, 2 * feat_count), 0) + first
    lane = lax.broadcasted_iota(jnp.int32, (count, 2 * feat_count), 1)
    later = lane >= feat_count
    place = jnp.where(later, 2 * place + 1, 2 * place)
    lane = jnp.where(later, lane - feat_count, lane)
    steps = place.astype(jnp.float32)
    band = jnp.where(lane > bands, lane - 1 - bands, lane - 1).astype(jnp.float32)
    frequency = 0.0001 + band * ((bands - 1 - 0.0001) / (bands - 1))
    sine, cosine = sine_pair(frequency * (steps * (2.0 * math.pi / length)))
    features = jnp.where(lane > bands, -sine, cosine)
    features = jnp.where(lane == 0, steps / (length - 1), features)
    column = lax.broadcasted_iota(jnp.int32, (count, 1), 0) + first
    times = [(2 * column + odd).astype(jnp.float32) / (length - 1) for odd in (0, 1)]
    return features, times


def norm_kernel(tokens, top, gain, bias, tokens_out, top_out, normed_out, held):
    low, f32 = jnp.bfloat16, jnp.float32
    count = tokens.shape[0] // 2
    for source, target in ((top, top_out), (tokens, tokens_out)):
        for place in range(held.shape[0]):
            cols = slice(place * LANES, (place + 1) * LANES)
            held[place] = source[:, cols].astype(f32)
            for odd in range(2):
                rows = held[place, pl.ds(odd, count, stride=2), :]
                target[odd * count : (odd + 1) * count, cols] = rows.astype(low)
    rows = [vector[...].astype(f32).reshape(1, vector.shape[0]) for vector in (gain, bias)]
    normed, _, _ = norm_forward(tokens_out[...].astype(f32), *rows)
    normed_out[...] = normed.astype(low)


def wave_kernel(channels, start, *refs):
    (
        pre_gain,
        pre_bias,
        in_bias,
        tap_bias,
        taps,
        skips,
        post_gain,
        post_bias,
        out_bias,
        down_bias,
        up_bias,
        pos_bias,
        inner_bias,
        third_bias,
        sine_freq,
        filter_weight,
        decay,
        in_weight_in,
        wave_out,
        turn_out,
        rows_out,
        in_out,
        local_out,
        weights_out,
        rates_out,
        vectors_out,
        tables,
        wave,
        in_weight,
        sems,
    ) = refs
    half = wave.shape[1]
    width = in_weight.shape[0]
    step = tables.shape[1]
    low, f32 = jnp.bfloat16, jnp.float32
    load = pltpu.make_async_copy(in_weight_in, in_weight, sems.at[1])
    load.start()

    unit = math.pi / (4 * half)

    def table(which, carry):
        at = lax.broadcasted_iota(jnp.int32, (step, half), 0)
        place = lax.broadcasted_iota(jnp.int32, (step, half), 1)
        left = jnp.where(which == 0, 2 * step * at, 2 * at + 1)
        turn = (left * (2 * place + 1)) & (8 * half - 1)
        sine, cosine = sine_pair(turn.astype(f32) * unit)
        tables[2 * which] = cosine
        tables[2 * which + 1] = sine
        return carry

    lax.fori_loop(0, 2, table, 0)
    per_block = WAVE_BLOCK // step

    def fill(index, carry):
        base = (index // per_block) * (2 * WAVE_BLOCK) + (index % per_block) * step
        upper = pl.ds(pl.multiple_of(base, step), step)
        lower = pl.ds(pl.multiple_of(base + WAVE_BLOCK, step), step)
        one = pl.ds(index, 1)
        cos_a, sin_a = tables[0, one, :], tables[1, one, :]
        cos_b, sin_b = tables[2], tables[3]
        wave[upper, :] = (cos_a * cos_b - sin_a * sin_b).astype(low)
        wave[lower, :] = (sin_a * cos_b + cos_a * sin_b).astype(low)
        return carry

    lax.fori_loop(0, half // step, fill, 0)
    sent = [pltpu.make_async_copy(wave, wave_out, sems.at[0])]
    for copy in sent:
        copy.start()

    def turn(index, carry):
        upper, lower = wave_pair(index)
        at = lax.broadcasted_iota(jnp.int32, (WAVE_BLOCK, LANES), 0) + index * WAVE_BLOCK
        sine, cosine = sine_pair((2 * at + 1).astype(f32) * unit)
        turn_out[upper, :] = cosine
        turn_out[lower, :] = sine
        return carry

    lax.fori_loop(0, half // WAVE_BLOCK, turn, 0)
    rows_out[...] = jnp.zeros_like(rows_out)

    def place_rows(name, vector):
        for number in range(vector.shape[0] // width):
            piece = vector[number * width : (number + 1) * width].astype(f32)
            at = ROW_AT[name] + number
            rows_out[at : at + 1, :] = piece.reshape(1, width)

    for name, vector in (
        ("pre_gain", pre_gain),
        ("pre_bias", pre_bias),
        ("in_bias", in_bias),
        ("tap_bias", tap_bias),
        ("post_gain", post_gain),
        ("post_bias", post_bias),
        ("out_bias", out_bias),
        ("down_bias", down_bias),
        ("up_bias", up_bias),
    ):
        place_rows(name, vector)
    wide_taps = taps[...].astype(f32)
    for tap in range(3):
        for group in range(3):
            at = ROW_AT["taps"] + 3 * tap + group
            rows_out[at : at + 1, :] = wide_taps[tap : tap + 1, group * width : (group + 1) * width]
    at = ROW_AT["skips"]
    rows_out[at : at + 2, :] = skips[...].astype(f32)
    for number, vector in enumerate((pos_bias, inner_bias, third_bias, sine_freq)):
        row = vector[...].astype(f32).reshape(1, vector.shape[0])
        vectors_out[number : number + 1, :] = row

    source = lax.broadcasted_iota(jnp.int32, (width, LANES), 0)
    target = lax.broadcasted_iota(jnp.int32, (width, LANES), 1)
    chosen = (source == start[0] + target) & (target < channels)
    select_wide = jnp.where(chosen, 1.0, 0.0)
    select = select_wide.astype(low)
    local_out[...] = plain_dot(rows_out[...].astype(low), select)
    padded = jnp.concatenate([decay[...], jnp.zeros((6, width), f32)], axis=0)
    rates = exact_nn(padded, select_wide)
    for order in range(2):
        cols = slice(order * LANES, (order + 1) * LANES)
        weights_out[:, cols] = plain_dot(filter_weight[order], select)
        rates_out[:, cols] = rates[order : order + 1]
    load.wait()
    for group in range(3):
        cols = slice(group * LANES, (group + 1) * LANES)
        whole = in_weight[:, group * width : (group + 1) * width]
        in_out[:, cols] = plain_dot(whole, select).astype(low)
    for copy in sent:
        copy.wait()


def doubled(weight):
    zero = jnp.zeros_like(weight)
    return jnp.concatenate(
        [jnp.concatenate([weight, zero], axis=1), jnp.concatenate([zero, weight], axis=1)], axis=0
    )


def twice(row):
    return jnp.concatenate([row, row], axis=1)


def filter_kernel(
    pos_weight,
    inner_weight,
    third_weight,
    vectors,
    weights,
    rates,
    turn,
    wave_in,
    spectrum_out,
    kernel_out,
    waves_out,
    high,
    rest,
    wave,
    sems,
):
    half = wave.shape[1]
    length = 2 * half
    low, f32 = jnp.bfloat16, jnp.float32
    loads = row_chunks(wave_in, wave, sems, 0, 1)
    for copy in loads:
        copy.start()
    feat_count = pos_weight.shape[0]
    freq = twice(vectors[3:4, :])

    def network(index, carry):
        here = block_rows(index, BLOCK)
        there = pl.ds(pl.multiple_of(index * BLOCK + half, BLOCK), BLOCK)
        layer_in, times = feature_block(index * BLOCK, BLOCK, length, feat_count)
        for layer, weight in enumerate((pos_weight, inner_weight, third_weight)):
            matrix = doubled(weight[...].astype(f32))
            inner = fine_nn(layer_in, matrix) + twice(vectors[layer : layer + 1, :])
            layer_in, cosine = sine_pair(freq * inner)
            waves_out[layer, here, :] = jnp.concatenate([layer_in, cosine], axis=1)
        both = fine_nn(layer_in, doubled(weights[...]))
        cols = 2 * LANES
        for part, rows in enumerate((here, there)):
            kernels = both[:, part * cols : (part + 1) * cols]
            kernels = kernels * jnp.exp(-rates[...] * times[part])
            kernel_out[rows, :] = kernels
            upper = kernels.astype(low)
            high[rows, :] = upper
            rest[rows, :] = (kernels - upper.astype(f32)).astype(low)
        return carry

    lax.fori_loop(0, half // BLOCK, network, 0, unroll=True)
    for copy in loads:
        copy.wait()

    def spectra(index, carry):
        matrix = wave[block_rows(index, 2 * WAVE_BLOCK), :]
        even, odd = (
            plain_dot(matrix, high[rows, :]) + plain_dot(matrix, rest[rows, :])
            for rows in (slice(0, half), slice(half, length))
        )
        upper, lower = wave_pair(index)
        for order in range(2):
            cols = slice(order * LANES, (order + 1) * LANES)
            parts = butterfly(even[:, cols], odd[:, cols], turn, upper, lower)
            for side, (real, imag) in enumerate(parts):
                spectrum_out[side, upper, cols] = real * (1.0 / length)
                spectrum_out[side, lower, cols] = imag * (1.0 / length)
        return carry

    lax.fori_loop(0, half // WAVE_BLOCK, spectra, 0, unroll=True)


def butterfly(even, odd, turn, upper, lower):
    cosine, sine = turn[upper, :], turn[lower, :]
    even_real, even_imag = even[:WAVE_BLOCK], even[WAVE_BLOCK:]
    odd_real, odd_imag = odd[:WAVE_BLOCK], odd[WAVE_BLOCK:]
    real = even_real * cosine + even_imag * sine
    imag = even_imag * cosine - even_real * sine
    return (real + odd_real, imag + odd_imag), (real - odd_real, odd_imag - imag)


def unbutterfly(first, second, turn, upper, lower):
    cosine, sine = turn[upper, :], turn[lower, :]
    real, imag = first[0] + second[0], first[1] - second[1]
    even = (real * cosine - imag * sine, imag * cosine + real * sine)
    return even, (first[0] - second[0], first[1] + second[1])


def short_mix(rows, projected, index, group):
    cols = slice(group * LANES, (group + 1) * LANES)
    here = pl.ds(pl.multiple_of(index * CHUNK, CHUNK), CHUNK + PAD)
    even, odd = projected[0, here, cols], projected[1, here, cols]
    taps = [row_of(rows, "taps", 3 * tap + group) for tap in range(3)]
    shift = row_of(rows, "tap_bias", group)
    last = slice(PAD - 1, PAD - 1 + CHUNK)
    return (
        taps[0] * even[last] + taps[1] * odd[last] + taps[2] * even[PAD:] + shift,
        taps[0] * odd[last] + taps[1] * even[PAD:] + taps[2] * odd[PAD:] + shift,
    )


def spread_rows(tile, held, target):
    count = tile.shape[0] // 2
    for place in range(held.shape[0]):
        cols = slice(place * LANES, (place + 1) * LANES)
        for odd in range(2):
            rows = tile[odd * count : (odd + 1) * count, cols]
            held[place, pl.ds(odd, count, stride=2), :] = rows
        target[:, cols] = held[place]


def inverse_block(wave, reals, imags, index):
    upper, lower = wave_pair(index)
    return plain_dot(wave[upper, :], reals[...]) + plain_dot(wave[lower, :], imags[...])


def store_inverse(reals, imags, here, at, parts):
    for place, (real, imag) in enumerate(parts):
        cols = slice((at + place) * LANES, (at + place + 1) * LANES)
        reals[here, cols] = real.astype(jnp.bfloat16)
        imags[here, cols] = imag.astype(jnp.bfloat16)


def convolve(wave, turn, signal, spectrum, cols, kept, reals, imags, finish):
    half = wave.shape[1]

    def ahead(index, carry):
        both = plain_dot(wave[block_rows(index, 2 * WAVE_BLOCK), :], signal[...])
        upper, lower = wave_pair(index)
        sides = butterfly(both[:, :LANES], both[:, LANES:], turn, upper, lower)
        outs = []
        for side, (real, imag) in enumerate(sides):
            kept[side, upper, :], kept[side, lower, :] = real, imag
            outs.append(
                times_spec(real, imag, spectrum[side, upper, cols], spectrum[side, lower, cols])
            )
        parts = unbutterfly(*outs, turn, upper, lower)
        store_inverse(reals, imags, block_rows(index, WAVE_BLOCK), 0, parts)
        return carry

    lax.fori_loop(0, half // WAVE_BLOCK, ahead, 0, unroll=True)

    def behind(index, carry):
        finish(block_rows(index, WAVE_BLOCK), inverse_block(wave, reals, imags, index))
        return carry

    lax.fori_loop(0, half // WAVE_BLOCK, behind, 0, unroll=True)


def correlate(wave, turn, signal, spectrum, cols, kept, reals, imags, finish):
    half = wave.shape[1]
    wide = 2 * LANES

    def ahead(index, carry):
        both = plain_dot(wave[block_rows(index, 2 * WAVE_BLOCK), :], signal[...])
        upper, lower = wave_pair(index)
        sides = butterfly(both[:, :LANES], both[:, LANES:], turn, upper, lower)
        here = block_rows(index, WAVE_BLOCK)
        for number, (other, columns) in enumerate(((spectrum, cols), (kept, slice(0, LANES)))):
            outs = [
                times_conj(*pair, other[side, upper, columns], other[side, lower, columns])
                for side, pair in enumerate(sides)
            ]
            parts = unbutterfly(*outs, turn, upper, lower)
            store_inverse(reals, imags, here, 2 * number, parts)
        return carry

    lax.fori_loop(0, half // WAVE_BLOCK, ahead, 0, unroll=True)

    def behind(index, carry):
        both = inverse_block(wave, reals, imags, index)
        kernel = both[:, wide:] * (0.5 / half)
        return finish(block_rows(index, WAVE_BLOCK), both[:, :wide], kernel, carry)

    zero = jnp.zeros((1, wide), jnp.float32)
    return lax.fori_loop(0, half // WAVE_BLOCK, behind, zero, unroll=True)


def front_kernel(parts, index, *refs):
    chunks = refs[:parts]
    (weight, rows, wave_in, turn_in, spectrum_in) = refs[parts : 5 + parts]
    (
        normed_out,
        projected_out,
        product_hbm,
        gate_hbm,
        after_hbm,
        gated_hbm,
        product_wave_out,
        gated_wave_out,
        mixed_out,
        mixer_out,
        product_out,
        gate_out,
        after_out,
        gated_out,
        held,
        reals,
        imags,
        wave,
        turn,
        spectrum,
        projected,
        product_wave,
        gated_wave,
        mixed,
        mixer,
        sems,
    ) = refs[5 + parts :]
    tok_count, width = chunks[0].shape
    half = wave.shape[1]
    channels = width // parts
    low, f32 = jnp.bfloat16, jnp.float32
    loads = [
        pltpu.make_async_copy(source, target, sems.at[place])
        for place, (source, target) in enumerate(
            [(wave_in, wave), (turn_in, turn), (spectrum_in, spectrum)]
        )
    ]
    stores = [
        pltpu.make_async_copy(source, target, sems.at[3 + place])
        for place, (source, target) in enumerate(
            [
                (held, normed_out),
                (projected, projected_out),
                (product_wave, product_wave_out),
                (gated_wave, gated_wave_out),
                (mixed, mixed_out),
                (product_out, product_hbm),
                (gate_out, gate_hbm),
                (after_out, after_hbm),
                (gated_out, gated_hbm),
            ]
        )
    ]
    for copy in loads:
        copy.start()
    count = tok_count // 2
    for part in range(parts):
        place = index[0] ^ part
        for odd in range(2):
            at = pl.ds(pl.multiple_of(odd * half + place * count, count), count)
            held[at, :] = chunks[part][odd * count : (odd + 1) * count, :]
    stores[0].start()
    in_bias = jnp.concatenate([row_of(rows, "in_bias", group) for group in range(3)], axis=1)
    projected[:, :PAD, :] = jnp.zeros((2, PAD, projected.shape[2]), f32)

    def project(odd, carry):
        projected[odd, PAD:, :] = plain_dot(held[block_rows(odd, half), :], weight[...]) + in_bias
        return carry

    lax.fori_loop(0, 2, project, 0, unroll=True)
    stores[1].start()

    def mix(step, carry):
        here = block_rows(step, CHUNK)
        value, gate_one, gate_two = (short_mix(rows, projected, step, group) for group in range(3))
        for odd in range(2):
            cols = slice(odd * LANES, (odd + 1) * LANES)
            mixed[0, here, cols] = value[odd]
            mixed[1, here, cols] = gate_one[odd]
            product_out[here, cols] = (value[odd] * gate_one[odd]).astype(low)
            gate_out[here, cols] = gate_two[odd].astype(low)
        return carry

    lax.fori_loop(0, half // CHUNK, mix, 0)
    for copy in stores[4:7]:
        copy.start()
    skips = [twice(row_of(rows, "skips", order)) for order in range(2)]

    def first(here, convolved):
        product = product_out[here, :].astype(f32)
        after = (convolved + skips[0] * product).astype(low)
        after_out[here, :] = after
        gated_out[here, :] = (after.astype(f32) * gate_out[here, :].astype(f32)).astype(low)

    def second(here, convolved):
        gated = gated_out[here, :].astype(f32)
        mixer[here, :] = (convolved + skips[1] * gated).astype(low)

    for copy in loads:
        copy.wait()
    cols = [slice(order * LANES, (order + 1) * LANES) for order in range(2)]
    convolve(wave, turn, product_out, spectrum, cols[0], product_wave, reals, imags, first)
    for copy in (stores[2], stores[7], stores[8]):
        copy.start()
    convolve(wave, turn, gated_out, spectrum, cols[1], gated_wave, reals, imags, second)
    stores[3].start()
    for part in range(parts):
        at = slice(part * count, (part + 1) * count)
        tiles = [mixer[at, odd * LANES : odd * LANES + channels] for odd in range(2)]
        mixer_out[part] = dense_rows(jnp.concatenate(tiles, axis=0))
    for copy in stores:
        copy.wait()


def back_kernel(
    channels,
    grad_mixer,
    rows,
    product_in,
    gate_in,
    after_in,
    gated_in,
    turn_in,
    product_wave_in,
    gated_wave_in,
    spectrum_in,
    wave_in,
    projected_in,
    mixed_in,
    packed_out,
    padded_out,
    grad_kernel_out,
    sums_out,
    grad_mix,
    grad_after,
    grad_value,
    grad_gate,
    product_ref,
    gate_ref,
    after_ref,
    gated_ref,
    turn,
    reals,
    imags,
    wave,
    spectrum,
    product_wave,
    gated_wave,
    projected,
    mixed,
    shifted,
    sems,
):
    parts = grad_mixer.shape[0]
    half = wave.shape[1]
    count = half // parts
    low, f32 = jnp.bfloat16, jnp.float32
    loads = [
        pltpu.make_async_copy(source, target, sems.at[place])
        for place, (source, target) in enumerate(
            [
                (wave_in, wave),
                (turn_in, turn),
                (spectrum_in, spectrum),
                (gated_wave_in, gated_wave),
                (gate_in, gate_ref),
                (after_in, after_ref),
                (gated_in, gated_ref),
                (product_in, product_ref),
                (product_wave_in, product_wave),
                (projected_in, projected),
                (mixed_in, mixed),
            ]
        )
    ]
    for copy in loads:
        copy.start()
    padding = jnp.zeros((count, LANES - channels), low)
    for part in range(parts):
        tile = loose_rows(grad_mixer[part], 2 * count, channels)
        here = slice(part * count, (part + 1) * count)
        pieces = [tile[:count], padding, tile[count:], padding]
        grad_mix[here, :] = jnp.concatenate(pieces, axis=1)
    skips = [twice(row_of(rows, "skips", order)) for order in range(2)]

    def store_kernel(here, order, kernel):
        cols = slice(order * LANES, (order + 1) * LANES)
        grad_kernel_out[0, here, cols] = kernel[:, :LANES]
        grad_kernel_out[1, here, cols] = kernel[:, LANES:]

    def first(here, data, kernel, total):
        store_kernel(here, 1, kernel)
        top = grad_mix[here, :].astype(f32)
        grad_gated = (data + skips[1] * top).astype(low).astype(f32)
        grad_after[here, :] = (grad_gated * gate_ref[here, :].astype(f32)).astype(low)
        grad_gate[here, :] = (grad_gated * after_ref[here, :].astype(f32)).astype(low)
        return total + jnp.sum(top * gated_ref[here, :].astype(f32), axis=0, keepdims=True)

    def second(here, data, kernel, total):
        store_kernel(here, 0, kernel)
        top = grad_after[here, :].astype(f32)
        grad_value[here, :] = (data + skips[0] * top).astype(low)
        return total + jnp.sum(top * product_ref[here, :].astype(f32), axis=0, keepdims=True)

    cols = [slice(order * LANES, (order + 1) * LANES) for order in range(2)]
    for copy in loads[:7]:
        copy.wait()
    skip_second = correlate(
        wave, turn, grad_mix, spectrum, cols[1], gated_wave, reals, imags, first
    )
    for copy in loads[7:9]:
        copy.wait()
    skip_first = correlate(
        wave, turn, grad_after, spectrum, cols[0], product_wave, reals, imags, second
    )
    sums_out[15:16, :] = skip_first[:, :LANES] + skip_first[:, LANES:]
    sums_out[16:17, :] = skip_second[:, :LANES] + skip_second[:, LANES:]
    sums_out[17:24, :] = jnp.zeros((7, LANES), f32)
    for copy in loads[9:]:
        copy.wait()
    shifted[:, :, half:, :] = jnp.zeros((3, 2, PAD, LANES), f32)
    sides = [slice(odd * LANES, (odd + 1) * LANES) for odd in range(2)]

    def folded(value):
        return jnp.sum(value.reshape(CHUNK // 8, 8, LANES), axis=0)

    def taps_back(step, totals):
        here = block_rows(step, CHUNK)
        window = pl.ds(pl.multiple_of(step * CHUNK, CHUNK), CHUNK + PAD)
        last = slice(PAD - 1, PAD - 1 + CHUNK)
        totals = list(totals)
        for group in range(3):
            cols = slice(group * LANES, (group + 1) * LANES)
            if group == 2:
                even, odd = (grad_gate[here, side].astype(f32) for side in sides)
            else:
                even, odd = (
                    grad_value[here, side].astype(f32) * mixed[1 - group, here, side]
                    for side in sides
                )
            shifted[group, 0, here, :], shifted[group, 1, here, :] = even, odd
            even_rows, odd_rows = projected[0, window, cols], projected[1, window, cols]
            terms = (
                even * even_rows[last] + odd * odd_rows[last],
                even * odd_rows[last] + odd * even_rows[PAD:],
                even * even_rows[PAD:] + odd * odd_rows[PAD:],
                even + odd,
            )
            for number, term in enumerate(terms):
                totals[3 * number + group] = totals[3 * number + group] + folded(term)
        return tuple(totals)

    zero = jnp.zeros((8, LANES), f32)
    totals = lax.fori_loop(0, half // CHUNK, taps_back, (zero,) * 12)

    def project_back(step, totals):
        window = pl.ds(pl.multiple_of(step * CHUNK, CHUNK), CHUNK + PAD)
        following = slice(1, 1 + CHUNK)
        totals = list(totals)
        for group in range(3):
            cols = slice(group * LANES, (group + 1) * LANES)
            even, odd = shifted[group, 0, window, :], shifted[group, 1, window, :]
            taps = [row_of(rows, "taps", 3 * tap + group) for tap in range(3)]
            now = slice(0, CHUNK)
            grads = (
                taps[0] * even[following] + taps[1] * odd[now] + taps[2] * even[now],
                taps[0] * odd[following] + taps[1] * even[following] + taps[2] * odd[now],
            )
            grads = [grad.astype(low) for grad in grads]
            for place, grad in enumerate(grads):
                at = pl.ds(pl.multiple_of(place * half + step * CHUNK, CHUNK), CHUNK)
                padded_out[at, cols] = grad
            wide = grads[0].astype(f32) + grads[1].astype(f32)
            totals[group] = totals[group] + folded(wide)
        return tuple(totals)

    totals = totals + lax.fori_loop(0, half // CHUNK, project_back, (zero,) * 3)
    for number, value in enumerate(totals):
        sums_out[number : number + 1, :] = jnp.sum(value, axis=0, keepdims=True)
    dense = packed_out.shape[1] // 3

    def pack(part, carry):
        for group in range(3):
            cols = slice(group * LANES, group * LANES + channels)
            tiles = [
                padded_out[
                    pl.ds(pl.multiple_of(odd * half + part * count, count), count), cols
                ]
                for odd in range(2)
            ]
            packed = dense_rows(jnp.concatenate(tiles, axis=0))
            packed_out[part, group * dense : (group + 1) * dense, :] = packed
        return carry

    lax.fori_loop(0, parts, pack, 0)


def store_rows(target, at, value):
    per = target.shape[1]
    place = 0
    while place < value.shape[0]:
        quarter, inside = divmod(at + place, per)
        count = min(value.shape[0] - place, per - inside)
        target[quarter, inside : inside + count, :] = value[place : place + count]
        place += count


def lane_rows(vector):
    count = vector.shape[1] // LANES
    return jnp.concatenate(
        [vector[:, place * LANES : (place + 1) * LANES] for place in range(count)], axis=0
    )


def middle_kernel(
    parts,
    batch_index,
    received,
    tokens,
    top,
    rows,
    out_in,
    up_in,
    down_in,
    outputs_out,
    residual_out,
    send_out,
    sums_out,
    *refs,
):
    batch = len(refs) - 14
    sides, parts_out = refs[0], refs[1 : 1 + batch]
    (
        out_w,
        up_w,
        down_w,
        residual,
        total,
        flow,
        act,
        upper_grad,
        act_parts,
        branch_parts,
        up_rows,
        held,
        sems,
    ) = refs[1 + batch :]
    tok_count, width = tokens.shape
    channels = width // parts
    f32, low = jnp.float32, jnp.bfloat16
    quarters = up_w.shape[0]
    quarter = up_w.shape[2]
    load_out = pltpu.make_async_copy(out_in, out_w, sems.at[0])
    load_out.start()

    def loads(place):
        cols = pl.ds(pl.multiple_of(place * quarter, quarter), quarter)
        return (
            pltpu.make_async_copy(up_in.at[:, cols], up_w.at[place], sems.at[1 + place]),
            pltpu.make_async_copy(
                down_in.at[cols, :], down_w.at[place], sems.at[1 + quarters + place]
            ),
        )

    for place in range(quarters):
        for copy in loads(place):
            copy.start()
    tiles = [
        loose_rows(received[part], tok_count, channels) for part in range(parts)
    ]
    mixer = jnp.concatenate(tiles, axis=1)
    load_out.wait()
    branch = plain_dot(mixer, out_w[...]) + row_of(rows, "out_bias")
    residual[...] = tokens[...].astype(f32) + branch
    gain = row_of(rows, "post_gain")
    bias = row_of(rows, "post_bias")
    normed, _, _ = norm_forward(residual[...], gain, bias)
    sides[:, :width] = normed.astype(low)
    sides[:, width:] = mixer
    for place in range(quarters):
        up_rows[place] = row_of(rows, "up_bias", place)
    total[...] = jnp.zeros_like(total)
    flow[...] = jnp.zeros_like(flow)

    def body(place, carry):
        for copy in loads(place):
            copy.wait()
        upper = plain_dot(sides[:, :width], up_w[place]) + up_rows[place]
        gauss = 0.5 * (1.0 + lax.erf(upper * 0.7071067811865476))
        active = (upper * gauss).astype(low)
        act[place] = active
        total[...] += plain_dot(active, down_w[place])
        grad_act = right_dot(top[...], down_w[place])
        slope = gauss + upper * jnp.exp(-0.5 * upper * upper) * 0.3989422804014327
        grad_upper = (grad_act * slope).astype(low)
        upper_grad[place] = grad_upper
        flow[...] += right_dot(grad_upper, up_w[place])
        return carry

    lax.fori_loop(0, quarters, body, 0, unroll=True)
    spread_rows(residual[...] + total[...] + row_of(rows, "down_bias"), held, outputs_out)
    _, unit, inv_std = norm_forward(residual[...], gain, bias)
    grad_norm, grad_gain, grad_bias = norm_backward(flow[...], unit, inv_std, gain)
    grad_residual = top[...].astype(f32) + grad_norm
    residual_out[...] = grad_residual
    grad_branch = grad_residual.astype(low)
    grad_mixer = right_dot(grad_branch, out_w[...]).astype(low)
    for part in range(parts):
        tile = grad_mixer[:, part * channels : (part + 1) * channels]
        send_out[part] = dense_rows(tile)
    wide_branch = grad_branch.astype(f32)
    vectors = [
        jnp.sum(wide_branch, axis=0, keepdims=True),
        grad_gain[None],
        grad_bias[None],
        jnp.sum(top[...].astype(f32), axis=0, keepdims=True),
    ]
    vectors += [
        jnp.sum(upper_grad[place].astype(f32), axis=0, keepdims=True) for place in range(quarters)
    ]
    per = width // LANES
    for number, vector in enumerate(vectors):
        sums_out[number * per : (number + 1) * per, :] = lane_rows(vector)
    piece = width // batch
    for place in range(batch):
        part = wide_branch[:, place * piece : (place + 1) * piece]
        spare = branch_parts.shape[2] - piece
        part = jnp.concatenate([part, jnp.zeros((tok_count, spare), f32)], axis=1)
        branch_parts[place] = part.astype(low)
    step = quarters * quarter // (parts * batch)
    per_part = quarters * quarter // parts
    for place in range(batch):
        tiles = []
        for part in range(parts):
            at = part * per_part + place * step
            inside = at % quarter
            tiles.append(act[at // quarter, :, inside : inside + step])
        act_parts[place] = jnp.concatenate(tiles, axis=1)
    for bits in range(batch):
        place = batch_index[0] ^ bits
        parts_out[bits][:, :quarter] = upper_grad[place]
        parts_out[bits][:, quarter : 2 * quarter] = act_parts[place]
        parts_out[bits][:, 2 * quarter :] = branch_parts[place]


def store_halves(part, bit, bits, keep_out, send_out):
    count = keep_out.shape[0]
    size = keep_out.shape[1]
    for entry in range(count):
        lower, upper = entry % bits, entry // bits
        base = upper * 2 * bits + lower
        mine = pl.ds(pl.multiple_of((base + bit * bits) * size, size), size)
        other = pl.ds(pl.multiple_of((base + (1 - bit) * bits) * size, size), size)
        keep_out[entry] = part[mine, :]
        send_out[entry] = part[other, :].astype(jnp.bfloat16)


def flip(tile):
    return tile.T


def weight_kernel(batch, orders, index, *refs):
    sides, tops, gots = (refs[batch * place : batch * (place + 1)] for place in range(3))
    up_keep, up_send, rest_keep, rest_send, flipped, columns, part, rest = refs[3 * batch :]
    tok_count, width = tops[0].shape
    for entry in range(batch):
        here = slice(entry * tok_count, (entry + 1) * tok_count)
        columns[here, :width] = gots[entry][:, :width]
        columns[here, width : 2 * width] = tops[entry][...]
        columns[here, 2 * width :] = gots[entry][:, 2 * width :]
        flipped[:width, here] = flip(sides[entry][:, :width])
        flipped[width : 2 * width, here] = flip(gots[entry][:, width : 2 * width])
        flipped[2 * width :, here] = flip(sides[entry][:, width:])
    part[...] = plain_dot(flipped[:width, :], columns[:, :width])
    store_halves(part, index[0], orders[0], up_keep, up_send)
    rest[:, :width] = plain_dot(flipped[width : 2 * width, :], columns[:, width : 2 * width])
    last = plain_dot(flipped[2 * width :, :], columns[:, 2 * width :])
    rest[:, width:] = last[:, : rest.shape[1] - width]
    store_halves(rest, index[1], orders[1], rest_keep, rest_send)


def fold_kernel(bits, bit, keep, got, keep_out, send_out):
    for entry in range(keep_out.shape[0]):
        lower, upper = entry % bits, entry // bits
        base = upper * 2 * bits + lower
        mine, other = base + bit[0] * bits, base + (1 - bit[0]) * bits
        keep_out[entry] = keep[mine] + got[mine].astype(jnp.float32)
        send_out[entry] = (keep[other] + got[other].astype(jnp.float32)).astype(jnp.bfloat16)


def collect_kernel(batch, batch_index, *refs):
    entries = refs[:batch]
    down_out, up_out, out_out, held = refs[batch:]
    rows, total = entries[0].shape
    width = down_out.shape[1]
    piece = width // batch
    f32 = jnp.float32
    for entry in range(batch):
        held[batch_index[0] ^ entry] = entries[entry][...]
    for place in range(batch):
        up_out[:, place * width : (place + 1) * width] = held[place, :, :width].astype(f32)
        down = held[place, :, width : 2 * width].astype(f32)
        down_out[place * rows : (place + 1) * rows, :] = down
    tiles = [held[place, :, 2 * width : 2 * width + piece].astype(f32) for place in range(batch)]
    out_out[...] = jnp.concatenate(tiles, axis=1)


def final_kernel(received, tokens, residual, rows, weight_in, out, weight, joined, held, sems):
    parts = received.shape[0]
    tok_count, width = tokens.shape
    channels = width // parts
    f32, low = jnp.float32, jnp.bfloat16
    load = pltpu.make_async_copy(weight_in, weight, sems.at[0])
    load.start()
    dense = received.shape[1] // 3
    for group in range(3):
        tiles = [
            loose_rows(
                received[part, group * dense : (group + 1) * dense, :],
                tok_count,
                channels,
            )
            for part in range(parts)
        ]
        joined[:, group * width : (group + 1) * width] = jnp.concatenate(tiles, axis=1)
    gain = row_of(rows, "pre_gain")
    bias = row_of(rows, "pre_bias")
    _, unit, inv_std = norm_forward(tokens[...].astype(f32), gain, bias)
    load.wait()
    grad_normed = jnp.zeros((tok_count, width), f32)
    for group in range(3):
        cols = slice(group * width, (group + 1) * width)
        grad_normed = grad_normed + right_dot(joined[:, cols], weight[:, cols])
    grad_tokens, _, _ = norm_backward(grad_normed, unit, inv_std, gain)
    spread_rows(residual[...] + grad_tokens, held, out)


SHARED_ROWS = 48
LAID_ROWS = 8
OWN_ROWS = 40


def chain_kernel(
    norm_rows,
    in_local,
    sums,
    middle_sums,
    pos_weight,
    inner_weight,
    third_weight,
    vectors,
    weights,
    rates,
    grad_kernels_in,
    kernels_in,
    waves_in,
    pair_in,
    small_out,
    weight_total,
    rate_total,
    shared,
    pairs,
    grad_kernels,
    kernels,
    waves,
    pair_sums,
    sems,
):
    length = kernels.shape[0]
    blocks = length // BLOCK

    def loads(index):
        here = block_rows(index, BLOCK)
        later = pl.ds(pl.multiple_of(index * BLOCK + length // 2, BLOCK), BLOCK)
        pieces = [
            (source.at[rows], target.at[rows])
            for source, target in ((grad_kernels_in, grad_kernels), (kernels_in, kernels))
            for rows in (here, later)
        ]
        pieces.append((waves_in.at[:, here], waves.at[:, here]))
        return [
            pltpu.make_async_copy(source, target, sems.at[number * (blocks // 2) + index])
            for number, (source, target) in enumerate(pieces)
        ]

    for block in range(blocks // 2):
        for copy in loads(block):
            copy.start()
    width = in_local.shape[0]
    pair_load = pltpu.make_async_copy(pair_in, pair_sums, sems.at[5 * (blocks // 2)])
    pair_load.start()
    feat_count, fhid = pos_weight.shape
    f32 = jnp.float32
    freq = vectors[3:4, :]
    weight_total[...] = jnp.zeros_like(weight_total)
    rate_total[...] = jnp.zeros_like(rate_total)
    pairs[...] = jnp.zeros_like(pairs)

    half = length // 2
    cols = 2 * LANES
    weight_pair = doubled(weights[...])
    freq_pair = twice(freq)

    def body(index, carry):
        here = block_rows(index, BLOCK)
        there = pl.ds(pl.multiple_of(index * BLOCK + half, BLOCK), BLOCK)
        for copy in loads(index):
            copy.wait()
        features, times = feature_block(index * BLOCK, BLOCK, length, feat_count)
        windowed = []
        for rows, time in zip((here, there), times):
            grads = grad_kernels[rows, :]
            decayed = jnp.sum(grads * kernels[rows, :] * time, axis=0, keepdims=True)
            rate_total[...] = rate_total[...] - decayed
            windowed.append(grads * jnp.exp(-rates[...] * time))
        windowed = jnp.concatenate(windowed, axis=1)
        weight_total[...] = weight_total[...] + fine_tn(waves[2, here, :LANES], windowed)
        flow = fine_nt(windowed, weight_pair)
        for layer in (2, 1, 0):
            slope = flow * waves[layer, here, LANES:]
            below = waves[layer - 1, here, :LANES] if layer else features
            count = below.shape[1]
            pairs[layer, :count, :] = pairs[layer, :count, :] + fine_tn(below, slope)
            row = slice(LANES, LANES + 1)
            pairs[layer, row, :] = pairs[layer, row, :] + jnp.sum(slope, axis=0, keepdims=True)
            if layer:
                weight = inner_weight if layer == 1 else third_weight
                flow = fine_nt(slope * freq_pair, doubled(weight[...].astype(f32)))
        return carry

    lax.fori_loop(0, blocks // 2, body, 0, unroll=True)
    grad_freq = jnp.zeros_like(freq)
    at, bias_at = 0, 2 * fhid + feat_count
    for layer, weight in ((2, third_weight), (1, inner_weight), (0, pos_weight)):
        count = weight.shape[0]
        matrix = pairs[layer, :count, :fhid] + pairs[layer, count : 2 * count, fhid:]
        both = pairs[layer, LANES : LANES + 1, :]
        vector = both[:, :fhid] + both[:, fhid:]
        grad_freq = grad_freq + jnp.sum(weight[...].astype(f32) * matrix, axis=0, keepdims=True)
        grad_freq = grad_freq + vectors[layer : layer + 1, :] * vector
        shared[at : at + count, :] = matrix * freq
        shared[bias_at + layer : bias_at + layer + 1, :] = vector * freq
        at += count
    shared[bias_at + 3 : bias_at + 4, :] = grad_freq
    pair_load.wait()
    small_out[...] = jnp.zeros_like(small_out)
    ones = jnp.ones((16, in_local.shape[1]), jnp.bfloat16)
    high, rest = split_low(in_local[...].astype(f32) * pair_sums[...])
    gain = (right_dot(ones, high) + right_dot(ones, rest))[0:1]
    column_sums = jnp.concatenate([sums[12 + group : 13 + group, :] for group in range(3)], axis=1)
    high, rest = split_low(jnp.broadcast_to(column_sums, ones.shape))
    bias = (right_dot(high, in_local[...]) + right_dot(rest, in_local[...]))[0:1]
    everywhere = small_out.at[:, :SHARED_ROWS, :]
    per = width // LANES
    gain = (gain - row_of(norm_rows, "pre_bias") * bias) / row_of(norm_rows, "pre_gain")
    store_rows(everywhere, 0, lane_rows(gain))
    store_rows(everywhere, per, lane_rows(bias))
    at = 2 * per
    store_rows(everywhere, at, middle_sums[...])
    at += middle_sums.shape[0]
    store_rows(everywhere, at, jnp.concatenate([shared[:fhid, :], shared[fhid : 2 * fhid, :]], axis=1))
    at += fhid
    tail = shared[2 * fhid : 2 * fhid + feat_count + 4, :]
    store_rows(everywhere, at, jnp.concatenate([tail, jnp.zeros_like(tail)], axis=1))
    store_rows(small_out.at[:, SHARED_ROWS : SHARED_ROWS + LAID_ROWS, :], 0, sums[:15, :])
    own = small_out.at[:, SHARED_ROWS + LAID_ROWS :, :]
    for order in range(2):
        first = slice(order * LANES, (order + 1) * LANES)
        second = slice(cols + order * LANES, cols + (order + 1) * LANES)
        both = weight_total[:fhid, first] + weight_total[fhid:, second]
        store_rows(own, order * fhid, both)
        store_rows(own, 2 * fhid + order, rate_total[:, first])
    store_rows(own, 2 * fhid + 2, sums[15:17, :])


def spread_kernel(in_keep, in_got, small_keep, small_got, send_out, small_out):
    low, f32 = jnp.bfloat16, jnp.float32
    parts = send_out.shape[0]
    small = small_keep[...] + small_got[...]
    small_out[...] = small
    both = SHARED_ROWS + LAID_ROWS
    high, rest = split_low(small[:both])
    count = in_keep.shape[0] // parts
    for part in range(parts):
        here = slice(part * count, (part + 1) * count)
        send_out[part, :count, :] = (in_keep[here, :] + in_got[here, :].astype(f32)).astype(low)
        send_out[part, count : count + both, :] = high
        send_out[part, count + both :, :] = rest


def merge_kernel(received, small, out):
    f32 = jnp.float32
    parts = received.shape[0]
    both = SHARED_ROWS + LAID_ROWS
    count = received.shape[1] - 2 * both
    total = jnp.zeros((SHARED_ROWS, LANES), f32)
    done = parts * count
    rows = SHARED_ROWS + parts * LAID_ROWS + OWN_ROWS
    for part in range(parts):
        out[part * count : (part + 1) * count, :] = received[part, :count, :]
        high = received[part, count : count + both, :].astype(f32)
        rest = received[part, count + both :, :].astype(f32)
        total = total + high[:SHARED_ROWS] + rest[:SHARED_ROWS]
        at = done + SHARED_ROWS + part * LAID_ROWS
        laid = received[part, count : count + both, :].astype(f32)[SHARED_ROWS:]
        out[at : at + LAID_ROWS, :] = laid.astype(jnp.bfloat16)
        laid = received[part, count + both :, :].astype(f32)[SHARED_ROWS:]
        out[at + rows : at + rows + LAID_ROWS, :] = laid.astype(jnp.bfloat16)
    for at, value in ((0, total), (rows - OWN_ROWS, small[SHARED_ROWS + LAID_ROWS :, :])):
        high, rest = split_low(value)
        count = value.shape[0]
        out[done + at : done + at + count, :] = high
        out[done + rows + at : done + rows + at + count, :] = rest


def take_rows(source, at, count):
    per = source.shape[1]
    pieces = []
    while count:
        quarter, inside = divmod(at, per)
        size = min(count, per - inside)
        pieces.append(source[quarter, inside : inside + size, :])
        at += size
        count -= size
    return pieces[0] if len(pieces) == 1 else jnp.concatenate(pieces, axis=0)


def lane_row(block):
    return jnp.concatenate([block[place : place + 1] for place in range(block.shape[0])], axis=1)


def last_fold_kernel(up_keep, up_got, rest_keep, rest_got, out):
    f32, low = jnp.float32, jnp.bfloat16
    width = up_keep.shape[2]
    wide = width + rest_keep.shape[2]
    out[:, :width] = (up_keep[0] + up_got[0].astype(f32)).astype(low)
    out[:, width:wide] = (rest_keep[0] + rest_got[0].astype(f32)).astype(low)
    out[:, wide:] = jnp.zeros((out.shape[0], out.shape[1] - wide), low)


def finish_kernel(batch, channels, batch_index, *refs):
    entries = refs[:batch]
    (
        in_out,
        pre_gain_out,
        pre_bias_out,
        out_bias_out,
        post_gain_out,
        post_bias_out,
        down_bias_out,
        up_bias_out,
        third_out,
        inner_out,
        pos_out,
        pos_bias_out,
        inner_bias_out,
        third_bias_out,
        freq_out,
        taps_out,
        tap_bias_out,
        in_bias_out,
        filter_out,
        rates_out,
        skips_out,
        held,
        small,
    ) = refs[batch:]
    f32 = jnp.float32
    for bits in range(batch):
        held[batch_index[0] ^ bits] = entries[bits][...]
    in_rows = in_out.shape[0] // batch
    width = pre_gain_out.shape[0]
    parts = width // channels
    total = parts * 3 * in_rows
    rows = small.shape[1]
    for place in range(batch):
        small[place] = held[place, total : total + rows, :].astype(f32) + held[
            place, total + rows :, :
        ].astype(f32)

    def gather(place, carry):
        block = held[place, :total, :].astype(f32)
        tiles = []
        for group in range(3):
            for part in range(parts):
                at = (part * 3 + group) * in_rows
                tiles.append(block[at : at + in_rows, :channels])
        in_out[pl.ds(pl.multiple_of(place * in_rows, in_rows), in_rows), :] = jnp.concatenate(
            tiles, axis=1
        )
        return carry

    lax.fori_loop(0, batch, gather, 0)
    everywhere = small.at[:, :SHARED_ROWS, :]
    per = width // LANES
    at = 0
    for target in (
        pre_gain_out,
        pre_bias_out,
        out_bias_out,
        post_gain_out,
        post_bias_out,
        down_bias_out,
        up_bias_out,
    ):
        count = target.shape[0] // LANES
        target[...] = lane_row(take_rows(everywhere, at, count)).reshape(target.shape)
        at += count
    fhid = third_out.shape[0]
    pair = take_rows(everywhere, at, fhid)
    third_out[...] = pair[:, :fhid]
    inner_out[...] = pair[:, fhid : 2 * fhid]
    at += fhid
    tail = take_rows(everywhere, at, pos_out.shape[0] + 4)
    pos_out[...] = tail[: pos_out.shape[0], :fhid]
    for place, target in enumerate((pos_bias_out, inner_bias_out, third_bias_out, freq_out)):
        row = pos_out.shape[0] + place
        target[...] = tail[row : row + 1, :fhid].reshape(target.shape)

    def laid(number):
        place, row = divmod(number, LAID_ROWS)
        return [
            small[place, SHARED_ROWS + part * LAID_ROWS + row :][:1, :channels]
            for part in range(parts)
        ]

    for number in range(5):
        tiles = [tile for group in range(3) for tile in laid(3 * number + group)]
        row = jnp.concatenate(tiles, axis=1)
        if number < 3:
            taps_out[number : number + 1, :] = row
        elif number == 3:
            tap_bias_out[...] = row.reshape(tap_bias_out.shape)
        else:
            in_bias_out[...] = row.reshape(in_bias_out.shape)
    own = small.at[:, SHARED_ROWS + parts * LAID_ROWS :, :]
    for order in range(2):
        filter_out[order] = take_rows(own, order * fhid, fhid)[:, :channels]
    rates_out[...] = take_rows(own, 2 * fhid, 2)[:, :channels]
    skips_out[...] = take_rows(own, 2 * fhid + 2, 2)[:, :channels]


def swapped(value, axis, bits):
    count = lax.axis_size(axis)
    return lax.ppermute(value, axis, [(source, source ^ bits) for source in range(count)])


def over_batch(value):
    held = {0: value}
    bits = lax.axis_size("batch") // 2
    while bits:
        held.update({place ^ bits: swapped(member, "batch", bits) for place, member in held.items()})
        bits //= 2
    return [held[place] for place in range(len(held))]


def natural(entries, index):
    stacked = jnp.stack(entries)
    return [
        lax.dynamic_index_in_dim(stacked, index ^ place, 0, keepdims=False)
        for place in range(len(entries))
    ]


def halves(total, index, bits, left):
    shape = total.shape[1:]
    place = left.index(bits)
    before = 1 << (len(left) - 1 - place)
    after = 1 << place
    view = total.reshape((before, 2, after) + shape)
    bit = (index // bits) % 2
    keep = lax.dynamic_index_in_dim(view, bit, 1, keepdims=False)
    send = lax.dynamic_index_in_dim(view, 1 - bit, 1, keepdims=False)
    return keep.reshape((before * after,) + shape), send.reshape((before * after,) + shape)


def halved(total, axis, index, order):
    count = lax.axis_size(axis)
    left = [1 << k for k in range(count.bit_length() - 1)]
    for bits in order:
        keep, send = halves(total, index, bits, left)
        got = swapped(send.astype(jnp.bfloat16), axis, bits)
        total = keep + got.astype(jnp.float32)
        left.remove(bits)
    return total[0]


def dense_device(
    inputs,
    pre_gain,
    pre_bias,
    in_weight,
    input_projection_bias,
    short_weight,
    short_bias,
    pos_weight,
    pos_bias,
    inner_weight,
    inner_bias,
    filter_third_weight,
    third_bias,
    sine_freq,
    filter_weight,
    decay_rates,
    skip_gains,
    out_weight,
    out_bias,
    post_gain,
    post_bias,
    up_weight,
    up_bias,
    down_weight,
    down_bias,
    cotangent,
):
    seq_parts = lax.axis_size("seq")
    batch_parts = lax.axis_size("batch")
    seq_rank = lax.axis_index("seq")
    batch_rank = lax.axis_index("batch")
    tokens = inputs[0]
    tok_count, width = tokens.shape
    length = tok_count * seq_parts
    channels = width // seq_parts
    hidden_units = up_weight.shape[1]
    fhid = pos_weight.shape[1]
    f32, low = jnp.float32, jnp.bfloat16
    wide = 3 * LANES
    start = seq_rank * channels
    bit_list = [1 << k for k in range(seq_parts.bit_length() - 1)]
    swap_list = [bit_list[1], bit_list[0]] + bit_list[2:]
    batch_bits = [1 << k for k in range(batch_parts.bit_length() - 1)]

    tokens, grad_top, own_normed = call_kernel(
        norm_kernel,
        [((tok_count, width), low)] * 3,
        [tokens, cotangent[0], pre_gain, pre_bias],
        micros=1,
        scratch=[((width // LANES, tok_count, LANES), f32)],
        name="norm",
    )
    chunks = {0: own_normed}
    for bits in range(2, seq_parts, 2):
        chunks[bits] = swapped(own_normed, "seq", bits)

    quarters = hidden_units // width
    half = length // 2
    seq_scalar = seq_rank.astype(jnp.int32)[None]
    batch_scalar = batch_rank.astype(jnp.int32)[None]
    start_scalar = start.astype(jnp.int32)[None]
    wave, turn, rows, in_local, rows_local, weights_local, rates_local, vectors = call_kernel(
        lambda *refs: wave_kernel(channels, *refs),
        [
            ((length, half), low),
            ((length, LANES), f32),
            ((ROW_COUNT, width), f32),
            ((width, wide), low),
            ((ROW_COUNT, LANES), f32),
            ((fhid, 2 * LANES), f32),
            ((1, 2 * LANES), f32),
            ((4, fhid), f32),
        ],
        [
            start_scalar,
            pre_gain,
            pre_bias,
            input_projection_bias,
            short_bias,
            short_weight,
            skip_gains,
            post_gain,
            post_bias,
            out_bias,
            down_bias,
            up_bias,
            pos_bias,
            inner_bias,
            third_bias,
            sine_freq,
            filter_weight,
            decay_rates,
            in_weight,
        ],
        micros=8.5,
        spaces="s" + "v" * 17 + "h" + "h" + "v" * 7,
        scratch=[
            ((4, 32, half), f32),
            ((length, half), low),
            ((width, 3 * width), low),
            2,
        ],
        name="waves",
    )
    early = [bits for bits in (0, 2) if bits < seq_parts]
    for bits in early:
        chunks[bits + 1] = swapped(chunks[bits], "seq", 1)
    places = sorted(place for place in chunks if place)
    wave, *gathered = lax.optimization_barrier((wave, *[chunks[place] for place in places]))
    chunks.update(zip(places, gathered))
    for bits in range(4, seq_parts, 2):
        chunks[bits + 1] = swapped(chunks[bits], "seq", 1)
    spectrum, kernels, filter_waves = call_kernel(
        filter_kernel,
        [
            ((2, length, 2 * LANES), f32),
            ((length, 2 * LANES), f32),
            ((3, half, 4 * fhid), f32),
        ],
        [
            pos_weight,
            inner_weight,
            filter_third_weight,
            vectors,
            weights_local,
            rates_local,
            turn,
            wave,
        ],
        micros=13,
        spaces="v" * 7 + "h" + "vvv",
        scratch=[
            ((length, 2 * LANES), low),
            ((length, 2 * LANES), low),
            ((length, half), low),
            1,
        ],
        name="filters",
    )
    dense = tok_count * channels // LANES
    (
        normed,
        projected,
        product,
        gate,
        after,
        gated,
        product_wave,
        gated_wave,
        mixed,
        mixer_chan,
    ) = call_kernel(
        lambda *refs: front_kernel(seq_parts, *refs),
        [
            ((length, width), low),
            ((2, PAD + half, wide), f32),
            ((half, 2 * LANES), low),
            ((half, 2 * LANES), low),
            ((half, 2 * LANES), low),
            ((half, 2 * LANES), low),
            ((2, length, LANES), f32),
            ((2, length, LANES), f32),
            ((2, half, 2 * LANES), f32),
            ((seq_parts, dense, LANES), low),
        ],
        [seq_scalar]
        + [chunks[part] for part in range(seq_parts)]
        + [in_local, rows_local, wave, turn, spectrum],
        micros=13,
        spaces="s" + "v" * seq_parts + "vvhhh" + "hhhhhhhhhv",
        scratch=[((half, 2 * LANES), low)] * 4
        + [
            ((length, width), low),
            ((half, 2 * LANES), low),
            ((half, 2 * LANES), low),
            ((length, half), low),
            ((length, LANES), f32),
            ((2, length, 2 * LANES), f32),
            ((2, PAD + half, wide), f32),
            ((2, length, LANES), f32),
            ((2, length, LANES), f32),
            ((2, half, 2 * LANES), f32),
            ((half, 2 * LANES), low),
            12,
        ],
        name="front",
    )
    tops = over_batch(grad_top)
    mixer_back = lax.all_to_all(mixer_chan, "seq", 0, 0, tiled=True)
    mixer_back, *tops = lax.optimization_barrier((mixer_back, *tops))

    quarter = hidden_units // batch_parts
    branch_quarter = width // batch_parts
    rows_quarter = hidden_units // (seq_parts * batch_parts)
    assert quarter == width and seq_parts * rows_quarter == width
    up_width = quarter + branch_quarter
    padded = quarter + -(-branch_quarter // LANES) * LANES
    message = padded + width
    outputs, grad_residual, grad_mixer, middle_sums, sides, *gots = call_kernel(
        lambda *refs: middle_kernel(seq_parts, *refs),
        [
            ((tok_count, width), f32),
            ((tok_count, width), f32),
            ((seq_parts, dense, LANES), low),
            (((4 * width + hidden_units) // LANES, LANES), f32),
        ]
        + [((tok_count, 2 * width), low)]
        + [((tok_count, message), low)] * batch_parts,
        [
            batch_scalar,
            mixer_back,
            tokens,
            grad_top,
            rows,
            out_weight,
            up_weight,
            down_weight,
        ],
        micros=11,
        spaces="svvvvhhh" + "v" * (5 + batch_parts),
        scratch=[
            ((width, width), low),
            ((quarters, width, width), low),
            ((quarters, width, width), low),
            ((tok_count, width), f32),
            ((tok_count, width), f32),
            ((tok_count, width), f32),
            ((quarters, tok_count, width), low),
            ((quarters, tok_count, width), low),
            ((batch_parts, tok_count, width), low),
            ((batch_parts, tok_count, padded - quarter), low),
            ((quarters, 1, width), f32),
            ((width // LANES, tok_count, LANES), f32),
            1 + 2 * quarters,
        ],
        name="middle",
    )
    grad_mixer_chan = lax.all_to_all(grad_mixer, "seq", 0, 0, tiled=True)

    def bit_of(bits):
        return ((seq_rank // bits) % 2).astype(jnp.int32)[None]

    def fold(keep, got, bits, left):
        size = keep.shape[0] // 2
        block = keep.shape[1:]
        place = left.index(bits)
        return call_kernel(
            lambda *refs: fold_kernel(1 << place, *refs),
            [((size,) + block, f32), ((size,) + block, low)],
            [bit_of(bits), keep, got],
            micros=1,
            spaces="svvvv",
            limit=12,
        name="fold",
        )

    grad_mixer_chan = lax.all_to_all(grad_mixer, "seq", 0, 0, tiled=True)
    sides = over_batch(sides)
    gots = [gots[0]] + [swapped(gots[bits], "batch", bits) for bits in range(1, batch_parts)]
    rows_each = width // seq_parts

    blocks = length // BLOCK
    packed, grad_proj, grad_kernels, sums = call_kernel(
        lambda *refs: back_kernel(channels, *refs),
        [
            ((seq_parts, 3 * dense, LANES), low),
            ((length, wide), low),
            ((2, half, 2 * LANES), f32),
            ((24, LANES), f32),
        ],
        [
            grad_mixer_chan,
            rows_local,
            product,
            gate,
            after,
            gated,
            turn,
            product_wave,
            gated_wave,
            spectrum,
            wave,
            projected,
            mixed,
        ],
        micros=15,
        spaces="vv" + "h" * 11 + "vvvv",
        scratch=[((half, 2 * LANES), low)] * 8
        + [
            ((length, LANES), f32),
            ((half, 4 * LANES), low),
            ((half, 4 * LANES), low),
            ((length, half), low),
            ((2, length, 2 * LANES), f32),
            ((2, length, LANES), f32),
            ((2, length, LANES), f32),
            ((2, PAD + half, wide), f32),
            ((2, half, 2 * LANES), f32),
            ((3, 2, half + PAD, LANES), f32),
            11,
        ],
        name="back",
    )
    proj_back = lax.all_to_all(packed, "seq", 0, 0, tiled=True)
    orders = (bit_list, swap_list)
    halves_of = [
        ((seq_parts // 2, rows_each, columns), dtype)
        for columns in (width, width + branch_quarter)
        for dtype in (f32, low)
    ]
    up_keep, up_send, rest_keep, rest_send = call_kernel(
        lambda *refs: weight_kernel(batch_parts, (orders[0][0], orders[1][0]), *refs),
        halves_of,
        [jnp.concatenate([bit_of(order[0]) for order in orders])] + sides + tops + gots,
        micros=6,
        spaces="s" + "v" * (3 * batch_parts + 4),
        scratch=[
            ((3 * width, batch_parts * tok_count), low),
            ((batch_parts * tok_count, width + padded), low),
            ((width, width), f32),
            ((width, width + branch_quarter), f32),
        ],
        name="weights",
    )
    up_got = swapped(up_send, "seq", orders[0][0])
    rest_got = swapped(rest_send, "seq", orders[1][0])

    pair_part = left_dot(normed, grad_proj)
    in_rows = width // (seq_parts * batch_parts)
    in_count = 3 * in_rows
    in_part = (
        pair_part.reshape(seq_parts, batch_parts, in_rows, 3, LANES)
        .transpose(1, 0, 3, 2, 4)
        .reshape(batch_parts, seq_parts * in_count, LANES)
    )
    small_rows = SHARED_ROWS + LAID_ROWS + OWN_ROWS
    in_part, pair_part, up_keep, rest_keep = lax.optimization_barrier(
        (in_part, pair_part, up_keep, rest_keep)
    )
    (small,) = call_kernel(
        chain_kernel,
        [((batch_parts, small_rows, LANES), f32)],
        [
            rows,
            in_local,
            sums,
            middle_sums,
            pos_weight,
            inner_weight,
            filter_third_weight,
            vectors,
            weights_local,
            rates_local,
            grad_kernels.reshape(length, 2 * LANES),
            kernels,
            filter_waves,
            pair_part,
        ],
        micros=12,
        spaces="v" * 10 + "hhhh" + "v",
        scratch=[
            ((2 * fhid, 4 * LANES), f32),
            ((1, 2 * LANES), f32),
            ((2 * fhid + 40, fhid), f32),
            ((3, LANES + 8, 2 * fhid), f32),
            ((length, 2 * LANES), f32),
            ((length, 2 * LANES), f32),
            ((3, length // 2, 4 * fhid), f32),
            ((width, wide), f32),
            5 * (blocks // 2) + 1,
        ],
        name="chain",
    )
    small, proj_back = lax.optimization_barrier((small, proj_back))

    def next_fold(keep, got, order, step):
        left = [bits for bits in bit_list if bits not in order[:step]]
        return fold(keep, got, order[step], left)

    left = list(batch_bits)
    for bits in batch_bits[:-1]:
        in_keep, in_send = halves(in_part, batch_rank, bits, left)
        small_keep, small_send = halves(small, batch_rank, bits, left)
        in_part = in_keep + swapped(in_send.astype(low), "batch", bits).astype(f32)
        small = small_keep + swapped(small_send, "batch", bits)
        left.remove(bits)
    in_keep, in_send = halves(in_part, batch_rank, batch_bits[-1], left)
    small_keep, small_send = halves(small, batch_rank, batch_bits[-1], left)
    shared_count = in_count + 2 * (SHARED_ROWS + LAID_ROWS)
    mixed_send, small = call_kernel(
        spread_kernel,
        [((seq_parts, shared_count, LANES), low), ((small_rows, LANES), f32)],
        [
            in_keep[0],
            swapped(in_send.astype(low), "batch", batch_bits[-1])[0],
            small_keep[0],
            swapped(small_send, "batch", batch_bits[-1])[0],
        ],
        micros=2,
        limit=12,
        name="spread",
    )
    up_keep, up_send = next_fold(up_keep, up_got, orders[0], 1)
    rest_keep, rest_send = next_fold(rest_keep, rest_got, orders[1], 1)
    up_got = swapped(up_send, "seq", orders[0][1])
    rest_got = swapped(rest_send, "seq", orders[1][1])
    mixed_send, proj_back = lax.optimization_barrier((mixed_send, proj_back))
    mixed_got = lax.all_to_all(mixed_send, "seq", 0, 0, tiled=True)
    (grad_inputs,) = call_kernel(
        final_kernel,
        [((tok_count, width), f32)],
        [proj_back, tokens, grad_residual, rows, in_weight],
        micros=5.5,
        spaces="vvvvhv",
        scratch=[
            ((width, 3 * width), low),
            ((tok_count, 3 * width), low),
            ((width // LANES, tok_count, LANES), f32),
            1,
        ],
        name="final",
    )
    done_rows = SHARED_ROWS + seq_parts * LAID_ROWS + OWN_ROWS
    (last,) = call_kernel(
        merge_kernel,
        [((seq_parts * in_count + 2 * done_rows, LANES), low)],
        [mixed_got, small],
        micros=2,
        limit=12,
        name="merge",
    )
    up_keep, up_send = next_fold(up_keep, up_got, orders[0], 2)
    rest_keep, rest_send = next_fold(rest_keep, rest_got, orders[1], 2)
    up_got = swapped(up_send, "seq", orders[0][2])
    rest_got = swapped(rest_send, "seq", orders[1][2])
    lasts = over_batch(last)
    up_got, grad_inputs, last = lax.optimization_barrier((up_got, grad_inputs, last))
    total = -(-(2 * width + branch_quarter) // LANES) * LANES
    (weights_done,) = call_kernel(
        last_fold_kernel,
        [((rows_each, total), low)],
        [up_keep, up_got, rest_keep, rest_got],
        micros=1,
        limit=12,
        name="last_fold",
    )
    (
        final_in,
        grad_pre_gain,
        grad_pre_bias,
        grad_out_bias,
        grad_post_gain,
        grad_post_bias,
        grad_down_bias,
        grad_up_bias,
        grad_third,
        grad_inner,
        grad_pos,
        grad_pos_bias,
        grad_inner_bias,
        grad_third_bias,
        grad_freq,
        grad_taps,
        grad_tap_bias,
        grad_in_bias,
        grad_filter,
        grad_rates,
        grad_skips,
    ) = call_kernel(
        lambda *refs: finish_kernel(batch_parts, channels, *refs),
        [
            ((batch_parts * in_rows, 3 * width), f32),
            ((width,), f32),
            ((width,), f32),
            ((width,), f32),
            ((width,), f32),
            ((width,), f32),
            ((width,), f32),
            ((hidden_units,), f32),
            (filter_third_weight.shape, f32),
            (inner_weight.shape, f32),
            (pos_weight.shape, f32),
            ((fhid,), f32),
            ((fhid,), f32),
            ((fhid,), f32),
            ((fhid,), f32),
            ((3, 3 * width), f32),
            ((3 * width,), f32),
            ((3 * width,), f32),
            ((2, fhid, channels), f32),
            ((2, channels), f32),
            ((2, channels), f32),
        ],
        [batch_scalar] + lasts,
        micros=3,
        spaces="s" + "v" * batch_parts + "v" * 21,
        scratch=[
            ((batch_parts,) + last.shape, low),
            ((batch_parts, done_rows, LANES), f32),
        ],
        limit=12,
        name="finish",
    )
    entries = {0: weights_done, batch_parts // 2: swapped(weights_done, "batch", batch_parts // 2)}
    entries[batch_parts // 2], final_in = lax.optimization_barrier(
        (entries[batch_parts // 2], final_in)
    )
    bits = batch_parts // 4
    while bits:
        entries.update(
            {place ^ bits: swapped(member, "batch", bits) for place, member in entries.items()}
        )
        bits //= 2
    entries = [entries[place] for place in range(batch_parts)]
    final_down, final_up, final_out = call_kernel(
        lambda *refs: collect_kernel(batch_parts, *refs),
        [
            ((batch_parts * rows_each, width), f32),
            ((rows_each, hidden_units), f32),
            ((rows_each, width), f32),
        ],
        [batch_scalar] + entries,
        micros=3,
        spaces="s" + "v" * (batch_parts + 3),
        scratch=[((batch_parts, rows_each, total), low)],
        limit=12,
        name="collect",
    )
    return (
        outputs[None],
        grad_inputs[None],
        grad_pre_gain,
        grad_pre_bias,
        final_in,
        grad_in_bias,
        grad_taps,
        grad_tap_bias,
        grad_pos,
        grad_pos_bias,
        grad_inner,
        grad_inner_bias,
        grad_third,
        grad_third_bias,
        grad_freq,
        grad_filter,
        grad_rates,
        grad_skips,
        final_out,
        grad_out_bias,
        grad_post_gain,
        grad_post_bias,
        final_up,
        grad_up_bias,
        final_down,
        grad_down_bias,
    )


def per_device(*args):
    tokens, parts = args[0].shape[1], lax.axis_size("seq")
    channels = args[0].shape[2] // parts
    dense = tokens * parts <= DENSE_LIMIT and lays_dense(tokens, channels)
    return (dense_device if dense else factored_device)(*args)


def solution(mesh):
    in_specs = (
        P("batch", "seq", None),
        P(),
        P(),
        P(),
        P(),
        P(),
        P(),
        P(),
        P(),
        P(),
        P(),
        P(),
        P(),
        P(),
        P(),
        P(),
        P(),
        P(),
        P(),
        P(),
        P(),
        P(),
        P(),
        P(),
        P(),
        P("batch", "seq", None),
    )
    out_specs = (
        P("batch", "seq", None),
        P("batch", "seq", None),
        P(),
        P(),
        P("seq", None),
        P(),
        P(),
        P(),
        P(),
        P(),
        P(),
        P(),
        P(),
        P(),
        P(),
        P(None, None, "seq"),
        P(None, "seq"),
        P(None, "seq"),
        P("seq", None),
        P(),
        P(),
        P(),
        P("seq", None),
        P(),
        P("seq", None),
        P(),
    )
    return jax.shard_map(
        per_device, mesh=mesh, in_specs=in_specs, out_specs=out_specs, check_vma=False
    )
```
